128 devices in a mesh: sx: 16 (over z, x), sy: 8 (over y, core).
Axes of the slice: x: 4, y: 4, z: 4, core: 2. Of those that a mesh axis runs over, the one named last changes fastest.
Arguments:
- features: bfloat16 [128, 128, 32, 256], P('sx', 'sy'), may hold values from -6 to 6
- conv_weight: bfloat16 [27, 32, 32], replicated, may hold values from -0.21875 to 0.21875
- conv_bias: float32 [32], replicated, may hold values from -3 to 3
- occupancy: int32 [128, 128, 256], P('sx', 'sy'), may hold values 0 or 1
- block_ids: int32 [128, 128, 2, 27], P('sx', 'sy'), may hold values from -1 to 32767, as said below
- ridge: float32 [128, 128, 256], P('sx', 'sy'), may hold values from 0.5 to 2
- target: float32 [128, 128, 256], P('sx', 'sy'), may hold values from -6 to 6
Outputs:
- solution: float32 [128, 128, 256], P('sx', 'sy')
- residual: float32 [128, 128, 256], P('sx', 'sy')
The draws below stay inside these ranges and needn't reach their ends.
Inputs may be any that keep to these rules, and one draw needn't show every extreme that they name: `block_ids`: entry t of block (x, y, z) is the id (x' 128 + y') * 2 + z' of the block (x', y', z') = (x + a, y + b, z + c) at offset t when that block lies in the grid and is present, else -1; a block is present exactly when its own entry 13 is its id, and every entry naming a block agrees on its presence.
All inputs are finite; a program needn't handle non-finite values. No bound on the sum of `occupancy` on one device may be relied on, other than what follows from the above.
Results may differ from the reference program's by a relative error of at most 0.0047.
Values may be sent and summed in bfloat16 or wider, within the bound.
No kernel may reach another device: no remote copies, remote signals or barrier semaphores. Data moves between devices by JAX's collectives and lax.ppermute only.
A program may use at most 192 MiB of HBM per device.

```python
import math
import jax
import jax.numpy as jnp
from jax import lax

C = 32
VOX = 128
TZ = 2
ITERS = 2
GX = 128
GY = 128
DEPTH = 256


def draw_block_ids(key, part):
    level_draw = jax.random.randint(key, (GX, GY, TZ), 0, 3 * GX)
    coord_x = jnp.arange(GX, dtype=jnp.int32)[:, None, None]
    coord_y = jnp.arange(GY, dtype=jnp.int32)[None, :, None]
    coord_z = jnp.arange(TZ, dtype=jnp.int32)[None, None, :]
    present = level_draw < GX + 2 * coord_x
    last_block = (coord_x == GX - 1) & (coord_y == GY - 1) & (coord_z == TZ - 1)
    present = present | last_block
    block_id = (coord_x * GY + coord_y) * TZ + coord_z
    listed = jnp.where(present, block_id, -1).astype(jnp.int32)
    padded = jnp.pad(listed, 1, constant_values=-1)
    columns = []
    for off_x in (-1, 0, 1):
        for off_y in (-1, 0, 1):
            for off_z in (-1, 0, 1):
                columns.append(padded[1 + off_x:1 + off_x + GX, 1 + off_y:1 + off_y + GY, 1 + off_z:1 + off_z + TZ])
    return jnp.stack(columns, axis=-1).astype(jnp.int32)


def place_ends(drawn, rng, low, top_value):
    place = [jax.random.randint(jax.random.fold_in(rng, axis), (), 0, length) for axis, length in enumerate(drawn.shape)]
    longest = drawn.shape.index(max(drawn.shape))
    next_to = place[:longest] + [(place[longest] + 1) % drawn.shape[longest]] + place[longest + 1:]
    return drawn.at[tuple(place)].set(low).at[tuple(next_to)].set(top_value)


def block_levels(own_key, dims, shards, low, top_value):
    def one(dim, blocks):
        heights = jax.random.uniform(jax.random.fold_in(jax.random.fold_in(own_key, 6), dim), (blocks,), jnp.float32, low / len(shards), top_value / len(shards))
        return jnp.repeat(jnp.exp(heights), dims[dim] // blocks).reshape((-1,) + (1,) * (len(dims) - dim - 1))

    loudness = one(*shards[0])
    for cut in shards[1:]:
        loudness = loudness * one(*cut)
    return loudness


def scatter_about(rng, shape, width, limit, pieces=(), held_as=jnp.bfloat16):
    level = block_levels(rng, shape, pieces, -0.22, 0.18) if pieces else 1.0
    values = jax.random.normal(rng, shape, jnp.float32) * width * level
    return jnp.minimum(jnp.maximum(values, -limit), limit).astype(held_as)


def setup_inputs(seed: int = 0) -> dict:
    streams_of = jax.random.split(jax.random.key(seed), 8)
    return {
        "features": scatter_about(streams_of[0], (GX, GY, C, DEPTH), 1.0, 6.0, ((0, 16), (1, 8))),
        "conv_weight": scatter_about(streams_of[1], (27, C, C), (27 * C) ** -0.5, 0.21875),
        "conv_bias": scatter_about(streams_of[2], (C,), 0.5, 3.0, (), jnp.float32),
        "occupancy": place_ends((jax.random.randint(streams_of[3], (GX, GY, DEPTH), 0, 4) < 3).astype(jnp.int32), jax.random.fold_in(streams_of[3], 1), 0, 1),
        "block_ids": draw_block_ids(jax.random.fold_in(streams_of[7], 71), 0),
        "ridge": jnp.clip(jnp.exp(math.log(2.0) - 1.3862944 * jax.random.uniform(streams_of[5], (GX, GY, DEPTH), jnp.float32) ** block_levels(streams_of[5], (GX, GY, DEPTH), ((0, 16), (1, 8)), -0.2, 0.2)), 0.5, 2.0),
        "target": scatter_about(streams_of[6], (GX, GY, DEPTH), 1.0, 6.0, ((0, 16), (1, 8)), jnp.float32),
    }


def offset_list():
    return [(off_x, off_y, off_z) for off_x in (-1, 0, 1) for off_y in (-1, 0, 1) for off_z in (-1, 0, 1)]


def spline_weight(off_x, off_y, off_z):
    return 0.5 ** (abs(off_x) + abs(off_y) + abs(off_z))


def reference(features, conv_weight, conv_bias, occupancy, block_ids, ridge, target):
    present = (block_ids[:, :, :, 13] >= 0).astype(jnp.float32)
    weight_mask = occupancy.astype(jnp.float32) * jnp.repeat(present, VOX, axis=2)
    masked = features * weight_mask.astype(jnp.bfloat16)[:, :, None, :]
    padded = jnp.pad(masked, ((1, 1), (1, 1), (0, 0), (1, 1)))
    kernel_full = conv_weight.astype(jnp.float32)
    bias_col = conv_bias.astype(jnp.float32)[None, :, None]
    slabs = jnp.arange(GX, dtype=jnp.int32)

    def conv_slab(index):
        rows = lax.dynamic_slice_in_dim(padded, index, 3, 0).astype(jnp.float32)
        total = jnp.zeros((GY, C, DEPTH), jnp.float32)
        for tap, (off_x, off_y, off_z) in enumerate(offset_list()):
            window_part = rows[off_x + 1, off_y + 1:off_y + 1 + GY, :, off_z + 1:off_z + 1 + DEPTH]
            total = total + jnp.einsum("oi,yiz->yoz", kernel_full[tap], window_part)
        mask_row = lax.dynamic_index_in_dim(weight_mask, index, 0, keepdims=False)
        return (mask_row[:, None, :] * (total + bias_col)).astype(jnp.bfloat16)

    feature_field = lax.map(conv_slab, slabs)
    field_pad = jnp.pad(feature_field, ((1, 1), (1, 1), (0, 0), (1, 1)))

    def operate(values):
        value_pad = jnp.pad(values, ((1, 1), (1, 1), (1, 1)))

        def apply_slab(index):
            field_rows = lax.dynamic_slice_in_dim(field_pad, index, 3, 0).astype(jnp.float32)
            value_rows = lax.dynamic_slice_in_dim(value_pad, index, 3, 0)
            center = field_rows[1, 1:1 + GY, :, 1:1 + DEPTH]
            total = lax.dynamic_index_in_dim(ridge, index, 0, keepdims=False) * lax.dynamic_index_in_dim(values, index, 0, keepdims=False)
            for off_x, off_y, off_z in offset_list():
                beside = field_rows[off_x + 1, off_y + 1:off_y + 1 + GY, :, off_z + 1:off_z + 1 + DEPTH]
                coupling = jnp.sum(center * beside, axis=1) * (spline_weight(off_x, off_y, off_z) / C)
                total = total + coupling * value_rows[off_x + 1, off_y + 1:off_y + 1 + GY, off_z + 1:off_z + 1 + DEPTH]
            return total

        return lax.map(apply_slab, slabs)

    residual = weight_mask * target
    solution = jnp.zeros_like(residual)
    direction = residual
    norm_now = jnp.sum(residual * residual)
    for step in range(ITERS):
        image = operate(direction)
        alpha = norm_now / jnp.sum(direction * image)
        solution = solution + alpha * direction
        residual = residual - alpha * image
        norm_next = jnp.sum(residual * residual)
        direction = residual + (norm_next / norm_now) * direction
        norm_now = norm_next
    return solution, residual
```

```python
import jax
import jax.numpy as jnp
from jax import lax
from jax.experimental import pallas as pl
from jax.experimental.pallas import tpu as pltpu
from jax.sharding import PartitionSpec as P

AXES = ("sx", "sy")
VMEM_LIMIT = 56 * 1024 * 1024


def shift(value, axis, step):
    peers = lax.axis_size(axis)
    return lax.ppermute(value, axis, [(i, (i + step) % peers) for i in range(peers)])


def halo(value, axis, dim, width):
    length = value.shape[dim]
    before = shift(lax.slice_in_dim(value, length - width, length, axis=dim), axis, 1)
    after = shift(lax.slice_in_dim(value, 0, width, axis=dim), axis, -1)
    return before, after


def clear_ends(before, after, axis):
    where = lax.axis_index(axis)
    before = jnp.where(where == 0, jnp.zeros_like(before), before)
    after = jnp.where(where == lax.axis_size(axis) - 1, jnp.zeros_like(after), after)
    return before, after


def extend(value, axis, dim, width):
    before, after = clear_ends(*halo(value, axis, dim, width), axis)
    return jnp.concatenate([before, value, after], axis=dim)


def block_weights(conv_weight):
    channels = conv_weight.shape[1]
    taps = conv_weight.reshape(3, 3, 3, channels, channels).transpose(2, 3, 0, 1, 4)
    rows = []
    for out_x in range(2):
        for out_y in range(2):
            rows.append(
                jnp.pad(taps, ((0, 0), (0, 0), (out_x, 1 - out_x), (out_y, 1 - out_y), (0, 0)))
            )
    block = jnp.stack(rows, axis=1)
    return block.reshape(3 * 4 * channels, 16 * channels)


def conv_kernel(own, y_lo, y_hi, x_lo, x_hi, mask, weights, bias, out, grid, sems):
    rows, cols = (own.shape[0], own.shape[1])
    channels, depth = (own.shape[2], own.shape[3])
    copies = [
        pltpu.make_async_copy(own, grid.at[2 : 2 + rows, 1 : 1 + cols], sems.at[0]),
        pltpu.make_async_copy(y_lo, grid.at[2 : 2 + rows, 0:1], sems.at[1]),
        pltpu.make_async_copy(y_hi, grid.at[2 : 2 + rows, 1 + cols : 2 + cols], sems.at[2]),
        pltpu.make_async_copy(x_lo, grid.at[0:2], sems.at[3]),
        pltpu.make_async_copy(x_hi, grid.at[2 + rows : 4 + rows], sems.at[4]),
    ]
    for copy in copies:
        copy.start()
    for copy in copies:
        copy.wait()

    def mask_row(x, carry):
        for y in range(cols + 2):
            keep = mask[x, y : y + 1, :].astype(jnp.bfloat16)
            grid[x, y] = grid[x, y] * keep
        return carry

    lax.fori_loop(0, rows + 4, mask_row, 0)
    lane = lax.broadcasted_iota(jnp.int32, (4 * channels, depth), 1)
    bias_all = jnp.broadcast_to(bias[...], (channels, depth))
    wide = weights[...]

    def block(step, carry):
        i = step // (cols // 2)
        j = step % (cols // 2)
        window = jnp.concatenate(
            [grid[2 * i + k, pl.ds(2 * j, 4)].reshape(4 * channels, depth) for k in range(4)], axis=0
        )
        parts = jnp.dot(wide, window, preferred_element_type=jnp.float32)
        low = pltpu.roll(parts[0 : 4 * channels], 1, 1)
        high = pltpu.roll(parts[8 * channels :], depth - 1, 1)
        total = parts[4 * channels : 8 * channels]
        total = total + jnp.where(lane == 0, 0.0, low) + jnp.where(lane == depth - 1, 0.0, high)
        for out_x in range(2):
            for out_y in range(2):
                at = (out_x * 2 + out_y) * channels
                keep = mask[2 * i + out_x + 1, pl.ds(2 * j + out_y + 1, 1), :]
                value = keep * (total[at : at + channels] + bias_all)
                out[2 * i + out_x, 2 * j + out_y] = value.astype(jnp.bfloat16)
        return carry

    lax.fori_loop(0, (rows + 2) // 2 * (cols // 2), block, 0)


def two_sum(a, b):
    s = a + b
    t = s - a
    return s, (a - (s - t)) + (b - t)


def split(a):
    c = a * 4097.0
    high = c - (c - a)
    return high, a - high


def two_prod(a, b):
    p = a * b
    a_hi, a_lo = split(a)
    b_hi, b_lo = split(b)
    return p, ((a_hi * b_hi - p) + a_hi * b_lo + a_lo * b_hi) + a_lo * b_lo


def pair_add(a, b):
    s, t = two_sum(a[0], b[0])
    return two_sum(s, t + (a[1] + b[1]))


def pair_scale(a, c):
    p, t = two_prod(a[0], c)
    return two_sum(p, t + a[1] * c)


def apply_rows(field, f_lo, f_hi, values, ridge, out, smooth):
    rows, cols, depth = out.shape
    channels = field.shape[2]

    def along_y(x, carry):
        def product(y):
            ref, at = (f_lo, 0) if y == 0 else (f_hi, 0) if y == cols + 1 else (field, y - 1)
            return ref[x, at].astype(jnp.float32) * values[x, y : y + 1, :]

        last = product(0)
        here = product(1)
        pair = last + here
        for y in range(cols):
            following = product(y + 2)
            pair_next = here + following
            smooth[x, y] = pair + pair_next
            here = following
            pair = pair_next
        return carry

    lax.fori_loop(0, rows + 2, along_y, 0)
    lane = lax.broadcasted_iota(jnp.int32, (channels, depth), 1)

    def along_x(x, carry):
        sums = []
        for y in range(cols):
            mid = smooth[x + 1, y]
            both = (smooth[x, y] + mid) + (mid + smooth[x + 2, y])
            up = jnp.where(lane == depth - 1, 0.0, pltpu.roll(both, depth - 1, 1))
            down = jnp.where(lane == 0, 0.0, pltpu.roll(both, 1, 1))
            both = (both + both) + (up + down)
            prod = both * field[x + 1, y].astype(jnp.float32)
            sums.append(jnp.sum(prod, axis=0, keepdims=True))
        inner = jnp.concatenate(sums, axis=0)
        own = values[x + 1, 1 : 1 + cols, :]
        out[x] = ridge[x] * own + inner * (1.0 / (8 * channels))
        return carry

    lax.fori_loop(0, rows, along_x, 0)


def first_kernel(field, f_lo, f_hi, values, ridge, out, smooth):
    apply_rows(field, f_lo, f_hi, values, ridge, out, smooth)


def second_kernel(field, f_lo, f_hi, values, ridge, start, out, share, smooth):
    apply_rows(field, f_lo, f_hi, values, ridge, out, smooth)
    rows, cols, depth = out.shape
    zero = jnp.zeros((cols, depth), jnp.float32)
    sums = [(zero, zero) for _ in range(5)]
    for x in range(rows):
        w0 = start[x]
        w1 = values[x + 1, 1 : 1 + cols, :]
        w2 = out[x]
        for k, (a, b) in enumerate(((w0, w0), (w0, w1), (w1, w1), (w0, w2), (w1, w2))):
            p, e = two_prod(a, b)
            s, t = two_sum(sums[k][0], p)
            sums[k] = (s, sums[k][1] + (t + e))
    row = jnp.zeros((8, 128), jnp.float32)
    lane = lax.broadcasted_iota(jnp.int32, (8, 128), 1)
    for k, (s, e) in enumerate(sums):
        while s.shape[0] > 8:
            half = s.shape[0] // 2
            t, d = two_sum(s[:half], s[half:])
            s, e = (t, e[:half] + e[half:] + d)
        while s.shape[1] > 128:
            half = s.shape[1] // 2
            t, d = two_sum(s[:, :half], s[:, half:])
            s, e = (t, e[:, :half] + e[:, half:] + d)
        for axis, steps in ((0, (4, 2, 1)), (1, (64, 32, 16, 8, 4, 2, 1))):
            for step in steps:
                t, d = two_sum(s, pltpu.roll(s, step, axis))
                s, e = (t, (e + pltpu.roll(e, step, axis)) + d)
        row = jnp.where(lane == k, s, row)
        row = jnp.where(lane == 8 + k, e, row)
    share[...] = row[0:1]


def final_kernel(shares, start, first, second, solution_out, residual_out):
    s = shares[...]
    e = jnp.zeros_like(s)
    while s.shape[0] > 8:
        half = s.shape[0] // 2
        t, d = two_sum(s[:half], s[half:])
        s, e = (t, e[:half] + e[half:] + d)
    for step in (4, 2, 1):
        t, d = two_sum(s, pltpu.roll(s, step, 0))
        s, e = (t, (e + pltpu.roll(e, step, 0)) + d)
    lane = lax.broadcasted_iota(jnp.int32, s.shape, 1)

    def pick(value, k):
        return jnp.broadcast_to(
            jnp.sum(jnp.where(lane == k, value, 0.0), axis=1, keepdims=True), s.shape
        )

    g00, g01, g11, g02, g12 = [
        two_sum(pick(s, k), pick(e, k) + pick(s, 8 + k)) for k in range(5)
    ]
    alpha = g00[0] / g01[0]
    fresh = pair_add(pair_add(g00, pair_scale(g01, -2.0 * alpha)), pair_scale(pair_scale(g11, alpha), alpha))
    grow = 1.0 + fresh[0] / g00[0]
    curve = pair_add(
        pair_add(
            pair_scale(pair_scale(g01, grow), grow),
            pair_scale(pair_scale(pair_add(g02, g11), -alpha), grow),
        ),
        pair_scale(pair_scale(g12, alpha), alpha),
    )
    beta = fresh[0] / curve[0]
    near = (alpha + beta * grow)[0:1, 0:1]
    far = (alpha * beta)[0:1, 0:1]
    for x in range(start.shape[0]):
        w0, w1, w2 = (start[x], first[x], second[x])
        solution_out[x] = near * w0 - far * w1
        residual_out[x] = (w0 - near * w1) + far * w2


def per_device(features, conv_weight, conv_bias, occupancy, block_ids, ridge, target):
    rows, cols, channels, depth = features.shape
    voxels = depth // block_ids.shape[2]
    f32 = jnp.float32
    vmem = pl.BlockSpec(memory_space=pltpu.VMEM)
    anywhere = pl.BlockSpec(memory_space=pl.ANY)
    params = pltpu.CompilerParams(vmem_limit_bytes=VMEM_LIMIT)

    feat_y = halo(features, "sy", 1, 1)
    edges_lo = jnp.concatenate([feat_y[0][:2], features[:2], feat_y[1][:2]], axis=1)
    edges_hi = jnp.concatenate([feat_y[0][-2:], features[-2:], feat_y[1][-2:]], axis=1)
    feat_x = (shift(edges_hi, "sx", 1), shift(edges_lo, "sx", -1))

    present = (block_ids[:, :, :, 13] >= 0).astype(f32)
    weight_mask = occupancy.astype(f32) * jnp.repeat(present, voxels, axis=2)
    residual = weight_mask * target
    both = jnp.stack([weight_mask, residual])
    both = extend(extend(both, "sy", 2, 1), "sx", 1, 2)
    mask_ext = both[0]
    start_ext = both[1, 1:-1]

    field = pl.pallas_call(
        conv_kernel,
        out_shape=jax.ShapeDtypeStruct((rows + 2, cols, channels, depth), jnp.bfloat16),
        in_specs=[anywhere] * 5 + [vmem] * 3,
        out_specs=vmem,
        scratch_shapes=[
            pltpu.VMEM((rows + 4, cols + 2, channels, depth), jnp.bfloat16),
            pltpu.SemaphoreType.DMA((5,)),
        ],
        compiler_params=params,
        name="conv",
    )(
        features,
        *feat_y,
        *feat_x,
        mask_ext,
        block_weights(conv_weight),
        conv_bias[:, None],
    )
    field_y = halo(field, "sy", 1, 1)

    grid_shape = jax.ShapeDtypeStruct((rows, cols, depth), f32)
    smooth = pltpu.VMEM((rows + 2, cols, channels, depth), f32)
    first = pl.pallas_call(
        first_kernel,
        out_shape=grid_shape,
        in_specs=[vmem] * 5,
        out_specs=vmem,
        scratch_shapes=[smooth],
        compiler_params=params,
        name="first",
    )(field, *field_y, start_ext, ridge)
    first_ext = extend(extend(first, "sy", 1, 1), "sx", 0, 1)
    second, share = pl.pallas_call(
        second_kernel,
        out_shape=(grid_shape, jax.ShapeDtypeStruct((1, 128), f32)),
        in_specs=[vmem] * 6,
        out_specs=(vmem, vmem),
        scratch_shapes=[smooth],
        compiler_params=params,
        name="second",
    )(field, *field_y, first_ext, ridge, residual)

    peers = lax.axis_size("sx") * lax.axis_size("sy")
    shares = lax.all_to_all(jnp.broadcast_to(share[None], (peers, 1, 128)), AXES, 0, 0)
    return pl.pallas_call(
        final_kernel,
        out_shape=(grid_shape, grid_shape),
        in_specs=[vmem] * 4,
        out_specs=(vmem, vmem),
        compiler_params=params,
        name="final",
    )(shares.reshape(peers, 128), residual, first, second)


def solution(mesh):
    placed = (
        P("sx", "sy", None, None),
        P(),
        P(),
        P("sx", "sy", None),
        P("sx", "sy", None, None),
        P("sx", "sy", None),
        P("sx", "sy", None),
    )
    return jax.shard_map(
        per_device,
        mesh=mesh,
        in_specs=placed,
        out_specs=(P("sx", "sy", None), P("sx", "sy", None)),
        check_vma=False,
    )
```

```python
import jax
import jax.numpy as jnp
from jax import lax
from jax.experimental import pallas as pl
from jax.experimental.pallas import tpu as pltpu
from jax.sharding import PartitionSpec as P

AXES = ("sx", "sy")


def shift(value, axis, step):
    peers = lax.axis_size(axis)
    return lax.ppermute(value, axis, [(i, (i + step) % peers) for i in range(peers)])


def halo(value, axis, dim, width):
    length = value.shape[dim]
    before = shift(lax.slice_in_dim(value, length - width, length, axis=dim), axis, 1)
    after = shift(lax.slice_in_dim(value, 0, width, axis=dim), axis, -1)
    return before, after


def clear_ends(before, after, axis):
    where = lax.axis_index(axis)
    before = jnp.where(where == 0, jnp.zeros_like(before), before)
    after = jnp.where(where == lax.axis_size(axis) - 1, jnp.zeros_like(after), after)
    return before, after


def block_weights(conv_weight):
    channels = conv_weight.shape[1]
    taps = conv_weight.reshape(3, 3, 3, channels, channels).transpose(2, 3, 0, 1, 4)
    rows = []
    for out_x in range(2):
        for out_y in range(2):
            rows.append(
                jnp.pad(taps, ((0, 0), (0, 0), (out_x, 1 - out_x), (out_y, 1 - out_y), (0, 0)))
            )
    block = jnp.stack(rows, axis=1)
    return block.reshape(3 * 4 * channels, 16 * channels)


def conv_block(grid, mask, wide, bias_all, lane, grid_x, mask_x, y, out, out_x):
    channels, depth = bias_all.shape
    window = jnp.concatenate(
        [grid[grid_x + k, y : y + 4].reshape(4 * channels, depth) for k in range(4)], axis=0
    )
    parts = jnp.dot(wide[...], window, preferred_element_type=jnp.float32)
    low = pltpu.roll(parts[0 : 4 * channels], 1, 1)
    high = pltpu.roll(parts[8 * channels :], depth - 1, 1)
    total = parts[4 * channels : 8 * channels]
    total = total + jnp.where(lane == 0, 0.0, low) + jnp.where(lane == depth - 1, 0.0, high)
    for step_x in range(2):
        for step_y in range(2):
            at = (step_x * 2 + step_y) * channels
            at_y = y + step_y + 1
            keep = mask[mask_x + step_x + 1, at_y : at_y + 1, :]
            value = keep * (total[at : at + channels] + bias_all)
            out[out_x + step_x, y + step_y] = value.astype(jnp.bfloat16)


def mask_columns(grid, grid_x, mask, mask_x, pieces):
    for y, ref, x, at in pieces:
        grid[grid_x, y] = ref[x, at] * mask[mask_x, y : y + 1, :].astype(jnp.bfloat16)


def own_pieces(own, y_lo, y_hi, x):
    cols = own.shape[1]
    inner = [(y + 1, own, x, y) for y in range(cols)]
    return [(0, y_lo, x, 0)] + inner + [(cols + 1, y_hi, x, 0)]


def side_pieces(side, corner, x):
    cols = side.shape[1]
    inner = [(y + 1, side, x, y) for y in range(cols)]
    return [(0, corner, x, 0)] + inner + [(cols + 1, corner, x, 1)]


def conv_inner_kernel(own, y_lo, y_hi, mask, wide, bias, out, grid):
    rows, cols, channels, depth = own.shape

    def mask_row(x, carry):
        mask_columns(grid, x, mask, x, own_pieces(own, y_lo, y_hi, x))
        return carry

    lax.fori_loop(0, rows, mask_row, 0)
    lane = lax.broadcasted_iota(jnp.int32, (4 * channels, depth), 1)
    bias_all = jnp.broadcast_to(bias[...], (channels, depth))

    def pair(i, carry):
        for y in range(0, cols, 2):
            conv_block(grid, mask, wide, bias_all, lane, 2 * i, 2 * i, y, out, 2 * i)
        return carry

    lax.fori_loop(0, rows // 2 - 1, pair, 0)


def conv_edge_kernel(own, y_lo, y_hi, x_lo, x_hi, c_lo, c_hi, mask, wide, bias, out, grid):
    rows, cols, channels, depth = own.shape
    for x in range(2):
        mask_columns(grid, x, mask, x, side_pieces(x_lo, c_lo, x))
        mask_columns(grid, 2 + x, mask, 2 + x, own_pieces(own, y_lo, y_hi, x))
        mask_columns(grid, 4 + x, mask, rows + x, own_pieces(own, y_lo, y_hi, rows - 2 + x))
        mask_columns(grid, 6 + x, mask, rows + 2 + x, side_pieces(x_hi, c_hi, x))
    lane = lax.broadcasted_iota(jnp.int32, (4 * channels, depth), 1)
    bias_all = jnp.broadcast_to(bias[...], (channels, depth))
    for side in range(2):
        for y in range(0, cols, 2):
            conv_block(grid, mask, wide, bias_all, lane, 4 * side, rows * side, y, out, 2 * side)


def two_sum(a, b):
    s = a + b
    t = s - a
    return s, (a - (s - t)) + (b - t)


def split(a):
    c = a * 4097.0
    high = c - (c - a)
    return high, a - high


def two_prod(a, b):
    p = a * b
    a_hi, a_lo = split(a)
    b_hi, b_lo = split(b)
    return p, ((a_hi * b_hi - p) + a_hi * b_lo + a_lo * b_hi) + a_lo * b_lo


def pair_add(a, b):
    s, t = two_sum(a[0], b[0])
    return two_sum(s, t + (a[1] + b[1]))


def pair_scale(a, c):
    p, t = two_prod(a[0], c)
    return two_sum(p, t + a[1] * c)


def along_y(smooth, dst, field, f_lo, f_hi, row, flags, value_at):
    cols = smooth.shape[1]

    def product(y):
        if y == 0:
            return f_lo[row, 0].astype(jnp.float32) * (value_at(y) * flags[0])
        if y == cols + 1:
            return f_hi[row, 0].astype(jnp.float32) * (value_at(y) * flags[1])
        return field[row, y - 1].astype(jnp.float32) * value_at(y)

    here = product(1)
    pair = product(0) + here
    for y in range(cols):
        following = product(y + 2)
        pair_next = here + following
        smooth[dst, y] = pair + pair_next
        here = following
        pair = pair_next


def own_row(own, lo, hi, x):
    cols = own.shape[1]

    def at(y):
        if y == 0:
            return lo[x]
        if y == cols + 1:
            return hi[x]
        return own[x, y - 1 : y, :]

    return at


def side_row(side):
    return lambda y: side[0, y : y + 1, :]


def along_x(before, here, after, field, row, ridge_row, value_row):
    ref, x = here
    cols, channels, depth = ref.shape[1:]
    lane = lax.broadcasted_iota(jnp.int32, (channels, depth), 1)
    sums = []
    for y in range(cols):
        mid = ref[x, y]
        both = (before[0][before[1], y] + mid) + (mid + after[0][after[1], y])
        up = jnp.where(lane == depth - 1, 0.0, pltpu.roll(both, depth - 1, 1))
        down = jnp.where(lane == 0, 0.0, pltpu.roll(both, 1, 1))
        both = (both + both) + (up + down)
        prod = both * field[row, y].astype(jnp.float32)
        sums.append(jnp.sum(prod, axis=0, keepdims=True))
    inner = jnp.concatenate(sums, axis=0)
    return ridge_row * value_row + inner * (1.0 / (8 * channels))


def first_inner_kernel(inner, i_lo, i_hi, flags, start, s_lo, s_hi, ridge, smooth, out):
    rows = inner.shape[0]

    def stage_y(k, carry):
        along_y(smooth, k, inner, i_lo, i_hi, k, flags, own_row(start, s_lo, s_hi, k + 1))
        return carry

    lax.fori_loop(0, rows, stage_y, 0)

    def stage_x(k, carry):
        out[k] = along_x(
            (smooth, k), (smooth, k + 1), (smooth, k + 2), inner, k + 1, ridge[k + 2], start[k + 2]
        )
        return carry

    lax.fori_loop(0, rows - 2, stage_x, 0)


def first_edge_kernel(
    inner, edge, e_lo, e_hi, flags, start, s_lo, s_hi, x_lo, x_hi, ridge, smooth, part, out, rim
):
    n = inner.shape[0]
    last = n + 1
    along_y(rim, 0, edge, e_lo, e_hi, 0, flags, side_row(x_lo))
    along_y(rim, 1, edge, e_lo, e_hi, 1, flags, own_row(start, s_lo, s_hi, 0))
    along_y(rim, 2, edge, e_lo, e_hi, 2, flags, own_row(start, s_lo, s_hi, last))
    along_y(rim, 3, edge, e_lo, e_hi, 3, flags, side_row(x_hi))
    for x, before, here, after, field, row in (
        (0, (rim, 0), (rim, 1), (smooth, 0), edge, 1),
        (1, (rim, 1), (smooth, 0), (smooth, 1), inner, 0),
        (last - 1, (smooth, n - 2), (smooth, n - 1), (rim, 2), inner, n - 1),
        (last, (smooth, n - 1), (rim, 2), (rim, 3), edge, 2),
    ):
        out[x] = along_x(before, here, after, field, row, ridge[x], start[x])
    for x in range(n - 2):
        out[x + 2] = part[x]


PRODUCTS = ((0, 0), (0, 1), (1, 1), (0, 2), (1, 2))


def add_products(sums, which, fields):
    for k in which:
        a, b = PRODUCTS[k]
        p, e = two_prod(fields[a], fields[b])
        s, t = two_sum(sums[k][0], p)
        sums[k] = (s, sums[k][1] + (t + e))


def second_inner_kernel(
    inner, edge, i_lo, i_hi, e_lo, e_hi, flags, start, first, w_lo, w_hi, ridge, smooth, out, grams
):
    n = inner.shape[0]

    def stage_y(k, carry):
        along_y(smooth, k + 1, inner, i_lo, i_hi, k, flags, own_row(first, w_lo, w_hi, k + 1))
        return carry

    lax.fori_loop(0, n, stage_y, 0)
    along_y(smooth, 0, edge, e_lo, e_hi, 1, flags, own_row(first, w_lo, w_hi, 0))
    along_y(smooth, n + 1, edge, e_lo, e_hi, 2, flags, own_row(first, w_lo, w_hi, n + 1))

    def stage_x(k, carry):
        out[k] = along_x(
            (smooth, k), (smooth, k + 1), (smooth, k + 2), inner, k, ridge[k + 1], first[k + 1]
        )
        return carry

    lax.fori_loop(0, n, stage_x, 0)
    zero = jnp.zeros(start.shape[1:], jnp.float32)
    sums = [(zero, zero) for _ in PRODUCTS]
    for x in range(n + 2):
        inside = 0 < x < n + 1
        fields = (start[x], first[x], out[x - 1] if inside else None)
        add_products(sums, range(5) if inside else range(3), fields)
    for k, (s, e) in enumerate(sums):
        grams[2 * k] = s
        grams[2 * k + 1] = e


def second_edge_kernel(
    edge, e_lo, e_hi, flags, start, first, x_lo, x_hi, ridge, smooth, grams, out, share, rim
):
    n = smooth.shape[0]
    along_y(rim, 0, edge, e_lo, e_hi, 0, flags, side_row(x_lo))
    along_y(rim, 1, edge, e_lo, e_hi, 3, flags, side_row(x_hi))
    out[0] = along_x((rim, 0), (smooth, 0), (smooth, 1), edge, 1, ridge[0], first[0])
    out[1] = along_x(
        (smooth, n - 2), (smooth, n - 1), (rim, 1), edge, 2, ridge[n - 1], first[n - 1]
    )
    sums = [(grams[2 * k], grams[2 * k + 1]) for k in range(5)]
    for x, k in ((0, 0), (n - 1, 1)):
        add_products(sums, (3, 4), (start[x], first[x], out[k]))
    row = jnp.zeros((8, 128), jnp.float32)
    lane = lax.broadcasted_iota(jnp.int32, (8, 128), 1)
    for k, (s, e) in enumerate(sums):
        while s.shape[0] > 8:
            half = s.shape[0] // 2
            t, d = two_sum(s[:half], s[half:])
            s, e = (t, e[:half] + e[half:] + d)
        while s.shape[1] > 128:
            half = s.shape[1] // 2
            t, d = two_sum(s[:, :half], s[:, half:])
            s, e = (t, e[:, :half] + e[:, half:] + d)
        for axis, steps in ((0, (4, 2, 1)), (1, (64, 32, 16, 8, 4, 2, 1))):
            for step in steps:
                t, d = two_sum(s, pltpu.roll(s, step, axis))
                s, e = (t, (e + pltpu.roll(e, step, axis)) + d)
        row = jnp.where(lane == k, s, row)
        row = jnp.where(lane == 8 + k, e, row)
    share[...] = row[0:1]


def final_kernel(shares, start, first, inside, sides, solution_out, residual_out):
    s = shares[...]
    e = jnp.zeros_like(s)
    while s.shape[0] > 8:
        half = s.shape[0] // 2
        t, d = two_sum(s[:half], s[half:])
        s, e = (t, e[:half] + e[half:] + d)
    for step in (4, 2, 1):
        t, d = two_sum(s, pltpu.roll(s, step, 0))
        s, e = (t, (e + pltpu.roll(e, step, 0)) + d)
    lane = lax.broadcasted_iota(jnp.int32, s.shape, 1)

    def pick(value, k):
        return jnp.broadcast_to(
            jnp.sum(jnp.where(lane == k, value, 0.0), axis=1, keepdims=True), s.shape
        )

    g00, g01, g11, g02, g12 = [
        two_sum(pick(s, k), pick(e, k) + pick(s, 8 + k)) for k in range(5)
    ]
    alpha = g00[0] / g01[0]
    fresh = pair_add(pair_add(g00, pair_scale(g01, -2.0 * alpha)), pair_scale(pair_scale(g11, alpha), alpha))
    grow = 1.0 + fresh[0] / g00[0]
    curve = pair_add(
        pair_add(
            pair_scale(pair_scale(g01, grow), grow),
            pair_scale(pair_scale(pair_add(g02, g11), -alpha), grow),
        ),
        pair_scale(pair_scale(g12, alpha), alpha),
    )
    beta = fresh[0] / curve[0]
    near = (alpha + beta * grow)[0:1, 0:1]
    far = (alpha * beta)[0:1, 0:1]
    last = start.shape[0] - 1
    for x in range(last + 1):
        w2 = sides[0] if x == 0 else sides[1] if x == last else inside[x - 1]
        w0, w1 = (start[x], first[x])
        solution_out[x] = near * w0 - far * w1
        residual_out[x] = (w0 - near * w1) + far * w2


def per_device(features, conv_weight, conv_bias, occupancy, block_ids, ridge, target):
    rows, cols, channels, depth = features.shape
    voxels = depth // block_ids.shape[2]
    f32, bf16 = (jnp.float32, jnp.bfloat16)
    vmem = pl.BlockSpec(memory_space=pltpu.VMEM)
    smem = pl.BlockSpec(memory_space=pltpu.SMEM)

    def call(kernel, specs, outs, scratch, limit, name):
        return pl.pallas_call(
            kernel,
            out_shape=[jax.ShapeDtypeStruct(shape, dtype) for shape, dtype in outs],
            in_specs=[smem if s == "s" else vmem for s in specs],
            out_specs=[vmem for _ in outs],
            scratch_shapes=[pltpu.VMEM(shape, dtype) for shape, dtype in scratch],
            compiler_params=pltpu.CompilerParams(vmem_limit_bytes=limit << 20),
            name=name,
        )

    edges = (features[-2:], features[:2], features[:, -1:], features[:, :1])
    edges, occupancy, block_ids, target, conv_weight = lax.optimization_barrier(
        (edges, occupancy, block_ids, target, conv_weight)
    )
    x_lo, x_hi = (shift(edges[0], "sx", 1), shift(edges[1], "sx", -1))
    y_lo, y_hi = (shift(edges[2], "sy", 1), shift(edges[3], "sy", -1))
    c_lo = shift(jnp.concatenate([y_lo[-2:], y_hi[-2:]], axis=1), "sx", 1)
    c_hi = shift(jnp.concatenate([y_lo[:2], y_hi[:2]], axis=1), "sx", -1)

    present = (block_ids[:, :, :, 13] >= 0).astype(f32)
    weight_mask = occupancy.astype(f32) * jnp.repeat(present, voxels, axis=2)
    residual = weight_mask * target
    both = jnp.stack([weight_mask, residual])
    both_lo, both_hi = clear_ends(*halo(both, "sy", 2, 1), "sy")
    both_y = jnp.concatenate([both_lo, both, both_hi], axis=2)
    side_lo, side_hi = clear_ends(*halo(both_y, "sx", 1, 2), "sx")
    mask_y = both_y[0]
    mask_all = jnp.concatenate([side_lo[0], mask_y, side_hi[0]], axis=0)
    where = lax.axis_index("sy")
    flags = jnp.stack([where > 0, where < lax.axis_size("sy") - 1]).astype(f32)

    wide = block_weights(conv_weight)
    bias = conv_bias[:, None]
    grid_scratch = [((rows, cols + 2, channels, depth), bf16)]
    inner_shape = (rows - 2, cols, channels, depth)
    edge_shape = (4, cols, channels, depth)
    (inner,) = call(conv_inner_kernel, "vvvvvv", [(inner_shape, bf16)], grid_scratch, 12, "conv_inner")(
        features, y_lo, y_hi, mask_y, wide, bias
    )
    i_lo, i_hi = halo(inner, "sy", 1, 1)
    smooth, part = call(
        first_inner_kernel,
        "vvvsvvvv",
        [(inner_shape, f32), ((rows - 4, cols, depth), f32)],
        [],
        8,
        "first_inner",
    )(inner, i_lo, i_hi, flags, residual, both_lo[1], both_hi[1], ridge)
    (edge,) = call(conv_edge_kernel, "vvvvvvvvvv", [(edge_shape, bf16)], grid_scratch, 12, "conv_edge")(
        features, y_lo, y_hi, x_lo, x_hi, c_lo, c_hi, mask_all, wide, bias
    )
    e_lo, e_hi = halo(edge, "sy", 1, 1)
    plane = ((rows, cols, depth), f32)
    (first,) = call(
        first_edge_kernel, "vvvvsvvvvvvvv", [plane], [(edge_shape, f32)], 8, "first_edge"
    )(
        inner,
        edge,
        e_lo,
        e_hi,
        flags,
        residual,
        both_lo[1],
        both_hi[1],
        side_lo[1, 1:],
        side_hi[1, :1],
        ridge,
        smooth,
        part,
    )
    w_lo, w_hi = halo(first, "sy", 1, 1)
    rims = [jnp.concatenate([w_lo[x], first[x], w_hi[x]], axis=0)[None] for x in (-1, 0)]
    r_lo, r_hi = (shift(rims[0], "sx", 1), shift(rims[1], "sx", -1))
    smooth, inside, grams = call(
        second_inner_kernel,
        "vvvvvvsvvvvv",
        [
            ((rows, cols, channels, depth), f32),
            ((rows - 2, cols, depth), f32),
            ((2 * len(PRODUCTS), cols, depth), f32),
        ],
        [],
        8,
        "second_inner",
    )(inner, edge, i_lo, i_hi, e_lo, e_hi, flags, residual, first, w_lo, w_hi, ridge)
    sides, share = call(
        second_edge_kernel,
        "vvvsvvvvvvv",
        [((2, cols, depth), f32), ((1, 128), f32)],
        [((2, cols, channels, depth), f32)],
        8,
        "second_edge",
    )(edge, e_lo, e_hi, flags, residual, first, r_lo, r_hi, ridge, smooth, grams)

    peers = lax.axis_size("sx") * lax.axis_size("sy")
    shares = lax.all_to_all(jnp.broadcast_to(share[None], (peers, 1, 128)), AXES, 0, 0)
    return tuple(
        call(final_kernel, "vvvvv", [plane, plane], [], 8, "final")(
            shares.reshape(peers, 128), residual, first, inside, sides
        )
    )


def solution(mesh):
    placed = (
        P("sx", "sy", None, None),
        P(),
        P(),
        P("sx", "sy", None),
        P("sx", "sy", None, None),
        P("sx", "sy", None),
        P("sx", "sy", None),
    )
    return jax.shard_map(
        per_device,
        mesh=mesh,
        in_specs=placed,
        out_specs=(P("sx", "sy", None), P("sx", "sy", None)),
        check_vma=False,
    )
```

```python
import jax
import jax.numpy as jnp
from jax import lax
from jax.experimental import pallas as pl
from jax.experimental.pallas import tpu as pltpu
from jax.sharding import PartitionSpec as P

AXES = ("sx", "sy")


def shift(value, axis, step):
    peers = lax.axis_size(axis)
    return lax.ppermute(value, axis, [(i, (i + step) % peers) for i in range(peers)])


def halo(value, axis, dim, width):
    length = value.shape[dim]
    before = shift(lax.slice_in_dim(value, length - width, length, axis=dim), axis, 1)
    after = shift(lax.slice_in_dim(value, 0, width, axis=dim), axis, -1)
    return before, after


def block_weights(conv_weight):
    channels = conv_weight.shape[1]
    taps = conv_weight.reshape(3, 3, 3, channels, channels).transpose(2, 3, 0, 1, 4)
    rows = []
    for out_x in range(2):
        for out_y in range(2):
            rows.append(
                jnp.pad(taps, ((0, 0), (0, 0), (out_x, 1 - out_x), (out_y, 1 - out_y), (0, 0)))
            )
    block = jnp.stack(rows, axis=1)
    return block.reshape(3 * 4 * channels, 16 * channels)


def conv_block(grid, masks, wide, bias_all, lane, grid_x, y, out, out_x):
    channels, depth = bias_all.shape
    window = jnp.concatenate(
        [grid[grid_x + k, y : y + 4].reshape(4 * channels, depth) for k in range(4)], axis=0
    )
    parts = jnp.dot(wide[...], window, preferred_element_type=jnp.float32)
    low = pltpu.roll(parts[0 : 4 * channels], 1, 1)
    high = pltpu.roll(parts[8 * channels :], depth - 1, 1)
    total = parts[4 * channels : 8 * channels]
    total = total + jnp.where(lane == 0, 0.0, low) + jnp.where(lane == depth - 1, 0.0, high)
    for step_x in range(2):
        for step_y in range(2):
            at = (step_x * 2 + step_y) * channels
            keep = masks[step_x](y + step_y)
            value = keep * (total[at : at + channels] + bias_all)
            out[out_x + step_x, y + step_y] = value.astype(jnp.bfloat16)


def as_bf16(row, flag):
    return (row * flag).astype(jnp.bfloat16)


def fill_row(grid, grid_x, mask, middle, low, high):
    cols = grid.shape[1] - 2
    grid[grid_x, 0] = low
    for y in range(cols):
        grid[grid_x, y + 1] = middle(y) * mask(y).astype(jnp.bfloat16)
    grid[grid_x, cols + 1] = high


def fill_own(grid, grid_x, own, mask, y_lo, y_hi, m_lo, m_hi, flags, x):
    low = y_lo[x, 0] * as_bf16(m_lo[0, x], flags[0])
    high = y_hi[x, 0] * as_bf16(m_hi[0, x], flags[1])
    fill_row(grid, grid_x, mask_of(mask, x), lambda y: own[x, y], low, high)


def mask_of(mask, x):
    return lambda y: mask[x, y : y + 1, :]


def conv_inner_kernel(own, y_lo, y_hi, m_lo, m_hi, mask, flags, wide, bias, out, grid):
    rows, cols, channels, depth = own.shape

    def fill(x, carry):
        fill_own(grid, x, own, mask, y_lo, y_hi, m_lo, m_hi, flags, x)
        return carry

    lax.fori_loop(0, rows, fill, 0)
    lane = lax.broadcasted_iota(jnp.int32, (4 * channels, depth), 1)
    bias_all = jnp.broadcast_to(bias[...], (channels, depth))

    def pair(i, carry):
        masks = (mask_of(mask, 2 * i + 1), mask_of(mask, 2 * i + 2))
        for y in range(0, cols, 2):
            conv_block(grid, masks, wide, bias_all, lane, 2 * i, y, out, 2 * i)
        return carry

    lax.fori_loop(0, rows // 2 - 1, pair, 0)


def sides_kernel(y_lo, y_hi, m_lo, m_hi, mask, start, flags, out_hi, out_lo):
    rows, cols, depth = mask.shape

    def three(value):
        high = value.astype(jnp.bfloat16).astype(jnp.float32)
        rest = value - high
        mid = rest.astype(jnp.bfloat16).astype(jnp.float32)
        return high, mid, rest - mid

    for out, pair, row in ((out_hi, (rows - 2, rows - 1), rows - 1), (out_lo, (0, 1), 0)):
        for k, x in enumerate(pair):
            out[2 * k] = y_lo[x, 0] * as_bf16(m_lo[0, x], flags[0])
            out[2 * k + 1] = y_hi[x, 0] * as_bf16(m_hi[0, x], flags[1])
        out[4] = jnp.concatenate([mask[x] for x in pair], axis=0).astype(jnp.bfloat16)
        high, mid, low = three(start[row])
        rims = three(jnp.concatenate([m_lo[1, row], m_hi[1, row]], axis=0))
        blank = jnp.zeros((10, depth), jnp.float32)
        out[5] = jnp.concatenate([high, mid], axis=0).astype(jnp.bfloat16)
        out[6] = jnp.concatenate([low, *rims, blank], axis=0).astype(jnp.bfloat16)


def conv_edge_kernel(
    own,
    y_lo,
    y_hi,
    m_lo,
    m_hi,
    x_lo,
    x_hi,
    side_lo,
    side_hi,
    mask,
    flags,
    wide,
    bias,
    out,
    grid,
    side_mask,
):
    rows, cols, channels, depth = own.shape
    for k, side in enumerate((side_lo, side_hi)):
        both = side[4].astype(jnp.float32) * flags[2 + k]
        side_mask[2 * k] = both[:cols]
        side_mask[2 * k + 1] = both[cols:]
    for x in range(2):
        for k, ref, side in ((0, x_lo, side_lo), (1, x_hi, side_hi)):
            clear = jnp.full((channels, depth), flags[2 + k], jnp.float32).astype(jnp.bfloat16)
            fill_row(
                grid,
                6 * k + x,
                mask_of(side_mask, 2 * k + x),
                lambda y: ref[x, y],
                side[2 * x] * clear,
                side[2 * x + 1] * clear,
            )
        fill_own(grid, 2 + x, own, mask, y_lo, y_hi, m_lo, m_hi, flags, x)
        fill_own(grid, 4 + x, own, mask, y_lo, y_hi, m_lo, m_hi, flags, rows - 2 + x)
    lane = lax.broadcasted_iota(jnp.int32, (4 * channels, depth), 1)
    bias_all = jnp.broadcast_to(bias[...], (channels, depth))
    for side, masks in (
        (0, (mask_of(side_mask, 1), mask_of(mask, 0))),
        (1, (mask_of(mask, rows - 1), mask_of(side_mask, 2))),
    ):
        for y in range(0, cols, 2):
            conv_block(grid, masks, wide, bias_all, lane, 4 * side, y, out, 2 * side)


def two_sum(a, b):
    s = a + b
    t = s - a
    return s, (a - (s - t)) + (b - t)


def split(a):
    c = a * 4097.0
    high = c - (c - a)
    return high, a - high


def two_prod(a, b):
    p = a * b
    a_hi, a_lo = split(a)
    b_hi, b_lo = split(b)
    return p, ((a_hi * b_hi - p) + a_hi * b_lo + a_lo * b_hi) + a_lo * b_lo


def pair_add(a, b):
    s, t = two_sum(a[0], b[0])
    return two_sum(s, t + (a[1] + b[1]))


def pair_scale(a, c):
    p, t = two_prod(a[0], c)
    return two_sum(p, t + a[1] * c)


def along_y(smooth, dst, field, f_lo, f_hi, row, flags, value_at):
    cols = smooth.shape[1]

    def product(y):
        if y == 0:
            return f_lo[row, 0].astype(jnp.float32) * (value_at(y) * flags[0])
        if y == cols + 1:
            return f_hi[row, 0].astype(jnp.float32) * (value_at(y) * flags[1])
        return field[row, y - 1].astype(jnp.float32) * value_at(y)

    here = product(1)
    pair = product(0) + here
    for y in range(cols):
        following = product(y + 2)
        pair_next = here + following
        smooth[dst, y] = pair + pair_next
        here = following
        pair = pair_next


def own_row(own, lo, hi, x):
    cols = own.shape[1]

    def at(y):
        if y == 0:
            return lo(x)
        if y == cols + 1:
            return hi(x)
        return own[x, y - 1 : y, :]

    return at


def side_row(side):
    return lambda y: side[y : y + 1, :]


def rim_of(ref, *index):
    return lambda x: ref[(*index, x)]


def along_x(before, here, after, field, row, ridge_row, value_row):
    ref, x = here
    cols, channels, depth = ref.shape[1:]
    lane = lax.broadcasted_iota(jnp.int32, (channels, depth), 1)
    sums = []
    for y in range(cols):
        mid = ref[x, y]
        both = (before[0][before[1], y] + mid) + (mid + after[0][after[1], y])
        up = jnp.where(lane == depth - 1, 0.0, pltpu.roll(both, depth - 1, 1))
        down = jnp.where(lane == 0, 0.0, pltpu.roll(both, 1, 1))
        both = (both + both) + (up + down)
        prod = both * field[row, y].astype(jnp.float32)
        sums.append(jnp.sum(prod, axis=0, keepdims=True))
    inner = jnp.concatenate(sums, axis=0)
    return ridge_row * value_row + inner * (1.0 / (8 * channels))


def first_inner_kernel(inner, i_lo, i_hi, flags, start, m_lo, m_hi, ridge, smooth, out):
    rows = inner.shape[0]
    s_lo, s_hi = (rim_of(m_lo, 1), rim_of(m_hi, 1))

    def stage_y(k, carry):
        along_y(smooth, k, inner, i_lo, i_hi, k, flags, own_row(start, s_lo, s_hi, k + 1))
        return carry

    lax.fori_loop(0, rows, stage_y, 0)

    def stage_x(k, carry):
        out[k] = along_x(
            (smooth, k), (smooth, k + 1), (smooth, k + 2), inner, k + 1, ridge[k + 2], start[k + 2]
        )
        return carry

    lax.fori_loop(0, rows - 2, stage_x, 0)


def first_edge_kernel(
    inner,
    edge,
    e_lo,
    e_hi,
    flags,
    start,
    m_lo,
    m_hi,
    side_lo,
    side_hi,
    ridge,
    smooth,
    part,
    out,
    rim,
    side_start,
    side_rims,
):
    n = inner.shape[0]
    last = n + 1
    cols = inner.shape[1]
    s_lo, s_hi = (rim_of(m_lo, 1), rim_of(m_hi, 1))
    for k, side in enumerate((side_lo, side_hi)):
        upper = side[5].astype(jnp.float32)
        lower = side[6].astype(jnp.float32)
        side_start[k] = (upper[:cols] + upper[cols:]) + lower[:cols]
        ends = lower[cols : cols + 8]
        side_rims[k, 0:2] = (ends[0:2] + ends[2:4]) + ends[4:6]

    def side_values(k):
        def at(y):
            if y == 0:
                return side_rims[k, 0:1]
            if y == cols + 1:
                return side_rims[k, 1:2]
            return side_start[k, y - 1 : y]

        return at

    along_y(rim, 0, edge, e_lo, e_hi, 0, flags, side_values(0))
    along_y(rim, 1, edge, e_lo, e_hi, 1, flags, own_row(start, s_lo, s_hi, 0))
    along_y(rim, 2, edge, e_lo, e_hi, 2, flags, own_row(start, s_lo, s_hi, last))
    along_y(rim, 3, edge, e_lo, e_hi, 3, flags, side_values(1))
    for x, before, here, after, field, row in (
        (0, (rim, 0), (rim, 1), (smooth, 0), edge, 1),
        (1, (rim, 1), (smooth, 0), (smooth, 1), inner, 0),
        (last - 1, (smooth, n - 2), (smooth, n - 1), (rim, 2), inner, n - 1),
        (last, (smooth, n - 1), (rim, 2), (rim, 3), edge, 2),
    ):
        out[x] = along_x(before, here, after, field, row, ridge[x], start[x])
    for x in range(n - 2):
        out[x + 2] = part[x]


PRODUCTS = ((0, 0), (0, 1), (1, 1), (0, 2), (1, 2))


def add_products(sums, which, fields):
    for k in which:
        a, b = PRODUCTS[k]
        p, e = two_prod(fields[a], fields[b])
        s, t = two_sum(sums[k][0], p)
        sums[k] = (s, sums[k][1] + (t + e))


def second_inner_kernel(
    inner, edge, i_lo, i_hi, e_lo, e_hi, flags, start, first, w_lo, w_hi, ridge, smooth, out, grams
):
    n = inner.shape[0]
    w_lo, w_hi = (rim_of(w_lo), rim_of(w_hi))

    def stage_y(k, carry):
        along_y(smooth, k + 1, inner, i_lo, i_hi, k, flags, own_row(first, w_lo, w_hi, k + 1))
        return carry

    lax.fori_loop(0, n, stage_y, 0)
    along_y(smooth, 0, edge, e_lo, e_hi, 1, flags, own_row(first, w_lo, w_hi, 0))
    along_y(smooth, n + 1, edge, e_lo, e_hi, 2, flags, own_row(first, w_lo, w_hi, n + 1))

    def stage_x(k, carry):
        out[k] = along_x(
            (smooth, k), (smooth, k + 1), (smooth, k + 2), inner, k, ridge[k + 1], first[k + 1]
        )
        return carry

    lax.fori_loop(0, n, stage_x, 0)
    zero = jnp.zeros(start.shape[1:], jnp.float32)
    sums = [(zero, zero) for _ in PRODUCTS]
    for x in range(n + 2):
        inside = 0 < x < n + 1
        fields = (start[x], first[x], out[x - 1] if inside else None)
        add_products(sums, range(5) if inside else range(3), fields)
    for k, (s, e) in enumerate(sums):
        grams[2 * k] = s
        grams[2 * k + 1] = e


def second_edge_kernel(
    edge, e_lo, e_hi, flags, start, first, x_lo, x_hi, ridge, smooth, grams, out, share, rim
):
    n = smooth.shape[0]
    along_y(rim, 0, edge, e_lo, e_hi, 0, flags, side_row(x_lo))
    along_y(rim, 1, edge, e_lo, e_hi, 3, flags, side_row(x_hi))
    out[0] = along_x((rim, 0), (smooth, 0), (smooth, 1), edge, 1, ridge[0], first[0])
    out[1] = along_x(
        (smooth, n - 2), (smooth, n - 1), (rim, 1), edge, 2, ridge[n - 1], first[n - 1]
    )
    sums = [(grams[2 * k], grams[2 * k + 1]) for k in range(5)]
    for x, k in ((0, 0), (n - 1, 1)):
        add_products(sums, (3, 4), (start[x], first[x], out[k]))
    row = jnp.zeros((8, 128), jnp.float32)
    lane = lax.broadcasted_iota(jnp.int32, (8, 128), 1)
    for k, (s, e) in enumerate(sums):
        while s.shape[0] > 8:
            half = s.shape[0] // 2
            t, d = two_sum(s[:half], s[half:])
            s, e = (t, e[:half] + e[half:] + d)
        while s.shape[1] > 128:
            half = s.shape[1] // 2
            t, d = two_sum(s[:, :half], s[:, half:])
            s, e = (t, e[:, :half] + e[:, half:] + d)
        for axis, steps in ((0, (4, 2, 1)), (1, (64, 32, 16, 8, 4, 2, 1))):
            for step in steps:
                t, d = two_sum(s, pltpu.roll(s, step, axis))
                s, e = (t, (e + pltpu.roll(e, step, axis)) + d)
        row = jnp.where(lane == k, s, row)
        row = jnp.where(lane == 8 + k, e, row)
    share[...] = row[0:1]


def final_kernel(shares, start, first, inside, sides, solution_out, residual_out):
    s = shares[...]
    e = jnp.zeros_like(s)
    while s.shape[0] > 8:
        half = s.shape[0] // 2
        t, d = two_sum(s[:half], s[half:])
        s, e = (t, e[:half] + e[half:] + d)
    for step in (4, 2, 1):
        t, d = two_sum(s, pltpu.roll(s, step, 0))
        s, e = (t, (e + pltpu.roll(e, step, 0)) + d)
    lane = lax.broadcasted_iota(jnp.int32, s.shape, 1)

    def pick(value, k):
        return jnp.broadcast_to(
            jnp.sum(jnp.where(lane == k, value, 0.0), axis=1, keepdims=True), s.shape
        )

    g00, g01, g11, g02, g12 = [
        two_sum(pick(s, k), pick(e, k) + pick(s, 8 + k)) for k in range(5)
    ]
    alpha = g00[0] / g01[0]
    fresh = pair_add(pair_add(g00, pair_scale(g01, -2.0 * alpha)), pair_scale(pair_scale(g11, alpha), alpha))
    grow = 1.0 + fresh[0] / g00[0]
    curve = pair_add(
        pair_add(
            pair_scale(pair_scale(g01, grow), grow),
            pair_scale(pair_scale(pair_add(g02, g11), -alpha), grow),
        ),
        pair_scale(pair_scale(g12, alpha), alpha),
    )
    beta = fresh[0] / curve[0]
    near = (alpha + beta * grow)[0:1, 0:1]
    far = (alpha * beta)[0:1, 0:1]
    last = start.shape[0] - 1
    for x in range(last + 1):
        w2 = sides[0] if x == 0 else sides[1] if x == last else inside[x - 1]
        w0, w1 = (start[x], first[x])
        solution_out[x] = near * w0 - far * w1
        residual_out[x] = (w0 - near * w1) + far * w2


def per_device(features, conv_weight, conv_bias, occupancy, block_ids, ridge, target):
    rows, cols, channels, depth = features.shape
    voxels = depth // block_ids.shape[2]
    f32, bf16 = (jnp.float32, jnp.bfloat16)
    vmem = pl.BlockSpec(memory_space=pltpu.VMEM)
    smem = pl.BlockSpec(memory_space=pltpu.SMEM)

    def call(kernel, specs, outs, scratch, limit, name):
        return pl.pallas_call(
            kernel,
            out_shape=[jax.ShapeDtypeStruct(shape, dtype) for shape, dtype in outs],
            in_specs=[smem if s == "s" else vmem for s in specs],
            out_specs=[vmem for _ in outs],
            scratch_shapes=[pltpu.VMEM(shape, dtype) for shape, dtype in scratch],
            compiler_params=pltpu.CompilerParams(vmem_limit_bytes=limit << 20),
            name=name,
        )

    edges = (features[-2:], features[:2])
    edges, occupancy, block_ids, target, conv_weight = lax.optimization_barrier(
        (edges, occupancy, block_ids, target, conv_weight)
    )
    x_lo, x_hi = (shift(edges[0], "sx", 1), shift(edges[1], "sx", -1))

    present = (block_ids[:, :, :, 13] >= 0).astype(f32)
    weight_mask = occupancy.astype(f32) * jnp.repeat(present, voxels, axis=2)
    residual = weight_mask * target
    y_lo, y_hi = halo(features, "sy", 1, 1)
    weight_mask, residual, y_lo, y_hi = lax.optimization_barrier(
        (weight_mask, residual, y_lo, y_hi)
    )
    m_lo, m_hi = halo(jnp.stack([weight_mask, residual]), "sy", 2, 1)
    flags = jnp.stack(
        [
            keep
            for axis in ("sy", "sx")
            for keep in (lax.axis_index(axis) > 0, lax.axis_index(axis) < lax.axis_size(axis) - 1)
        ]
    ).astype(f32)

    wide = block_weights(conv_weight)
    bias = conv_bias[:, None]
    grid_scratch = ((rows, cols + 2, channels, depth), bf16)
    inner_shape = (rows - 2, cols, channels, depth)
    edge_shape = (4, cols, channels, depth)
    side_shape = (7, channels, depth)
    side_hi, side_lo = call(
        sides_kernel, "vvvvvvs", [(side_shape, bf16), (side_shape, bf16)], [], 4, "sides"
    )(y_lo, y_hi, m_lo, m_hi, weight_mask, residual, flags)
    side_lo, side_hi = (shift(side_hi, "sx", 1), shift(side_lo, "sx", -1))
    (inner,) = call(
        conv_inner_kernel, "vvvvvvsvv", [(inner_shape, bf16)], [grid_scratch], 12, "conv_inner"
    )(features, y_lo, y_hi, m_lo, m_hi, weight_mask, flags, wide, bias)
    i_lo, i_hi = halo(inner, "sy", 1, 1)
    smooth, part = call(
        first_inner_kernel,
        "vvvsvvvv",
        [(inner_shape, f32), ((rows - 4, cols, depth), f32)],
        [],
        8,
        "first_inner",
    )(inner, i_lo, i_hi, flags, residual, m_lo, m_hi, ridge)
    (edge,) = call(
        conv_edge_kernel,
        "vvvvvvvvvvsvv",
        [(edge_shape, bf16)],
        [grid_scratch, ((4, cols, depth), f32)],
        12,
        "conv_edge",
    )(features, y_lo, y_hi, m_lo, m_hi, x_lo, x_hi, side_lo, side_hi, weight_mask, flags, wide, bias)
    e_lo, e_hi = halo(edge, "sy", 1, 1)
    plane = ((rows, cols, depth), f32)
    (first,) = call(
        first_edge_kernel,
        "vvvvsvvvvvvvv",
        [plane],
        [(edge_shape, f32), ((2, cols, depth), f32), ((2, 8, depth), f32)],
        8,
        "first_edge",
    )(
        inner,
        edge,
        e_lo,
        e_hi,
        flags,
        residual,
        m_lo,
        m_hi,
        side_lo,
        side_hi,
        ridge,
        smooth,
        part,
    )
    w_lo, w_hi = halo(first, "sy", 1, 1)
    rims = [jnp.concatenate([w_lo[x], first[x], w_hi[x]], axis=0) for x in (-1, 0)]
    r_lo, r_hi = (shift(rims[0], "sx", 1), shift(rims[1], "sx", -1))
    smooth, inside, grams = call(
        second_inner_kernel,
        "vvvvvvsvvvvv",
        [
            ((rows, cols, channels, depth), f32),
            ((rows - 2, cols, depth), f32),
            ((2 * len(PRODUCTS), cols, depth), f32),
        ],
        [],
        8,
        "second_inner",
    )(inner, edge, i_lo, i_hi, e_lo, e_hi, flags, residual, first, w_lo, w_hi, ridge)
    sides, share = call(
        second_edge_kernel,
        "vvvsvvvvvvv",
        [((2, cols, depth), f32), ((1, 128), f32)],
        [((2, cols, channels, depth), f32)],
        8,
        "second_edge",
    )(edge, e_lo, e_hi, flags, residual, first, r_lo, r_hi, ridge, smooth, grams)

    peers = lax.axis_size("sx") * lax.axis_size("sy")
    shares = lax.all_to_all(jnp.broadcast_to(share[None], (peers, 1, 128)), AXES, 0, 0)
    return tuple(
        call(final_kernel, "vvvvv", [plane, plane], [], 8, "final")(
            shares.reshape(peers, 128), residual, first, inside, sides
        )
    )


def solution(mesh):
    placed = (
        P("sx", "sy", None, None),
        P(),
        P(),
        P("sx", "sy", None),
        P("sx", "sy", None, None),
        P("sx", "sy", None),
        P("sx", "sy", None),
    )
    return jax.shard_map(
        per_device,
        mesh=mesh,
        in_specs=placed,
        out_specs=(P("sx", "sy", None), P("sx", "sy", None)),
        check_vma=False,
    )
```

```python
import jax
import jax.numpy as jnp
from jax import lax
from jax.experimental import pallas as pl
from jax.experimental.pallas import tpu as pltpu
from jax.sharding import PartitionSpec as P

AXES = ("sx", "sy")


def shift(value, axis, step):
    peers = lax.axis_size(axis)
    return lax.ppermute(value, axis, [(i, (i + step) % peers) for i in range(peers)])


def halo(value, axis, dim, width):
    length = value.shape[dim]
    before = shift(lax.slice_in_dim(value, length - width, length, axis=dim), axis, 1)
    after = shift(lax.slice_in_dim(value, 0, width, axis=dim), axis, -1)
    return before, after


def edges_kernel(own, x_hi, x_lo, y_hi, y_lo, sems):
    rows, cols = own.shape[:2]
    copies = [
        pltpu.make_async_copy(own.at[rows - 2 : rows], x_hi, sems.at[0]),
        pltpu.make_async_copy(own.at[0:2], x_lo, sems.at[1]),
        pltpu.make_async_copy(own.at[:, cols - 1 : cols], y_hi, sems.at[2]),
        pltpu.make_async_copy(own.at[:, 0:1], y_lo, sems.at[3]),
    ]
    for copy in copies:
        copy.start()
    for copy in copies:
        copy.wait()


def weights_kernel(taps, bias, wide, bias_col):
    channels = taps.shape[1]
    width = 16 * channels
    row = lax.broadcasted_iota(jnp.int32, (channels, width), 0)
    lane = lax.broadcasted_iota(jnp.int32, (channels, width), 1)
    repeat = jnp.where(lane % channels == row, 1.0, 0.0).astype(jnp.bfloat16)
    group = lane // channels
    for z in range(3):
        every = [
            jnp.dot(taps[3 * k + z], repeat, preferred_element_type=jnp.float32) for k in range(9)
        ]
        for out_x in range(2):
            for out_y in range(2):
                total = jnp.zeros((channels, width), jnp.float32)
                for k in range(9):
                    at = (out_x + k // 3) * 4 + out_y + k % 3
                    total = jnp.where(group == at, every[k], total)
                start = ((z * 2 + out_x) * 2 + out_y) * channels
                wide[start : start + channels] = total.astype(jnp.bfloat16)
    square = (channels, channels)
    same = lax.broadcasted_iota(jnp.int32, square, 0) == lax.broadcasted_iota(jnp.int32, square, 1)
    column = jnp.sum(jnp.where(same, bias[...], 0.0), axis=1, keepdims=True)
    bias_col[...] = jnp.broadcast_to(column, bias_col.shape)


def mesh_flags():
    keep = []
    for axis in ("sy", "sx"):
        where = lax.axis_index(axis)
        keep += [where > 0, where < lax.axis_size(axis) - 1]
    return [jnp.where(k, 1.0, 0.0) for k in keep]


def conv_block(grid, masks, wide, bias_all, lane, grid_x, y, out, out_x):
    channels, depth = bias_all.shape
    window = jnp.concatenate(
        [grid[grid_x + k, y : y + 4].reshape(4 * channels, depth) for k in range(4)], axis=0
    )
    parts = jnp.dot(wide[...], window, preferred_element_type=jnp.float32)
    low = pltpu.roll(parts[0 : 4 * channels], 1, 1)
    high = pltpu.roll(parts[8 * channels :], depth - 1, 1)
    total = parts[4 * channels : 8 * channels]
    total = total + jnp.where(lane == 0, 0.0, low) + jnp.where(lane == depth - 1, 0.0, high)
    for step_x in range(2):
        for step_y in range(2):
            at = (step_x * 2 + step_y) * channels
            keep = masks[step_x](y + step_y)
            value = keep * (total[at : at + channels] + bias_all)
            out[out_x + step_x, y + step_y] = value.astype(jnp.bfloat16)


def as_bf16(row, flag):
    return (row * flag).astype(jnp.bfloat16)


def fill_row(grid, grid_x, mask, middle, low, high):
    cols = grid.shape[1] - 2
    grid[grid_x, 0] = low
    for y in range(cols):
        grid[grid_x, y + 1] = middle(y) * mask(y).astype(jnp.bfloat16)
    grid[grid_x, cols + 1] = high


def fill_own(grid, grid_x, own, mask, y_lo, y_hi, m_lo, m_hi, flags, x):
    low = y_lo[x, 0] * as_bf16(m_lo[0, pl.ds(x, 1)], flags[0])
    high = y_hi[x, 0] * as_bf16(m_hi[0, pl.ds(x, 1)], flags[1])
    fill_row(grid, grid_x, mask_of(mask, x), lambda y: own[x, y], low, high)


def mask_of(mask, x):
    return lambda y: mask[x, y : y + 1, :]


def conv_inner_kernel(own, y_lo, y_hi, m_lo, m_hi, mask, wide, bias, out, grid):
    rows, cols, channels, depth = own.shape
    flags = mesh_flags()

    def fill(x, carry):
        fill_own(grid, x, own, mask, y_lo, y_hi, m_lo, m_hi, flags, x)
        return carry

    lax.fori_loop(0, rows, fill, 0)
    lane = lax.broadcasted_iota(jnp.int32, (4 * channels, depth), 1)
    bias_all = bias[...]

    def pair(i, carry):
        masks = (mask_of(mask, 2 * i + 1), mask_of(mask, 2 * i + 2))
        for y in range(0, cols, 2):
            conv_block(grid, masks, wide, bias_all, lane, 2 * i, y, out, 2 * i)
        return carry

    lax.fori_loop(0, rows // 2 - 1, pair, 0)


def sides_kernel(y_lo, y_hi, m_lo, m_hi, mask, start, out_hi, out_lo):
    rows, cols, depth = mask.shape
    flags = mesh_flags()

    def three(value):
        high = value.astype(jnp.bfloat16).astype(jnp.float32)
        rest = value - high
        mid = rest.astype(jnp.bfloat16).astype(jnp.float32)
        return high, mid, rest - mid

    for out, pair, row in ((out_hi, (rows - 2, rows - 1), rows - 1), (out_lo, (0, 1), 0)):
        for k, x in enumerate(pair):
            out[2 * k] = y_lo[x, 0] * as_bf16(m_lo[0, pl.ds(x, 1)], flags[0])
            out[2 * k + 1] = y_hi[x, 0] * as_bf16(m_hi[0, pl.ds(x, 1)], flags[1])
        out[4] = jnp.concatenate([mask[x] for x in pair], axis=0).astype(jnp.bfloat16)
        high, mid, low = three(start[row])
        rims = three(jnp.concatenate([m_lo[1, row : row + 1], m_hi[1, row : row + 1]], axis=0))
        blank = jnp.zeros((10, depth), jnp.float32)
        out[5] = jnp.concatenate([high, mid], axis=0).astype(jnp.bfloat16)
        out[6] = jnp.concatenate([low, *rims, blank], axis=0).astype(jnp.bfloat16)


def conv_edge_kernel(
    own,
    y_lo,
    y_hi,
    m_lo,
    m_hi,
    x_lo,
    x_hi,
    side_lo,
    side_hi,
    mask,
    wide,
    bias,
    out,
    grid,
    side_mask,
):
    rows, cols, channels, depth = own.shape
    flags = mesh_flags()
    for k, side in enumerate((side_lo, side_hi)):
        both = side[4].astype(jnp.float32) * flags[2 + k]
        side_mask[2 * k] = both[:cols]
        side_mask[2 * k + 1] = both[cols:]
    for x in range(2):
        for k, ref, side in ((0, x_lo, side_lo), (1, x_hi, side_hi)):
            clear = jnp.full((channels, depth), flags[2 + k], jnp.float32).astype(jnp.bfloat16)
            fill_row(
                grid,
                6 * k + x,
                mask_of(side_mask, 2 * k + x),
                lambda y: ref[x, y],
                side[2 * x] * clear,
                side[2 * x + 1] * clear,
            )
        fill_own(grid, 2 + x, own, mask, y_lo, y_hi, m_lo, m_hi, flags, x)
        fill_own(grid, 4 + x, own, mask, y_lo, y_hi, m_lo, m_hi, flags, rows - 2 + x)
    lane = lax.broadcasted_iota(jnp.int32, (4 * channels, depth), 1)
    bias_all = bias[...]
    for side, masks in (
        (0, (mask_of(side_mask, 1), mask_of(mask, 0))),
        (1, (mask_of(mask, rows - 1), mask_of(side_mask, 2))),
    ):
        for y in range(0, cols, 2):
            conv_block(grid, masks, wide, bias_all, lane, 4 * side, y, out, 2 * side)


def two_sum(a, b):
    s = a + b
    t = s - a
    return s, (a - (s - t)) + (b - t)


def split(a):
    c = a * 4097.0
    high = c - (c - a)
    return high, a - high


def two_prod(a, b):
    p = a * b
    a_hi, a_lo = split(a)
    b_hi, b_lo = split(b)
    return p, ((a_hi * b_hi - p) + a_hi * b_lo + a_lo * b_hi) + a_lo * b_lo


def pair_add(a, b):
    s, t = two_sum(a[0], b[0])
    return two_sum(s, t + (a[1] + b[1]))


def pair_scale(a, c):
    p, t = two_prod(a[0], c)
    return two_sum(p, t + a[1] * c)


def along_y(smooth, dst, field, f_lo, f_hi, row, flags, value_at):
    cols = smooth.shape[1]

    def product(y):
        if y == 0:
            return f_lo[row, 0].astype(jnp.float32) * (value_at(y) * flags[0])
        if y == cols + 1:
            return f_hi[row, 0].astype(jnp.float32) * (value_at(y) * flags[1])
        return field[row, y - 1].astype(jnp.float32) * value_at(y)

    here = product(1)
    pair = product(0) + here
    for y in range(cols):
        following = product(y + 2)
        pair_next = here + following
        smooth[dst, y] = pair + pair_next
        here = following
        pair = pair_next


def own_row(own, lo, hi, x):
    cols = own.shape[1]

    def at(y):
        if y == 0:
            return lo(x)
        if y == cols + 1:
            return hi(x)
        return own[x, y - 1 : y, :]

    return at


def side_row(side):
    return lambda y: side[y : y + 1, :]


def rim_of(ref, *index):
    return lambda x: ref[(*index, pl.ds(x, 1))]


def along_x(before, here, after, field, row, ridge_row, value_row):
    ref, x = here
    cols, channels, depth = ref.shape[1:]
    lane = lax.broadcasted_iota(jnp.int32, (channels, depth), 1)
    sums = []
    for y in range(cols):
        mid = ref[x, y]
        both = (before[0][before[1], y] + mid) + (mid + after[0][after[1], y])
        up = jnp.where(lane == depth - 1, 0.0, pltpu.roll(both, depth - 1, 1))
        down = jnp.where(lane == 0, 0.0, pltpu.roll(both, 1, 1))
        both = (both + both) + (up + down)
        prod = both * field[row, y].astype(jnp.float32)
        sums.append(jnp.sum(prod, axis=0, keepdims=True))
    inner = jnp.concatenate(sums, axis=0)
    return ridge_row * value_row + inner * (1.0 / (8 * channels))


def first_inner_kernel(inner, i_lo, i_hi, start, m_lo, m_hi, ridge, smooth, out):
    rows = inner.shape[0]
    flags = mesh_flags()
    s_lo, s_hi = (rim_of(m_lo, 1), rim_of(m_hi, 1))

    def stage_y(k, carry):
        along_y(smooth, k, inner, i_lo, i_hi, k, flags, own_row(start, s_lo, s_hi, k + 1))
        return carry

    lax.fori_loop(0, rows, stage_y, 0)

    def stage_x(k, carry):
        out[k] = along_x(
            (smooth, k), (smooth, k + 1), (smooth, k + 2), inner, k + 1, ridge[k + 2], start[k + 2]
        )
        return carry

    lax.fori_loop(0, rows - 2, stage_x, 0)


def first_edge_kernel(
    inner,
    edge,
    e_lo,
    e_hi,
    start,
    m_lo,
    m_hi,
    side_lo,
    side_hi,
    ridge,
    smooth,
    part,
    out,
    rim,
    side_start,
    side_rims,
):
    n = inner.shape[0]
    flags = mesh_flags()
    last = n + 1
    cols = inner.shape[1]
    s_lo, s_hi = (rim_of(m_lo, 1), rim_of(m_hi, 1))
    for k, side in enumerate((side_lo, side_hi)):
        upper = side[5].astype(jnp.float32)
        lower = side[6].astype(jnp.float32)
        side_start[k] = (upper[:cols] + upper[cols:]) + lower[:cols]
        ends = lower[cols : cols + 8]
        side_rims[k, 0:2] = (ends[0:2] + ends[2:4]) + ends[4:6]

    def side_values(k):
        def at(y):
            if y == 0:
                return side_rims[k, 0:1]
            if y == cols + 1:
                return side_rims[k, 1:2]
            return side_start[k, y - 1 : y]

        return at

    along_y(rim, 0, edge, e_lo, e_hi, 0, flags, side_values(0))
    along_y(rim, 1, edge, e_lo, e_hi, 1, flags, own_row(start, s_lo, s_hi, 0))
    along_y(rim, 2, edge, e_lo, e_hi, 2, flags, own_row(start, s_lo, s_hi, last))
    along_y(rim, 3, edge, e_lo, e_hi, 3, flags, side_values(1))
    for x, before, here, after, field, row in (
        (0, (rim, 0), (rim, 1), (smooth, 0), edge, 1),
        (1, (rim, 1), (smooth, 0), (smooth, 1), inner, 0),
        (last - 1, (smooth, n - 2), (smooth, n - 1), (rim, 2), inner, n - 1),
        (last, (smooth, n - 1), (rim, 2), (rim, 3), edge, 2),
    ):
        out[x] = along_x(before, here, after, field, row, ridge[x], start[x])
    for x in range(n - 2):
        out[x + 2] = part[x]


PRODUCTS = ((0, 0), (0, 1), (1, 1), (0, 2), (1, 2))


def add_products(sums, which, fields):
    for k in which:
        a, b = PRODUCTS[k]
        p, e = two_prod(fields[a], fields[b])
        s, t = two_sum(sums[k][0], p)
        sums[k] = (s, sums[k][1] + (t + e))


def second_inner_kernel(
    inner, edge, i_lo, i_hi, e_lo, e_hi, start, first, w_lo, w_hi, ridge, smooth, out, grams
):
    n = inner.shape[0]
    flags = mesh_flags()
    w_lo, w_hi = (rim_of(w_lo), rim_of(w_hi))

    def stage_y(k, carry):
        along_y(smooth, k + 1, inner, i_lo, i_hi, k, flags, own_row(first, w_lo, w_hi, k + 1))
        return carry

    lax.fori_loop(0, n, stage_y, 0)
    along_y(smooth, 0, edge, e_lo, e_hi, 1, flags, own_row(first, w_lo, w_hi, 0))
    along_y(smooth, n + 1, edge, e_lo, e_hi, 2, flags, own_row(first, w_lo, w_hi, n + 1))

    def stage_x(k, carry):
        out[k] = along_x(
            (smooth, k), (smooth, k + 1), (smooth, k + 2), inner, k, ridge[k + 1], first[k + 1]
        )
        return carry

    lax.fori_loop(0, n, stage_x, 0)
    zero = jnp.zeros(start.shape[1:], jnp.float32)
    sums = [(zero, zero) for _ in PRODUCTS]
    for x in range(n + 2):
        inside = 0 < x < n + 1
        fields = (start[x], first[x], out[x - 1] if inside else None)
        add_products(sums, range(5) if inside else range(3), fields)
    for k, (s, e) in enumerate(sums):
        grams[2 * k] = s
        grams[2 * k + 1] = e


def second_edge_kernel(
    edge, e_lo, e_hi, start, first, x_lo, x_hi, ridge, smooth, grams, out, share, rim
):
    n = smooth.shape[0]
    flags = mesh_flags()
    along_y(rim, 0, edge, e_lo, e_hi, 0, flags, side_row(x_lo))
    along_y(rim, 1, edge, e_lo, e_hi, 3, flags, side_row(x_hi))
    out[0] = along_x((rim, 0), (smooth, 0), (smooth, 1), edge, 1, ridge[0], first[0])
    out[1] = along_x(
        (smooth, n - 2), (smooth, n - 1), (rim, 1), edge, 2, ridge[n - 1], first[n - 1]
    )
    sums = [(grams[2 * k], grams[2 * k + 1]) for k in range(5)]
    for x, k in ((0, 0), (n - 1, 1)):
        add_products(sums, (3, 4), (start[x], first[x], out[k]))
    row = jnp.zeros((8, 128), jnp.float32)
    lane = lax.broadcasted_iota(jnp.int32, (8, 128), 1)
    for k, (s, e) in enumerate(sums):
        while s.shape[0] > 8:
            half = s.shape[0] // 2
            t, d = two_sum(s[:half], s[half:])
            s, e = (t, e[:half] + e[half:] + d)
        while s.shape[1] > 128:
            half = s.shape[1] // 2
            t, d = two_sum(s[:, :half], s[:, half:])
            s, e = (t, e[:, :half] + e[:, half:] + d)
        for axis, steps in ((0, (4, 2, 1)), (1, (64, 32, 16, 8, 4, 2, 1))):
            for step in steps:
                t, d = two_sum(s, pltpu.roll(s, step, axis))
                s, e = (t, (e + pltpu.roll(e, step, axis)) + d)
        row = jnp.where(lane == k, s, row)
        row = jnp.where(lane == 8 + k, e, row)
    share[...] = row[0:1]


def final_kernel(shares, start, first, inside, sides, solution_out, residual_out):
    s = shares[...]
    e = jnp.zeros_like(s)
    while s.shape[0] > 8:
        half = s.shape[0] // 2
        t, d = two_sum(s[:half], s[half:])
        s, e = (t, e[:half] + e[half:] + d)
    for step in (4, 2, 1):
        t, d = two_sum(s, pltpu.roll(s, step, 0))
        s, e = (t, (e + pltpu.roll(e, step, 0)) + d)
    lane = lax.broadcasted_iota(jnp.int32, s.shape, 1)

    def pick(value, k):
        return jnp.broadcast_to(
            jnp.sum(jnp.where(lane == k, value, 0.0), axis=1, keepdims=True), s.shape
        )

    g00, g01, g11, g02, g12 = [
        two_sum(pick(s, k), pick(e, k) + pick(s, 8 + k)) for k in range(5)
    ]
    alpha = g00[0] / g01[0]
    fresh = pair_add(pair_add(g00, pair_scale(g01, -2.0 * alpha)), pair_scale(pair_scale(g11, alpha), alpha))
    grow = 1.0 + fresh[0] / g00[0]
    curve = pair_add(
        pair_add(
            pair_scale(pair_scale(g01, grow), grow),
            pair_scale(pair_scale(pair_add(g02, g11), -alpha), grow),
        ),
        pair_scale(pair_scale(g12, alpha), alpha),
    )
    beta = fresh[0] / curve[0]
    near = (alpha + beta * grow)[0:1, 0:1]
    far = (alpha * beta)[0:1, 0:1]
    last = start.shape[0] - 1
    for x in range(last + 1):
        w2 = sides[0] if x == 0 else sides[1] if x == last else inside[x - 1]
        w0, w1 = (start[x], first[x])
        solution_out[x] = near * w0 - far * w1
        residual_out[x] = (w0 - near * w1) + far * w2


def per_device(features, conv_weight, conv_bias, occupancy, block_ids, ridge, target):
    rows, cols, channels, depth = features.shape
    voxels = depth // block_ids.shape[2]
    f32, bf16 = (jnp.float32, jnp.bfloat16)
    vmem = pl.BlockSpec(memory_space=pltpu.VMEM)
    anywhere = pl.BlockSpec(memory_space=pl.ANY)

    def call(kernel, args, outs, scratch, limit, name):
        return pl.pallas_call(
            kernel,
            out_shape=[jax.ShapeDtypeStruct(shape, dtype) for shape, dtype in outs],
            in_specs=[vmem for _ in args],
            out_specs=[vmem for _ in outs],
            scratch_shapes=[pltpu.VMEM(shape, dtype) for shape, dtype in scratch],
            compiler_params=pltpu.CompilerParams(vmem_limit_bytes=limit << 20),
            name=name,
        )(*args)

    edges = pl.pallas_call(
        edges_kernel,
        out_shape=[
            jax.ShapeDtypeStruct(shape + (channels, depth), bf16)
            for shape in ((2, cols), (2, cols), (rows, 1), (rows, 1))
        ],
        in_specs=[pl.BlockSpec(memory_space=pltpu.HBM)],
        out_specs=[anywhere] * 4,
        scratch_shapes=[pltpu.SemaphoreType.DMA((4,))],
        compiler_params=pltpu.CompilerParams(vmem_limit_bytes=1 << 20),
        name="edges",
    )(features)
    edges, occupancy, block_ids, target, conv_weight = lax.optimization_barrier(
        (edges, occupancy, block_ids, target, conv_weight)
    )
    x_lo, x_hi = (shift(edges[0], "sx", 1), shift(edges[1], "sx", -1))
    y_lo, y_hi = (shift(edges[2], "sy", 1), shift(edges[3], "sy", -1))

    present = (block_ids[:, :, :, 13] >= 0).astype(f32)
    weight_mask = occupancy.astype(f32) * jnp.repeat(present, voxels, axis=2)
    residual = weight_mask * target
    weight_mask, residual, y_lo, y_hi = lax.optimization_barrier(
        (weight_mask, residual, y_lo, y_hi)
    )
    m_lo, m_hi = [
        shift(jnp.stack([weight_mask[:, y], residual[:, y]]), "sy", step)
        for y, step in ((cols - 1, 1), (0, -1))
    ]
    wide, bias = call(
        weights_kernel,
        (conv_weight, conv_bias[None]),
        [((12 * channels, 16 * channels), bf16), ((channels, depth), f32)],
        [],
        8,
        "weights",
    )
    grid_scratch = ((rows, cols + 2, channels, depth), bf16)
    inner_shape = (rows - 2, cols, channels, depth)
    edge_shape = (4, cols, channels, depth)
    side_shape = (7, channels, depth)
    plane = ((rows, cols, depth), f32)
    side_hi, side_lo = call(
        sides_kernel,
        (y_lo, y_hi, m_lo, m_hi, weight_mask, residual),
        [(side_shape, bf16), (side_shape, bf16)],
        [],
        4,
        "sides",
    )
    side_lo, side_hi = (shift(side_hi, "sx", 1), shift(side_lo, "sx", -1))
    (inner,) = call(
        conv_inner_kernel,
        (features, y_lo, y_hi, m_lo, m_hi, weight_mask, wide, bias),
        [(inner_shape, bf16)],
        [grid_scratch],
        12,
        "conv_inner",
    )
    i_lo, i_hi = halo(inner, "sy", 1, 1)
    smooth, part = call(
        first_inner_kernel,
        (inner, i_lo, i_hi, residual, m_lo, m_hi, ridge),
        [(inner_shape, f32), ((rows - 4, cols, depth), f32)],
        [],
        8,
        "first_inner",
    )
    (edge,) = call(
        conv_edge_kernel,
        (features, y_lo, y_hi, m_lo, m_hi, x_lo, x_hi, side_lo, side_hi, weight_mask, wide, bias),
        [(edge_shape, bf16)],
        [grid_scratch, ((4, cols, depth), f32)],
        12,
        "conv_edge",
    )
    e_lo, e_hi = halo(edge, "sy", 1, 1)
    (first,) = call(
        first_edge_kernel,
        (inner, edge, e_lo, e_hi, residual, m_lo, m_hi, side_lo, side_hi, ridge, smooth, part),
        [plane],
        [(edge_shape, f32), ((2, cols, depth), f32), ((2, 8, depth), f32)],
        8,
        "first_edge",
    )
    w_lo, w_hi = (shift(first[:, -1], "sy", 1), shift(first[:, 0], "sy", -1))
    rims = [jnp.concatenate([w_lo[x : x + 1], first[x], w_hi[x : x + 1]]) for x in (rows - 1, 0)]
    r_lo, r_hi = (shift(rims[0], "sx", 1), shift(rims[1], "sx", -1))
    smooth, inside, grams = call(
        second_inner_kernel,
        (inner, edge, i_lo, i_hi, e_lo, e_hi, residual, first, w_lo, w_hi, ridge),
        [
            ((rows, cols, channels, depth), f32),
            ((rows - 2, cols, depth), f32),
            ((2 * len(PRODUCTS), cols, depth), f32),
        ],
        [],
        8,
        "second_inner",
    )
    sides, share = call(
        second_edge_kernel,
        (edge, e_lo, e_hi, residual, first, r_lo, r_hi, ridge, smooth, grams),
        [((2, cols, depth), f32), ((1, 128), f32)],
        [((2, cols, channels, depth), f32)],
        8,
        "second_edge",
    )

    peers = lax.axis_size("sx") * lax.axis_size("sy")
    shares = lax.all_to_all(jnp.broadcast_to(share[None], (peers, 1, 128)), AXES, 0, 0)
    return tuple(
        call(
            final_kernel,
            (shares.reshape(peers, 128), residual, first, inside, sides),
            [plane, plane],
            [],
            8,
            "final",
        )
    )


def solution(mesh):
    placed = (
        P("sx", "sy", None, None),
        P(),
        P(),
        P("sx", "sy", None),
        P("sx", "sy", None, None),
        P("sx", "sy", None),
        P("sx", "sy", None),
    )
    return jax.shard_map(
        per_device,
        mesh=mesh,
        in_specs=placed,
        out_specs=(P("sx", "sy", None), P("sx", "sy", None)),
        check_vma=False,
    )
```

```python
import jax
import jax.numpy as jnp
from jax import lax
from jax.experimental import pallas as pl
from jax.experimental.pallas import tpu as pltpu
from jax.sharding import PartitionSpec as P

AXES = ("sx", "sy")


def shift(value, axis, step):
    peers = lax.axis_size(axis)
    return lax.ppermute(value, axis, [(i, (i + step) % peers) for i in range(peers)])


def halo(value, axis, dim, width):
    length = value.shape[dim]
    before = shift(lax.slice_in_dim(value, length - width, length, axis=dim), axis, 1)
    after = shift(lax.slice_in_dim(value, 0, width, axis=dim), axis, -1)
    return before, after


def edges_kernel(own, x_hi, x_lo, token, sems):
    rows = own.shape[0]
    copies = [
        pltpu.make_async_copy(own.at[rows - 2 : rows], x_hi, sems.at[0]),
        pltpu.make_async_copy(own.at[0:2], x_lo, sems.at[1]),
    ]
    for copy in copies:
        copy.start()
    token[...] = jnp.zeros_like(token)
    for copy in copies:
        copy.wait()


def three(value):
    high = value.astype(jnp.bfloat16).astype(jnp.float32)
    rest = value - high
    mid = rest.astype(jnp.bfloat16).astype(jnp.float32)
    return high, mid, rest - mid


def prep_kernel(token, own, ids, occupancy, target, mask, start, out_hi, out_lo, present):
    rows, cols, channels, depth = own.shape
    half = present.shape[1]
    present[...] = jnp.broadcast_to(
        jnp.where(ids[:, 13:14] >= 0, 1.0, 0.0).astype(jnp.float32), present.shape
    )
    for x in range(rows):
        blocks = [present[pl.ds(2 * cols * x + z, cols, stride=2), :] for z in range(depth // half)]
        mask[x] = occupancy[x].astype(jnp.float32) * jnp.concatenate(blocks, axis=1)
        start[x] = mask[x] * target[x]
    for out, y in ((out_hi, cols - 1), (out_lo, 0)):
        for x in range(rows):
            out[x] = own[x, y] * mask[x, y : y + 1, :].astype(jnp.bfloat16)
        edge = jnp.concatenate([start[x, y : y + 1, :] for x in range(rows)], axis=0)
        blank = jnp.zeros((channels - 3 * rows, depth), jnp.float32)
        out[rows] = jnp.concatenate([*three(edge), blank], axis=0).astype(jnp.bfloat16)


def start_rims(y_lo, y_hi, out):
    rows = y_lo.shape[0] - 1
    for k, ref in enumerate((y_lo, y_hi)):
        terms = ref[rows].astype(jnp.float32)
        out[k] = (terms[:rows] + terms[rows : 2 * rows]) + terms[2 * rows : 3 * rows]


def weights_kernel(taps, bias, wide, bias_col):
    channels = taps.shape[1]
    width = 16 * channels
    row = lax.broadcasted_iota(jnp.int32, (channels, width), 0)
    lane = lax.broadcasted_iota(jnp.int32, (channels, width), 1)
    repeat = jnp.where(lane % channels == row, 1.0, 0.0).astype(jnp.bfloat16)
    group = lane // channels
    for z in range(3):
        every = [
            jnp.dot(taps[3 * k + z], repeat, preferred_element_type=jnp.float32) for k in range(9)
        ]
        for out_x in range(2):
            for out_y in range(2):
                total = jnp.zeros((channels, width), jnp.float32)
                for k in range(9):
                    at = (out_x + k // 3) * 4 + out_y + k % 3
                    total = jnp.where(group == at, every[k], total)
                start = ((z * 2 + out_x) * 2 + out_y) * channels
                wide[start : start + channels] = total.astype(jnp.bfloat16)
    square = (channels, channels)
    same = lax.broadcasted_iota(jnp.int32, square, 0) == lax.broadcasted_iota(jnp.int32, square, 1)
    column = jnp.sum(jnp.where(same, bias[...], 0.0), axis=1, keepdims=True)
    bias_col[...] = jnp.broadcast_to(column, bias_col.shape)


def mesh_flags():
    keep = []
    for axis in ("sy", "sx"):
        where = lax.axis_index(axis)
        keep += [where > 0, where < lax.axis_size(axis) - 1]
    return [jnp.where(k, 1.0, 0.0) for k in keep]


def conv_block(grid, masks, wide, bias_all, lane, grid_x, y, out, out_x):
    channels, depth = bias_all.shape
    window = jnp.concatenate(
        [grid[grid_x + k, y : y + 4].reshape(4 * channels, depth) for k in range(4)], axis=0
    )
    parts = jnp.dot(wide[...], window, preferred_element_type=jnp.float32)
    low = pltpu.roll(parts[0 : 4 * channels], 1, 1)
    high = pltpu.roll(parts[8 * channels :], depth - 1, 1)
    total = parts[4 * channels : 8 * channels]
    total = total + jnp.where(lane == 0, 0.0, low) + jnp.where(lane == depth - 1, 0.0, high)
    for step_x in range(2):
        for step_y in range(2):
            at = (step_x * 2 + step_y) * channels
            keep = masks[step_x](y + step_y)
            value = keep * (total[at : at + channels] + bias_all)
            out[out_x + step_x, y + step_y] = value.astype(jnp.bfloat16)


def splat(flag, shape):
    return jnp.full(shape, flag, jnp.float32).astype(jnp.bfloat16)


def fill_row(grid, grid_x, mask, middle, low, high):
    cols = grid.shape[1] - 2
    grid[grid_x, 0] = low
    for y in range(cols):
        grid[grid_x, y + 1] = middle(y) * mask(y).astype(jnp.bfloat16)
    grid[grid_x, cols + 1] = high


def fill_own(grid, grid_x, own, mask, y_lo, y_hi, flags, x):
    low = y_lo[x] * splat(flags[0], y_lo.shape[1:])
    high = y_hi[x] * splat(flags[1], y_hi.shape[1:])
    fill_row(grid, grid_x, mask_of(mask, x), lambda y: own[x, y], low, high)


def mask_of(mask, x):
    return lambda y: mask[x, y : y + 1, :]


def conv_inner_kernel(own, y_lo, y_hi, mask, wide, bias, out, grid):
    rows, cols, channels, depth = own.shape
    flags = mesh_flags()

    def fill(x, carry):
        fill_own(grid, x, own, mask, y_lo, y_hi, flags, x)
        return carry

    lax.fori_loop(0, rows, fill, 0)
    lane = lax.broadcasted_iota(jnp.int32, (4 * channels, depth), 1)
    bias_all = bias[...]

    def pair(i, carry):
        masks = (mask_of(mask, 2 * i + 1), mask_of(mask, 2 * i + 2))
        for y in range(0, cols, 2):
            conv_block(grid, masks, wide, bias_all, lane, 2 * i, y, out, 2 * i)
        return carry

    lax.fori_loop(0, rows // 2 - 1, pair, 0)


def sides_kernel(y_lo, y_hi, mask, start, out_hi, out_lo):
    rows, cols, depth = mask.shape
    flags = mesh_flags()
    clear = [splat(flag, y_lo.shape[1:]) for flag in flags[:2]]
    low_terms = y_lo[rows].astype(jnp.float32)
    high_terms = y_hi[rows].astype(jnp.float32)
    for out, pair, row in ((out_hi, (rows - 2, rows - 1), rows - 1), (out_lo, (0, 1), 0)):
        for k, x in enumerate(pair):
            out[2 * k] = y_lo[x] * clear[0]
            out[2 * k + 1] = y_hi[x] * clear[1]
        out[4] = jnp.concatenate([mask[x] for x in pair], axis=0).astype(jnp.bfloat16)
        high, mid, low = three(start[row])
        rims = [
            terms[at : at + 1]
            for at in (row, rows + row, 2 * rows + row)
            for terms in (low_terms, high_terms)
        ]
        blank = jnp.zeros((10, depth), jnp.float32)
        out[5] = jnp.concatenate([high, mid], axis=0).astype(jnp.bfloat16)
        out[6] = jnp.concatenate([low, *rims, blank], axis=0).astype(jnp.bfloat16)


def conv_edge_kernel(
    own,
    y_lo,
    y_hi,
    x_lo,
    x_hi,
    side_lo,
    side_hi,
    mask,
    wide,
    bias,
    out,
    grid,
    side_mask,
):
    rows, cols, channels, depth = own.shape
    flags = mesh_flags()
    for k, side in enumerate((side_lo, side_hi)):
        both = side[4].astype(jnp.float32) * flags[2 + k]
        side_mask[2 * k] = both[:cols]
        side_mask[2 * k + 1] = both[cols:]
    for x in range(2):
        for k, ref, side in ((0, x_lo, side_lo), (1, x_hi, side_hi)):
            clear = splat(flags[2 + k], (channels, depth))
            fill_row(
                grid,
                6 * k + x,
                mask_of(side_mask, 2 * k + x),
                lambda y: ref[x, y],
                side[2 * x] * clear,
                side[2 * x + 1] * clear,
            )
        fill_own(grid, 2 + x, own, mask, y_lo, y_hi, flags, x)
        fill_own(grid, 4 + x, own, mask, y_lo, y_hi, flags, rows - 2 + x)
    lane = lax.broadcasted_iota(jnp.int32, (4 * channels, depth), 1)
    bias_all = bias[...]
    for side, masks in (
        (0, (mask_of(side_mask, 1), mask_of(mask, 0))),
        (1, (mask_of(mask, rows - 1), mask_of(side_mask, 2))),
    ):
        for y in range(0, cols, 2):
            conv_block(grid, masks, wide, bias_all, lane, 4 * side, y, out, 2 * side)


def two_sum(a, b):
    s = a + b
    t = s - a
    return s, (a - (s - t)) + (b - t)


def split(a):
    c = a * 4097.0
    high = c - (c - a)
    return high, a - high


def two_prod(a, b):
    p = a * b
    a_hi, a_lo = split(a)
    b_hi, b_lo = split(b)
    return p, ((a_hi * b_hi - p) + a_hi * b_lo + a_lo * b_hi) + a_lo * b_lo


def pair_add(a, b):
    s, t = two_sum(a[0], b[0])
    return two_sum(s, t + (a[1] + b[1]))


def pair_scale(a, c):
    p, t = two_prod(a[0], c)
    return two_sum(p, t + a[1] * c)


def along_y(smooth, dst, field, f_lo, f_hi, row, flags, value_at):
    cols = smooth.shape[1]

    def product(y):
        if y == 0:
            return f_lo[row, 0].astype(jnp.float32) * (value_at(y) * flags[0])
        if y == cols + 1:
            return f_hi[row, 0].astype(jnp.float32) * (value_at(y) * flags[1])
        return field[row, y - 1].astype(jnp.float32) * value_at(y)

    here = product(1)
    pair = product(0) + here
    for y in range(cols):
        following = product(y + 2)
        pair_next = here + following
        smooth[dst, y] = pair + pair_next
        here = following
        pair = pair_next


def own_row(own, lo, hi, x):
    cols = own.shape[1]

    def at(y):
        if y == 0:
            return lo(x)
        if y == cols + 1:
            return hi(x)
        return own[x, y - 1 : y, :]

    return at


def side_row(side):
    return lambda y: side[y : y + 1, :]


def rim_of(ref, *index):
    return lambda x: ref[(*index, pl.ds(x, 1))]


def along_x(before, here, after, field, row, ridge_row, value_row):
    ref, x = here
    cols, channels, depth = ref.shape[1:]
    lane = lax.broadcasted_iota(jnp.int32, (channels, depth), 1)
    sums = []
    for y in range(cols):
        mid = ref[x, y]
        both = (before[0][before[1], y] + mid) + (mid + after[0][after[1], y])
        up = jnp.where(lane == depth - 1, 0.0, pltpu.roll(both, depth - 1, 1))
        down = jnp.where(lane == 0, 0.0, pltpu.roll(both, 1, 1))
        both = (both + both) + (up + down)
        prod = both * field[row, y].astype(jnp.float32)
        sums.append(jnp.sum(prod, axis=0, keepdims=True))
    inner = jnp.concatenate(sums, axis=0)
    return ridge_row * value_row + inner * (1.0 / (8 * channels))


def first_inner_kernel(inner, i_lo, i_hi, start, y_lo, y_hi, ridge, smooth, out, rims):
    rows = inner.shape[0]
    flags = mesh_flags()
    start_rims(y_lo, y_hi, rims)
    s_lo, s_hi = (rim_of(rims, 0), rim_of(rims, 1))

    def stage_y(k, carry):
        along_y(smooth, k, inner, i_lo, i_hi, k, flags, own_row(start, s_lo, s_hi, k + 1))
        return carry

    lax.fori_loop(0, rows, stage_y, 0)

    def stage_x(k, carry):
        out[k] = along_x(
            (smooth, k), (smooth, k + 1), (smooth, k + 2), inner, k + 1, ridge[k + 2], start[k + 2]
        )
        return carry

    lax.fori_loop(0, rows - 2, stage_x, 0)


def first_edge_kernel(
    inner,
    edge,
    e_lo,
    e_hi,
    start,
    y_lo,
    y_hi,
    side_lo,
    side_hi,
    ridge,
    smooth,
    part,
    out,
    out_hi,
    out_lo,
    rim,
    side_start,
    side_rims,
    rims,
):
    n = inner.shape[0]
    flags = mesh_flags()
    last = n + 1
    cols = inner.shape[1]
    start_rims(y_lo, y_hi, rims)
    s_lo, s_hi = (rim_of(rims, 0), rim_of(rims, 1))
    for k, side in enumerate((side_lo, side_hi)):
        upper = side[5].astype(jnp.float32)
        lower = side[6].astype(jnp.float32)
        side_start[k] = (upper[:cols] + upper[cols:]) + lower[:cols]
        ends = lower[cols : cols + 8]
        side_rims[k, 0:2] = (ends[0:2] + ends[2:4]) + ends[4:6]

    def side_values(k):
        def at(y):
            if y == 0:
                return side_rims[k, 0:1]
            if y == cols + 1:
                return side_rims[k, 1:2]
            return side_start[k, y - 1 : y]

        return at

    along_y(rim, 0, edge, e_lo, e_hi, 0, flags, side_values(0))
    along_y(rim, 1, edge, e_lo, e_hi, 1, flags, own_row(start, s_lo, s_hi, 0))
    along_y(rim, 2, edge, e_lo, e_hi, 2, flags, own_row(start, s_lo, s_hi, last))
    along_y(rim, 3, edge, e_lo, e_hi, 3, flags, side_values(1))
    for x, before, here, after, field, row in (
        (0, (rim, 0), (rim, 1), (smooth, 0), edge, 1),
        (1, (rim, 1), (smooth, 0), (smooth, 1), inner, 0),
        (last - 1, (smooth, n - 2), (smooth, n - 1), (rim, 2), inner, n - 1),
        (last, (smooth, n - 1), (rim, 2), (rim, 3), edge, 2),
    ):
        out[x] = along_x(before, here, after, field, row, ridge[x], start[x])
    for x in range(n - 2):
        out[x + 2] = part[x]
    for ref, y in ((out_hi, cols - 1), (out_lo, 0)):
        ref[...] = jnp.concatenate([out[x, y : y + 1, :] for x in range(n + 2)], axis=0)


PRODUCTS = ((0, 0), (0, 1), (1, 1), (0, 2), (1, 2))


def add_products(sums, which, fields):
    for k in which:
        a, b = PRODUCTS[k]
        p, e = two_prod(fields[a], fields[b])
        s, t = two_sum(sums[k][0], p)
        sums[k] = (s, sums[k][1] + (t + e))


def second_inner_kernel(
    inner, edge, i_lo, i_hi, e_lo, e_hi, start, first, w_lo, w_hi, ridge, smooth, out, grams
):
    n = inner.shape[0]
    flags = mesh_flags()
    w_lo, w_hi = (rim_of(w_lo), rim_of(w_hi))

    def stage_y(k, carry):
        along_y(smooth, k + 1, inner, i_lo, i_hi, k, flags, own_row(first, w_lo, w_hi, k + 1))
        return carry

    lax.fori_loop(0, n, stage_y, 0)
    along_y(smooth, 0, edge, e_lo, e_hi, 1, flags, own_row(first, w_lo, w_hi, 0))
    along_y(smooth, n + 1, edge, e_lo, e_hi, 2, flags, own_row(first, w_lo, w_hi, n + 1))

    def stage_x(k, carry):
        out[k] = along_x(
            (smooth, k), (smooth, k + 1), (smooth, k + 2), inner, k, ridge[k + 1], first[k + 1]
        )
        return carry

    lax.fori_loop(0, n, stage_x, 0)
    zero = jnp.zeros(start.shape[1:], jnp.float32)
    sums = [(zero, zero) for _ in PRODUCTS]
    for x in range(n + 2):
        inside = 0 < x < n + 1
        fields = (start[x], first[x], out[x - 1] if inside else None)
        add_products(sums, range(5) if inside else range(3), fields)
    for k, (s, e) in enumerate(sums):
        grams[2 * k] = s
        grams[2 * k + 1] = e


def second_edge_kernel(
    edge, e_lo, e_hi, start, first, x_lo, x_hi, ridge, smooth, grams, out, share, rim
):
    n = smooth.shape[0]
    flags = mesh_flags()
    along_y(rim, 0, edge, e_lo, e_hi, 0, flags, side_row(x_lo))
    along_y(rim, 1, edge, e_lo, e_hi, 3, flags, side_row(x_hi))
    out[0] = along_x((rim, 0), (smooth, 0), (smooth, 1), edge, 1, ridge[0], first[0])
    out[1] = along_x(
        (smooth, n - 2), (smooth, n - 1), (rim, 1), edge, 2, ridge[n - 1], first[n - 1]
    )
    sums = [(grams[2 * k], grams[2 * k + 1]) for k in range(5)]
    for x, k in ((0, 0), (n - 1, 1)):
        add_products(sums, (3, 4), (start[x], first[x], out[k]))
    row = jnp.zeros((8, 128), jnp.float32)
    lane = lax.broadcasted_iota(jnp.int32, (8, 128), 1)
    for k, (s, e) in enumerate(sums):
        while s.shape[0] > 8:
            half = s.shape[0] // 2
            t, d = two_sum(s[:half], s[half:])
            s, e = (t, e[:half] + e[half:] + d)
        while s.shape[1] > 128:
            half = s.shape[1] // 2
            t, d = two_sum(s[:, :half], s[:, half:])
            s, e = (t, e[:, :half] + e[:, half:] + d)
        for axis, steps in ((0, (4, 2, 1)), (1, (64, 32, 16, 8, 4, 2, 1))):
            for step in steps:
                t, d = two_sum(s, pltpu.roll(s, step, axis))
                s, e = (t, (e + pltpu.roll(e, step, axis)) + d)
        row = jnp.where(lane == k, s, row)
        row = jnp.where(lane == 8 + k, e, row)
    share[...] = row[0:1]


def final_kernel(shares, start, first, inside, sides, solution_out, residual_out):
    s = shares[...]
    e = jnp.zeros_like(s)
    while s.shape[0] > 8:
        half = s.shape[0] // 2
        t, d = two_sum(s[:half], s[half:])
        s, e = (t, e[:half] + e[half:] + d)
    for step in (4, 2, 1):
        t, d = two_sum(s, pltpu.roll(s, step, 0))
        s, e = (t, (e + pltpu.roll(e, step, 0)) + d)
    lane = lax.broadcasted_iota(jnp.int32, s.shape, 1)

    def pick(value, k):
        return jnp.broadcast_to(
            jnp.sum(jnp.where(lane == k, value, 0.0), axis=1, keepdims=True), s.shape
        )

    g00, g01, g11, g02, g12 = [
        two_sum(pick(s, k), pick(e, k) + pick(s, 8 + k)) for k in range(5)
    ]
    alpha = g00[0] / g01[0]
    fresh = pair_add(pair_add(g00, pair_scale(g01, -2.0 * alpha)), pair_scale(pair_scale(g11, alpha), alpha))
    grow = 1.0 + fresh[0] / g00[0]
    curve = pair_add(
        pair_add(
            pair_scale(pair_scale(g01, grow), grow),
            pair_scale(pair_scale(pair_add(g02, g11), -alpha), grow),
        ),
        pair_scale(pair_scale(g12, alpha), alpha),
    )
    beta = fresh[0] / curve[0]
    near = (alpha + beta * grow)[0:1, 0:1]
    far = (alpha * beta)[0:1, 0:1]
    last = start.shape[0] - 1
    for x in range(last + 1):
        w2 = sides[0] if x == 0 else sides[1] if x == last else inside[x - 1]
        w0, w1 = (start[x], first[x])
        solution_out[x] = near * w0 - far * w1
        residual_out[x] = (w0 - near * w1) + far * w2


def per_device(features, conv_weight, conv_bias, occupancy, block_ids, ridge, target):
    rows, cols, channels, depth = features.shape
    f32, bf16 = (jnp.float32, jnp.bfloat16)
    vmem = pl.BlockSpec(memory_space=pltpu.VMEM)
    anywhere = pl.BlockSpec(memory_space=pl.ANY)

    def call(kernel, args, outs, scratch, limit, name):
        return pl.pallas_call(
            kernel,
            out_shape=[jax.ShapeDtypeStruct(shape, dtype) for shape, dtype in outs],
            in_specs=[vmem for _ in args],
            out_specs=[vmem for _ in outs],
            scratch_shapes=[pltpu.VMEM(shape, dtype) for shape, dtype in scratch],
            compiler_params=pltpu.CompilerParams(vmem_limit_bytes=limit << 20),
            name=name,
        )(*args)

    x_hi, x_lo, token = pl.pallas_call(
        edges_kernel,
        out_shape=[jax.ShapeDtypeStruct((2, cols, channels, depth), bf16) for _ in range(2)]
        + [jax.ShapeDtypeStruct((8, 128), f32)],
        in_specs=[anywhere],
        out_specs=[anywhere, anywhere, vmem],
        scratch_shapes=[pltpu.SemaphoreType.DMA((2,))],
        compiler_params=pltpu.CompilerParams(vmem_limit_bytes=60 << 20),
        name="edges",
    )(features)
    x_lo, x_hi = (shift(x_hi, "sx", 1), shift(x_lo, "sx", -1))

    plane = ((rows, cols, depth), f32)
    blocks = block_ids.reshape(-1, block_ids.shape[3])
    edge_column = ((rows + 1, channels, depth), bf16)
    weight_mask, residual, y_hi, y_lo = call(
        prep_kernel,
        (token, features, blocks, occupancy, target),
        [plane, plane, edge_column, edge_column],
        [((blocks.shape[0], depth // block_ids.shape[2]), f32)],
        4,
        "prep",
    )
    y_lo, y_hi = (shift(y_hi, "sy", 1), shift(y_lo, "sy", -1))
    wide, bias = call(
        weights_kernel,
        (conv_weight, conv_bias[None]),
        [((12 * channels, 16 * channels), bf16), ((channels, depth), f32)],
        [],
        8,
        "weights",
    )
    rims_scratch = ((2, rows, depth), f32)
    grid_scratch = ((rows, cols + 2, channels, depth), bf16)
    inner_shape = (rows - 2, cols, channels, depth)
    edge_shape = (4, cols, channels, depth)
    side_shape = (7, channels, depth)
    side_hi, side_lo = call(
        sides_kernel,
        (y_lo, y_hi, weight_mask, residual),
        [(side_shape, bf16), (side_shape, bf16)],
        [],
        4,
        "sides",
    )
    side_lo, side_hi = (shift(side_hi, "sx", 1), shift(side_lo, "sx", -1))
    (inner,) = call(
        conv_inner_kernel,
        (features, y_lo, y_hi, weight_mask, wide, bias),
        [(inner_shape, bf16)],
        [grid_scratch],
        12,
        "conv_inner",
    )
    i_lo, i_hi = halo(inner, "sy", 1, 1)
    smooth, part = call(
        first_inner_kernel,
        (inner, i_lo, i_hi, residual, y_lo, y_hi, ridge),
        [(inner_shape, f32), ((rows - 4, cols, depth), f32)],
        [rims_scratch],
        8,
        "first_inner",
    )
    (edge,) = call(
        conv_edge_kernel,
        (features, y_lo, y_hi, x_lo, x_hi, side_lo, side_hi, weight_mask, wide, bias),
        [(edge_shape, bf16)],
        [grid_scratch, ((4, cols, depth), f32)],
        12,
        "conv_edge",
    )
    e_lo, e_hi = halo(edge, "sy", 1, 1)
    first, w_hi, w_lo = call(
        first_edge_kernel,
        (inner, edge, e_lo, e_hi, residual, y_lo, y_hi, side_lo, side_hi, ridge, smooth, part),
        [plane, ((rows, depth), f32), ((rows, depth), f32)],
        [(edge_shape, f32), ((2, cols, depth), f32), ((2, 8, depth), f32), rims_scratch],
        8,
        "first_edge",
    )
    w_lo, w_hi = (shift(w_hi, "sy", 1), shift(w_lo, "sy", -1))
    rims = [jnp.concatenate([w_lo[x : x + 1], first[x], w_hi[x : x + 1]]) for x in (rows - 1, 0)]
    r_lo, r_hi = (shift(rims[0], "sx", 1), shift(rims[1], "sx", -1))
    smooth, inside, grams = call(
        second_inner_kernel,
        (inner, edge, i_lo, i_hi, e_lo, e_hi, residual, first, w_lo, w_hi, ridge),
        [
            ((rows, cols, channels, depth), f32),
            ((rows - 2, cols, depth), f32),
            ((2 * len(PRODUCTS), cols, depth), f32),
        ],
        [],
        8,
        "second_inner",
    )
    sides, share = call(
        second_edge_kernel,
        (edge, e_lo, e_hi, residual, first, r_lo, r_hi, ridge, smooth, grams),
        [((2, cols, depth), f32), ((1, 128), f32)],
        [((2, cols, channels, depth), f32)],
        8,
        "second_edge",
    )

    peers = lax.axis_size("sx") * lax.axis_size("sy")
    shares = lax.all_to_all(jnp.broadcast_to(share[None], (peers, 1, 128)), AXES, 0, 0)
    return tuple(
        call(
            final_kernel,
            (shares.reshape(peers, 128), residual, first, inside, sides),
            [plane, plane],
            [],
            8,
            "final",
        )
    )


def solution(mesh):
    placed = (
        P("sx", "sy", None, None),
        P(),
        P(),
        P("sx", "sy", None),
        P("sx", "sy", None, None),
        P("sx", "sy", None),
        P("sx", "sy", None),
    )
    return jax.shard_map(
        per_device,
        mesh=mesh,
        in_specs=placed,
        out_specs=(P("sx", "sy", None), P("sx", "sy", None)),
        check_vma=False,
    )
```

```python
import jax
import jax.numpy as jnp
from jax import lax
from jax.experimental import pallas as pl
from jax.experimental.pallas import tpu as pltpu
from jax.sharding import PartitionSpec as P

AXES = ("sx", "sy")


def shift(value, axis, step):
    peers = lax.axis_size(axis)
    return lax.ppermute(value, axis, [(i, (i + step) % peers) for i in range(peers)])


def halo(value, axis, dim, width):
    length = value.shape[dim]
    before = shift(lax.slice_in_dim(value, length - width, length, axis=dim), axis, 1)
    after = shift(lax.slice_in_dim(value, 0, width, axis=dim), axis, -1)
    return before, after


def three(value):
    high = value.astype(jnp.bfloat16).astype(jnp.float32)
    rest = value - high
    mid = rest.astype(jnp.bfloat16).astype(jnp.float32)
    return high, mid, rest - mid


def prep_kernel(own, ids, occupancy, target, mask, start, out_hi, out_lo, present):
    rows, cols, channels, depth = own.shape
    half = present.shape[1]
    present[...] = jnp.broadcast_to(
        jnp.where(ids[:, 13:14] >= 0, 1.0, 0.0).astype(jnp.float32), present.shape
    )
    for x in range(rows):
        blocks = [present[pl.ds(2 * cols * x + z, cols, stride=2), :] for z in range(depth // half)]
        mask[x] = occupancy[x].astype(jnp.float32) * jnp.concatenate(blocks, axis=1)
        start[x] = mask[x] * target[x]
    for out, y in ((out_hi, cols - 1), (out_lo, 0)):
        for x in range(rows):
            out[x] = own[x, y] * mask[x, y : y + 1, :].astype(jnp.bfloat16)
        edge = jnp.concatenate([start[x, y : y + 1, :] for x in range(rows)], axis=0)
        blank = jnp.zeros((channels - 3 * rows, depth), jnp.float32)
        out[rows] = jnp.concatenate([*three(edge), blank], axis=0).astype(jnp.bfloat16)


def start_rims(y_lo, y_hi, out):
    rows = y_lo.shape[0] - 1
    for k, ref in enumerate((y_lo, y_hi)):
        terms = ref[rows].astype(jnp.float32)
        out[k] = (terms[:rows] + terms[rows : 2 * rows]) + terms[2 * rows : 3 * rows]


def weights_kernel(taps, bias, wide, bias_col):
    channels = taps.shape[1]
    width = 16 * channels
    row = lax.broadcasted_iota(jnp.int32, (channels, width), 0)
    lane = lax.broadcasted_iota(jnp.int32, (channels, width), 1)
    repeat = jnp.where(lane % channels == row, 1.0, 0.0).astype(jnp.bfloat16)
    group = lane // channels
    for z in range(3):
        every = [
            jnp.dot(taps[3 * k + z], repeat, preferred_element_type=jnp.float32) for k in range(9)
        ]
        for out_x in range(2):
            for out_y in range(2):
                total = jnp.zeros((channels, width), jnp.float32)
                for k in range(9):
                    at = (out_x + k // 3) * 4 + out_y + k % 3
                    total = jnp.where(group == at, every[k], total)
                start = ((z * 2 + out_x) * 2 + out_y) * channels
                wide[start : start + channels] = total.astype(jnp.bfloat16)
    square = (channels, channels)
    same = lax.broadcasted_iota(jnp.int32, square, 0) == lax.broadcasted_iota(jnp.int32, square, 1)
    column = jnp.sum(jnp.where(same, bias[...], 0.0), axis=1, keepdims=True)
    bias_col[...] = jnp.broadcast_to(column, bias_col.shape)


def mesh_flags():
    keep = []
    for axis in ("sy", "sx"):
        where = lax.axis_index(axis)
        keep += [where > 0, where < lax.axis_size(axis) - 1]
    return [jnp.where(k, 1.0, 0.0) for k in keep]


def conv_block(grid, masks, wide, bias_all, lane, grid_x, y, out, out_x):
    channels, depth = bias_all.shape
    window = jnp.concatenate(
        [grid[grid_x + k, y : y + 4].reshape(4 * channels, depth) for k in range(4)], axis=0
    )
    parts = jnp.dot(wide[...], window, preferred_element_type=jnp.float32)
    low = pltpu.roll(parts[0 : 4 * channels], 1, 1)
    high = pltpu.roll(parts[8 * channels :], depth - 1, 1)
    total = parts[4 * channels : 8 * channels]
    total = total + jnp.where(lane == 0, 0.0, low) + jnp.where(lane == depth - 1, 0.0, high)
    for step_x in range(2):
        for step_y in range(2):
            at = (step_x * 2 + step_y) * channels
            keep = masks[step_x](y + step_y)
            value = keep * (total[at : at + channels] + bias_all)
            out[out_x + step_x, y + step_y] = value.astype(jnp.bfloat16)


def splat(flag, shape):
    return jnp.full(shape, flag, jnp.float32).astype(jnp.bfloat16)


def fill_row(grid, grid_x, mask, middle, low, high):
    cols = grid.shape[1] - 2
    grid[grid_x, 0] = low
    for y in range(cols):
        grid[grid_x, y + 1] = middle(y) * mask(y).astype(jnp.bfloat16)
    grid[grid_x, cols + 1] = high


def fill_own(grid, grid_x, own, mask, y_lo, y_hi, flags, x):
    low = y_lo[x] * splat(flags[0], y_lo.shape[1:])
    high = y_hi[x] * splat(flags[1], y_hi.shape[1:])
    fill_row(grid, grid_x, mask_of(mask, x), lambda y: own[x, y], low, high)


def mask_of(mask, x):
    return lambda y: mask[x, y : y + 1, :]


def conv_inner_kernel(own, y_lo, y_hi, mask, wide, bias, out, grid):
    rows, cols, channels, depth = own.shape
    flags = mesh_flags()

    def fill(x, carry):
        fill_own(grid, x, own, mask, y_lo, y_hi, flags, x)
        return carry

    lax.fori_loop(0, rows, fill, 0)
    lane = lax.broadcasted_iota(jnp.int32, (4 * channels, depth), 1)
    bias_all = bias[...]

    def pair(i, carry):
        masks = (mask_of(mask, 2 * i + 1), mask_of(mask, 2 * i + 2))
        for y in range(0, cols, 2):
            conv_block(grid, masks, wide, bias_all, lane, 2 * i, y, out, 2 * i)
        return carry

    lax.fori_loop(0, rows // 2 - 1, pair, 0)


def sides_kernel(y_lo, y_hi, mask, start, out_hi, out_lo):
    rows, cols, depth = mask.shape
    flags = mesh_flags()
    clear = [splat(flag, y_lo.shape[1:]) for flag in flags[:2]]
    low_terms = y_lo[rows].astype(jnp.float32)
    high_terms = y_hi[rows].astype(jnp.float32)
    for out, pair, row in ((out_hi, (rows - 2, rows - 1), rows - 1), (out_lo, (0, 1), 0)):
        for k, x in enumerate(pair):
            out[2 * k] = y_lo[x] * clear[0]
            out[2 * k + 1] = y_hi[x] * clear[1]
        out[4] = jnp.concatenate([mask[x] for x in pair], axis=0).astype(jnp.bfloat16)
        high, mid, low = three(start[row])
        rims = [
            terms[at : at + 1]
            for at in (row, rows + row, 2 * rows + row)
            for terms in (low_terms, high_terms)
        ]
        blank = jnp.zeros((10, depth), jnp.float32)
        out[5] = jnp.concatenate([high, mid], axis=0).astype(jnp.bfloat16)
        out[6] = jnp.concatenate([low, *rims, blank], axis=0).astype(jnp.bfloat16)


def conv_edge_kernel(
    own,
    y_lo,
    y_hi,
    x_lo,
    x_hi,
    side_lo,
    side_hi,
    mask,
    wide,
    bias,
    out,
    grid,
    side_mask,
):
    rows, cols, channels, depth = own.shape
    flags = mesh_flags()
    for k, side in enumerate((side_lo, side_hi)):
        both = side[4].astype(jnp.float32) * flags[2 + k]
        side_mask[2 * k] = both[:cols]
        side_mask[2 * k + 1] = both[cols:]
    for x in range(2):
        for k, ref, side in ((0, x_lo, side_lo), (1, x_hi, side_hi)):
            clear = splat(flags[2 + k], (channels, depth))
            fill_row(
                grid,
                6 * k + x,
                mask_of(side_mask, 2 * k + x),
                lambda y: ref[x, y],
                side[2 * x] * clear,
                side[2 * x + 1] * clear,
            )
        fill_own(grid, 2 + x, own, mask, y_lo, y_hi, flags, x)
        fill_own(grid, 4 + x, own, mask, y_lo, y_hi, flags, rows - 2 + x)
    lane = lax.broadcasted_iota(jnp.int32, (4 * channels, depth), 1)
    bias_all = bias[...]
    for side, masks in (
        (0, (mask_of(side_mask, 1), mask_of(mask, 0))),
        (1, (mask_of(mask, rows - 1), mask_of(side_mask, 2))),
    ):
        for y in range(0, cols, 2):
            conv_block(grid, masks, wide, bias_all, lane, 4 * side, y, out, 2 * side)


def two_sum(a, b):
    s = a + b
    t = s - a
    return s, (a - (s - t)) + (b - t)


def split(a):
    c = a * 4097.0
    high = c - (c - a)
    return high, a - high


def two_prod(a, b):
    p = a * b
    a_hi, a_lo = split(a)
    b_hi, b_lo = split(b)
    return p, ((a_hi * b_hi - p) + a_hi * b_lo + a_lo * b_hi) + a_lo * b_lo


def pair_add(a, b):
    s, t = two_sum(a[0], b[0])
    return two_sum(s, t + (a[1] + b[1]))


def pair_scale(a, c):
    p, t = two_prod(a[0], c)
    return two_sum(p, t + a[1] * c)


def along_y(smooth, dst, field, f_lo, f_hi, row, flags, value_at):
    cols = smooth.shape[1]

    def product(y):
        if y == 0:
            return f_lo[row, 0].astype(jnp.float32) * (value_at(y) * flags[0])
        if y == cols + 1:
            return f_hi[row, 0].astype(jnp.float32) * (value_at(y) * flags[1])
        return field[row, y - 1].astype(jnp.float32) * value_at(y)

    here = product(1)
    pair = product(0) + here
    for y in range(cols):
        following = product(y + 2)
        pair_next = here + following
        smooth[dst, y] = pair + pair_next
        here = following
        pair = pair_next


def own_row(own, lo, hi, x):
    cols = own.shape[1]

    def at(y):
        if y == 0:
            return lo(x)
        if y == cols + 1:
            return hi(x)
        return own[x, y - 1 : y, :]

    return at


def side_row(side):
    return lambda y: side[y : y + 1, :]


def rim_of(ref, *index):
    return lambda x: ref[(*index, pl.ds(x, 1))]


def along_x(before, here, after, field, row, ridge_row, value_row):
    ref, x = here
    cols, channels, depth = ref.shape[1:]
    lane = lax.broadcasted_iota(jnp.int32, (channels, depth), 1)
    sums = []
    for y in range(cols):
        mid = ref[x, y]
        both = (before[0][before[1], y] + mid) + (mid + after[0][after[1], y])
        up = jnp.where(lane == depth - 1, 0.0, pltpu.roll(both, depth - 1, 1))
        down = jnp.where(lane == 0, 0.0, pltpu.roll(both, 1, 1))
        both = (both + both) + (up + down)
        prod = both * field[row, y].astype(jnp.float32)
        sums.append(jnp.sum(prod, axis=0, keepdims=True))
    inner = jnp.concatenate(sums, axis=0)
    return ridge_row * value_row + inner * (1.0 / (8 * channels))


def first_inner_kernel(inner, i_lo, i_hi, start, y_lo, y_hi, ridge, smooth, out, rims):
    rows = inner.shape[0]
    flags = mesh_flags()
    start_rims(y_lo, y_hi, rims)
    s_lo, s_hi = (rim_of(rims, 0), rim_of(rims, 1))

    def stage_y(k, carry):
        along_y(smooth, k, inner, i_lo, i_hi, k, flags, own_row(start, s_lo, s_hi, k + 1))
        return carry

    lax.fori_loop(0, rows, stage_y, 0)

    def stage_x(k, carry):
        out[k] = along_x(
            (smooth, k), (smooth, k + 1), (smooth, k + 2), inner, k + 1, ridge[k + 2], start[k + 2]
        )
        return carry

    lax.fori_loop(0, rows - 2, stage_x, 0)


def first_edge_kernel(
    inner,
    edge,
    e_lo,
    e_hi,
    start,
    y_lo,
    y_hi,
    side_lo,
    side_hi,
    ridge,
    smooth,
    part,
    out,
    out_hi,
    out_lo,
    rim,
    side_start,
    side_rims,
    rims,
):
    n = inner.shape[0]
    flags = mesh_flags()
    last = n + 1
    cols = inner.shape[1]
    start_rims(y_lo, y_hi, rims)
    s_lo, s_hi = (rim_of(rims, 0), rim_of(rims, 1))
    for k, side in enumerate((side_lo, side_hi)):
        upper = side[5].astype(jnp.float32)
        lower = side[6].astype(jnp.float32)
        side_start[k] = (upper[:cols] + upper[cols:]) + lower[:cols]
        ends = lower[cols : cols + 8]
        side_rims[k, 0:2] = (ends[0:2] + ends[2:4]) + ends[4:6]

    def side_values(k):
        def at(y):
            if y == 0:
                return side_rims[k, 0:1]
            if y == cols + 1:
                return side_rims[k, 1:2]
            return side_start[k, y - 1 : y]

        return at

    along_y(rim, 0, edge, e_lo, e_hi, 0, flags, side_values(0))
    along_y(rim, 1, edge, e_lo, e_hi, 1, flags, own_row(start, s_lo, s_hi, 0))
    along_y(rim, 2, edge, e_lo, e_hi, 2, flags, own_row(start, s_lo, s_hi, last))
    along_y(rim, 3, edge, e_lo, e_hi, 3, flags, side_values(1))
    for x, before, here, after, field, row in (
        (0, (rim, 0), (rim, 1), (smooth, 0), edge, 1),
        (1, (rim, 1), (smooth, 0), (smooth, 1), inner, 0),
        (last - 1, (smooth, n - 2), (smooth, n - 1), (rim, 2), inner, n - 1),
        (last, (smooth, n - 1), (rim, 2), (rim, 3), edge, 2),
    ):
        out[x] = along_x(before, here, after, field, row, ridge[x], start[x])
    for x in range(n - 2):
        out[x + 2] = part[x]
    for ref, y in ((out_hi, cols - 1), (out_lo, 0)):
        ref[...] = jnp.concatenate([out[x, y : y + 1, :] for x in range(n + 2)], axis=0)


PRODUCTS = ((0, 0), (0, 1), (1, 1), (0, 2), (1, 2))


def add_products(sums, which, fields):
    for k in which:
        a, b = PRODUCTS[k]
        p, e = two_prod(fields[a], fields[b])
        s, t = two_sum(sums[k][0], p)
        sums[k] = (s, sums[k][1] + (t + e))


def second_inner_kernel(
    inner, edge, i_lo, i_hi, e_lo, e_hi, start, first, w_lo, w_hi, ridge, smooth, out, grams
):
    n = inner.shape[0]
    flags = mesh_flags()
    w_lo, w_hi = (rim_of(w_lo), rim_of(w_hi))

    def stage_y(k, carry):
        along_y(smooth, k + 1, inner, i_lo, i_hi, k, flags, own_row(first, w_lo, w_hi, k + 1))
        return carry

    lax.fori_loop(0, n, stage_y, 0)
    along_y(smooth, 0, edge, e_lo, e_hi, 1, flags, own_row(first, w_lo, w_hi, 0))
    along_y(smooth, n + 1, edge, e_lo, e_hi, 2, flags, own_row(first, w_lo, w_hi, n + 1))

    def stage_x(k, carry):
        out[k] = along_x(
            (smooth, k), (smooth, k + 1), (smooth, k + 2), inner, k, ridge[k + 1], first[k + 1]
        )
        return carry

    lax.fori_loop(0, n, stage_x, 0)
    zero = jnp.zeros(start.shape[1:], jnp.float32)
    sums = [(zero, zero) for _ in PRODUCTS]
    for x in range(n + 2):
        inside = 0 < x < n + 1
        fields = (start[x], first[x], out[x - 1] if inside else None)
        add_products(sums, range(5) if inside else range(3), fields)
    for k, (s, e) in enumerate(sums):
        grams[2 * k] = s
        grams[2 * k + 1] = e


def second_edge_kernel(
    edge, e_lo, e_hi, start, first, x_lo, x_hi, ridge, smooth, grams, out, share, rim
):
    n = smooth.shape[0]
    flags = mesh_flags()
    along_y(rim, 0, edge, e_lo, e_hi, 0, flags, side_row(x_lo))
    along_y(rim, 1, edge, e_lo, e_hi, 3, flags, side_row(x_hi))
    out[0] = along_x((rim, 0), (smooth, 0), (smooth, 1), edge, 1, ridge[0], first[0])
    out[1] = along_x(
        (smooth, n - 2), (smooth, n - 1), (rim, 1), edge, 2, ridge[n - 1], first[n - 1]
    )
    sums = [(grams[2 * k], grams[2 * k + 1]) for k in range(5)]
    for x, k in ((0, 0), (n - 1, 1)):
        add_products(sums, (3, 4), (start[x], first[x], out[k]))
    row = jnp.zeros((8, 128), jnp.float32)
    lane = lax.broadcasted_iota(jnp.int32, (8, 128), 1)
    for k, (s, e) in enumerate(sums):
        while s.shape[0] > 8:
            half = s.shape[0] // 2
            t, d = two_sum(s[:half], s[half:])
            s, e = (t, e[:half] + e[half:] + d)
        while s.shape[1] > 128:
            half = s.shape[1] // 2
            t, d = two_sum(s[:, :half], s[:, half:])
            s, e = (t, e[:, :half] + e[:, half:] + d)
        for axis, steps in ((0, (4, 2, 1)), (1, (64, 32, 16, 8, 4, 2, 1))):
            for step in steps:
                t, d = two_sum(s, pltpu.roll(s, step, axis))
                s, e = (t, (e + pltpu.roll(e, step, axis)) + d)
        row = jnp.where(lane == k, s, row)
        row = jnp.where(lane == 8 + k, e, row)
    share[...] = row[0:1]


def final_kernel(shares, start, first, inside, sides, solution_out, residual_out):
    s = shares[...]
    e = jnp.zeros_like(s)
    while s.shape[0] > 8:
        half = s.shape[0] // 2
        t, d = two_sum(s[:half], s[half:])
        s, e = (t, e[:half] + e[half:] + d)
    for step in (4, 2, 1):
        t, d = two_sum(s, pltpu.roll(s, step, 0))
        s, e = (t, (e + pltpu.roll(e, step, 0)) + d)
    lane = lax.broadcasted_iota(jnp.int32, s.shape, 1)

    def pick(value, k):
        return jnp.broadcast_to(
            jnp.sum(jnp.where(lane == k, value, 0.0), axis=1, keepdims=True), s.shape
        )

    g00, g01, g11, g02, g12 = [
        two_sum(pick(s, k), pick(e, k) + pick(s, 8 + k)) for k in range(5)
    ]
    alpha = g00[0] / g01[0]
    fresh = pair_add(pair_add(g00, pair_scale(g01, -2.0 * alpha)), pair_scale(pair_scale(g11, alpha), alpha))
    grow = 1.0 + fresh[0] / g00[0]
    curve = pair_add(
        pair_add(
            pair_scale(pair_scale(g01, grow), grow),
            pair_scale(pair_scale(pair_add(g02, g11), -alpha), grow),
        ),
        pair_scale(pair_scale(g12, alpha), alpha),
    )
    beta = fresh[0] / curve[0]
    near = (alpha + beta * grow)[0:1, 0:1]
    far = (alpha * beta)[0:1, 0:1]
    last = start.shape[0] - 1
    for x in range(last + 1):
        w2 = sides[0] if x == 0 else sides[1] if x == last else inside[x - 1]
        w0, w1 = (start[x], first[x])
        solution_out[x] = near * w0 - far * w1
        residual_out[x] = (w0 - near * w1) + far * w2


def per_device(features, conv_weight, conv_bias, occupancy, block_ids, ridge, target):
    rows, cols, channels, depth = features.shape
    f32, bf16 = (jnp.float32, jnp.bfloat16)
    vmem = pl.BlockSpec(memory_space=pltpu.VMEM)

    def call(kernel, args, outs, scratch, limit, name):
        return pl.pallas_call(
            kernel,
            out_shape=[jax.ShapeDtypeStruct(shape, dtype) for shape, dtype in outs],
            in_specs=[vmem for _ in args],
            out_specs=[vmem for _ in outs],
            scratch_shapes=[pltpu.VMEM(shape, dtype) for shape, dtype in scratch],
            compiler_params=pltpu.CompilerParams(vmem_limit_bytes=limit << 20),
            name=name,
        )(*args)

    edges, target = lax.optimization_barrier(((features[-2:], features[:2]), target))
    x_lo, x_hi = (shift(edges[0], "sx", 1), shift(edges[1], "sx", -1))

    plane = ((rows, cols, depth), f32)
    blocks = block_ids.reshape(-1, block_ids.shape[3])
    edge_column = ((rows + 1, channels, depth), bf16)
    weight_mask, residual, y_hi, y_lo = call(
        prep_kernel,
        (features, blocks, occupancy, target),
        [plane, plane, edge_column, edge_column],
        [((blocks.shape[0], depth // block_ids.shape[2]), f32)],
        4,
        "prep",
    )
    y_lo, y_hi = (shift(y_hi, "sy", 1), shift(y_lo, "sy", -1))
    wide, bias = call(
        weights_kernel,
        (conv_weight, conv_bias[None]),
        [((12 * channels, 16 * channels), bf16), ((channels, depth), f32)],
        [],
        8,
        "weights",
    )
    rims_scratch = ((2, rows, depth), f32)
    grid_scratch = ((rows, cols + 2, channels, depth), bf16)
    inner_shape = (rows - 2, cols, channels, depth)
    edge_shape = (4, cols, channels, depth)
    side_shape = (7, channels, depth)
    side_hi, side_lo = call(
        sides_kernel,
        (y_lo, y_hi, weight_mask, residual),
        [(side_shape, bf16), (side_shape, bf16)],
        [],
        4,
        "sides",
    )
    side_lo, side_hi = (shift(side_hi, "sx", 1), shift(side_lo, "sx", -1))
    (inner,) = call(
        conv_inner_kernel,
        (features, y_lo, y_hi, weight_mask, wide, bias),
        [(inner_shape, bf16)],
        [grid_scratch],
        12,
        "conv_inner",
    )
    i_lo, i_hi = halo(inner, "sy", 1, 1)
    smooth, part = call(
        first_inner_kernel,
        (inner, i_lo, i_hi, residual, y_lo, y_hi, ridge),
        [(inner_shape, f32), ((rows - 4, cols, depth), f32)],
        [rims_scratch],
        8,
        "first_inner",
    )
    (edge,) = call(
        conv_edge_kernel,
        (features, y_lo, y_hi, x_lo, x_hi, side_lo, side_hi, weight_mask, wide, bias),
        [(edge_shape, bf16)],
        [grid_scratch, ((4, cols, depth), f32)],
        12,
        "conv_edge",
    )
    e_lo, e_hi = halo(edge, "sy", 1, 1)
    first, w_hi, w_lo = call(
        first_edge_kernel,
        (inner, edge, e_lo, e_hi, residual, y_lo, y_hi, side_lo, side_hi, ridge, smooth, part),
        [plane, ((rows, depth), f32), ((rows, depth), f32)],
        [(edge_shape, f32), ((2, cols, depth), f32), ((2, 8, depth), f32), rims_scratch],
        8,
        "first_edge",
    )
    w_lo, w_hi = (shift(w_hi, "sy", 1), shift(w_lo, "sy", -1))
    rims = [jnp.concatenate([w_lo[x : x + 1], first[x], w_hi[x : x + 1]]) for x in (rows - 1, 0)]
    r_lo, r_hi = (shift(rims[0], "sx", 1), shift(rims[1], "sx", -1))
    smooth, inside, grams = call(
        second_inner_kernel,
        (inner, edge, i_lo, i_hi, e_lo, e_hi, residual, first, w_lo, w_hi, ridge),
        [
            ((rows, cols, channels, depth), f32),
            ((rows - 2, cols, depth), f32),
            ((2 * len(PRODUCTS), cols, depth), f32),
        ],
        [],
        8,
        "second_inner",
    )
    sides, share = call(
        second_edge_kernel,
        (edge, e_lo, e_hi, residual, first, r_lo, r_hi, ridge, smooth, grams),
        [((2, cols, depth), f32), ((1, 128), f32)],
        [((2, cols, channels, depth), f32)],
        8,
        "second_edge",
    )

    peers = lax.axis_size("sx") * lax.axis_size("sy")
    shares = lax.all_to_all(jnp.broadcast_to(share[None], (peers, 1, 128)), AXES, 0, 0)
    return tuple(
        call(
            final_kernel,
            (shares.reshape(peers, 128), residual, first, inside, sides),
            [plane, plane],
            [],
            8,
            "final",
        )
    )


def solution(mesh):
    placed = (
        P("sx", "sy", None, None),
        P(),
        P(),
        P("sx", "sy", None),
        P("sx", "sy", None, None),
        P("sx", "sy", None),
        P("sx", "sy", None),
    )
    return jax.shard_map(
        per_device,
        mesh=mesh,
        in_specs=placed,
        out_specs=(P("sx", "sy", None), P("sx", "sy", None)),
        check_vma=False,
    )
```

```python
import jax
import jax.numpy as jnp
from jax import lax
from jax.experimental import pallas as pl
from jax.experimental.pallas import tpu as pltpu
from jax.sharding import PartitionSpec as P

AXES = ("sx", "sy")


def shift(value, axis, step):
    peers = lax.axis_size(axis)
    return lax.ppermute(value, axis, [(i, (i + step) % peers) for i in range(peers)])


def three(value):
    high = value.astype(jnp.bfloat16).astype(jnp.float32)
    rest = value - high
    mid = rest.astype(jnp.bfloat16).astype(jnp.float32)
    return high, mid, rest - mid


def prep_kernel(own, ids, occupancy, target, mask, start, out_hi, out_lo, present):
    rows, cols, channels, depth = own.shape
    half = present.shape[1]
    present[...] = jnp.broadcast_to(
        jnp.where(ids[:, 13:14] >= 0, 1.0, 0.0).astype(jnp.float32), present.shape
    )
    for x in range(rows):
        blocks = [present[pl.ds(2 * cols * x + z, cols, stride=2), :] for z in range(depth // half)]
        mask[x] = occupancy[x].astype(jnp.float32) * jnp.concatenate(blocks, axis=1)
        start[x] = mask[x] * target[x]
    for out, y in ((out_hi, cols - 1), (out_lo, 0)):
        for x in range(rows):
            out[x] = own[x, y] * mask[x, y : y + 1, :].astype(jnp.bfloat16)
        edge = jnp.concatenate([start[x, y : y + 1, :] for x in range(rows)], axis=0)
        blank = jnp.zeros((channels - 3 * rows, depth), jnp.float32)
        out[rows] = jnp.concatenate([*three(edge), blank], axis=0).astype(jnp.bfloat16)


def weights_kernel(taps, bias, wide, bias_col):
    channels = taps.shape[1]
    width = 16 * channels
    row = lax.broadcasted_iota(jnp.int32, (channels, width), 0)
    lane = lax.broadcasted_iota(jnp.int32, (channels, width), 1)
    repeat = jnp.where(lane % channels == row, 1.0, 0.0).astype(jnp.bfloat16)
    group = lane // channels
    for z in range(3):
        every = [
            jnp.dot(taps[3 * k + z], repeat, preferred_element_type=jnp.float32) for k in range(9)
        ]
        for out_x in range(2):
            for out_y in range(2):
                total = jnp.zeros((channels, width), jnp.float32)
                for k in range(9):
                    at = (out_x + k // 3) * 4 + out_y + k % 3
                    total = jnp.where(group == at, every[k], total)
                start = ((z * 2 + out_x) * 2 + out_y) * channels
                wide[start : start + channels] = total.astype(jnp.bfloat16)
    square = (channels, channels)
    same = lax.broadcasted_iota(jnp.int32, square, 0) == lax.broadcasted_iota(jnp.int32, square, 1)
    column = jnp.sum(jnp.where(same, bias[...], 0.0), axis=1, keepdims=True)
    bias_col[...] = jnp.broadcast_to(column, bias_col.shape)


def mesh_flags():
    keep = []
    for axis in ("sy", "sx"):
        where = lax.axis_index(axis)
        keep += [where > 0, where < lax.axis_size(axis) - 1]
    return [jnp.where(k, 1.0, 0.0) for k in keep]


def conv_block(grid, masks, wide, bias_all, lane, grid_x, y, out, out_x):
    channels, depth = bias_all.shape
    window = jnp.concatenate(
        [grid[grid_x + k, y : y + 4].reshape(4 * channels, depth) for k in range(4)], axis=0
    )
    parts = jnp.dot(wide[...], window, preferred_element_type=jnp.float32)
    low = pltpu.roll(parts[0 : 4 * channels], 1, 1)
    high = pltpu.roll(parts[8 * channels :], depth - 1, 1)
    total = parts[4 * channels : 8 * channels]
    total = total + jnp.where(lane == 0, 0.0, low) + jnp.where(lane == depth - 1, 0.0, high)
    for step_x in range(2):
        for step_y in range(2):
            at = (step_x * 2 + step_y) * channels
            keep = masks[step_x](y + step_y)
            value = keep * (total[at : at + channels] + bias_all)
            out[out_x + step_x, y + step_y] = value.astype(jnp.bfloat16)


def splat(flag, shape):
    return jnp.full(shape, flag, jnp.float32).astype(jnp.bfloat16)


def fill_row(grid, grid_x, mask, middle, low, high):
    cols = grid.shape[1] - 2
    grid[grid_x, 0] = low
    for y in range(cols):
        grid[grid_x, y + 1] = middle(y) * mask(y).astype(jnp.bfloat16)
    grid[grid_x, cols + 1] = high


def fill_own(grid, grid_x, own, mask, y_lo, y_hi, flags, x):
    low = y_lo[x] * splat(flags[0], y_lo.shape[1:])
    high = y_hi[x] * splat(flags[1], y_hi.shape[1:])
    fill_row(grid, grid_x, mask_of(mask, x), lambda y: own[x, y], low, high)


def mask_of(mask, x):
    return lambda y: mask[x, y : y + 1, :]


def conv_inner_kernel(own, y_lo, y_hi, mask, wide, bias, out, grid):
    rows, cols, channels, depth = own.shape
    flags = mesh_flags()

    def fill(x, carry):
        fill_own(grid, x, own, mask, y_lo, y_hi, flags, x)
        return carry

    lax.fori_loop(0, rows, fill, 0)
    lane = lax.broadcasted_iota(jnp.int32, (4 * channels, depth), 1)
    bias_all = bias[...]

    def pair(i, carry):
        masks = (mask_of(mask, 2 * i + 1), mask_of(mask, 2 * i + 2))
        for y in range(0, cols, 2):
            conv_block(grid, masks, wide, bias_all, lane, 2 * i, y, out, 2 * i)
        return carry

    lax.fori_loop(0, rows // 2 - 1, pair, 0)


def sides_kernel(y_lo, y_hi, mask, start, out_hi, out_lo):
    rows, cols, depth = mask.shape
    flags = mesh_flags()
    clear = [splat(flag, y_lo.shape[1:]) for flag in flags[:2]]
    low_terms = y_lo[rows].astype(jnp.float32)
    high_terms = y_hi[rows].astype(jnp.float32)
    for out, pair, row in ((out_hi, (rows - 2, rows - 1), rows - 1), (out_lo, (0, 1), 0)):
        for k, x in enumerate(pair):
            out[2 * k] = y_lo[x] * clear[0]
            out[2 * k + 1] = y_hi[x] * clear[1]
        out[4] = jnp.concatenate([mask[x] for x in pair], axis=0).astype(jnp.bfloat16)
        high, mid, low = three(start[row])
        rims = [
            terms[at : at + 1]
            for at in (row, rows + row, 2 * rows + row)
            for terms in (low_terms, high_terms)
        ]
        blank = jnp.zeros((10, depth), jnp.float32)
        out[5] = jnp.concatenate([high, mid], axis=0).astype(jnp.bfloat16)
        out[6] = jnp.concatenate([low, *rims, blank], axis=0).astype(jnp.bfloat16)


def conv_edge_kernel(
    own,
    y_lo,
    y_hi,
    x_lo,
    x_hi,
    side_lo,
    side_hi,
    mask,
    wide,
    bias,
    inner,
    out,
    out_hi,
    out_lo,
    grid,
    side_mask,
):
    rows, cols, channels, depth = own.shape
    flags = mesh_flags()
    for k, side in enumerate((side_lo, side_hi)):
        both = side[4].astype(jnp.float32) * flags[2 + k]
        side_mask[2 * k] = both[:cols]
        side_mask[2 * k + 1] = both[cols:]
    for x in range(2):
        for k, ref, side in ((0, x_lo, side_lo), (1, x_hi, side_hi)):
            clear = splat(flags[2 + k], (channels, depth))
            fill_row(
                grid,
                6 * k + x,
                mask_of(side_mask, 2 * k + x),
                lambda y: ref[x, y],
                side[2 * x] * clear,
                side[2 * x + 1] * clear,
            )
        fill_own(grid, 2 + x, own, mask, y_lo, y_hi, flags, x)
        fill_own(grid, 4 + x, own, mask, y_lo, y_hi, flags, rows - 2 + x)
    lane = lax.broadcasted_iota(jnp.int32, (4 * channels, depth), 1)
    bias_all = bias[...]
    for side, masks in (
        (0, (mask_of(side_mask, 1), mask_of(mask, 0))),
        (1, (mask_of(mask, rows - 1), mask_of(side_mask, 2))),
    ):
        for y in range(0, cols, 2):
            conv_block(grid, masks, wide, bias_all, lane, 4 * side, y, out, 2 * side)
    for ref, y in ((out_hi, cols - 1), (out_lo, 0)):
        for x in range(rows + 2):
            at = field_at(inner, out, x)
            ref[x] = at[0][at[1], y]


def two_sum(a, b):
    s = a + b
    t = s - a
    return s, (a - (s - t)) + (b - t)


def split(a):
    c = a * 4097.0
    high = c - (c - a)
    return high, a - high


def two_prod(a, b):
    p = a * b
    a_hi, a_lo = split(a)
    b_hi, b_lo = split(b)
    return p, ((a_hi * b_hi - p) + a_hi * b_lo + a_lo * b_hi) + a_lo * b_lo


def pair_add(a, b):
    s, t = two_sum(a[0], b[0])
    return two_sum(s, t + (a[1] + b[1]))


def pair_scale(a, c):
    p, t = two_prod(a[0], c)
    return two_sum(p, t + a[1] * c)


def field_at(inner, edge, x):
    n = inner.shape[0]
    if x < 2:
        return edge, x
    return (inner, x - 2) if x < n + 2 else (edge, x - n)


def along_y(smooth, dst, field, row, value_at):
    cols = smooth.shape[1]

    def product(y):
        return field[row, y].astype(jnp.float32) * value_at(y)

    here = product(0)
    pair = here
    for y in range(cols):
        if y + 1 < cols:
            following = product(y + 1)
            pair_next = here + following
        else:
            pair_next = here
            following = here
        smooth[dst, y] = pair + pair_next
        here = following
        pair = pair_next


def row_of(ref, x):
    return lambda y: ref[x, y : y + 1, :]


def close_column(both, lane, field):
    depth = both.shape[1]
    up = jnp.where(lane == depth - 1, 0.0, pltpu.roll(both, depth - 1, 1))
    down = jnp.where(lane == 0, 0.0, pltpu.roll(both, 1, 1))
    prod = ((both + both) + (up + down)) * field.astype(jnp.float32)
    return jnp.sum(prod, axis=0, keepdims=True)


def lanes(shape):
    return lax.broadcasted_iota(jnp.int32, shape, 1)


def along_x(smooth, x, ends, field, row, scale):
    cols, channels, depth = smooth.shape[1:]
    lane = lanes((channels, depth))
    sums = []
    for y in range(cols):
        mid = smooth[x, y]
        low = (smooth[x - 1, y] + mid) if ends[0] else mid
        high = (mid + smooth[x + 1, y]) if ends[1] else mid
        sums.append(close_column(low + high, lane, field[row, y]))
    return jnp.concatenate(sums, axis=0) * scale


def first_core_kernel(inner, edge, start, side_lo, side_hi, ridge, out, smooth, side_start):
    n, cols, channels, depth = inner.shape
    scale = 1.0 / (8 * channels)
    for k, side in enumerate((side_lo, side_hi)):
        upper = side[5].astype(jnp.float32)
        lower = side[6].astype(jnp.float32)
        side_start[k] = (upper[:cols] + upper[cols:]) + lower[:cols]
    along_y(smooth, 0, edge, 0, row_of(side_start, 0))
    along_y(smooth, 1, edge, 1, row_of(start, 0))
    along_y(smooth, n + 2, edge, 2, row_of(start, n + 1))
    along_y(smooth, n + 3, edge, 3, row_of(side_start, 1))

    def stage_y(k, carry):
        along_y(smooth, k + 2, inner, k, row_of(start, k + 1))
        return carry

    lax.fori_loop(0, n, stage_y, 0)

    def stage_x(k, carry):
        image = along_x(smooth, k + 2, (True, True), inner, k, scale)
        out[k + 1] = ridge[k + 1] * start[k + 1] + image
        return carry

    lax.fori_loop(0, n, stage_x, 0)
    for x, row in ((0, 1), (n + 1, 2)):
        image = along_x(smooth, x + 1, (True, True), edge, row, scale)
        out[x] = ridge[x] * start[x] + image


def rim_rows(g, inner, edge, y, lane, scale):
    sums = []
    for x in range(inner.shape[0] + 2):
        low, mid, high = g[x : x + 3]
        both = mid + mid
        both = both if low is None else both + low
        both = both if high is None else both + high
        at = field_at(inner, edge, x + 1)
        sums.append(close_column(both, lane, at[0][at[1], y]))
    return jnp.concatenate(sums, axis=0) * scale


def column_of(ref, y):
    return jnp.concatenate([ref[x, y : y + 1, :] for x in range(ref.shape[0])], axis=0)


def first_rim_kernel(
    inner, edge, f_lo, f_hi, y_lo, y_hi, side_lo, side_hi, core, out, out_hi, out_lo
):
    n, cols, channels, depth = inner.shape
    rows = n + 2
    lane = lanes((channels, depth))
    out[...] = core[...]
    ends = []
    for side in (side_lo, side_hi):
        terms = side[6].astype(jnp.float32)[cols : cols + 8]
        ends.append((terms[0:2] + terms[2:4]) + terms[4:6])
    for k, (ref, rim, flag, y, send) in enumerate(
        zip((f_lo, f_hi), (y_lo, y_hi), mesh_flags(), (0, cols - 1), (out_lo, out_hi))
    ):
        terms = rim[rows].astype(jnp.float32)
        values = (terms[:rows] + terms[rows : 2 * rows]) + terms[2 * rows : 3 * rows]
        values = [ends[0][k : k + 1], *(values[x : x + 1] for x in range(rows)), ends[1][k : k + 1]]
        g = [ref[x].astype(jnp.float32) * (value * flag) for x, value in enumerate(values)]
        column = column_of(core, y) + rim_rows(g, inner, edge, y, lane, 1.0 / (8 * channels))
        send[...] = column
        for x in range(rows):
            out[x, y : y + 1, :] = column[x : x + 1]


PRODUCTS = ((0, 0), (0, 1), (1, 1), (0, 2), (1, 2))


def add_products(sums, which, fields):
    for k in which:
        a, b = PRODUCTS[k]
        p, e = two_prod(fields[a], fields[b])
        s, t = two_sum(sums[k][0], p)
        sums[k] = (s, sums[k][1] + (t + e))


def second_core_kernel(inner, edge, start, first, ridge, out, grams, smooth):
    n, cols, channels, depth = inner.shape
    scale = 1.0 / (8 * channels)

    def stage_y(k, carry):
        along_y(smooth, k + 1, inner, k, row_of(first, k + 1))
        return carry

    lax.fori_loop(0, n, stage_y, 0)
    along_y(smooth, 0, edge, 1, row_of(first, 0))
    along_y(smooth, n + 1, edge, 2, row_of(first, n + 1))

    def stage_x(k, carry):
        image = along_x(smooth, k + 1, (True, True), inner, k, scale)
        out[k + 1] = ridge[k + 1] * first[k + 1] + image
        return carry

    lax.fori_loop(0, n, stage_x, 0)
    for x, row, ends in ((0, 1, (False, True)), (n + 1, 2, (True, False))):
        out[x] = ridge[x] * first[x] + along_x(smooth, x, ends, edge, row, scale)
    zero = jnp.zeros((cols, depth), jnp.float32)
    sums = [(zero, zero) for _ in PRODUCTS]
    for x in range(n + 2):
        add_products(sums, range(5), (start[x], first[x], out[x]))
    for k, (s, e) in enumerate(sums):
        grams[2 * k] = s
        grams[2 * k + 1] = e


def second_rim_kernel(
    inner, edge, f_lo, f_hi, start, first, w_lo, w_hi, x_lo, x_hi, core, grams, out, share
):
    n, cols, channels, depth = inner.shape
    rows = n + 2
    scale = 1.0 / (8 * channels)
    lane = lanes((channels, depth))
    flags = mesh_flags()
    out[...] = core[...]
    sums = [(grams[2 * k], grams[2 * k + 1]) for k in range(5)]
    added = []
    for ref, rim, flag, y in ((f_lo, w_lo, flags[0], 0), (f_hi, w_hi, flags[1], cols - 1)):
        g = [ref[x + 1].astype(jnp.float32) * (rim[x : x + 1] * flag) for x in range(rows)]
        added.append(rim_rows([None, *g, None], inner, edge, y, lane, scale))
    columns = [jnp.concatenate([column_of(ref, y) for y in (0, cols - 1)]) for ref in (start, first)]
    add_products(sums, (3, 4), (*columns, jnp.concatenate(added, axis=0)))
    for delta, y in zip(added, (0, cols - 1)):
        for x in range(rows):
            out[x, y : y + 1, :] = out[x, y : y + 1, :] + delta[x : x + 1]
    for rim, at, row, x, far in ((x_lo, 0, 1, 0, 0), (x_hi, 3, 2, rows - 1, rows + 1)):

        def product(y):
            value = rim[y : y + 1]
            if y == 0:
                return f_lo[far].astype(jnp.float32) * (value * flags[0])
            if y == cols + 1:
                return f_hi[far].astype(jnp.float32) * (value * flags[1])
            return edge[at, y - 1].astype(jnp.float32) * value

        parts = []
        here = product(1)
        pair = product(0) + here
        for y in range(cols):
            following = product(y + 2)
            pair_next = here + following
            parts.append(close_column(pair + pair_next, lane, edge[row, y]))
            here = following
            pair = pair_next
        delta = jnp.concatenate(parts, axis=0) * scale
        add_products(sums, (3, 4), (start[x], first[x], delta))
        out[x] = out[x] + delta
    row = jnp.zeros((8, 128), jnp.float32)
    lane = lanes((8, 128))
    for k, (s, e) in enumerate(sums):
        while s.shape[0] > 8:
            half = s.shape[0] // 2
            t, d = two_sum(s[:half], s[half:])
            s, e = (t, e[:half] + e[half:] + d)
        while s.shape[1] > 128:
            half = s.shape[1] // 2
            t, d = two_sum(s[:, :half], s[:, half:])
            s, e = (t, e[:, :half] + e[:, half:] + d)
        for axis, steps in ((0, (4, 2, 1)), (1, (64, 32, 16, 8, 4, 2, 1))):
            for step in steps:
                t, d = two_sum(s, pltpu.roll(s, step, axis))
                s, e = (t, (e + pltpu.roll(e, step, axis)) + d)
        row = jnp.where(lane == k, s, row)
        row = jnp.where(lane == 8 + k, e, row)
    share[...] = row[0:1]


def final_kernel(shares, start, first, second, solution_out, residual_out):
    s = shares[...]
    e = jnp.zeros_like(s)
    while s.shape[0] > 8:
        half = s.shape[0] // 2
        t, d = two_sum(s[:half], s[half:])
        s, e = (t, e[:half] + e[half:] + d)
    for step in (4, 2, 1):
        t, d = two_sum(s, pltpu.roll(s, step, 0))
        s, e = (t, (e + pltpu.roll(e, step, 0)) + d)
    lane = lax.broadcasted_iota(jnp.int32, s.shape, 1)

    def pick(value, k):
        return jnp.broadcast_to(
            jnp.sum(jnp.where(lane == k, value, 0.0), axis=1, keepdims=True), s.shape
        )

    g00, g01, g11, g02, g12 = [
        two_sum(pick(s, k), pick(e, k) + pick(s, 8 + k)) for k in range(5)
    ]
    alpha = g00[0] / g01[0]
    fresh = pair_add(pair_add(g00, pair_scale(g01, -2.0 * alpha)), pair_scale(pair_scale(g11, alpha), alpha))
    grow = 1.0 + fresh[0] / g00[0]
    curve = pair_add(
        pair_add(
            pair_scale(pair_scale(g01, grow), grow),
            pair_scale(pair_scale(pair_add(g02, g11), -alpha), grow),
        ),
        pair_scale(pair_scale(g12, alpha), alpha),
    )
    beta = fresh[0] / curve[0]
    near = (alpha + beta * grow)[0:1, 0:1]
    far = (alpha * beta)[0:1, 0:1]
    for x in range(start.shape[0]):
        w0, w1, w2 = (start[x], first[x], second[x])
        solution_out[x] = near * w0 - far * w1
        residual_out[x] = (w0 - near * w1) + far * w2


def per_device(features, conv_weight, conv_bias, occupancy, block_ids, ridge, target):
    rows, cols, channels, depth = features.shape
    f32, bf16 = (jnp.float32, jnp.bfloat16)
    vmem = pl.BlockSpec(memory_space=pltpu.VMEM)

    def call(kernel, args, outs, scratch, limit, name):
        return pl.pallas_call(
            kernel,
            out_shape=[jax.ShapeDtypeStruct(shape, dtype) for shape, dtype in outs],
            in_specs=[vmem for _ in args],
            out_specs=[vmem for _ in outs],
            scratch_shapes=[pltpu.VMEM(shape, dtype) for shape, dtype in scratch],
            compiler_params=pltpu.CompilerParams(vmem_limit_bytes=limit << 20),
            name=name,
        )(*args)

    edges, target = lax.optimization_barrier(((features[-2:], features[:2]), target))
    x_lo, x_hi = (shift(edges[0], "sx", 1), shift(edges[1], "sx", -1))

    plane = ((rows, cols, depth), f32)
    blocks = block_ids.reshape(-1, block_ids.shape[3])
    edge_column = ((rows + 1, channels, depth), bf16)
    weight_mask, residual, y_hi, y_lo = call(
        prep_kernel,
        (features, blocks, occupancy, target),
        [plane, plane, edge_column, edge_column],
        [((blocks.shape[0], depth // block_ids.shape[2]), f32)],
        4,
        "prep",
    )
    y_lo, y_hi = (shift(y_hi, "sy", 1), shift(y_lo, "sy", -1))
    wide, bias = call(
        weights_kernel,
        (conv_weight, conv_bias[None]),
        [((12 * channels, 16 * channels), bf16), ((channels, depth), f32)],
        [],
        8,
        "weights",
    )
    grid_scratch = ((rows, cols + 2, channels, depth), bf16)
    inner_shape = (rows - 2, cols, channels, depth)
    edge_shape = (4, cols, channels, depth)
    side_shape = (7, channels, depth)
    side_hi, side_lo = call(
        sides_kernel,
        (y_lo, y_hi, weight_mask, residual),
        [(side_shape, bf16), (side_shape, bf16)],
        [],
        4,
        "sides",
    )
    side_lo, side_hi = (shift(side_hi, "sx", 1), shift(side_lo, "sx", -1))
    (inner,) = call(
        conv_inner_kernel,
        (features, y_lo, y_hi, weight_mask, wide, bias),
        [(inner_shape, bf16)],
        [grid_scratch],
        12,
        "conv_inner",
    )
    column = ((rows + 2, channels, depth), bf16)
    edge, f_hi, f_lo = call(
        conv_edge_kernel,
        (features, y_lo, y_hi, x_lo, x_hi, side_lo, side_hi, weight_mask, wide, bias, inner),
        [(edge_shape, bf16), column, column],
        [grid_scratch, ((4, cols, depth), f32)],
        12,
        "conv_edge",
    )
    f_lo, f_hi = (shift(f_hi, "sy", 1), shift(f_lo, "sy", -1))
    (core,) = call(
        first_core_kernel,
        (inner, edge, residual, side_lo, side_hi, ridge),
        [plane],
        [((rows + 2, cols, channels, depth), f32), ((2, cols, depth), f32)],
        10,
        "first_core",
    )
    line = ((rows, depth), f32)
    first, w_hi, w_lo = call(
        first_rim_kernel,
        (inner, edge, f_lo, f_hi, y_lo, y_hi, side_lo, side_hi, core),
        [plane, line, line],
        [],
        4,
        "first_rim",
    )
    w_lo, w_hi = (shift(w_hi, "sy", 1), shift(w_lo, "sy", -1))
    rims = [jnp.concatenate([w_lo[x : x + 1], first[x], w_hi[x : x + 1]]) for x in (rows - 1, 0)]
    r_lo, r_hi = (shift(rims[0], "sx", 1), shift(rims[1], "sx", -1))
    core, grams = call(
        second_core_kernel,
        (inner, edge, residual, first, ridge),
        [plane, ((2 * len(PRODUCTS), cols, depth), f32)],
        [((rows, cols, channels, depth), f32)],
        10,
        "second_core",
    )
    second, share = call(
        second_rim_kernel,
        (inner, edge, f_lo, f_hi, residual, first, w_lo, w_hi, r_lo, r_hi, core, grams),
        [plane, ((1, 128), f32)],
        [],
        4,
        "second_rim",
    )

    peers = lax.axis_size("sx") * lax.axis_size("sy")
    shares = lax.all_to_all(jnp.broadcast_to(share[None], (peers, 1, 128)), AXES, 0, 0)
    return tuple(
        call(
            final_kernel,
            (shares.reshape(peers, 128), residual, first, second),
            [plane, plane],
            [],
            8,
            "final",
        )
    )


def solution(mesh):
    placed = (
        P("sx", "sy", None, None),
        P(),
        P(),
        P("sx", "sy", None),
        P("sx", "sy", None, None),
        P("sx", "sy", None),
        P("sx", "sy", None),
    )
    return jax.shard_map(
        per_device,
        mesh=mesh,
        in_specs=placed,
        out_specs=(P("sx", "sy", None), P("sx", "sy", None)),
        check_vma=False,
    )
```

```python
import jax
import jax.numpy as jnp
from jax import lax
from jax.experimental import pallas as pl
from jax.experimental.pallas import tpu as pltpu
from jax.sharding import PartitionSpec as P

AXES = ("sx", "sy")
PREP_LIMIT = 58


def shift(value, axis, step):
    peers = lax.axis_size(axis)
    return lax.ppermute(value, axis, [(i, (i + step) % peers) for i in range(peers)])


def three(value):
    high = value.astype(jnp.bfloat16).astype(jnp.float32)
    rest = value - high
    mid = rest.astype(jnp.bfloat16).astype(jnp.float32)
    return high, mid, rest - mid


def prep_kernel(
    own,
    ids_in,
    occupancy_in,
    target_in,
    mask,
    start,
    y_hi,
    y_lo,
    x_hi,
    x_lo,
    ids,
    occupancy,
    target,
    columns,
    present,
    sems,
):
    rows, cols, channels, depth = own.shape
    half = present.shape[1]
    copies = [
        pltpu.make_async_copy(source, goal, sems.at[k])
        for k, (source, goal) in enumerate(
            (
                (ids_in, ids),
                (occupancy_in, occupancy),
                (target_in, target),
                (own.at[:, 0:1], columns.at[0]),
                (own.at[:, cols - 1 : cols], columns.at[1]),
                (own.at[rows - 2], x_hi.at[0:cols]),
                (own.at[rows - 1], x_hi.at[cols : 2 * cols]),
                (own.at[0], x_lo.at[0:cols]),
                (own.at[1], x_lo.at[cols : 2 * cols]),
            )
        )
    ]
    for copy in copies:
        copy.start()
    copies[0].wait()
    copies[1].wait()
    present[...] = jnp.broadcast_to(
        jnp.where(ids[:, 13:14] >= 0, 1.0, 0.0).astype(jnp.float32), present.shape
    )
    for x in range(rows):
        blocks = [present[pl.ds(2 * cols * x + z, cols, stride=2), :] for z in range(depth // half)]
        mask[x] = occupancy[x].astype(jnp.float32) * jnp.concatenate(blocks, axis=1)
    copies[2].wait()
    for x in range(rows):
        start[x] = mask[x] * target[x]
    copies[3].wait()
    copies[4].wait()
    for k, (out, y) in enumerate(((y_lo, 0), (y_hi, cols - 1))):
        for x in range(rows):
            out[x] = columns[k, x, 0] * mask[x, y : y + 1, :].astype(jnp.bfloat16)
        edge = jnp.concatenate([start[x, y : y + 1, :] for x in range(rows)], axis=0)
        blank = jnp.zeros((channels - 3 * rows, depth), jnp.float32)
        out[rows] = jnp.concatenate([*three(edge), blank], axis=0).astype(jnp.bfloat16)
    for out, pair, row in ((x_hi, (rows - 2, rows - 1), rows - 1), (x_lo, (0, 1), 0)):
        out[2 * cols] = jnp.concatenate([mask[x] for x in pair], axis=0).astype(jnp.bfloat16)
        high, mid, low = three(start[row])
        out[2 * cols + 1] = jnp.concatenate([high, mid], axis=0).astype(jnp.bfloat16)
        out[2 * cols + 2] = jnp.concatenate([low, jnp.zeros_like(low)], axis=0).astype(jnp.bfloat16)
    for copy in copies[5:]:
        copy.wait()


def weights_kernel(taps, bias, wide, bias_col):
    channels = taps.shape[1]
    width = 16 * channels
    row = lax.broadcasted_iota(jnp.int32, (channels, width), 0)
    lane = lax.broadcasted_iota(jnp.int32, (channels, width), 1)
    repeat = jnp.where(lane % channels == row, 1.0, 0.0).astype(jnp.bfloat16)
    group = lane // channels
    for z in range(3):
        every = [
            jnp.dot(taps[3 * k + z], repeat, preferred_element_type=jnp.float32) for k in range(9)
        ]
        for out_x in range(2):
            for out_y in range(2):
                total = jnp.zeros((channels, width), jnp.float32)
                for k in range(9):
                    at = (out_x + k // 3) * 4 + out_y + k % 3
                    total = jnp.where(group == at, every[k], total)
                start = ((z * 2 + out_x) * 2 + out_y) * channels
                wide[start : start + channels] = total.astype(jnp.bfloat16)
    square = (channels, channels)
    same = lax.broadcasted_iota(jnp.int32, square, 0) == lax.broadcasted_iota(jnp.int32, square, 1)
    column = jnp.sum(jnp.where(same, bias[...], 0.0), axis=1, keepdims=True)
    bias_col[...] = jnp.broadcast_to(column, bias_col.shape)


def mesh_flags():
    keep = []
    for axis in ("sy", "sx"):
        where = lax.axis_index(axis)
        keep += [where > 0, where < lax.axis_size(axis) - 1]
    return [jnp.where(k, 1.0, 0.0) for k in keep]


def conv_block(grid, masks, wide, bias_all, lane, grid_x, y, out, out_x):
    channels, depth = bias_all.shape
    window = jnp.concatenate(
        [grid[grid_x + k, y : y + 4].reshape(4 * channels, depth) for k in range(4)], axis=0
    )
    parts = jnp.dot(wide[...], window, preferred_element_type=jnp.float32)
    low = pltpu.roll(parts[0 : 4 * channels], 1, 1)
    high = pltpu.roll(parts[8 * channels :], depth - 1, 1)
    total = parts[4 * channels : 8 * channels]
    total = total + jnp.where(lane == 0, 0.0, low) + jnp.where(lane == depth - 1, 0.0, high)
    for step_x in range(2):
        for step_y in range(2):
            at = (step_x * 2 + step_y) * channels
            keep = masks[step_x](y + step_y)
            value = keep * (total[at : at + channels] + bias_all)
            out[out_x + step_x, y + step_y] = value.astype(jnp.bfloat16)


def splat(flag, shape):
    return jnp.full(shape, flag, jnp.float32).astype(jnp.bfloat16)


def fill_row(grid, grid_x, mask, middle, low, high):
    cols = grid.shape[1] - 2
    grid[grid_x, 0] = low
    for y in range(cols):
        grid[grid_x, y + 1] = middle(y) * mask(y).astype(jnp.bfloat16)
    grid[grid_x, cols + 1] = high


def fill_own(grid, grid_x, own, mask, y_lo, y_hi, flags, x):
    low = y_lo[x] * splat(flags[0], y_lo.shape[1:])
    high = y_hi[x] * splat(flags[1], y_hi.shape[1:])
    fill_row(grid, grid_x, mask_of(mask, x), lambda y: own[x, y], low, high)


def mask_of(mask, x):
    return lambda y: mask[x, y : y + 1, :]


def conv_inner_kernel(own, y_lo, y_hi, mask, wide, bias, out, grid):
    rows, cols, channels, depth = own.shape
    flags = mesh_flags()

    def fill(x, carry):
        fill_own(grid, x, own, mask, y_lo, y_hi, flags, x)
        return carry

    lax.fori_loop(0, rows, fill, 0)
    lane = lax.broadcasted_iota(jnp.int32, (4 * channels, depth), 1)
    bias_all = bias[...]

    def pair(i, carry):
        masks = (mask_of(mask, 2 * i + 1), mask_of(mask, 2 * i + 2))
        for y in range(0, cols, 2):
            conv_block(grid, masks, wide, bias_all, lane, 2 * i, y, out, 2 * i)
        return carry

    lax.fori_loop(0, rows // 2 - 1, pair, 0)


def sides_kernel(y_lo, y_hi, out_hi, out_lo):
    rows = y_lo.shape[0] - 1
    channels, depth = y_lo.shape[1:]
    clear = [splat(flag, y_lo.shape[1:]) for flag in mesh_flags()[:2]]
    low_terms = y_lo[rows].astype(jnp.float32)
    high_terms = y_hi[rows].astype(jnp.float32)
    for out, pair, row in ((out_hi, (rows - 2, rows - 1), rows - 1), (out_lo, (0, 1), 0)):
        for k, x in enumerate(pair):
            out[2 * k] = y_lo[x] * clear[0]
            out[2 * k + 1] = y_hi[x] * clear[1]
        rims = [
            terms[at : at + 1]
            for at in (row, rows + row, 2 * rows + row)
            for terms in (low_terms, high_terms)
        ]
        blank = jnp.zeros((channels - 6, depth), jnp.float32)
        out[4] = jnp.concatenate([*rims, blank], axis=0).astype(jnp.bfloat16)


def conv_edge_kernel(
    own,
    y_lo,
    y_hi,
    x_lo,
    x_hi,
    side_lo,
    side_hi,
    mask,
    wide,
    bias,
    inner,
    out,
    out_hi,
    out_lo,
    grid,
    side_mask,
):
    rows, cols, channels, depth = own.shape
    flags = mesh_flags()
    for k, side in enumerate((x_lo, x_hi)):
        both = side[2 * cols].astype(jnp.float32) * flags[2 + k]
        side_mask[2 * k] = both[:cols]
        side_mask[2 * k + 1] = both[cols:]
    for x in range(2):
        for k, ref, side in ((0, x_lo, side_lo), (1, x_hi, side_hi)):
            clear = splat(flags[2 + k], (channels, depth))
            fill_row(
                grid,
                6 * k + x,
                mask_of(side_mask, 2 * k + x),
                lambda y: ref[x * cols + y],
                side[2 * x] * clear,
                side[2 * x + 1] * clear,
            )
        fill_own(grid, 2 + x, own, mask, y_lo, y_hi, flags, x)
        fill_own(grid, 4 + x, own, mask, y_lo, y_hi, flags, rows - 2 + x)
    lane = lax.broadcasted_iota(jnp.int32, (4 * channels, depth), 1)
    bias_all = bias[...]
    for side, masks in (
        (0, (mask_of(side_mask, 1), mask_of(mask, 0))),
        (1, (mask_of(mask, rows - 1), mask_of(side_mask, 2))),
    ):
        for y in range(0, cols, 2):
            conv_block(grid, masks, wide, bias_all, lane, 4 * side, y, out, 2 * side)
    for ref, y in ((out_hi, cols - 1), (out_lo, 0)):
        for x in range(rows + 2):
            at = field_at(inner, out, x)
            ref[x] = at[0][at[1], y]


def two_sum(a, b):
    s = a + b
    t = s - a
    return s, (a - (s - t)) + (b - t)


def split(a):
    c = a * 4097.0
    high = c - (c - a)
    return high, a - high


def two_prod(a, b):
    p = a * b
    a_hi, a_lo = split(a)
    b_hi, b_lo = split(b)
    return p, ((a_hi * b_hi - p) + a_hi * b_lo + a_lo * b_hi) + a_lo * b_lo


def pair_add(a, b):
    s, t = two_sum(a[0], b[0])
    return two_sum(s, t + (a[1] + b[1]))


def pair_scale(a, c):
    p, t = two_prod(a[0], c)
    return two_sum(p, t + a[1] * c)


def field_at(inner, edge, x):
    n = inner.shape[0]
    if x < 2:
        return edge, x
    return (inner, x - 2) if x < n + 2 else (edge, x - n)


def along_y(smooth, dst, field, row, value_at):
    cols = smooth.shape[1]

    def product(y):
        return field[row, y].astype(jnp.float32) * value_at(y)

    here = product(0)
    pair = here
    for y in range(cols):
        if y + 1 < cols:
            following = product(y + 1)
            pair_next = here + following
        else:
            pair_next = here
            following = here
        smooth[dst, y] = pair + pair_next
        here = following
        pair = pair_next


def row_of(ref, x):
    return lambda y: ref[x, y : y + 1, :]


def close_column(both, lane, field):
    depth = both.shape[1]
    up = jnp.where(lane == depth - 1, 0.0, pltpu.roll(both, depth - 1, 1))
    down = jnp.where(lane == 0, 0.0, pltpu.roll(both, 1, 1))
    prod = ((both + both) + (up + down)) * field.astype(jnp.float32)
    return jnp.sum(prod, axis=0, keepdims=True)


def lanes(shape):
    return lax.broadcasted_iota(jnp.int32, shape, 1)


def along_x(smooth, x, ends, field, row, scale):
    cols, channels, depth = smooth.shape[1:]
    lane = lanes((channels, depth))
    sums = []
    for y in range(cols):
        mid = smooth[x, y]
        low = (smooth[x - 1, y] + mid) if ends[0] else mid
        high = (mid + smooth[x + 1, y]) if ends[1] else mid
        sums.append(close_column(low + high, lane, field[row, y]))
    return jnp.concatenate(sums, axis=0) * scale


def first_core_kernel(inner, edge, start, x_lo, x_hi, ridge, out, smooth, side_start):
    n, cols, channels, depth = inner.shape
    scale = 1.0 / (8 * channels)
    for k, side in enumerate((x_lo, x_hi)):
        upper = side[2 * cols + 1].astype(jnp.float32)
        lower = side[2 * cols + 2].astype(jnp.float32)
        side_start[k] = (upper[:cols] + upper[cols:]) + lower[:cols]
    along_y(smooth, 0, edge, 0, row_of(side_start, 0))
    along_y(smooth, 1, edge, 1, row_of(start, 0))
    along_y(smooth, n + 2, edge, 2, row_of(start, n + 1))
    along_y(smooth, n + 3, edge, 3, row_of(side_start, 1))

    def stage_y(k, carry):
        along_y(smooth, k + 2, inner, k, row_of(start, k + 1))
        return carry

    lax.fori_loop(0, n, stage_y, 0)

    def stage_x(k, carry):
        image = along_x(smooth, k + 2, (True, True), inner, k, scale)
        out[k + 1] = ridge[k + 1] * start[k + 1] + image
        return carry

    lax.fori_loop(0, n, stage_x, 0)
    for x, row in ((0, 1), (n + 1, 2)):
        image = along_x(smooth, x + 1, (True, True), edge, row, scale)
        out[x] = ridge[x] * start[x] + image


def rim_rows(g, inner, edge, y, lane, scale):
    sums = []
    for x in range(inner.shape[0] + 2):
        low, mid, high = g[x : x + 3]
        both = mid + mid
        both = both if low is None else both + low
        both = both if high is None else both + high
        at = field_at(inner, edge, x + 1)
        sums.append(close_column(both, lane, at[0][at[1], y]))
    return jnp.concatenate(sums, axis=0) * scale


def column_of(ref, y):
    return jnp.concatenate([ref[x, y : y + 1, :] for x in range(ref.shape[0])], axis=0)


def first_rim_kernel(
    inner, edge, f_lo, f_hi, y_lo, y_hi, side_lo, side_hi, core, out, out_hi, out_lo
):
    n, cols, channels, depth = inner.shape
    rows = n + 2
    lane = lanes((channels, depth))
    out[...] = core[...]
    ends = []
    for side in (side_lo, side_hi):
        terms = side[4].astype(jnp.float32)
        ends.append((terms[0:2] + terms[2:4]) + terms[4:6])
    for k, (ref, rim, flag, y, send) in enumerate(
        zip((f_lo, f_hi), (y_lo, y_hi), mesh_flags(), (0, cols - 1), (out_lo, out_hi))
    ):
        terms = rim[rows].astype(jnp.float32)
        values = (terms[:rows] + terms[rows : 2 * rows]) + terms[2 * rows : 3 * rows]
        values = [ends[0][k : k + 1], *(values[x : x + 1] for x in range(rows)), ends[1][k : k + 1]]
        g = [ref[x].astype(jnp.float32) * (value * flag) for x, value in enumerate(values)]
        column = column_of(core, y) + rim_rows(g, inner, edge, y, lane, 1.0 / (8 * channels))
        send[...] = column
        for x in range(rows):
            out[x, y : y + 1, :] = column[x : x + 1]


PRODUCTS = ((0, 0), (0, 1), (1, 1), (0, 2), (1, 2))


def add_products(sums, which, fields):
    for k in which:
        a, b = PRODUCTS[k]
        p, e = two_prod(fields[a], fields[b])
        s, t = two_sum(sums[k][0], p)
        sums[k] = (s, sums[k][1] + (t + e))


def second_core_kernel(inner, edge, start, first, ridge, out, grams, smooth):
    n, cols, channels, depth = inner.shape
    scale = 1.0 / (8 * channels)

    def stage_y(k, carry):
        along_y(smooth, k + 1, inner, k, row_of(first, k + 1))
        return carry

    lax.fori_loop(0, n, stage_y, 0)
    along_y(smooth, 0, edge, 1, row_of(first, 0))
    along_y(smooth, n + 1, edge, 2, row_of(first, n + 1))

    def stage_x(k, carry):
        image = along_x(smooth, k + 1, (True, True), inner, k, scale)
        out[k + 1] = ridge[k + 1] * first[k + 1] + image
        return carry

    lax.fori_loop(0, n, stage_x, 0)
    for x, row, ends in ((0, 1, (False, True)), (n + 1, 2, (True, False))):
        out[x] = ridge[x] * first[x] + along_x(smooth, x, ends, edge, row, scale)
    zero = jnp.zeros((cols, depth), jnp.float32)
    sums = [(zero, zero) for _ in PRODUCTS]
    for x in range(n + 2):
        add_products(sums, range(5), (start[x], first[x], out[x]))
    for k, (s, e) in enumerate(sums):
        grams[2 * k] = s
        grams[2 * k + 1] = e


def second_rim_kernel(
    inner, edge, f_lo, f_hi, start, first, w_lo, w_hi, x_lo, x_hi, core, grams, out, share
):
    n, cols, channels, depth = inner.shape
    rows = n + 2
    scale = 1.0 / (8 * channels)
    lane = lanes((channels, depth))
    flags = mesh_flags()
    out[...] = core[...]
    sums = [(grams[2 * k], grams[2 * k + 1]) for k in range(5)]
    added = []
    for ref, rim, flag, y in ((f_lo, w_lo, flags[0], 0), (f_hi, w_hi, flags[1], cols - 1)):
        g = [ref[x + 1].astype(jnp.float32) * (rim[x : x + 1] * flag) for x in range(rows)]
        added.append(rim_rows([None, *g, None], inner, edge, y, lane, scale))
    columns = [jnp.concatenate([column_of(ref, y) for y in (0, cols - 1)]) for ref in (start, first)]
    add_products(sums, (3, 4), (*columns, jnp.concatenate(added, axis=0)))
    for delta, y in zip(added, (0, cols - 1)):
        for x in range(rows):
            out[x, y : y + 1, :] = out[x, y : y + 1, :] + delta[x : x + 1]
    for rim, at, row, x, far in ((x_lo, 0, 1, 0, 0), (x_hi, 3, 2, rows - 1, rows + 1)):

        def product(y):
            value = rim[y : y + 1]
            if y == 0:
                return f_lo[far].astype(jnp.float32) * (value * flags[0])
            if y == cols + 1:
                return f_hi[far].astype(jnp.float32) * (value * flags[1])
            return edge[at, y - 1].astype(jnp.float32) * value

        parts = []
        here = product(1)
        pair = product(0) + here
        for y in range(cols):
            following = product(y + 2)
            pair_next = here + following
            parts.append(close_column(pair + pair_next, lane, edge[row, y]))
            here = following
            pair = pair_next
        delta = jnp.concatenate(parts, axis=0) * scale
        add_products(sums, (3, 4), (start[x], first[x], delta))
        out[x] = out[x] + delta
    row = jnp.zeros((8, 128), jnp.float32)
    lane = lanes((8, 128))
    for k, (s, e) in enumerate(sums):
        while s.shape[0] > 8:
            half = s.shape[0] // 2
            t, d = two_sum(s[:half], s[half:])
            s, e = (t, e[:half] + e[half:] + d)
        while s.shape[1] > 128:
            half = s.shape[1] // 2
            t, d = two_sum(s[:, :half], s[:, half:])
            s, e = (t, e[:, :half] + e[:, half:] + d)
        for axis, steps in ((0, (4, 2, 1)), (1, (64, 32, 16, 8, 4, 2, 1))):
            for step in steps:
                t, d = two_sum(s, pltpu.roll(s, step, axis))
                s, e = (t, (e + pltpu.roll(e, step, axis)) + d)
        row = jnp.where(lane == k, s, row)
        row = jnp.where(lane == 8 + k, e, row)
    share[...] = row[0:1]


def final_kernel(shares, start, first, second, solution_out, residual_out):
    s = shares[...]
    e = jnp.zeros_like(s)
    while s.shape[0] > 8:
        half = s.shape[0] // 2
        t, d = two_sum(s[:half], s[half:])
        s, e = (t, e[:half] + e[half:] + d)
    for step in (4, 2, 1):
        t, d = two_sum(s, pltpu.roll(s, step, 0))
        s, e = (t, (e + pltpu.roll(e, step, 0)) + d)
    lane = lax.broadcasted_iota(jnp.int32, s.shape, 1)

    def pick(value, k):
        return jnp.broadcast_to(
            jnp.sum(jnp.where(lane == k, value, 0.0), axis=1, keepdims=True), s.shape
        )

    g00, g01, g11, g02, g12 = [
        two_sum(pick(s, k), pick(e, k) + pick(s, 8 + k)) for k in range(5)
    ]
    alpha = g00[0] / g01[0]
    fresh = pair_add(pair_add(g00, pair_scale(g01, -2.0 * alpha)), pair_scale(pair_scale(g11, alpha), alpha))
    grow = 1.0 + fresh[0] / g00[0]
    curve = pair_add(
        pair_add(
            pair_scale(pair_scale(g01, grow), grow),
            pair_scale(pair_scale(pair_add(g02, g11), -alpha), grow),
        ),
        pair_scale(pair_scale(g12, alpha), alpha),
    )
    beta = fresh[0] / curve[0]
    near = (alpha + beta * grow)[0:1, 0:1]
    far = (alpha * beta)[0:1, 0:1]
    for x in range(start.shape[0]):
        w0, w1, w2 = (start[x], first[x], second[x])
        solution_out[x] = near * w0 - far * w1
        residual_out[x] = (w0 - near * w1) + far * w2


def per_device(features, conv_weight, conv_bias, occupancy, block_ids, ridge, target):
    rows, cols, channels, depth = features.shape
    f32, bf16 = (jnp.float32, jnp.bfloat16)
    vmem = pl.BlockSpec(memory_space=pltpu.VMEM)

    def call(kernel, args, outs, scratch, limit, name):
        return pl.pallas_call(
            kernel,
            out_shape=[jax.ShapeDtypeStruct(shape, dtype) for shape, dtype in outs],
            in_specs=[vmem for _ in args],
            out_specs=[vmem for _ in outs],
            scratch_shapes=[pltpu.VMEM(shape, dtype) for shape, dtype in scratch],
            compiler_params=pltpu.CompilerParams(vmem_limit_bytes=limit << 20),
            name=name,
        )(*args)

    plane = ((rows, cols, depth), f32)
    blocks = block_ids.reshape(-1, block_ids.shape[3])
    edge_column = ((rows + 1, channels, depth), bf16)
    edge_rows = ((2 * cols + 3, channels, depth), bf16)
    outs = [plane, plane, edge_column, edge_column, edge_rows, edge_rows]
    weight_mask, residual, y_hi, y_lo, x_hi, x_lo = pl.pallas_call(
        prep_kernel,
        out_shape=[jax.ShapeDtypeStruct(shape, dtype) for shape, dtype in outs],
        in_specs=[pl.BlockSpec(memory_space=pl.ANY)] * 4,
        out_specs=[vmem for _ in outs],
        scratch_shapes=[
            pltpu.VMEM(blocks.shape, jnp.int32),
            pltpu.VMEM(occupancy.shape, jnp.int32),
            pltpu.VMEM(target.shape, f32),
            pltpu.VMEM((2, rows, 1, channels, depth), bf16),
            pltpu.VMEM((blocks.shape[0], depth // block_ids.shape[2]), f32),
            pltpu.SemaphoreType.DMA((9,)),
        ],
        compiler_params=pltpu.CompilerParams(vmem_limit_bytes=PREP_LIMIT << 20),
        name="prep",
    )(features, blocks, occupancy, target)
    y_lo, y_hi = (shift(y_hi, "sy", 1), shift(y_lo, "sy", -1))
    x_lo, x_hi = (shift(x_hi, "sx", 1), shift(x_lo, "sx", -1))
    wide, bias = call(
        weights_kernel,
        (conv_weight, conv_bias[None]),
        [((12 * channels, 16 * channels), bf16), ((channels, depth), f32)],
        [],
        8,
        "weights",
    )
    grid_scratch = ((rows, cols + 2, channels, depth), bf16)
    inner_shape = (rows - 2, cols, channels, depth)
    edge_shape = (4, cols, channels, depth)
    side_shape = (5, channels, depth)
    side_hi, side_lo = call(
        sides_kernel,
        (y_lo, y_hi),
        [(side_shape, bf16), (side_shape, bf16)],
        [],
        4,
        "sides",
    )
    side_lo, side_hi = (shift(side_hi, "sx", 1), shift(side_lo, "sx", -1))
    (inner,) = call(
        conv_inner_kernel,
        (features, y_lo, y_hi, weight_mask, wide, bias),
        [(inner_shape, bf16)],
        [grid_scratch],
        12,
        "conv_inner",
    )
    column = ((rows + 2, channels, depth), bf16)
    edge, f_hi, f_lo = call(
        conv_edge_kernel,
        (features, y_lo, y_hi, x_lo, x_hi, side_lo, side_hi, weight_mask, wide, bias, inner),
        [(edge_shape, bf16), column, column],
        [grid_scratch, ((4, cols, depth), f32)],
        12,
        "conv_edge",
    )
    f_lo, f_hi = (shift(f_hi, "sy", 1), shift(f_lo, "sy", -1))
    (core,) = call(
        first_core_kernel,
        (inner, edge, residual, x_lo, x_hi, ridge),
        [plane],
        [((rows + 2, cols, channels, depth), f32), ((2, cols, depth), f32)],
        10,
        "first_core",
    )
    line = ((rows, depth), f32)
    first, w_hi, w_lo = call(
        first_rim_kernel,
        (inner, edge, f_lo, f_hi, y_lo, y_hi, side_lo, side_hi, core),
        [plane, line, line],
        [],
        4,
        "first_rim",
    )
    w_lo, w_hi = (shift(w_hi, "sy", 1), shift(w_lo, "sy", -1))
    rims = [jnp.concatenate([w_lo[x : x + 1], first[x], w_hi[x : x + 1]]) for x in (rows - 1, 0)]
    r_lo, r_hi = (shift(rims[0], "sx", 1), shift(rims[1], "sx", -1))
    core, grams = call(
        second_core_kernel,
        (inner, edge, residual, first, ridge),
        [plane, ((2 * len(PRODUCTS), cols, depth), f32)],
        [((rows, cols, channels, depth), f32)],
        10,
        "second_core",
    )
    second, share = call(
        second_rim_kernel,
        (inner, edge, f_lo, f_hi, residual, first, w_lo, w_hi, r_lo, r_hi, core, grams),
        [plane, ((1, 128), f32)],
        [],
        4,
        "second_rim",
    )

    peers = lax.axis_size("sx") * lax.axis_size("sy")
    shares = lax.all_to_all(jnp.broadcast_to(share[None], (peers, 1, 128)), AXES, 0, 0)
    return tuple(
        call(
            final_kernel,
            (shares.reshape(peers, 128), residual, first, second),
            [plane, plane],
            [],
            8,
            "final",
        )
    )


def solution(mesh):
    placed = (
        P("sx", "sy", None, None),
        P(),
        P(),
        P("sx", "sy", None),
        P("sx", "sy", None, None),
        P("sx", "sy", None),
        P("sx", "sy", None),
    )
    return jax.shard_map(
        per_device,
        mesh=mesh,
        in_specs=placed,
        out_specs=(P("sx", "sy", None), P("sx", "sy", None)),
        check_vma=False,
    )
```

```python
import jax
import jax.numpy as jnp
from jax import lax
from jax.experimental import pallas as pl
from jax.experimental.pallas import tpu as pltpu
from jax.sharding import PartitionSpec as P

AXES = ("sx", "sy")
PREP_LIMIT = 58


def shift(value, axis, step):
    peers = lax.axis_size(axis)
    return lax.ppermute(value, axis, [(i, (i + step) % peers) for i in range(peers)])


def three(value):
    high = value.astype(jnp.bfloat16).astype(jnp.float32)
    rest = value - high
    mid = rest.astype(jnp.bfloat16).astype(jnp.float32)
    return high, mid, rest - mid


def prep_kernel(
    own,
    ids_in,
    occupancy_in,
    target_in,
    ridge_in,
    mask,
    start,
    y_hi,
    y_lo,
    x_hi,
    x_lo,
    ids,
    occupancy,
    target,
    ridge,
    columns,
    present,
    sems,
):
    rows, cols, channels, depth = own.shape
    half = present.shape[1]
    copies = [
        pltpu.make_async_copy(source, goal, sems.at[k])
        for k, (source, goal) in enumerate(
            (
                (ids_in, ids),
                (occupancy_in, occupancy),
                (target_in, target),
                (own.at[:, 0:1], columns.at[0]),
                (own.at[:, cols - 1 : cols], columns.at[1]),
                (own.at[rows - 2], x_hi.at[0:cols]),
                (own.at[rows - 1], x_hi.at[cols : 2 * cols]),
                (own.at[0], x_lo.at[0:cols]),
                (own.at[1], x_lo.at[cols : 2 * cols]),
                (ridge_in, ridge),
            )
        )
    ]
    for copy in copies:
        copy.start()
    copies[0].wait()
    copies[1].wait()
    present[...] = jnp.broadcast_to(
        jnp.where(ids[:, 13:14] >= 0, 1.0, 0.0).astype(jnp.float32), present.shape
    )
    for x in range(rows):
        blocks = [present[pl.ds(2 * cols * x + z, cols, stride=2), :] for z in range(depth // half)]
        mask[x] = occupancy[x].astype(jnp.float32) * jnp.concatenate(blocks, axis=1)
    copies[2].wait()
    for x in range(rows):
        start[x] = mask[x] * target[x]
    copies[3].wait()
    copies[4].wait()
    copies[9].wait()
    blank = jnp.zeros((channels - 3 * rows, depth), jnp.float32)
    for k, (out, y, far) in enumerate(((y_lo, 0, 1), (y_hi, cols - 1, cols - 2))):
        for x in range(rows):
            out[x] = columns[k, x, 0] * mask[x, y : y + 1, :].astype(jnp.bfloat16)
        for at, value in enumerate((column_of(start, y), column_of(start, far), column_of(ridge, y))):
            terms = jnp.concatenate([*three(value), blank], axis=0)
            out[rows + at] = terms.astype(jnp.bfloat16)
    for out, pair, row in ((x_hi, (rows - 2, rows - 1), rows - 1), (x_lo, (0, 1), 0)):
        out[2 * cols] = jnp.concatenate([mask[x] for x in pair], axis=0).astype(jnp.bfloat16)
        high, mid, low = three(start[row])
        out[2 * cols + 1] = jnp.concatenate([high, mid], axis=0).astype(jnp.bfloat16)
        out[2 * cols + 2] = jnp.concatenate([low, jnp.zeros_like(low)], axis=0).astype(jnp.bfloat16)
    for copy in copies[5:9]:
        copy.wait()


def weights_kernel(taps, bias, wide, bias_col):
    channels = taps.shape[1]
    width = 16 * channels
    row = lax.broadcasted_iota(jnp.int32, (channels, width), 0)
    lane = lax.broadcasted_iota(jnp.int32, (channels, width), 1)
    repeat = jnp.where(lane % channels == row, 1.0, 0.0).astype(jnp.bfloat16)
    group = lane // channels
    for z in range(3):
        every = [
            jnp.dot(taps[3 * k + z], repeat, preferred_element_type=jnp.float32) for k in range(9)
        ]
        for out_x in range(2):
            for out_y in range(2):
                total = jnp.zeros((channels, width), jnp.float32)
                for k in range(9):
                    at = (out_x + k // 3) * 4 + out_y + k % 3
                    total = jnp.where(group == at, every[k], total)
                start = ((z * 2 + out_x) * 2 + out_y) * channels
                wide[start : start + channels] = total.astype(jnp.bfloat16)
    square = (channels, channels)
    same = lax.broadcasted_iota(jnp.int32, square, 0) == lax.broadcasted_iota(jnp.int32, square, 1)
    column = jnp.sum(jnp.where(same, bias[...], 0.0), axis=1, keepdims=True)
    bias_col[...] = jnp.broadcast_to(column, bias_col.shape)


def mesh_flags():
    keep = []
    for axis in ("sy", "sx"):
        where = lax.axis_index(axis)
        keep += [where > 0, where < lax.axis_size(axis) - 1]
    return [jnp.where(k, 1.0, 0.0) for k in keep]


def conv_block(grid, masks, wide, bias_all, lane, grid_x, y, out, out_x):
    channels, depth = bias_all.shape
    window = jnp.concatenate(
        [grid[grid_x + k, y : y + 4].reshape(4 * channels, depth) for k in range(4)], axis=0
    )
    parts = jnp.dot(wide[...], window, preferred_element_type=jnp.float32)
    low = pltpu.roll(parts[0 : 4 * channels], 1, 1)
    high = pltpu.roll(parts[8 * channels :], depth - 1, 1)
    total = parts[4 * channels : 8 * channels]
    total = total + jnp.where(lane == 0, 0.0, low) + jnp.where(lane == depth - 1, 0.0, high)
    for step_x in range(2):
        for step_y in range(2):
            at = (step_x * 2 + step_y) * channels
            keep = masks[step_x](y + step_y)
            value = keep * (total[at : at + channels] + bias_all)
            out[out_x + step_x, y + step_y] = value.astype(jnp.bfloat16)


def splat(flag, shape):
    return jnp.full(shape, flag, jnp.float32).astype(jnp.bfloat16)


def fill_row(grid, grid_x, mask, middle, low, high):
    cols = grid.shape[1] - 2
    grid[grid_x, 0] = low
    for y in range(cols):
        grid[grid_x, y + 1] = middle(y) * mask(y).astype(jnp.bfloat16)
    grid[grid_x, cols + 1] = high


def fill_own(grid, grid_x, own, mask, y_lo, y_hi, flags, x):
    low = y_lo[x] * splat(flags[0], y_lo.shape[1:])
    high = y_hi[x] * splat(flags[1], y_hi.shape[1:])
    fill_row(grid, grid_x, mask_of(mask, x), lambda y: own[x, y], low, high)


def mask_of(mask, x):
    return lambda y: mask[x, y : y + 1, :]


def conv_inner_kernel(own, y_lo, y_hi, mask, wide, bias, out, grid):
    rows, cols, channels, depth = own.shape
    flags = mesh_flags()

    def fill(x, carry):
        fill_own(grid, x, own, mask, y_lo, y_hi, flags, x)
        return carry

    lax.fori_loop(0, rows, fill, 0)
    lane = lax.broadcasted_iota(jnp.int32, (4 * channels, depth), 1)
    bias_all = bias[...]

    def pair(i, carry):
        masks = (mask_of(mask, 2 * i + 1), mask_of(mask, 2 * i + 2))
        for y in range(0, cols, 2):
            conv_block(grid, masks, wide, bias_all, lane, 2 * i, y, out, 2 * i)
        return carry

    lax.fori_loop(0, rows // 2 - 1, pair, 0)


def sides_kernel(y_lo, y_hi, out_hi, out_lo):
    rows = y_lo.shape[0] - 3
    channels, depth = y_lo.shape[1:]
    clear = [splat(flag, y_lo.shape[1:]) for flag in mesh_flags()[:2]]
    sources = [ref[rows + far].astype(jnp.float32) for far in range(2) for ref in (y_lo, y_hi)]
    for out, pair, row in ((out_hi, (rows - 2, rows - 1), rows - 1), (out_lo, (0, 1), 0)):
        for k, x in enumerate(pair):
            out[2 * k] = y_lo[x] * clear[0]
            out[2 * k + 1] = y_hi[x] * clear[1]
        rims = [
            terms[at : at + 1] for at in (row, rows + row, 2 * rows + row) for terms in sources
        ]
        blank = jnp.zeros((channels - 12, depth), jnp.float32)
        out[4] = jnp.concatenate([*rims, blank], axis=0).astype(jnp.bfloat16)


def conv_edge_kernel(
    own,
    y_lo,
    y_hi,
    x_lo,
    x_hi,
    side_lo,
    side_hi,
    mask,
    wide,
    bias,
    inner,
    out,
    out_hi,
    out_lo,
    grid,
    side_mask,
):
    rows, cols, channels, depth = own.shape
    flags = mesh_flags()
    for k, side in enumerate((x_lo, x_hi)):
        both = side[2 * cols].astype(jnp.float32) * flags[2 + k]
        side_mask[2 * k] = both[:cols]
        side_mask[2 * k + 1] = both[cols:]
    for x in range(2):
        for k, ref, side in ((0, x_lo, side_lo), (1, x_hi, side_hi)):
            clear = splat(flags[2 + k], (channels, depth))
            fill_row(
                grid,
                6 * k + x,
                mask_of(side_mask, 2 * k + x),
                lambda y: ref[x * cols + y],
                side[2 * x] * clear,
                side[2 * x + 1] * clear,
            )
        fill_own(grid, 2 + x, own, mask, y_lo, y_hi, flags, x)
        fill_own(grid, 4 + x, own, mask, y_lo, y_hi, flags, rows - 2 + x)
    lane = lax.broadcasted_iota(jnp.int32, (4 * channels, depth), 1)
    bias_all = bias[...]
    for side, masks in (
        (0, (mask_of(side_mask, 1), mask_of(mask, 0))),
        (1, (mask_of(mask, rows - 1), mask_of(side_mask, 2))),
    ):
        for y in range(0, cols, 2):
            conv_block(grid, masks, wide, bias_all, lane, 4 * side, y, out, 2 * side)
    for ref, ys in ((out_hi, (cols - 1, cols - 2)), (out_lo, (0, 1))):
        for far, y in enumerate(ys):
            for x in range(rows + 2):
                at = field_at(inner, out, x)
                ref[far * (rows + 2) + x] = at[0][at[1], y]


def two_sum(a, b):
    s = a + b
    t = s - a
    return s, (a - (s - t)) + (b - t)


def split(a):
    c = a * 4097.0
    high = c - (c - a)
    return high, a - high


def two_prod(a, b):
    p = a * b
    a_hi, a_lo = split(a)
    b_hi, b_lo = split(b)
    return p, ((a_hi * b_hi - p) + a_hi * b_lo + a_lo * b_hi) + a_lo * b_lo


def pair_add(a, b):
    s, t = two_sum(a[0], b[0])
    return two_sum(s, t + (a[1] + b[1]))


def pair_scale(a, c):
    p, t = two_prod(a[0], c)
    return two_sum(p, t + a[1] * c)


def field_at(inner, edge, x):
    n = inner.shape[0]
    if x < 2:
        return edge, x
    return (inner, x - 2) if x < n + 2 else (edge, x - n)


def along_y(smooth, dst, field, row, value_at):
    cols = smooth.shape[1]

    def product(y):
        return field[row, y].astype(jnp.float32) * value_at(y)

    here = product(0)
    pair = here
    for y in range(cols):
        if y + 1 < cols:
            following = product(y + 1)
            pair_next = here + following
        else:
            pair_next = here
            following = here
        smooth[dst, y] = pair + pair_next
        here = following
        pair = pair_next


def row_of(ref, x):
    return lambda y: ref[x, y : y + 1, :]


def close_column(both, lane, field):
    depth = both.shape[1]
    up = jnp.where(lane == depth - 1, 0.0, pltpu.roll(both, depth - 1, 1))
    down = jnp.where(lane == 0, 0.0, pltpu.roll(both, 1, 1))
    prod = ((both + both) + (up + down)) * field.astype(jnp.float32)
    return jnp.sum(prod, axis=0, keepdims=True)


def lanes(shape):
    return lax.broadcasted_iota(jnp.int32, shape, 1)


def along_x(smooth, x, ends, field, row, scale):
    cols, channels, depth = smooth.shape[1:]
    lane = lanes((channels, depth))
    sums = []
    for y in range(cols):
        mid = smooth[x, y]
        low = (smooth[x - 1, y] + mid) if ends[0] else mid
        high = (mid + smooth[x + 1, y]) if ends[1] else mid
        sums.append(close_column(low + high, lane, field[row, y]))
    return jnp.concatenate(sums, axis=0) * scale


def first_core_kernel(inner, edge, start, x_lo, x_hi, ridge, out, smooth, side_start):
    n, cols, channels, depth = inner.shape
    scale = 1.0 / (8 * channels)
    for k, side in enumerate((x_lo, x_hi)):
        upper = side[2 * cols + 1].astype(jnp.float32)
        lower = side[2 * cols + 2].astype(jnp.float32)
        side_start[k] = (upper[:cols] + upper[cols:]) + lower[:cols]
    along_y(smooth, 0, edge, 0, row_of(side_start, 0))
    along_y(smooth, 1, edge, 1, row_of(start, 0))
    along_y(smooth, n + 2, edge, 2, row_of(start, n + 1))
    along_y(smooth, n + 3, edge, 3, row_of(side_start, 1))

    def stage_y(k, carry):
        along_y(smooth, k + 2, inner, k, row_of(start, k + 1))
        return carry

    lax.fori_loop(0, n, stage_y, 0)

    def stage_x(k, carry):
        image = along_x(smooth, k + 2, (True, True), inner, k, scale)
        out[k + 1] = ridge[k + 1] * start[k + 1] + image
        return carry

    lax.fori_loop(0, n, stage_x, 0)
    for x, row in ((0, 1), (n + 1, 2)):
        image = along_x(smooth, x + 1, (True, True), edge, row, scale)
        out[x] = ridge[x] * start[x] + image


def rim_rows(g, inner, edge, y, lane, scale):
    sums = []
    for x in range(inner.shape[0] + 2):
        low, mid, high = g[x : x + 3]
        both = mid + mid
        both = both if low is None else both + low
        both = both if high is None else both + high
        at = field_at(inner, edge, x + 1)
        sums.append(close_column(both, lane, at[0][at[1], y]))
    return jnp.concatenate(sums, axis=0) * scale


def column_of(ref, y):
    return jnp.concatenate([ref[x, y : y + 1, :] for x in range(ref.shape[0])], axis=0)


def joined(terms, count, step):
    return (terms[:count] + terms[step : step + count]) + terms[2 * step : 2 * step + count]


def first_rim_kernel(
    inner,
    edge,
    f_lo,
    f_hi,
    y_lo,
    y_hi,
    x_lo,
    x_hi,
    side_lo,
    side_hi,
    start,
    core,
    out,
    w_lo,
    w_hi,
    out_hi,
    out_lo,
):
    n, cols, channels, depth = inner.shape
    rows = n + 2
    scale = 1.0 / (8 * channels)
    lane = lanes((channels, depth))
    out[...] = core[...]
    corners = [joined(side[4].astype(jnp.float32), 4, 4) for side in (side_lo, side_hi)]
    for k, (ref, rim, keep, flag, y) in enumerate(
        zip((f_lo, f_hi), (y_lo, y_hi), (w_lo, w_hi), mesh_flags(), (0, cols - 1))
    ):
        near, far, ridge = (
            joined(rim[rows + at].astype(jnp.float32), rows, rows) for at in range(3)
        )
        ends = []
        for side in (x_lo, x_hi):
            upper = side[2 * cols + 1].astype(jnp.float32)
            lower = side[2 * cols + 2].astype(jnp.float32)
            ends.append((upper[y : y + 1] + upper[cols + y : cols + y + 1]) + lower[y : y + 1])

        def products(fields, values, low, high):
            lines = [low, *(values[x : x + 1] for x in range(rows)), high]
            return [field.astype(jnp.float32) * line for field, line in zip(fields, lines)]

        beyond = [ref[x] for x in range(rows + 2)]
        g = products(beyond, near * flag, corners[0][k : k + 1] * flag, corners[1][k : k + 1] * flag)
        g_far = products(
            [ref[rows + 2 + x] for x in range(rows + 2)],
            far,
            corners[0][2 + k : 3 + k],
            corners[1][2 + k : 3 + k],
        )
        own = [field_at(inner, edge, x) for x in range(rows + 2)]
        g_own = products([at[0][at[1], y] for at in own], column_of(start, y), ends[0], ends[1])
        column = column_of(core, y) + rim_rows(g, inner, edge, y, lane, scale)
        smooth = [(a + b) + (b + c) for a, b, c in zip(g_far, g, g_own)]
        image = [
            close_column((smooth[x] + smooth[x + 1]) + (smooth[x + 1] + smooth[x + 2]), lane, beyond[x + 1])
            for x in range(rows)
        ]
        keep[...] = (ridge * near + jnp.concatenate(image, axis=0) * scale) * flag
        for x in range(rows):
            out[x, y : y + 1, :] = column[x : x + 1]
    for ref, x in ((out_hi, rows - 1), (out_lo, 0)):
        ref[0:1] = w_lo[x : x + 1]
        ref[1 : 1 + cols] = out[x]
        ref[1 + cols : 2 + cols] = w_hi[x : x + 1]


PRODUCTS = ((0, 0), (0, 1), (1, 1), (0, 2), (1, 2))


def add_products(sums, which, fields):
    for k in which:
        a, b = PRODUCTS[k]
        p, e = two_prod(fields[a], fields[b])
        s, t = two_sum(sums[k][0], p)
        sums[k] = (s, sums[k][1] + (t + e))


def second_core_kernel(inner, edge, start, first, ridge, out, grams, smooth):
    n, cols, channels, depth = inner.shape
    scale = 1.0 / (8 * channels)

    def stage_y(k, carry):
        along_y(smooth, k + 1, inner, k, row_of(first, k + 1))
        return carry

    lax.fori_loop(0, n, stage_y, 0)
    along_y(smooth, 0, edge, 1, row_of(first, 0))
    along_y(smooth, n + 1, edge, 2, row_of(first, n + 1))

    def stage_x(k, carry):
        image = along_x(smooth, k + 1, (True, True), inner, k, scale)
        out[k + 1] = ridge[k + 1] * first[k + 1] + image
        return carry

    lax.fori_loop(0, n, stage_x, 0)
    for x, row, ends in ((0, 1, (False, True)), (n + 1, 2, (True, False))):
        out[x] = ridge[x] * first[x] + along_x(smooth, x, ends, edge, row, scale)
    zero = jnp.zeros((cols, depth), jnp.float32)
    sums = [(zero, zero) for _ in PRODUCTS]
    for x in range(n + 2):
        add_products(sums, range(5), (start[x], first[x], out[x]))
    for k, (s, e) in enumerate(sums):
        grams[2 * k] = s
        grams[2 * k + 1] = e


def second_rim_kernel(
    inner, edge, f_lo, f_hi, start, first, w_lo, w_hi, x_lo, x_hi, core, grams, out, share
):
    n, cols, channels, depth = inner.shape
    rows = n + 2
    scale = 1.0 / (8 * channels)
    lane = lanes((channels, depth))
    flags = mesh_flags()
    out[...] = core[...]
    sums = [(grams[2 * k], grams[2 * k + 1]) for k in range(5)]
    added = []
    for ref, rim, flag, y in ((f_lo, w_lo, flags[0], 0), (f_hi, w_hi, flags[1], cols - 1)):
        g = [ref[x + 1].astype(jnp.float32) * (rim[x : x + 1] * flag) for x in range(rows)]
        added.append(rim_rows([None, *g, None], inner, edge, y, lane, scale))
    columns = [jnp.concatenate([column_of(ref, y) for y in (0, cols - 1)]) for ref in (start, first)]
    add_products(sums, (3, 4), (*columns, jnp.concatenate(added, axis=0)))
    for delta, y in zip(added, (0, cols - 1)):
        for x in range(rows):
            out[x, y : y + 1, :] = out[x, y : y + 1, :] + delta[x : x + 1]
    for rim, at, row, x, far in ((x_lo, 0, 1, 0, 0), (x_hi, 3, 2, rows - 1, rows + 1)):

        def product(y):
            value = rim[y : y + 1]
            if y == 0:
                return f_lo[far].astype(jnp.float32) * (value * flags[0])
            if y == cols + 1:
                return f_hi[far].astype(jnp.float32) * (value * flags[1])
            return edge[at, y - 1].astype(jnp.float32) * value

        parts = []
        here = product(1)
        pair = product(0) + here
        for y in range(cols):
            following = product(y + 2)
            pair_next = here + following
            parts.append(close_column(pair + pair_next, lane, edge[row, y]))
            here = following
            pair = pair_next
        delta = jnp.concatenate(parts, axis=0) * scale
        add_products(sums, (3, 4), (start[x], first[x], delta))
        out[x] = out[x] + delta
    row = jnp.zeros((8, 128), jnp.float32)
    lane = lanes((8, 128))
    for k, (s, e) in enumerate(sums):
        while s.shape[0] > 8:
            half = s.shape[0] // 2
            t, d = two_sum(s[:half], s[half:])
            s, e = (t, e[:half] + e[half:] + d)
        while s.shape[1] > 128:
            half = s.shape[1] // 2
            t, d = two_sum(s[:, :half], s[:, half:])
            s, e = (t, e[:, :half] + e[:, half:] + d)
        for axis, steps in ((0, (4, 2, 1)), (1, (64, 32, 16, 8, 4, 2, 1))):
            for step in steps:
                t, d = two_sum(s, pltpu.roll(s, step, axis))
                s, e = (t, (e + pltpu.roll(e, step, axis)) + d)
        row = jnp.where(lane == k, s, row)
        row = jnp.where(lane == 8 + k, e, row)
    share[...] = row[0:1]


def final_kernel(shares, start, first, second, solution_out, residual_out):
    s = shares[...]
    e = jnp.zeros_like(s)
    while s.shape[0] > 8:
        half = s.shape[0] // 2
        t, d = two_sum(s[:half], s[half:])
        s, e = (t, e[:half] + e[half:] + d)
    for step in (4, 2, 1):
        t, d = two_sum(s, pltpu.roll(s, step, 0))
        s, e = (t, (e + pltpu.roll(e, step, 0)) + d)
    lane = lax.broadcasted_iota(jnp.int32, s.shape, 1)

    def pick(value, k):
        return jnp.broadcast_to(
            jnp.sum(jnp.where(lane == k, value, 0.0), axis=1, keepdims=True), s.shape
        )

    g00, g01, g11, g02, g12 = [
        two_sum(pick(s, k), pick(e, k) + pick(s, 8 + k)) for k in range(5)
    ]
    alpha = g00[0] / g01[0]
    fresh = pair_add(pair_add(g00, pair_scale(g01, -2.0 * alpha)), pair_scale(pair_scale(g11, alpha), alpha))
    grow = 1.0 + fresh[0] / g00[0]
    curve = pair_add(
        pair_add(
            pair_scale(pair_scale(g01, grow), grow),
            pair_scale(pair_scale(pair_add(g02, g11), -alpha), grow),
        ),
        pair_scale(pair_scale(g12, alpha), alpha),
    )
    beta = fresh[0] / curve[0]
    near = (alpha + beta * grow)[0:1, 0:1]
    far = (alpha * beta)[0:1, 0:1]
    for x in range(start.shape[0]):
        w0, w1, w2 = (start[x], first[x], second[x])
        solution_out[x] = near * w0 - far * w1
        residual_out[x] = (w0 - near * w1) + far * w2


def per_device(features, conv_weight, conv_bias, occupancy, block_ids, ridge, target):
    rows, cols, channels, depth = features.shape
    f32, bf16 = (jnp.float32, jnp.bfloat16)
    vmem = pl.BlockSpec(memory_space=pltpu.VMEM)

    def call(kernel, args, outs, scratch, limit, name):
        return pl.pallas_call(
            kernel,
            out_shape=[jax.ShapeDtypeStruct(shape, dtype) for shape, dtype in outs],
            in_specs=[vmem for _ in args],
            out_specs=[vmem for _ in outs],
            scratch_shapes=[pltpu.VMEM(shape, dtype) for shape, dtype in scratch],
            compiler_params=pltpu.CompilerParams(vmem_limit_bytes=limit << 20),
            name=name,
        )(*args)

    plane = ((rows, cols, depth), f32)
    blocks = block_ids.reshape(-1, block_ids.shape[3])
    edge_column = ((rows + 3, channels, depth), bf16)
    edge_rows = ((2 * cols + 3, channels, depth), bf16)
    outs = [plane, plane, edge_column, edge_column, edge_rows, edge_rows]
    weight_mask, residual, y_hi, y_lo, x_hi, x_lo = pl.pallas_call(
        prep_kernel,
        out_shape=[jax.ShapeDtypeStruct(shape, dtype) for shape, dtype in outs],
        in_specs=[pl.BlockSpec(memory_space=pl.ANY)] * 5,
        out_specs=[vmem for _ in outs],
        scratch_shapes=[
            pltpu.VMEM(blocks.shape, jnp.int32),
            pltpu.VMEM(occupancy.shape, jnp.int32),
            pltpu.VMEM(target.shape, f32),
            pltpu.VMEM(ridge.shape, f32),
            pltpu.VMEM((2, rows, 1, channels, depth), bf16),
            pltpu.VMEM((blocks.shape[0], depth // block_ids.shape[2]), f32),
            pltpu.SemaphoreType.DMA((10,)),
        ],
        compiler_params=pltpu.CompilerParams(vmem_limit_bytes=PREP_LIMIT << 20),
        name="prep",
    )(features, blocks, occupancy, target, ridge)
    y_lo, y_hi = (shift(y_hi, "sy", 1), shift(y_lo, "sy", -1))
    x_lo, x_hi = (shift(x_hi, "sx", 1), shift(x_lo, "sx", -1))
    wide, bias = call(
        weights_kernel,
        (conv_weight, conv_bias[None]),
        [((12 * channels, 16 * channels), bf16), ((channels, depth), f32)],
        [],
        8,
        "weights",
    )
    grid_scratch = ((rows, cols + 2, channels, depth), bf16)
    inner_shape = (rows - 2, cols, channels, depth)
    edge_shape = (4, cols, channels, depth)
    side_shape = (5, channels, depth)
    side_hi, side_lo = call(
        sides_kernel,
        (y_lo, y_hi),
        [(side_shape, bf16), (side_shape, bf16)],
        [],
        4,
        "sides",
    )
    side_lo, side_hi = (shift(side_hi, "sx", 1), shift(side_lo, "sx", -1))
    (inner,) = call(
        conv_inner_kernel,
        (features, y_lo, y_hi, weight_mask, wide, bias),
        [(inner_shape, bf16)],
        [grid_scratch],
        12,
        "conv_inner",
    )
    column = ((2 * (rows + 2), channels, depth), bf16)
    edge, f_hi, f_lo = call(
        conv_edge_kernel,
        (features, y_lo, y_hi, x_lo, x_hi, side_lo, side_hi, weight_mask, wide, bias, inner),
        [(edge_shape, bf16), column, column],
        [grid_scratch, ((4, cols, depth), f32)],
        12,
        "conv_edge",
    )
    f_lo, f_hi = (shift(f_hi, "sy", 1), shift(f_lo, "sy", -1))
    (core,) = call(
        first_core_kernel,
        (inner, edge, residual, x_lo, x_hi, ridge),
        [plane],
        [((rows + 2, cols, channels, depth), f32), ((2, cols, depth), f32)],
        10,
        "first_core",
    )
    line = ((rows, depth), f32)
    row = ((cols + 2, depth), f32)
    first, w_lo, w_hi, r_hi, r_lo = call(
        first_rim_kernel,
        (inner, edge, f_lo, f_hi, y_lo, y_hi, x_lo, x_hi, side_lo, side_hi, residual, core),
        [plane, line, line, row, row],
        [],
        4,
        "first_rim",
    )
    r_lo, r_hi = (shift(r_hi, "sx", 1), shift(r_lo, "sx", -1))
    core, grams = call(
        second_core_kernel,
        (inner, edge, residual, first, ridge),
        [plane, ((2 * len(PRODUCTS), cols, depth), f32)],
        [((rows, cols, channels, depth), f32)],
        10,
        "second_core",
    )
    second, share = call(
        second_rim_kernel,
        (inner, edge, f_lo, f_hi, residual, first, w_lo, w_hi, r_lo, r_hi, core, grams),
        [plane, ((1, 128), f32)],
        [],
        4,
        "second_rim",
    )

    peers = lax.axis_size("sx") * lax.axis_size("sy")
    shares = lax.all_to_all(jnp.broadcast_to(share[None], (peers, 1, 128)), AXES, 0, 0)
    return tuple(
        call(
            final_kernel,
            (shares.reshape(peers, 128), residual, first, second),
            [plane, plane],
            [],
            8,
            "final",
        )
    )


def solution(mesh):
    placed = (
        P("sx", "sy", None, None),
        P(),
        P(),
        P("sx", "sy", None),
        P("sx", "sy", None, None),
        P("sx", "sy", None),
        P("sx", "sy", None),
    )
    return jax.shard_map(
        per_device,
        mesh=mesh,
        in_specs=placed,
        out_specs=(P("sx", "sy", None), P("sx", "sy", None)),
        check_vma=False,
    )
```

```python
import jax
import jax.numpy as jnp
from jax import lax
from jax.experimental import pallas as pl
from jax.experimental.pallas import tpu as pltpu
from jax.sharding import PartitionSpec as P

AXES = ("sx", "sy")
PREP_LIMIT = 58


def shift(value, axis, step):
    peers = lax.axis_size(axis)
    return lax.ppermute(value, axis, [(i, (i + step) % peers) for i in range(peers)])


def three(value):
    high = value.astype(jnp.bfloat16).astype(jnp.float32)
    rest = value - high
    mid = rest.astype(jnp.bfloat16).astype(jnp.float32)
    return high, mid, rest - mid


def prep_kernel(
    own,
    ids_in,
    occupancy_in,
    target_in,
    mask,
    start,
    y_hi,
    y_lo,
    x_hi,
    x_lo,
    ids,
    occupancy,
    target,
    columns,
    present,
    sems,
):
    rows, cols, channels, depth = own.shape
    half = present.shape[1]
    copies = [
        pltpu.make_async_copy(source, goal, sems.at[k])
        for k, (source, goal) in enumerate(
            (
                (ids_in, ids),
                (occupancy_in, occupancy),
                (target_in, target),
                (own.at[:, 0:1], columns.at[0]),
                (own.at[:, cols - 1 : cols], columns.at[1]),
                (own.at[rows - 2], x_hi.at[0:cols]),
                (own.at[rows - 1], x_hi.at[cols : 2 * cols]),
                (own.at[0], x_lo.at[0:cols]),
                (own.at[1], x_lo.at[cols : 2 * cols]),
            )
        )
    ]
    for copy in copies:
        copy.start()
    copies[0].wait()
    copies[1].wait()
    present[...] = jnp.broadcast_to(
        jnp.where(ids[:, 13:14] >= 0, 1.0, 0.0).astype(jnp.float32), present.shape
    )
    for x in range(rows):
        blocks = [present[pl.ds(2 * cols * x + z, cols, stride=2), :] for z in range(depth // half)]
        mask[x] = occupancy[x].astype(jnp.float32) * jnp.concatenate(blocks, axis=1)
    copies[2].wait()
    for x in range(rows):
        start[x] = mask[x] * target[x]
    copies[3].wait()
    copies[4].wait()
    blank = jnp.zeros((channels - 3 * rows, depth), jnp.float32)
    for k, (out, y) in enumerate(((y_lo, 0), (y_hi, cols - 1))):
        for x in range(rows):
            out[x] = columns[k, x, 0] * mask[x, y : y + 1, :].astype(jnp.bfloat16)
        terms = jnp.concatenate([*three(column_of(start, y)), blank], axis=0)
        out[rows] = terms.astype(jnp.bfloat16)
    for out, pair, row in ((x_hi, (rows - 2, rows - 1), rows - 1), (x_lo, (0, 1), 0)):
        out[2 * cols] = jnp.concatenate([mask[x] for x in pair], axis=0).astype(jnp.bfloat16)
        high, mid, low = three(start[row])
        out[2 * cols + 1] = jnp.concatenate([high, mid], axis=0).astype(jnp.bfloat16)
        out[2 * cols + 2] = jnp.concatenate([low, jnp.zeros_like(low)], axis=0).astype(jnp.bfloat16)
    for copy in copies[5:9]:
        copy.wait()


def weights_kernel(taps, bias, wide, bias_col):
    channels = taps.shape[1]
    width = 16 * channels
    row = lax.broadcasted_iota(jnp.int32, (channels, width), 0)
    lane = lax.broadcasted_iota(jnp.int32, (channels, width), 1)
    repeat = jnp.where(lane % channels == row, 1.0, 0.0).astype(jnp.bfloat16)
    group = lane // channels
    for z in range(3):
        every = [
            jnp.dot(taps[3 * k + z], repeat, preferred_element_type=jnp.float32) for k in range(9)
        ]
        for out_x in range(2):
            for out_y in range(2):
                total = jnp.zeros((channels, width), jnp.float32)
                for k in range(9):
                    at = (out_x + k // 3) * 4 + out_y + k % 3
                    total = jnp.where(group == at, every[k], total)
                start = ((z * 2 + out_x) * 2 + out_y) * channels
                wide[start : start + channels] = total.astype(jnp.bfloat16)
    square = (channels, channels)
    same = lax.broadcasted_iota(jnp.int32, square, 0) == lax.broadcasted_iota(jnp.int32, square, 1)
    column = jnp.sum(jnp.where(same, bias[...], 0.0), axis=1, keepdims=True)
    bias_col[...] = jnp.broadcast_to(column, bias_col.shape)


def mesh_flags():
    keep = []
    for axis in ("sy", "sx"):
        where = lax.axis_index(axis)
        keep += [where > 0, where < lax.axis_size(axis) - 1]
    return [jnp.where(k, 1.0, 0.0) for k in keep]


def conv_block(grid, masks, wide, bias_all, lane, grid_x, y, out, out_x):
    channels, depth = bias_all.shape
    window = jnp.concatenate(
        [grid[grid_x + k, y : y + 4].reshape(4 * channels, depth) for k in range(4)], axis=0
    )
    parts = jnp.dot(wide[...], window, preferred_element_type=jnp.float32)
    low = pltpu.roll(parts[0 : 4 * channels], 1, 1)
    high = pltpu.roll(parts[8 * channels :], depth - 1, 1)
    total = parts[4 * channels : 8 * channels]
    total = total + jnp.where(lane == 0, 0.0, low) + jnp.where(lane == depth - 1, 0.0, high)
    for step_x in range(2):
        for step_y in range(2):
            at = (step_x * 2 + step_y) * channels
            keep = masks[step_x](y + step_y)
            value = keep * (total[at : at + channels] + bias_all)
            out[out_x + step_x, y + step_y] = value.astype(jnp.bfloat16)


def splat(flag, shape):
    return jnp.full(shape, flag, jnp.float32).astype(jnp.bfloat16)


def fill_row(grid, grid_x, mask, middle, low, high):
    cols = grid.shape[1] - 2
    grid[grid_x, 0] = low
    for y in range(cols):
        grid[grid_x, y + 1] = middle(y) * mask(y).astype(jnp.bfloat16)
    grid[grid_x, cols + 1] = high


def fill_own(grid, grid_x, own, mask, y_lo, y_hi, flags, x):
    low = y_lo[x] * splat(flags[0], y_lo.shape[1:])
    high = y_hi[x] * splat(flags[1], y_hi.shape[1:])
    fill_row(grid, grid_x, mask_of(mask, x), lambda y: own[x, y], low, high)


def mask_of(mask, x):
    return lambda y: mask[x, y : y + 1, :]


def conv_inner_kernel(own, y_lo, y_hi, mask, wide, bias, out, grid):
    rows, cols, channels, depth = own.shape
    flags = mesh_flags()

    def fill(x, carry):
        fill_own(grid, x, own, mask, y_lo, y_hi, flags, x)
        return carry

    lax.fori_loop(0, rows, fill, 0)
    lane = lax.broadcasted_iota(jnp.int32, (4 * channels, depth), 1)
    bias_all = bias[...]

    def pair(i, carry):
        masks = (mask_of(mask, 2 * i + 1), mask_of(mask, 2 * i + 2))
        for y in range(0, cols, 2):
            conv_block(grid, masks, wide, bias_all, lane, 2 * i, y, out, 2 * i)
        return carry

    lax.fori_loop(0, rows // 2 - 1, pair, 0)


def sides_kernel(y_lo, y_hi, out_hi, out_lo):
    rows = y_lo.shape[0] - 1
    channels, depth = y_lo.shape[1:]
    clear = [splat(flag, y_lo.shape[1:]) for flag in mesh_flags()[:2]]
    sources = [ref[rows].astype(jnp.float32) for ref in (y_lo, y_hi)]
    for out, pair, row in ((out_hi, (rows - 2, rows - 1), rows - 1), (out_lo, (0, 1), 0)):
        for k, x in enumerate(pair):
            out[2 * k] = y_lo[x] * clear[0]
            out[2 * k + 1] = y_hi[x] * clear[1]
        rims = [
            terms[at : at + 1] for at in (row, rows + row, 2 * rows + row) for terms in sources
        ]
        blank = jnp.zeros((channels - 6, depth), jnp.float32)
        out[4] = jnp.concatenate([*rims, blank], axis=0).astype(jnp.bfloat16)


def conv_edge_kernel(
    own,
    y_lo,
    y_hi,
    x_lo,
    x_hi,
    side_lo,
    side_hi,
    mask,
    wide,
    bias,
    inner,
    start,
    ridge,
    out,
    out_hi,
    out_lo,
    grid,
    side_mask,
):
    rows, cols, channels, depth = own.shape
    flags = mesh_flags()
    for k, side in enumerate((x_lo, x_hi)):
        both = side[2 * cols].astype(jnp.float32) * flags[2 + k]
        side_mask[2 * k] = both[:cols]
        side_mask[2 * k + 1] = both[cols:]
    for x in range(2):
        for k, ref, side in ((0, x_lo, side_lo), (1, x_hi, side_hi)):
            clear = splat(flags[2 + k], (channels, depth))
            fill_row(
                grid,
                6 * k + x,
                mask_of(side_mask, 2 * k + x),
                lambda y: ref[x * cols + y],
                side[2 * x] * clear,
                side[2 * x + 1] * clear,
            )
        fill_own(grid, 2 + x, own, mask, y_lo, y_hi, flags, x)
        fill_own(grid, 4 + x, own, mask, y_lo, y_hi, flags, rows - 2 + x)
    lane = lax.broadcasted_iota(jnp.int32, (4 * channels, depth), 1)
    bias_all = bias[...]
    for side, masks in (
        (0, (mask_of(side_mask, 1), mask_of(mask, 0))),
        (1, (mask_of(mask, rows - 1), mask_of(side_mask, 2))),
    ):
        for y in range(0, cols, 2):
            conv_block(grid, masks, wide, bias_all, lane, 4 * side, y, out, 2 * side)
    lane = lanes((channels, depth))
    places = [field_at(inner, out, x) for x in range(rows + 2)]
    blank = jnp.zeros((channels - 3 * rows, depth), jnp.float32)
    for ref, y, beside in ((out_hi, cols - 1, cols - 2), (out_lo, 0, 1)):
        smooth = []
        for x, (field, at) in enumerate(places):
            ref[x] = field[at, y]
            near, next_in = (
                field[at, k].astype(jnp.float32) * start_at(start, x_lo, x_hi, x, k)
                for k in (y, beside)
            )
            smooth.append((near + near) + next_in)
        image = column_of(ridge, y) * column_of(start, y) + rim_rows(
            smooth, inner, out, y, lane, 1.0 / (8 * channels)
        )
        ref[rows + 2] = jnp.concatenate([*three(image), blank], axis=0).astype(jnp.bfloat16)


def two_sum(a, b):
    s = a + b
    t = s - a
    return s, (a - (s - t)) + (b - t)


def split(a):
    c = a * 4097.0
    high = c - (c - a)
    return high, a - high


def two_prod(a, b):
    p = a * b
    a_hi, a_lo = split(a)
    b_hi, b_lo = split(b)
    return p, ((a_hi * b_hi - p) + a_hi * b_lo + a_lo * b_hi) + a_lo * b_lo


def pair_add(a, b):
    s, t = two_sum(a[0], b[0])
    return two_sum(s, t + (a[1] + b[1]))


def pair_scale(a, c):
    p, t = two_prod(a[0], c)
    return two_sum(p, t + a[1] * c)


def field_at(inner, edge, x):
    n = inner.shape[0]
    if x < 2:
        return edge, x
    return (inner, x - 2) if x < n + 2 else (edge, x - n)


def along_y(smooth, dst, field, row, value_at):
    cols = smooth.shape[1]

    def product(y):
        return field[row, y].astype(jnp.float32) * value_at(y)

    here = product(0)
    pair = here
    for y in range(cols):
        if y + 1 < cols:
            following = product(y + 1)
            pair_next = here + following
        else:
            pair_next = here
            following = here
        smooth[dst, y] = pair + pair_next
        here = following
        pair = pair_next


def row_of(ref, x):
    return lambda y: ref[x, y : y + 1, :]


def close_column(both, lane, field):
    depth = both.shape[1]
    up = jnp.where(lane == depth - 1, 0.0, pltpu.roll(both, depth - 1, 1))
    down = jnp.where(lane == 0, 0.0, pltpu.roll(both, 1, 1))
    prod = ((both + both) + (up + down)) * field.astype(jnp.float32)
    return jnp.sum(prod, axis=0, keepdims=True)


def lanes(shape):
    return lax.broadcasted_iota(jnp.int32, shape, 1)


def along_x(smooth, x, ends, field, row, scale):
    cols, channels, depth = smooth.shape[1:]
    lane = lanes((channels, depth))
    sums = []
    for y in range(cols):
        mid = smooth[x, y]
        low = (smooth[x - 1, y] + mid) if ends[0] else mid
        high = (mid + smooth[x + 1, y]) if ends[1] else mid
        sums.append(close_column(low + high, lane, field[row, y]))
    return jnp.concatenate(sums, axis=0) * scale


def first_core_kernel(inner, edge, start, x_lo, x_hi, ridge, out, smooth, side_start):
    n, cols, channels, depth = inner.shape
    scale = 1.0 / (8 * channels)
    for k, side in enumerate((x_lo, x_hi)):
        upper = side[2 * cols + 1].astype(jnp.float32)
        lower = side[2 * cols + 2].astype(jnp.float32)
        side_start[k] = (upper[:cols] + upper[cols:]) + lower[:cols]
    along_y(smooth, 0, edge, 0, row_of(side_start, 0))
    along_y(smooth, 1, edge, 1, row_of(start, 0))
    along_y(smooth, n + 2, edge, 2, row_of(start, n + 1))
    along_y(smooth, n + 3, edge, 3, row_of(side_start, 1))

    def stage_y(k, carry):
        along_y(smooth, k + 2, inner, k, row_of(start, k + 1))
        return carry

    lax.fori_loop(0, n, stage_y, 0)

    def stage_x(k, carry):
        image = along_x(smooth, k + 2, (True, True), inner, k, scale)
        out[k + 1] = ridge[k + 1] * start[k + 1] + image
        return carry

    lax.fori_loop(0, n, stage_x, 0)
    for x, row in ((0, 1), (n + 1, 2)):
        image = along_x(smooth, x + 1, (True, True), edge, row, scale)
        out[x] = ridge[x] * start[x] + image


def rim_rows(g, inner, edge, y, lane, scale):
    sums = []
    for x in range(inner.shape[0] + 2):
        low, mid, high = g[x : x + 3]
        both = mid + mid
        both = both if low is None else both + low
        both = both if high is None else both + high
        at = field_at(inner, edge, x + 1)
        sums.append(close_column(both, lane, at[0][at[1], y]))
    return jnp.concatenate(sums, axis=0) * scale


def column_of(ref, y):
    return jnp.concatenate([ref[x, y : y + 1, :] for x in range(ref.shape[0])], axis=0)


def start_at(start, x_lo, x_hi, x, y):
    rows, cols = start.shape[:2]
    if 0 < x <= rows:
        return start[x - 1, y : y + 1, :]
    side = x_lo if x == 0 else x_hi
    upper = side[2 * cols + 1].astype(jnp.float32)
    lower = side[2 * cols + 2].astype(jnp.float32)
    return (upper[y : y + 1] + upper[cols + y : cols + y + 1]) + lower[y : y + 1]


def joined(terms, count, step):
    return (terms[:count] + terms[step : step + count]) + terms[2 * step : 2 * step + count]


def first_rim_kernel(
    inner,
    edge,
    f_lo,
    f_hi,
    y_lo,
    y_hi,
    x_lo,
    x_hi,
    side_lo,
    side_hi,
    start,
    core,
    out,
    w_lo,
    w_hi,
    out_hi,
    out_lo,
):
    n, cols, channels, depth = inner.shape
    rows = n + 2
    scale = 1.0 / (8 * channels)
    lane = lanes((channels, depth))
    out[...] = core[...]
    corners = [joined(side[4].astype(jnp.float32), 2, 2) for side in (side_lo, side_hi)]
    for k, (ref, rim, keep, flag, y) in enumerate(
        zip((f_lo, f_hi), (y_lo, y_hi), (w_lo, w_hi), mesh_flags(), (0, cols - 1))
    ):
        near = joined(rim[rows].astype(jnp.float32), rows, rows)
        values = [corners[0][k : k + 1], *(near[x : x + 1] for x in range(rows)), corners[1][k : k + 1]]
        beyond = [ref[x] for x in range(rows + 2)]
        g = [field.astype(jnp.float32) * (value * flag) for field, value in zip(beyond, values)]
        column = column_of(core, y) + rim_rows(g, inner, edge, y, lane, scale)
        g = [
            at[0][at[1], y].astype(jnp.float32) * start_at(start, x_lo, x_hi, x, y)
            for x, at in enumerate(field_at(inner, edge, x) for x in range(rows + 2))
        ]
        image = [
            close_column((g[x] + g[x + 1]) + (g[x + 1] + g[x + 2]), lane, beyond[x + 1])
            for x in range(rows)
        ]
        theirs = joined(ref[rows + 2].astype(jnp.float32), rows, rows)
        keep[...] = (theirs + jnp.concatenate(image, axis=0) * scale) * flag
        for x in range(rows):
            out[x, y : y + 1, :] = column[x : x + 1]
    for ref, x in ((out_hi, rows - 1), (out_lo, 0)):
        ref[0:1] = w_lo[x : x + 1]
        ref[1 : 1 + cols] = out[x]
        ref[1 + cols : 2 + cols] = w_hi[x : x + 1]


PRODUCTS = ((0, 0), (0, 1), (1, 1), (0, 2), (1, 2))


def add_products(sums, which, fields):
    for k in which:
        a, b = PRODUCTS[k]
        p, e = two_prod(fields[a], fields[b])
        s, t = two_sum(sums[k][0], p)
        sums[k] = (s, sums[k][1] + (t + e))


def second_core_kernel(inner, edge, start, first, ridge, out, grams, smooth):
    n, cols, channels, depth = inner.shape
    scale = 1.0 / (8 * channels)

    def stage_y(k, carry):
        along_y(smooth, k + 1, inner, k, row_of(first, k + 1))
        return carry

    lax.fori_loop(0, n, stage_y, 0)
    along_y(smooth, 0, edge, 1, row_of(first, 0))
    along_y(smooth, n + 1, edge, 2, row_of(first, n + 1))

    def stage_x(k, carry):
        image = along_x(smooth, k + 1, (True, True), inner, k, scale)
        out[k + 1] = ridge[k + 1] * first[k + 1] + image
        return carry

    lax.fori_loop(0, n, stage_x, 0)
    for x, row, ends in ((0, 1, (False, True)), (n + 1, 2, (True, False))):
        out[x] = ridge[x] * first[x] + along_x(smooth, x, ends, edge, row, scale)
    zero = jnp.zeros((cols, depth), jnp.float32)
    sums = [(zero, zero) for _ in PRODUCTS]
    for x in range(n + 2):
        add_products(sums, range(5), (start[x], first[x], out[x]))
    for k, (s, e) in enumerate(sums):
        grams[2 * k] = s
        grams[2 * k + 1] = e


def second_rim_kernel(
    inner, edge, f_lo, f_hi, start, first, w_lo, w_hi, x_lo, x_hi, core, grams, out, share
):
    n, cols, channels, depth = inner.shape
    rows = n + 2
    scale = 1.0 / (8 * channels)
    lane = lanes((channels, depth))
    flags = mesh_flags()
    out[...] = core[...]
    sums = [(grams[2 * k], grams[2 * k + 1]) for k in range(5)]
    added = []
    for ref, rim, flag, y in ((f_lo, w_lo, flags[0], 0), (f_hi, w_hi, flags[1], cols - 1)):
        g = [ref[x + 1].astype(jnp.float32) * (rim[x : x + 1] * flag) for x in range(rows)]
        added.append(rim_rows([None, *g, None], inner, edge, y, lane, scale))
    columns = [jnp.concatenate([column_of(ref, y) for y in (0, cols - 1)]) for ref in (start, first)]
    add_products(sums, (3, 4), (*columns, jnp.concatenate(added, axis=0)))
    for delta, y in zip(added, (0, cols - 1)):
        for x in range(rows):
            out[x, y : y + 1, :] = out[x, y : y + 1, :] + delta[x : x + 1]
    for rim, at, row, x, far in ((x_lo, 0, 1, 0, 0), (x_hi, 3, 2, rows - 1, rows + 1)):

        def product(y):
            value = rim[y : y + 1]
            if y == 0:
                return f_lo[far].astype(jnp.float32) * (value * flags[0])
            if y == cols + 1:
                return f_hi[far].astype(jnp.float32) * (value * flags[1])
            return edge[at, y - 1].astype(jnp.float32) * value

        parts = []
        here = product(1)
        pair = product(0) + here
        for y in range(cols):
            following = product(y + 2)
            pair_next = here + following
            parts.append(close_column(pair + pair_next, lane, edge[row, y]))
            here = following
            pair = pair_next
        delta = jnp.concatenate(parts, axis=0) * scale
        add_products(sums, (3, 4), (start[x], first[x], delta))
        out[x] = out[x] + delta
    row = jnp.zeros((8, 128), jnp.float32)
    lane = lanes((8, 128))
    for k, (s, e) in enumerate(sums):
        while s.shape[0] > 8:
            half = s.shape[0] // 2
            t, d = two_sum(s[:half], s[half:])
            s, e = (t, e[:half] + e[half:] + d)
        while s.shape[1] > 128:
            half = s.shape[1] // 2
            t, d = two_sum(s[:, :half], s[:, half:])
            s, e = (t, e[:, :half] + e[:, half:] + d)
        for axis, steps in ((0, (4, 2, 1)), (1, (64, 32, 16, 8, 4, 2, 1))):
            for step in steps:
                t, d = two_sum(s, pltpu.roll(s, step, axis))
                s, e = (t, (e + pltpu.roll(e, step, axis)) + d)
        row = jnp.where(lane == k, s, row)
        row = jnp.where(lane == 8 + k, e, row)
    share[...] = row[0:1]


def final_kernel(shares, start, first, second, solution_out, residual_out):
    s = shares[...]
    e = jnp.zeros_like(s)
    while s.shape[0] > 8:
        half = s.shape[0] // 2
        t, d = two_sum(s[:half], s[half:])
        s, e = (t, e[:half] + e[half:] + d)
    for step in (4, 2, 1):
        t, d = two_sum(s, pltpu.roll(s, step, 0))
        s, e = (t, (e + pltpu.roll(e, step, 0)) + d)
    lane = lax.broadcasted_iota(jnp.int32, s.shape, 1)

    def pick(value, k):
        return jnp.broadcast_to(
            jnp.sum(jnp.where(lane == k, value, 0.0), axis=1, keepdims=True), s.shape
        )

    g00, g01, g11, g02, g12 = [
        two_sum(pick(s, k), pick(e, k) + pick(s, 8 + k)) for k in range(5)
    ]
    alpha = g00[0] / g01[0]
    fresh = pair_add(pair_add(g00, pair_scale(g01, -2.0 * alpha)), pair_scale(pair_scale(g11, alpha), alpha))
    grow = 1.0 + fresh[0] / g00[0]
    curve = pair_add(
        pair_add(
            pair_scale(pair_scale(g01, grow), grow),
            pair_scale(pair_scale(pair_add(g02, g11), -alpha), grow),
        ),
        pair_scale(pair_scale(g12, alpha), alpha),
    )
    beta = fresh[0] / curve[0]
    near = (alpha + beta * grow)[0:1, 0:1]
    far = (alpha * beta)[0:1, 0:1]
    for x in range(start.shape[0]):
        w0, w1, w2 = (start[x], first[x], second[x])
        solution_out[x] = near * w0 - far * w1
        residual_out[x] = (w0 - near * w1) + far * w2


def per_device(features, conv_weight, conv_bias, occupancy, block_ids, ridge, target):
    rows, cols, channels, depth = features.shape
    f32, bf16 = (jnp.float32, jnp.bfloat16)
    vmem = pl.BlockSpec(memory_space=pltpu.VMEM)

    def call(kernel, args, outs, scratch, limit, name):
        return pl.pallas_call(
            kernel,
            out_shape=[jax.ShapeDtypeStruct(shape, dtype) for shape, dtype in outs],
            in_specs=[vmem for _ in args],
            out_specs=[vmem for _ in outs],
            scratch_shapes=[pltpu.VMEM(shape, dtype) for shape, dtype in scratch],
            compiler_params=pltpu.CompilerParams(vmem_limit_bytes=limit << 20),
            name=name,
        )(*args)

    plane = ((rows, cols, depth), f32)
    blocks = block_ids.reshape(-1, block_ids.shape[3])
    edge_column = ((rows + 1, channels, depth), bf16)
    edge_rows = ((2 * cols + 3, channels, depth), bf16)
    outs = [plane, plane, edge_column, edge_column, edge_rows, edge_rows]
    weight_mask, residual, y_hi, y_lo, x_hi, x_lo = pl.pallas_call(
        prep_kernel,
        out_shape=[jax.ShapeDtypeStruct(shape, dtype) for shape, dtype in outs],
        in_specs=[pl.BlockSpec(memory_space=pl.ANY)] * 4,
        out_specs=[vmem for _ in outs],
        scratch_shapes=[
            pltpu.VMEM(blocks.shape, jnp.int32),
            pltpu.VMEM(occupancy.shape, jnp.int32),
            pltpu.VMEM(target.shape, f32),
            pltpu.VMEM((2, rows, 1, channels, depth), bf16),
            pltpu.VMEM((blocks.shape[0], depth // block_ids.shape[2]), f32),
            pltpu.SemaphoreType.DMA((9,)),
        ],
        compiler_params=pltpu.CompilerParams(vmem_limit_bytes=PREP_LIMIT << 20),
        name="prep",
    )(features, blocks, occupancy, target)
    y_lo, y_hi = (shift(y_hi, "sy", 1), shift(y_lo, "sy", -1))
    x_lo, x_hi = (shift(x_hi, "sx", 1), shift(x_lo, "sx", -1))
    wide, bias = call(
        weights_kernel,
        (conv_weight, conv_bias[None]),
        [((12 * channels, 16 * channels), bf16), ((channels, depth), f32)],
        [],
        8,
        "weights",
    )
    grid_scratch = ((rows, cols + 2, channels, depth), bf16)
    inner_shape = (rows - 2, cols, channels, depth)
    edge_shape = (4, cols, channels, depth)
    side_shape = (5, channels, depth)
    side_hi, side_lo = call(
        sides_kernel,
        (y_lo, y_hi),
        [(side_shape, bf16), (side_shape, bf16)],
        [],
        4,
        "sides",
    )
    side_lo, side_hi = (shift(side_hi, "sx", 1), shift(side_lo, "sx", -1))
    (inner,) = call(
        conv_inner_kernel,
        (features, y_lo, y_hi, weight_mask, wide, bias),
        [(inner_shape, bf16)],
        [grid_scratch],
        12,
        "conv_inner",
    )
    column = ((rows + 3, channels, depth), bf16)
    edge, f_hi, f_lo = call(
        conv_edge_kernel,
        (
            features,
            y_lo,
            y_hi,
            x_lo,
            x_hi,
            side_lo,
            side_hi,
            weight_mask,
            wide,
            bias,
            inner,
            residual,
            ridge,
        ),
        [(edge_shape, bf16), column, column],
        [grid_scratch, ((4, cols, depth), f32)],
        12,
        "conv_edge",
    )
    f_lo, f_hi = (shift(f_hi, "sy", 1), shift(f_lo, "sy", -1))
    (core,) = call(
        first_core_kernel,
        (inner, edge, residual, x_lo, x_hi, ridge),
        [plane],
        [((rows + 2, cols, channels, depth), f32), ((2, cols, depth), f32)],
        10,
        "first_core",
    )
    line = ((rows, depth), f32)
    row = ((cols + 2, depth), f32)
    first, w_lo, w_hi, r_hi, r_lo = call(
        first_rim_kernel,
        (inner, edge, f_lo, f_hi, y_lo, y_hi, x_lo, x_hi, side_lo, side_hi, residual, core),
        [plane, line, line, row, row],
        [],
        4,
        "first_rim",
    )
    r_lo, r_hi = (shift(r_hi, "sx", 1), shift(r_lo, "sx", -1))
    core, grams = call(
        second_core_kernel,
        (inner, edge, residual, first, ridge),
        [plane, ((2 * len(PRODUCTS), cols, depth), f32)],
        [((rows, cols, channels, depth), f32)],
        10,
        "second_core",
    )
    second, share = call(
        second_rim_kernel,
        (inner, edge, f_lo, f_hi, residual, first, w_lo, w_hi, r_lo, r_hi, core, grams),
        [plane, ((1, 128), f32)],
        [],
        4,
        "second_rim",
    )

    peers = lax.axis_size("sx") * lax.axis_size("sy")
    shares = lax.all_to_all(jnp.broadcast_to(share[None], (peers, 1, 128)), AXES, 0, 0)
    return tuple(
        call(
            final_kernel,
            (shares.reshape(peers, 128), residual, first, second),
            [plane, plane],
            [],
            8,
            "final",
        )
    )


def solution(mesh):
    placed = (
        P("sx", "sy", None, None),
        P(),
        P(),
        P("sx", "sy", None),
        P("sx", "sy", None, None),
        P("sx", "sy", None),
        P("sx", "sy", None),
    )
    return jax.shard_map(
        per_device,
        mesh=mesh,
        in_specs=placed,
        out_specs=(P("sx", "sy", None), P("sx", "sy", None)),
        check_vma=False,
    )
```

```python
import jax
import jax.numpy as jnp
from jax import lax
from jax.experimental import pallas as pl
from jax.experimental.pallas import tpu as pltpu
from jax.sharding import PartitionSpec as P

AXES = ("sx", "sy")
PREP_LIMIT = 58


def shift(value, axis, step):
    peers = lax.axis_size(axis)
    return lax.ppermute(value, axis, [(i, (i + step) % peers) for i in range(peers)])


def three(value):
    high = value.astype(jnp.bfloat16).astype(jnp.float32)
    rest = value - high
    mid = rest.astype(jnp.bfloat16).astype(jnp.float32)
    return high, mid, rest - mid


def paired(value):
    high, mid, low = three(value)
    return jnp.concatenate([high, mid], axis=0), jnp.concatenate([low, jnp.zeros_like(low)], axis=0)


def prep_kernel(
    own,
    ids_in,
    occupancy_in,
    target_in,
    mask,
    start,
    y_hi,
    y_lo,
    x_hi,
    x_lo,
    ids,
    occupancy,
    target,
    columns,
    present,
    message,
    sems,
):
    rows, cols, channels, depth = own.shape
    half = present.shape[1]
    copies = [
        pltpu.make_async_copy(source, goal, sems.at[k])
        for k, (source, goal) in enumerate(
            (
                (ids_in, ids),
                (occupancy_in, occupancy),
                (target_in, target),
                (own.at[:, 0:1], columns.at[0]),
                (own.at[:, cols - 1 : cols], columns.at[1]),
                (own.at[rows - 2], message.at[0, 0:cols]),
                (own.at[rows - 1], message.at[0, cols : 2 * cols]),
                (own.at[0], message.at[1, 0:cols]),
                (own.at[1], message.at[1, cols : 2 * cols]),
                (message.at[0, 0 : 2 * cols], x_hi.at[0 : 2 * cols]),
                (message.at[1, 0 : 2 * cols], x_lo.at[0 : 2 * cols]),
                (message.at[0, 2 * cols :], x_hi.at[2 * cols :]),
                (message.at[1, 2 * cols :], x_lo.at[2 * cols :]),
            )
        )
    ]
    for copy in (*copies[5:9], *copies[:5]):
        copy.start()
    for k in range(2):
        copies[5 + 2 * k].wait()
        copies[6 + 2 * k].wait()
        copies[9 + k].start()
    copies[0].wait()
    copies[1].wait()
    present[...] = jnp.broadcast_to(
        jnp.where(ids[:, 13:14] >= 0, 1.0, 0.0).astype(jnp.float32), present.shape
    )
    for x in range(rows):
        blocks = [present[pl.ds(2 * cols * x + z, cols, stride=2), :] for z in range(depth // half)]
        mask[x] = occupancy[x].astype(jnp.float32) * jnp.concatenate(blocks, axis=1)
    copies[2].wait()
    for x in range(rows):
        start[x] = mask[x] * target[x]
    for k, (pair, row) in enumerate((((rows - 2, rows - 1), rows - 1), ((0, 1), 0))):
        pieces = (jnp.concatenate([mask[x] for x in pair], axis=0), *paired(start[row]))
        for at, piece in enumerate(pieces):
            message[k, 2 * cols + at] = piece.astype(jnp.bfloat16)
        copies[11 + k].start()
    copies[3].wait()
    copies[4].wait()
    blank = jnp.zeros((channels - 3 * rows, depth), jnp.float32)
    for k, (out, y) in enumerate(((y_lo, 0), (y_hi, cols - 1))):
        for x in range(rows):
            out[x] = columns[k, x, 0] * mask[x, y : y + 1, :].astype(jnp.bfloat16)
        terms = jnp.concatenate([*three(column_of(start, y)), blank], axis=0)
        out[rows] = terms.astype(jnp.bfloat16)
    for copy in copies[9:]:
        copy.wait()


def weights_kernel(taps, bias, mask, wide, bias_col, mask_out):
    mask_out[...] = mask[...]
    channels = taps.shape[1]
    width = 16 * channels
    row = lax.broadcasted_iota(jnp.int32, (channels, width), 0)
    lane = lax.broadcasted_iota(jnp.int32, (channels, width), 1)
    repeat = jnp.where(lane % channels == row, 1.0, 0.0).astype(jnp.bfloat16)
    group = lane // channels
    for z in range(3):
        every = [
            jnp.dot(taps[3 * k + z], repeat, preferred_element_type=jnp.float32) for k in range(9)
        ]
        for out_x in range(2):
            for out_y in range(2):
                total = jnp.zeros((channels, width), jnp.float32)
                for k in range(9):
                    at = (out_x + k // 3) * 4 + out_y + k % 3
                    total = jnp.where(group == at, every[k], total)
                start = ((z * 2 + out_x) * 2 + out_y) * channels
                wide[start : start + channels] = total.astype(jnp.bfloat16)
    square = (channels, channels)
    same = lax.broadcasted_iota(jnp.int32, square, 0) == lax.broadcasted_iota(jnp.int32, square, 1)
    column = jnp.sum(jnp.where(same, bias[...], 0.0), axis=1, keepdims=True)
    bias_col[...] = jnp.broadcast_to(column, bias_col.shape)


def mesh_flags():
    keep = []
    for axis in ("sy", "sx"):
        where = lax.axis_index(axis)
        keep += [where > 0, where < lax.axis_size(axis) - 1]
    return [jnp.where(k, 1.0, 0.0) for k in keep]


def conv_block(grid, masks, wide, bias_all, lane, grid_x, y, out, out_x):
    channels, depth = bias_all.shape
    window = jnp.concatenate(
        [grid[grid_x + k, y : y + 4].reshape(4 * channels, depth) for k in range(4)], axis=0
    )
    parts = jnp.dot(wide[...], window, preferred_element_type=jnp.float32)
    low = pltpu.roll(parts[0 : 4 * channels], 1, 1)
    high = pltpu.roll(parts[8 * channels :], depth - 1, 1)
    total = parts[4 * channels : 8 * channels]
    total = total + jnp.where(lane == 0, 0.0, low) + jnp.where(lane == depth - 1, 0.0, high)
    for step_x in range(2):
        for step_y in range(2):
            at = (step_x * 2 + step_y) * channels
            keep = masks[step_x](y + step_y)
            value = keep * (total[at : at + channels] + bias_all)
            out[out_x + step_x, y + step_y] = value.astype(jnp.bfloat16)


def splat(flag, shape):
    return jnp.full(shape, flag, jnp.float32).astype(jnp.bfloat16)


def fill_row(grid, grid_x, mask, middle, low, high):
    cols = grid.shape[1] - 2
    grid[grid_x, 0] = low
    for y in range(cols):
        grid[grid_x, y + 1] = middle(y) * mask(y).astype(jnp.bfloat16)
    grid[grid_x, cols + 1] = high


def fill_own(grid, grid_x, own, mask, y_lo, y_hi, flags, x):
    low = y_lo[x] * splat(flags[0], y_lo.shape[1:])
    high = y_hi[x] * splat(flags[1], y_hi.shape[1:])
    fill_row(grid, grid_x, mask_of(mask, x), lambda y: own[x, y], low, high)


def mask_of(mask, x):
    return lambda y: mask[x, y : y + 1, :]


def conv_inner_kernel(own, y_lo, y_hi, mask, wide, bias, out, grid):
    rows, cols, channels, depth = own.shape
    flags = mesh_flags()

    def fill(x, carry):
        fill_own(grid, x, own, mask, y_lo, y_hi, flags, x)
        return carry

    lax.fori_loop(0, rows, fill, 0)
    lane = lax.broadcasted_iota(jnp.int32, (4 * channels, depth), 1)
    bias_all = bias[...]

    def pair(i, carry):
        masks = (mask_of(mask, 2 * i + 1), mask_of(mask, 2 * i + 2))
        for y in range(0, cols, 2):
            conv_block(grid, masks, wide, bias_all, lane, 2 * i, y, out, 2 * i)
        return carry

    lax.fori_loop(0, rows // 2 - 1, pair, 0)


def sides_kernel(y_lo, y_hi, _, out_hi, out_lo):
    rows = y_lo.shape[0] - 1
    channels, depth = y_lo.shape[1:]
    clear = [splat(flag, y_lo.shape[1:]) for flag in mesh_flags()[:2]]
    sources = [ref[rows].astype(jnp.float32) for ref in (y_lo, y_hi)]
    for out, pair, row in ((out_hi, (rows - 2, rows - 1), rows - 1), (out_lo, (0, 1), 0)):
        for k, x in enumerate(pair):
            out[2 * k] = y_lo[x] * clear[0]
            out[2 * k + 1] = y_hi[x] * clear[1]
        rims = [
            terms[at : at + 1] for at in (row, rows + row, 2 * rows + row) for terms in sources
        ]
        blank = jnp.zeros((channels - 6, depth), jnp.float32)
        out[4] = jnp.concatenate([*rims, blank], axis=0).astype(jnp.bfloat16)


def conv_edge_kernel(
    own,
    y_lo,
    y_hi,
    x_lo,
    x_hi,
    side_lo,
    side_hi,
    mask,
    wide,
    bias,
    inner,
    start,
    ridge,
    out,
    out_hi,
    out_lo,
    grid,
    side_mask,
):
    rows, cols, channels, depth = own.shape
    flags = mesh_flags()
    for k, side in enumerate((x_lo, x_hi)):
        both = side[2 * cols].astype(jnp.float32) * flags[2 + k]
        side_mask[2 * k] = both[:cols]
        side_mask[2 * k + 1] = both[cols:]
    for x in range(2):
        for k, ref, side in ((0, x_lo, side_lo), (1, x_hi, side_hi)):
            clear = splat(flags[2 + k], (channels, depth))
            fill_row(
                grid,
                6 * k + x,
                mask_of(side_mask, 2 * k + x),
                lambda y: ref[x * cols + y],
                side[2 * x] * clear,
                side[2 * x + 1] * clear,
            )
        fill_own(grid, 2 + x, own, mask, y_lo, y_hi, flags, x)
        fill_own(grid, 4 + x, own, mask, y_lo, y_hi, flags, rows - 2 + x)
    lane = lax.broadcasted_iota(jnp.int32, (4 * channels, depth), 1)
    bias_all = bias[...]
    for side, masks in (
        (0, (mask_of(side_mask, 1), mask_of(mask, 0))),
        (1, (mask_of(mask, rows - 1), mask_of(side_mask, 2))),
    ):
        for y in range(0, cols, 2):
            conv_block(grid, masks, wide, bias_all, lane, 4 * side, y, out, 2 * side)
    lane = lanes((channels, depth))
    places = [field_at(inner, out, x) for x in range(rows + 2)]
    blank = jnp.zeros((channels - 3 * rows, depth), jnp.float32)
    for ref, y, beside in ((out_hi, cols - 1, cols - 2), (out_lo, 0, 1)):
        smooth = []
        for x, (field, at) in enumerate(places):
            ref[x] = field[at, y]
            near, next_in = (
                field[at, k].astype(jnp.float32) * start_at(start, x_lo, x_hi, x, k)
                for k in (y, beside)
            )
            smooth.append((near + near) + next_in)
        image = column_of(ridge, y) * column_of(start, y) + rim_rows(
            smooth, inner, out, y, lane, 1.0 / (8 * channels)
        )
        ref[rows + 2] = jnp.concatenate([*three(image), blank], axis=0).astype(jnp.bfloat16)


def two_sum(a, b):
    s = a + b
    t = s - a
    return s, (a - (s - t)) + (b - t)


def split(a):
    c = a * 4097.0
    high = c - (c - a)
    return high, a - high


def two_prod(a, b):
    p = a * b
    a_hi, a_lo = split(a)
    b_hi, b_lo = split(b)
    return p, ((a_hi * b_hi - p) + a_hi * b_lo + a_lo * b_hi) + a_lo * b_lo


def pair_add(a, b):
    s, t = two_sum(a[0], b[0])
    return two_sum(s, t + (a[1] + b[1]))


def pair_scale(a, c):
    p, t = two_prod(a[0], c)
    return two_sum(p, t + a[1] * c)


def field_at(inner, edge, x):
    n = inner.shape[0]
    if x < 2:
        return edge, x
    return (inner, x - 2) if x < n + 2 else (edge, x - n)


def along_y(smooth, dst, field, row, value_at):
    cols = smooth.shape[1]

    def product(y):
        return field[row, y].astype(jnp.float32) * value_at(y)

    here = product(0)
    pair = here
    for y in range(cols):
        if y + 1 < cols:
            following = product(y + 1)
            pair_next = here + following
        else:
            pair_next = here
            following = here
        smooth[dst, y] = pair + pair_next
        here = following
        pair = pair_next


def row_of(ref, x):
    return lambda y: ref[x, y : y + 1, :]


def close_column(both, lane, field):
    depth = both.shape[1]
    up = jnp.where(lane == depth - 1, 0.0, pltpu.roll(both, depth - 1, 1))
    down = jnp.where(lane == 0, 0.0, pltpu.roll(both, 1, 1))
    prod = ((both + both) + (up + down)) * field.astype(jnp.float32)
    return jnp.sum(prod, axis=0, keepdims=True)


def lanes(shape):
    return lax.broadcasted_iota(jnp.int32, shape, 1)


def along_x(smooth, x, ends, field, row, scale):
    cols, channels, depth = smooth.shape[1:]
    lane = lanes((channels, depth))
    sums = []
    for y in range(cols):
        mid = smooth[x, y]
        low = (smooth[x - 1, y] + mid) if ends[0] else mid
        high = (mid + smooth[x + 1, y]) if ends[1] else mid
        sums.append(close_column(low + high, lane, field[row, y]))
    return jnp.concatenate(sums, axis=0) * scale


def first_core_kernel(inner, edge, start, x_lo, x_hi, ridge, out, smooth, side_start):
    n, cols, channels, depth = inner.shape
    scale = 1.0 / (8 * channels)
    for k, side in enumerate((x_lo, x_hi)):
        upper = side[2 * cols + 1].astype(jnp.float32)
        lower = side[2 * cols + 2].astype(jnp.float32)
        side_start[k] = (upper[:cols] + upper[cols:]) + lower[:cols]
    along_y(smooth, 0, edge, 0, row_of(side_start, 0))
    along_y(smooth, 1, edge, 1, row_of(start, 0))
    along_y(smooth, n + 2, edge, 2, row_of(start, n + 1))
    along_y(smooth, n + 3, edge, 3, row_of(side_start, 1))

    def stage_y(k, carry):
        along_y(smooth, k + 2, inner, k, row_of(start, k + 1))
        return carry

    lax.fori_loop(0, n, stage_y, 0)

    def stage_x(k, carry):
        image = along_x(smooth, k + 2, (True, True), inner, k, scale)
        out[k + 1] = ridge[k + 1] * start[k + 1] + image
        return carry

    lax.fori_loop(0, n, stage_x, 0)
    for x, row in ((0, 1), (n + 1, 2)):
        image = along_x(smooth, x + 1, (True, True), edge, row, scale)
        out[x] = ridge[x] * start[x] + image


def rim_rows(g, inner, edge, y, lane, scale):
    sums = []
    for x in range(inner.shape[0] + 2):
        low, mid, high = g[x : x + 3]
        both = mid + mid
        both = both if low is None else both + low
        both = both if high is None else both + high
        at = field_at(inner, edge, x + 1)
        sums.append(close_column(both, lane, at[0][at[1], y]))
    return jnp.concatenate(sums, axis=0) * scale


def column_of(ref, y):
    return jnp.concatenate([ref[x, y : y + 1, :] for x in range(ref.shape[0])], axis=0)


def start_at(start, x_lo, x_hi, x, y):
    rows, cols = start.shape[:2]
    if 0 < x <= rows:
        return start[x - 1, y : y + 1, :]
    side = x_lo if x == 0 else x_hi
    upper = side[2 * cols + 1].astype(jnp.float32)
    lower = side[2 * cols + 2].astype(jnp.float32)
    return (upper[y : y + 1] + upper[cols + y : cols + y + 1]) + lower[y : y + 1]


def joined(terms, count, step):
    return (terms[:count] + terms[step : step + count]) + terms[2 * step : 2 * step + count]


def first_rim_kernel(
    inner,
    edge,
    f_lo,
    f_hi,
    y_lo,
    y_hi,
    x_lo,
    x_hi,
    side_lo,
    side_hi,
    start,
    core,
    out,
    w_lo,
    w_hi,
    out_hi,
    out_lo,
):
    n, cols, channels, depth = inner.shape
    rows = n + 2
    scale = 1.0 / (8 * channels)
    lane = lanes((channels, depth))
    out[...] = core[...]
    corners = [joined(side[4].astype(jnp.float32), 2, 2) for side in (side_lo, side_hi)]
    for k, (ref, rim, keep, flag, y) in enumerate(
        zip((f_lo, f_hi), (y_lo, y_hi), (w_lo, w_hi), mesh_flags(), (0, cols - 1))
    ):
        near = joined(rim[rows].astype(jnp.float32), rows, rows)
        values = [corners[0][k : k + 1], *(near[x : x + 1] for x in range(rows)), corners[1][k : k + 1]]
        beyond = [ref[x] for x in range(rows + 2)]
        g = [field.astype(jnp.float32) * (value * flag) for field, value in zip(beyond, values)]
        column = column_of(core, y) + rim_rows(g, inner, edge, y, lane, scale)
        g = [
            at[0][at[1], y].astype(jnp.float32) * start_at(start, x_lo, x_hi, x, y)
            for x, at in enumerate(field_at(inner, edge, x) for x in range(rows + 2))
        ]
        image = [
            close_column((g[x] + g[x + 1]) + (g[x + 1] + g[x + 2]), lane, beyond[x + 1])
            for x in range(rows)
        ]
        theirs = joined(ref[rows + 2].astype(jnp.float32), rows, rows)
        keep[...] = (theirs + jnp.concatenate(image, axis=0) * scale) * flag
        for x in range(rows):
            out[x, y : y + 1, :] = column[x : x + 1]
    for ref, x in ((out_hi, rows - 1), (out_lo, 0)):
        ref[0:1] = w_lo[x : x + 1]
        ref[1 : 1 + cols] = out[x]
        ref[1 + cols : 2 + cols] = w_hi[x : x + 1]


PRODUCTS = ((0, 0), (0, 1), (1, 1), (0, 2), (1, 2))


def add_products(sums, which, fields):
    for k in which:
        a, b = PRODUCTS[k]
        p, e = two_prod(fields[a], fields[b])
        s, t = two_sum(sums[k][0], p)
        sums[k] = (s, sums[k][1] + (t + e))


def second_core_kernel(inner, edge, start, first, ridge, out, grams, smooth):
    n, cols, channels, depth = inner.shape
    scale = 1.0 / (8 * channels)

    def stage_y(k, carry):
        along_y(smooth, k + 1, inner, k, row_of(first, k + 1))
        return carry

    lax.fori_loop(0, n, stage_y, 0)
    along_y(smooth, 0, edge, 1, row_of(first, 0))
    along_y(smooth, n + 1, edge, 2, row_of(first, n + 1))

    def stage_x(k, carry):
        image = along_x(smooth, k + 1, (True, True), inner, k, scale)
        out[k + 1] = ridge[k + 1] * first[k + 1] + image
        return carry

    lax.fori_loop(0, n, stage_x, 0)
    for x, row, ends in ((0, 1, (False, True)), (n + 1, 2, (True, False))):
        out[x] = ridge[x] * first[x] + along_x(smooth, x, ends, edge, row, scale)
    zero = jnp.zeros((cols, depth), jnp.float32)
    sums = [(zero, zero) for _ in PRODUCTS]
    for x in range(n + 2):
        add_products(sums, range(5), (start[x], first[x], out[x]))
    for k, (s, e) in enumerate(sums):
        grams[2 * k] = s
        grams[2 * k + 1] = e


def second_rim_kernel(
    inner, edge, f_lo, f_hi, start, first, w_lo, w_hi, x_lo, x_hi, core, grams, out, share
):
    n, cols, channels, depth = inner.shape
    rows = n + 2
    scale = 1.0 / (8 * channels)
    lane = lanes((channels, depth))
    flags = mesh_flags()
    out[...] = core[...]
    sums = [(grams[2 * k], grams[2 * k + 1]) for k in range(5)]
    added = []
    for ref, rim, flag, y in ((f_lo, w_lo, flags[0], 0), (f_hi, w_hi, flags[1], cols - 1)):
        g = [ref[x + 1].astype(jnp.float32) * (rim[x : x + 1] * flag) for x in range(rows)]
        added.append(rim_rows([None, *g, None], inner, edge, y, lane, scale))
    columns = [jnp.concatenate([column_of(ref, y) for y in (0, cols - 1)]) for ref in (start, first)]
    add_products(sums, (3, 4), (*columns, jnp.concatenate(added, axis=0)))
    for delta, y in zip(added, (0, cols - 1)):
        for x in range(rows):
            out[x, y : y + 1, :] = out[x, y : y + 1, :] + delta[x : x + 1]
    for rim, at, row, x, far in ((x_lo, 0, 1, 0, 0), (x_hi, 3, 2, rows - 1, rows + 1)):

        def product(y):
            value = rim[y : y + 1]
            if y == 0:
                return f_lo[far].astype(jnp.float32) * (value * flags[0])
            if y == cols + 1:
                return f_hi[far].astype(jnp.float32) * (value * flags[1])
            return edge[at, y - 1].astype(jnp.float32) * value

        parts = []
        here = product(1)
        pair = product(0) + here
        for y in range(cols):
            following = product(y + 2)
            pair_next = here + following
            parts.append(close_column(pair + pair_next, lane, edge[row, y]))
            here = following
            pair = pair_next
        delta = jnp.concatenate(parts, axis=0) * scale
        add_products(sums, (3, 4), (start[x], first[x], delta))
        out[x] = out[x] + delta
    row = jnp.zeros((8, 128), jnp.float32)
    lane = lanes((8, 128))
    for k, (s, e) in enumerate(sums):
        while s.shape[0] > 8:
            half = s.shape[0] // 2
            t, d = two_sum(s[:half], s[half:])
            s, e = (t, e[:half] + e[half:] + d)
        while s.shape[1] > 128:
            half = s.shape[1] // 2
            t, d = two_sum(s[:, :half], s[:, half:])
            s, e = (t, e[:, :half] + e[:, half:] + d)
        for axis, steps in ((0, (4, 2, 1)), (1, (64, 32, 16, 8, 4, 2, 1))):
            for step in steps:
                t, d = two_sum(s, pltpu.roll(s, step, axis))
                s, e = (t, (e + pltpu.roll(e, step, axis)) + d)
        row = jnp.where(lane == k, s, row)
        row = jnp.where(lane == 8 + k, e, row)
    share[...] = row[0:1]


def final_kernel(shares, start, first, second, solution_out, residual_out):
    s = shares[...]
    e = jnp.zeros_like(s)
    while s.shape[0] > 8:
        half = s.shape[0] // 2
        t, d = two_sum(s[:half], s[half:])
        s, e = (t, e[:half] + e[half:] + d)
    for step in (4, 2, 1):
        t, d = two_sum(s, pltpu.roll(s, step, 0))
        s, e = (t, (e + pltpu.roll(e, step, 0)) + d)
    lane = lax.broadcasted_iota(jnp.int32, s.shape, 1)

    def pick(value, k):
        return jnp.broadcast_to(
            jnp.sum(jnp.where(lane == k, value, 0.0), axis=1, keepdims=True), s.shape
        )

    g00, g01, g11, g02, g12 = [
        two_sum(pick(s, k), pick(e, k) + pick(s, 8 + k)) for k in range(5)
    ]
    alpha = g00[0] / g01[0]
    fresh = pair_add(pair_add(g00, pair_scale(g01, -2.0 * alpha)), pair_scale(pair_scale(g11, alpha), alpha))
    grow = 1.0 + fresh[0] / g00[0]
    curve = pair_add(
        pair_add(
            pair_scale(pair_scale(g01, grow), grow),
            pair_scale(pair_scale(pair_add(g02, g11), -alpha), grow),
        ),
        pair_scale(pair_scale(g12, alpha), alpha),
    )
    beta = fresh[0] / curve[0]
    near = (alpha + beta * grow)[0:1, 0:1]
    far = (alpha * beta)[0:1, 0:1]
    for x in range(start.shape[0]):
        w0, w1, w2 = (start[x], first[x], second[x])
        solution_out[x] = near * w0 - far * w1
        residual_out[x] = (w0 - near * w1) + far * w2


def per_device(features, conv_weight, conv_bias, occupancy, block_ids, ridge, target):
    rows, cols, channels, depth = features.shape
    f32, bf16 = (jnp.float32, jnp.bfloat16)
    vmem = pl.BlockSpec(memory_space=pltpu.VMEM)

    def call(kernel, args, outs, scratch, limit, name):
        return pl.pallas_call(
            kernel,
            out_shape=[jax.ShapeDtypeStruct(shape, dtype) for shape, dtype in outs],
            in_specs=[vmem for _ in args],
            out_specs=[vmem for _ in outs],
            scratch_shapes=[pltpu.VMEM(shape, dtype) for shape, dtype in scratch],
            compiler_params=pltpu.CompilerParams(vmem_limit_bytes=limit << 20),
            name=name,
        )(*args)

    plane = ((rows, cols, depth), f32)
    blocks = block_ids.reshape(-1, block_ids.shape[3])
    edge_column = ((rows + 1, channels, depth), bf16)
    edge_rows = ((2 * cols + 3, channels, depth), bf16)
    outs = [plane, plane, edge_column, edge_column, edge_rows, edge_rows]
    weight_mask, residual, y_hi, y_lo, x_hi, x_lo = pl.pallas_call(
        prep_kernel,
        out_shape=[jax.ShapeDtypeStruct(shape, dtype) for shape, dtype in outs],
        in_specs=[pl.BlockSpec(memory_space=pl.ANY)] * 4,
        out_specs=[vmem] * 4 + [pl.BlockSpec(memory_space=pl.ANY)] * 2,
        scratch_shapes=[
            pltpu.VMEM(blocks.shape, jnp.int32),
            pltpu.VMEM(occupancy.shape, jnp.int32),
            pltpu.VMEM(target.shape, f32),
            pltpu.VMEM((2, rows, 1, channels, depth), bf16),
            pltpu.VMEM((blocks.shape[0], depth // block_ids.shape[2]), f32),
            pltpu.VMEM((2, *edge_rows[0]), bf16),
            pltpu.SemaphoreType.DMA((13,)),
        ],
        compiler_params=pltpu.CompilerParams(vmem_limit_bytes=PREP_LIMIT << 20),
        name="prep",
    )(features, blocks, occupancy, target)
    y_lo, y_hi = (shift(y_hi, "sy", 1), shift(y_lo, "sy", -1))
    x_lo, x_hi = (shift(x_hi, "sx", 1), shift(x_lo, "sx", -1))
    wide, bias, weight_mask = call(
        weights_kernel,
        (conv_weight, conv_bias[None], weight_mask),
        [((12 * channels, 16 * channels), bf16), ((channels, depth), f32), plane],
        [],
        8,
        "weights",
    )
    grid_scratch = ((rows, cols + 2, channels, depth), bf16)
    inner_shape = (rows - 2, cols, channels, depth)
    edge_shape = (4, cols, channels, depth)
    side_shape = (5, channels, depth)
    side_hi, side_lo = call(
        sides_kernel,
        (y_lo, y_hi, bias),
        [(side_shape, bf16), (side_shape, bf16)],
        [],
        4,
        "sides",
    )
    side_lo, side_hi = (shift(side_hi, "sx", 1), shift(side_lo, "sx", -1))
    (inner,) = call(
        conv_inner_kernel,
        (features, y_lo, y_hi, weight_mask, wide, bias),
        [(inner_shape, bf16)],
        [grid_scratch],
        12,
        "conv_inner",
    )
    column = ((rows + 3, channels, depth), bf16)
    edge, f_hi, f_lo = call(
        conv_edge_kernel,
        (
            features,
            y_lo,
            y_hi,
            x_lo,
            x_hi,
            side_lo,
            side_hi,
            weight_mask,
            wide,
            bias,
            inner,
            residual,
            ridge,
        ),
        [(edge_shape, bf16), column, column],
        [grid_scratch, ((4, cols, depth), f32)],
        12,
        "conv_edge",
    )
    f_lo, f_hi = (shift(f_hi, "sy", 1), shift(f_lo, "sy", -1))
    (core,) = call(
        first_core_kernel,
        (inner, edge, residual, x_lo, x_hi, ridge),
        [plane],
        [((rows + 2, cols, channels, depth), f32), ((2, cols, depth), f32)],
        10,
        "first_core",
    )
    line = ((rows, depth), f32)
    row = ((cols + 2, depth), f32)
    first, w_lo, w_hi, r_hi, r_lo = call(
        first_rim_kernel,
        (inner, edge, f_lo, f_hi, y_lo, y_hi, x_lo, x_hi, side_lo, side_hi, residual, core),
        [plane, line, line, row, row],
        [],
        4,
        "first_rim",
    )
    r_lo, r_hi = (shift(r_hi, "sx", 1), shift(r_lo, "sx", -1))
    core, grams = call(
        second_core_kernel,
        (inner, edge, residual, first, ridge),
        [plane, ((2 * len(PRODUCTS), cols, depth), f32)],
        [((rows, cols, channels, depth), f32)],
        10,
        "second_core",
    )
    second, share = call(
        second_rim_kernel,
        (inner, edge, f_lo, f_hi, residual, first, w_lo, w_hi, r_lo, r_hi, core, grams),
        [plane, ((1, 128), f32)],
        [],
        4,
        "second_rim",
    )

    peers = lax.axis_size("sx") * lax.axis_size("sy")
    shares = lax.all_to_all(jnp.broadcast_to(share[None], (peers, 1, 128)), AXES, 0, 0)
    return tuple(
        call(
            final_kernel,
            (shares.reshape(peers, 128), residual, first, second),
            [plane, plane],
            [],
            8,
            "final",
        )
    )


def solution(mesh):
    placed = (
        P("sx", "sy", None, None),
        P(),
        P(),
        P("sx", "sy", None),
        P("sx", "sy", None, None),
        P("sx", "sy", None),
        P("sx", "sy", None),
    )
    return jax.shard_map(
        per_device,
        mesh=mesh,
        in_specs=placed,
        out_specs=(P("sx", "sy", None), P("sx", "sy", None)),
        check_vma=False,
    )
```

```python
import jax
import jax.numpy as jnp
from jax import lax
from jax.experimental import pallas as pl
from jax.experimental.pallas import tpu as pltpu
from jax.sharding import PartitionSpec as P

AXES = ("sx", "sy")
PREP_LIMIT = 58


def shift(value, axis, step):
    peers = lax.axis_size(axis)
    return lax.ppermute(value, axis, [(i, (i + step) % peers) for i in range(peers)])


def three(value):
    high = value.astype(jnp.bfloat16).astype(jnp.float32)
    rest = value - high
    mid = rest.astype(jnp.bfloat16).astype(jnp.float32)
    return high, mid, rest - mid


def paired(value):
    high, mid, low = three(value)
    return jnp.concatenate([high, mid], axis=0), jnp.concatenate([low, jnp.zeros_like(low)], axis=0)


def prep_kernel(
    own,
    ids_in,
    occupancy_in,
    target_in,
    mask,
    start,
    y_hi,
    y_lo,
    x_hi,
    x_lo,
    ids,
    occupancy,
    target,
    columns,
    present,
    message,
    sems,
):
    rows, cols, channels, depth = own.shape
    half = present.shape[1]
    copies = [
        pltpu.make_async_copy(source, goal, sems.at[k])
        for k, (source, goal) in enumerate(
            (
                (ids_in, ids),
                (occupancy_in, occupancy),
                (target_in, target),
                (own.at[:, 0:1], columns.at[0]),
                (own.at[:, cols - 1 : cols], columns.at[1]),
                (own.at[rows - 2], message.at[0, 0:cols]),
                (own.at[rows - 1], message.at[0, cols : 2 * cols]),
                (own.at[0], message.at[1, 0:cols]),
                (own.at[1], message.at[1, cols : 2 * cols]),
                (message.at[0, 0 : 2 * cols], x_hi.at[0 : 2 * cols]),
                (message.at[1, 0 : 2 * cols], x_lo.at[0 : 2 * cols]),
                (message.at[0, 2 * cols :], x_hi.at[2 * cols :]),
                (message.at[1, 2 * cols :], x_lo.at[2 * cols :]),
            )
        )
    ]
    for copy in (*copies[5:9], *copies[:5]):
        copy.start()
    for k in range(2):
        copies[5 + 2 * k].wait()
        copies[6 + 2 * k].wait()
        copies[9 + k].start()
    copies[0].wait()
    copies[1].wait()
    present[...] = jnp.broadcast_to(
        jnp.where(ids[:, 13:14] >= 0, 1.0, 0.0).astype(jnp.float32), present.shape
    )
    for x in range(rows):
        blocks = [present[pl.ds(2 * cols * x + z, cols, stride=2), :] for z in range(depth // half)]
        mask[x] = occupancy[x].astype(jnp.float32) * jnp.concatenate(blocks, axis=1)
    copies[2].wait()
    for x in range(rows):
        start[x] = mask[x] * target[x]
    for k, (pair, row) in enumerate((((rows - 2, rows - 1), rows - 1), ((0, 1), 0))):
        pieces = (jnp.concatenate([mask[x] for x in pair], axis=0), *paired(start[row]))
        for at, piece in enumerate(pieces):
            message[k, 2 * cols + at] = piece.astype(jnp.bfloat16)
        copies[11 + k].start()
    copies[3].wait()
    copies[4].wait()
    blank = jnp.zeros((channels - 3 * rows, depth), jnp.float32)
    for k, (out, y) in enumerate(((y_lo, 0), (y_hi, cols - 1))):
        for x in range(rows):
            out[x] = columns[k, x, 0] * mask[x, y : y + 1, :].astype(jnp.bfloat16)
        terms = jnp.concatenate([*three(column_of(start, y)), blank], axis=0)
        out[rows] = terms.astype(jnp.bfloat16)
    for copy in copies[9:]:
        copy.wait()


def weights_kernel(taps, bias, mask, wide, bias_col, mask_out):
    mask_out[...] = mask[...]
    channels = taps.shape[1]
    width = 16 * channels
    row = lax.broadcasted_iota(jnp.int32, (channels, width), 0)
    lane = lax.broadcasted_iota(jnp.int32, (channels, width), 1)
    repeat = jnp.where(lane % channels == row, 1.0, 0.0).astype(jnp.bfloat16)
    group = lane // channels
    for z in range(3):
        every = [
            jnp.dot(taps[3 * k + z], repeat, preferred_element_type=jnp.float32) for k in range(9)
        ]
        for out_x in range(2):
            for out_y in range(2):
                total = jnp.zeros((channels, width), jnp.float32)
                for k in range(9):
                    at = (out_x + k // 3) * 4 + out_y + k % 3
                    total = jnp.where(group == at, every[k], total)
                start = ((z * 2 + out_x) * 2 + out_y) * channels
                wide[start : start + channels] = total.astype(jnp.bfloat16)
    square = (channels, channels)
    same = lax.broadcasted_iota(jnp.int32, square, 0) == lax.broadcasted_iota(jnp.int32, square, 1)
    column = jnp.sum(jnp.where(same, bias[...], 0.0), axis=1, keepdims=True)
    bias_col[...] = jnp.broadcast_to(column, bias_col.shape)


def mesh_flags():
    keep = []
    for axis in ("sy", "sx"):
        where = lax.axis_index(axis)
        keep += [where > 0, where < lax.axis_size(axis) - 1]
    return [jnp.where(k, 1.0, 0.0) for k in keep]


def conv_block(grid, masks, wide, bias_all, lane, grid_x, y, out, out_x):
    channels, depth = bias_all.shape
    window = jnp.concatenate(
        [grid[grid_x + k, y : y + 4].reshape(4 * channels, depth) for k in range(4)], axis=0
    )
    parts = jnp.dot(wide[...], window, preferred_element_type=jnp.float32)
    low = pltpu.roll(parts[0 : 4 * channels], 1, 1)
    high = pltpu.roll(parts[8 * channels :], depth - 1, 1)
    total = parts[4 * channels : 8 * channels]
    total = total + jnp.where(lane == 0, 0.0, low) + jnp.where(lane == depth - 1, 0.0, high)
    for step_x in range(2):
        for step_y in range(2):
            at = (step_x * 2 + step_y) * channels
            keep = masks[step_x](y + step_y)
            value = keep * (total[at : at + channels] + bias_all)
            out[out_x + step_x, y + step_y] = value.astype(jnp.bfloat16)


def splat(flag, shape):
    return jnp.full(shape, flag, jnp.float32).astype(jnp.bfloat16)


def fill_row(grid, grid_x, mask, middle, low, high):
    cols = grid.shape[1] - 2
    grid[grid_x, 0] = low
    for y in range(cols):
        grid[grid_x, y + 1] = middle(y) * mask(y).astype(jnp.bfloat16)
    grid[grid_x, cols + 1] = high


def fill_own(grid, grid_x, own, mask, y_lo, y_hi, flags, x):
    low = y_lo[x] * splat(flags[0], y_lo.shape[1:])
    high = y_hi[x] * splat(flags[1], y_hi.shape[1:])
    fill_row(grid, grid_x, mask_of(mask, x), lambda y: own[x, y], low, high)


def mask_of(mask, x):
    return lambda y: mask[x, y : y + 1, :]


def conv_inner_kernel(own, y_lo, y_hi, mask, wide, bias, out, grid):
    rows, cols, channels, depth = own.shape
    flags = mesh_flags()

    def fill(x, carry):
        fill_own(grid, x, own, mask, y_lo, y_hi, flags, x)
        return carry

    lax.fori_loop(0, rows, fill, 0)
    lane = lax.broadcasted_iota(jnp.int32, (4 * channels, depth), 1)
    bias_all = bias[...]

    def pair(i, carry):
        masks = (mask_of(mask, 2 * i + 1), mask_of(mask, 2 * i + 2))
        for y in range(0, cols, 2):
            conv_block(grid, masks, wide, bias_all, lane, 2 * i, y, out, 2 * i)
        return carry

    lax.fori_loop(0, rows // 2 - 1, pair, 0)


def sides_kernel(y_lo, y_hi, _, out_hi, out_lo):
    rows = y_lo.shape[0] - 1
    channels, depth = y_lo.shape[1:]
    clear = [splat(flag, y_lo.shape[1:]) for flag in mesh_flags()[:2]]
    sources = [ref[rows].astype(jnp.float32) for ref in (y_lo, y_hi)]
    for out, pair, row in ((out_hi, (rows - 2, rows - 1), rows - 1), (out_lo, (0, 1), 0)):
        for k, x in enumerate(pair):
            out[2 * k] = y_lo[x] * clear[0]
            out[2 * k + 1] = y_hi[x] * clear[1]
        rims = [
            terms[at : at + 1] for at in (row, rows + row, 2 * rows + row) for terms in sources
        ]
        blank = jnp.zeros((channels - 6, depth), jnp.float32)
        out[4] = jnp.concatenate([*rims, blank], axis=0).astype(jnp.bfloat16)


def conv_edge_kernel(
    own,
    y_lo,
    y_hi,
    x_lo,
    x_hi,
    side_lo,
    side_hi,
    mask,
    wide,
    bias,
    inner,
    start,
    ridge,
    out,
    out_hi,
    out_lo,
    grid,
    side_mask,
):
    rows, cols, channels, depth = own.shape
    flags = mesh_flags()
    for k, side in enumerate((x_lo, x_hi)):
        both = side[2 * cols].astype(jnp.float32) * flags[2 + k]
        side_mask[2 * k] = both[:cols]
        side_mask[2 * k + 1] = both[cols:]
    for x in range(2):
        for k, ref, side in ((0, x_lo, side_lo), (1, x_hi, side_hi)):
            clear = splat(flags[2 + k], (channels, depth))
            fill_row(
                grid,
                6 * k + x,
                mask_of(side_mask, 2 * k + x),
                lambda y: ref[x * cols + y],
                side[2 * x] * clear,
                side[2 * x + 1] * clear,
            )
        fill_own(grid, 2 + x, own, mask, y_lo, y_hi, flags, x)
        fill_own(grid, 4 + x, own, mask, y_lo, y_hi, flags, rows - 2 + x)
    lane = lax.broadcasted_iota(jnp.int32, (4 * channels, depth), 1)
    bias_all = bias[...]
    for side, masks in (
        (0, (mask_of(side_mask, 1), mask_of(mask, 0))),
        (1, (mask_of(mask, rows - 1), mask_of(side_mask, 2))),
    ):
        for y in range(0, cols, 2):
            conv_block(grid, masks, wide, bias_all, lane, 4 * side, y, out, 2 * side)
    lane = lanes((channels, depth))
    places = [field_at(inner, out, x) for x in range(rows + 2)]
    blank = jnp.zeros((channels - 3 * rows, depth), jnp.float32)
    for ref, y, beside in ((out_hi, cols - 1, cols - 2), (out_lo, 0, 1)):
        smooth = []
        for x, (field, at) in enumerate(places):
            ref[x] = field[at, y]
            near, next_in = (
                field[at, k].astype(jnp.float32) * start_at(start, x_lo, x_hi, x, k)
                for k in (y, beside)
            )
            smooth.append((near + near) + next_in)
        image = column_of(ridge, y) * column_of(start, y) + rim_rows(
            smooth, inner, out, y, lane, 1.0 / (8 * channels)
        )
        ref[rows + 2] = jnp.concatenate([*three(image), blank], axis=0).astype(jnp.bfloat16)


def two_sum(a, b):
    s = a + b
    t = s - a
    return s, (a - (s - t)) + (b - t)


def split(a):
    c = a * 4097.0
    high = c - (c - a)
    return high, a - high


def two_prod(a, b):
    p = a * b
    a_hi, a_lo = split(a)
    b_hi, b_lo = split(b)
    return p, ((a_hi * b_hi - p) + a_hi * b_lo + a_lo * b_hi) + a_lo * b_lo


def pair_add(a, b):
    s, t = two_sum(a[0], b[0])
    return two_sum(s, t + (a[1] + b[1]))


def pair_scale(a, c):
    p, t = two_prod(a[0], c)
    return two_sum(p, t + a[1] * c)


def field_at(inner, edge, x):
    n = inner.shape[0]
    if x < 2:
        return edge, x
    return (inner, x - 2) if x < n + 2 else (edge, x - n)


def along_y(smooth, dst, field, row, value_at):
    cols = smooth.shape[1]

    def product(y):
        return field[row, y].astype(jnp.float32) * value_at(y)

    here = product(0)
    pair = here
    for y in range(cols):
        if y + 1 < cols:
            following = product(y + 1)
            pair_next = here + following
        else:
            pair_next = here
            following = here
        smooth[dst, y] = pair + pair_next
        here = following
        pair = pair_next


def row_of(ref, x):
    return lambda y: ref[x, y : y + 1, :]


def close_column(both, lane, field):
    depth = both.shape[1]
    up = jnp.where(lane == depth - 1, 0.0, pltpu.roll(both, depth - 1, 1))
    down = jnp.where(lane == 0, 0.0, pltpu.roll(both, 1, 1))
    prod = ((both + both) + (up + down)) * field.astype(jnp.float32)
    return jnp.sum(prod, axis=0, keepdims=True)


def lanes(shape):
    return lax.broadcasted_iota(jnp.int32, shape, 1)


def along_x(smooth, x, ends, field, row, scale):
    cols, channels, depth = smooth.shape[1:]
    lane = lanes((channels, depth))
    sums = []
    for y in range(cols):
        mid = smooth[x, y]
        low = (smooth[x - 1, y] + mid) if ends[0] else mid
        high = (mid + smooth[x + 1, y]) if ends[1] else mid
        sums.append(close_column(low + high, lane, field[row, y]))
    return jnp.concatenate(sums, axis=0) * scale


def first_core_kernel(inner, edge, start, x_lo, x_hi, ridge, out, smooth, side_start):
    n, cols, channels, depth = inner.shape
    scale = 1.0 / (8 * channels)
    for k, side in enumerate((x_lo, x_hi)):
        upper = side[2 * cols + 1].astype(jnp.float32)
        lower = side[2 * cols + 2].astype(jnp.float32)
        side_start[k] = (upper[:cols] + upper[cols:]) + lower[:cols]
    along_y(smooth, 0, edge, 0, row_of(side_start, 0))
    along_y(smooth, 1, edge, 1, row_of(start, 0))
    along_y(smooth, n + 2, edge, 2, row_of(start, n + 1))
    along_y(smooth, n + 3, edge, 3, row_of(side_start, 1))

    def stage_y(k, carry):
        along_y(smooth, k + 2, inner, k, row_of(start, k + 1))
        return carry

    lax.fori_loop(0, n, stage_y, 0)

    def stage_x(k, carry):
        image = along_x(smooth, k + 2, (True, True), inner, k, scale)
        out[k + 1] = ridge[k + 1] * start[k + 1] + image
        return carry

    lax.fori_loop(0, n, stage_x, 0)
    for x, row in ((0, 1), (n + 1, 2)):
        image = along_x(smooth, x + 1, (True, True), edge, row, scale)
        out[x] = ridge[x] * start[x] + image


def rim_rows(g, inner, edge, y, lane, scale):
    sums = []
    for x in range(inner.shape[0] + 2):
        low, mid, high = g[x : x + 3]
        both = mid + mid
        both = both if low is None else both + low
        both = both if high is None else both + high
        at = field_at(inner, edge, x + 1)
        sums.append(close_column(both, lane, at[0][at[1], y]))
    return jnp.concatenate(sums, axis=0) * scale


def column_of(ref, y):
    return jnp.concatenate([ref[x, y : y + 1, :] for x in range(ref.shape[0])], axis=0)


def start_at(start, x_lo, x_hi, x, y):
    rows, cols = start.shape[:2]
    if 0 < x <= rows:
        return start[x - 1, y : y + 1, :]
    side = x_lo if x == 0 else x_hi
    upper = side[2 * cols + 1].astype(jnp.float32)
    lower = side[2 * cols + 2].astype(jnp.float32)
    return (upper[y : y + 1] + upper[cols + y : cols + y + 1]) + lower[y : y + 1]


def joined(terms, count, step):
    return (terms[:count] + terms[step : step + count]) + terms[2 * step : 2 * step + count]


def first_rim_kernel(
    inner,
    edge,
    f_lo,
    f_hi,
    y_lo,
    y_hi,
    x_lo,
    x_hi,
    side_lo,
    side_hi,
    start,
    core,
    out,
    w_lo,
    w_hi,
    out_hi,
    out_lo,
):
    n, cols, channels, depth = inner.shape
    rows = n + 2
    scale = 1.0 / (8 * channels)
    lane = lanes((channels, depth))
    out[...] = core[...]
    corners = [joined(side[4].astype(jnp.float32), 2, 2) for side in (side_lo, side_hi)]
    for k, (ref, rim, keep, flag, y) in enumerate(
        zip((f_lo, f_hi), (y_lo, y_hi), (w_lo, w_hi), mesh_flags(), (0, cols - 1))
    ):
        near = joined(rim[rows].astype(jnp.float32), rows, rows)
        values = [corners[0][k : k + 1], *(near[x : x + 1] for x in range(rows)), corners[1][k : k + 1]]
        beyond = [ref[x] for x in range(rows + 2)]
        g = [field.astype(jnp.float32) * (value * flag) for field, value in zip(beyond, values)]
        column = column_of(core, y) + rim_rows(g, inner, edge, y, lane, scale)
        g = [
            at[0][at[1], y].astype(jnp.float32) * start_at(start, x_lo, x_hi, x, y)
            for x, at in enumerate(field_at(inner, edge, x) for x in range(rows + 2))
        ]
        image = [
            close_column((g[x] + g[x + 1]) + (g[x + 1] + g[x + 2]), lane, beyond[x + 1])
            for x in range(rows)
        ]
        theirs = joined(ref[rows + 2].astype(jnp.float32), rows, rows)
        keep[...] = (theirs + jnp.concatenate(image, axis=0) * scale) * flag
        for x in range(rows):
            out[x, y : y + 1, :] = column[x : x + 1]
    for ref, x in ((out_hi, rows - 1), (out_lo, 0)):
        ref[0:1] = w_lo[x : x + 1]
        ref[1 : 1 + cols] = out[x]
        ref[1 + cols : 2 + cols] = w_hi[x : x + 1]


PRODUCTS = ((0, 0), (0, 1), (1, 1), (0, 2), (1, 2))


def add_products(sums, which, fields):
    for k in which:
        a, b = PRODUCTS[k]
        p, e = two_prod(fields[a], fields[b])
        s, t = two_sum(sums[k][0], p)
        sums[k] = (s, sums[k][1] + (t + e))


def second_core_kernel(inner, edge, start, first, ridge, out, grams, smooth):
    n, cols, channels, depth = inner.shape
    scale = 1.0 / (8 * channels)

    def stage_y(k, carry):
        along_y(smooth, k + 1, inner, k, row_of(first, k + 1))
        return carry

    lax.fori_loop(0, n, stage_y, 0)
    along_y(smooth, 0, edge, 1, row_of(first, 0))
    along_y(smooth, n + 1, edge, 2, row_of(first, n + 1))

    def stage_x(k, carry):
        image = along_x(smooth, k + 1, (True, True), inner, k, scale)
        out[k + 1] = ridge[k + 1] * first[k + 1] + image
        return carry

    lax.fori_loop(0, n, stage_x, 0)
    for x, row, ends in ((0, 1, (False, True)), (n + 1, 2, (True, False))):
        out[x] = ridge[x] * first[x] + along_x(smooth, x, ends, edge, row, scale)
    zero = jnp.zeros((cols, depth), jnp.float32)
    sums = [(zero, zero) for _ in PRODUCTS]
    for x in range(n + 2):
        add_products(sums, range(5), (start[x], first[x], out[x]))
    for k, (s, e) in enumerate(sums):
        grams[2 * k] = s
        grams[2 * k + 1] = e


def second_rim_kernel(
    inner, edge, f_lo, f_hi, start, first, w_lo, w_hi, x_lo, x_hi, core, grams, out, share
):
    n, cols, channels, depth = inner.shape
    rows = n + 2
    scale = 1.0 / (8 * channels)
    lane = lanes((channels, depth))
    flags = mesh_flags()
    out[...] = core[...]
    sums = [(grams[2 * k], grams[2 * k + 1]) for k in range(5)]
    added = []
    for ref, rim, flag, y in ((f_lo, w_lo, flags[0], 0), (f_hi, w_hi, flags[1], cols - 1)):
        g = [ref[x + 1].astype(jnp.float32) * (rim[x : x + 1] * flag) for x in range(rows)]
        added.append(rim_rows([None, *g, None], inner, edge, y, lane, scale))
    columns = [jnp.concatenate([column_of(ref, y) for y in (0, cols - 1)]) for ref in (start, first)]
    add_products(sums, (3, 4), (*columns, jnp.concatenate(added, axis=0)))
    for delta, y in zip(added, (0, cols - 1)):
        for x in range(rows):
            out[x, y : y + 1, :] = out[x, y : y + 1, :] + delta[x : x + 1]
    for rim, at, row, x, far in ((x_lo, 0, 1, 0, 0), (x_hi, 3, 2, rows - 1, rows + 1)):

        def product(y):
            value = rim[y : y + 1]
            if y == 0:
                return f_lo[far].astype(jnp.float32) * (value * flags[0])
            if y == cols + 1:
                return f_hi[far].astype(jnp.float32) * (value * flags[1])
            return edge[at, y - 1].astype(jnp.float32) * value

        parts = []
        here = product(1)
        pair = product(0) + here
        for y in range(cols):
            following = product(y + 2)
            pair_next = here + following
            parts.append(close_column(pair + pair_next, lane, edge[row, y]))
            here = following
            pair = pair_next
        delta = jnp.concatenate(parts, axis=0) * scale
        add_products(sums, (3, 4), (start[x], first[x], delta))
        out[x] = out[x] + delta
    row = jnp.zeros((8, 128), jnp.float32)
    lane = lanes((8, 128))
    for k, (s, e) in enumerate(sums):
        while s.shape[0] > 8:
            half = s.shape[0] // 2
            t, d = two_sum(s[:half], s[half:])
            s, e = (t, e[:half] + e[half:] + d)
        while s.shape[1] > 128:
            half = s.shape[1] // 2
            t, d = two_sum(s[:, :half], s[:, half:])
            s, e = (t, e[:, :half] + e[:, half:] + d)
        for axis, steps in ((0, (4, 2, 1)), (1, (64, 32, 16, 8, 4, 2, 1))):
            for step in steps:
                t, d = two_sum(s, pltpu.roll(s, step, axis))
                s, e = (t, (e + pltpu.roll(e, step, axis)) + d)
        row = jnp.where(lane == k, s, row)
        row = jnp.where(lane == 8 + k, e, row)
    share[...] = row[0:1]


def final_kernel(shares, start, first, second, solution_out, residual_out):
    s = shares[...]
    e = jnp.zeros_like(s)
    while s.shape[0] > 8:
        half = s.shape[0] // 2
        t, d = two_sum(s[:half], s[half:])
        s, e = (t, e[:half] + e[half:] + d)
    for step in (4, 2, 1):
        t, d = two_sum(s, pltpu.roll(s, step, 0))
        s, e = (t, (e + pltpu.roll(e, step, 0)) + d)
    lane = lax.broadcasted_iota(jnp.int32, s.shape, 1)

    def pick(value, k):
        return jnp.broadcast_to(
            jnp.sum(jnp.where(lane == k, value, 0.0), axis=1, keepdims=True), s.shape
        )

    g00, g01, g11, g02, g12 = [
        two_sum(pick(s, k), pick(e, k) + pick(s, 8 + k)) for k in range(5)
    ]
    alpha = g00[0] / g01[0]
    fresh = pair_add(pair_add(g00, pair_scale(g01, -2.0 * alpha)), pair_scale(pair_scale(g11, alpha), alpha))
    grow = 1.0 + fresh[0] / g00[0]
    curve = pair_add(
        pair_add(
            pair_scale(pair_scale(g01, grow), grow),
            pair_scale(pair_scale(pair_add(g02, g11), -alpha), grow),
        ),
        pair_scale(pair_scale(g12, alpha), alpha),
    )
    beta = fresh[0] / curve[0]
    near = (alpha + beta * grow)[0:1, 0:1]
    far = (alpha * beta)[0:1, 0:1]
    for x in range(start.shape[0]):
        w0, w1, w2 = (start[x], first[x], second[x])
        solution_out[x] = near * w0 - far * w1
        residual_out[x] = (w0 - near * w1) + far * w2


def per_device(features, conv_weight, conv_bias, occupancy, block_ids, ridge, target):
    rows, cols, channels, depth = features.shape
    f32, bf16 = (jnp.float32, jnp.bfloat16)
    vmem = pl.BlockSpec(memory_space=pltpu.VMEM)

    def call(kernel, args, outs, scratch, limit, name):
        return pl.pallas_call(
            kernel,
            out_shape=[jax.ShapeDtypeStruct(shape, dtype) for shape, dtype in outs],
            in_specs=[vmem for _ in args],
            out_specs=[vmem for _ in outs],
            scratch_shapes=[pltpu.VMEM(shape, dtype) for shape, dtype in scratch],
            compiler_params=pltpu.CompilerParams(vmem_limit_bytes=limit << 20),
            name=name,
        )(*args)

    plane = ((rows, cols, depth), f32)
    blocks = block_ids.reshape(-1, block_ids.shape[3])
    edge_column = ((rows + 1, channels, depth), bf16)
    edge_rows = ((2 * cols + 3, channels, depth), bf16)
    outs = [plane, plane, edge_column, edge_column, edge_rows, edge_rows]
    weight_mask, residual, y_hi, y_lo, x_hi, x_lo = pl.pallas_call(
        prep_kernel,
        out_shape=[jax.ShapeDtypeStruct(shape, dtype) for shape, dtype in outs],
        in_specs=[pl.BlockSpec(memory_space=pl.ANY)] * 4,
        out_specs=[vmem] * 4 + [pl.BlockSpec(memory_space=pl.ANY)] * 2,
        scratch_shapes=[
            pltpu.VMEM(blocks.shape, jnp.int32),
            pltpu.VMEM(occupancy.shape, jnp.int32),
            pltpu.VMEM(target.shape, f32),
            pltpu.VMEM((2, rows, 1, channels, depth), bf16),
            pltpu.VMEM((blocks.shape[0], depth // block_ids.shape[2]), f32),
            pltpu.VMEM((2, *edge_rows[0]), bf16),
            pltpu.SemaphoreType.DMA((13,)),
        ],
        compiler_params=pltpu.CompilerParams(vmem_limit_bytes=PREP_LIMIT << 20),
        name="prep",
    )(features, blocks, occupancy, target)
    features, weight_mask = lax.optimization_barrier((features, weight_mask))
    y_lo, y_hi = (shift(y_hi, "sy", 1), shift(y_lo, "sy", -1))
    x_lo, x_hi = (shift(x_hi, "sx", 1), shift(x_lo, "sx", -1))
    wide, bias, weight_mask = call(
        weights_kernel,
        (conv_weight, conv_bias[None], weight_mask),
        [((12 * channels, 16 * channels), bf16), ((channels, depth), f32), plane],
        [],
        8,
        "weights",
    )
    grid_scratch = ((rows, cols + 2, channels, depth), bf16)
    inner_shape = (rows - 2, cols, channels, depth)
    edge_shape = (4, cols, channels, depth)
    side_shape = (5, channels, depth)
    side_hi, side_lo = call(
        sides_kernel,
        (y_lo, y_hi, bias),
        [(side_shape, bf16), (side_shape, bf16)],
        [],
        4,
        "sides",
    )
    side_lo, side_hi = (shift(side_hi, "sx", 1), shift(side_lo, "sx", -1))
    (inner,) = call(
        conv_inner_kernel,
        (features, y_lo, y_hi, weight_mask, wide, bias),
        [(inner_shape, bf16)],
        [grid_scratch],
        12,
        "conv_inner",
    )
    column = ((rows + 3, channels, depth), bf16)
    edge, f_hi, f_lo = call(
        conv_edge_kernel,
        (
            features,
            y_lo,
            y_hi,
            x_lo,
            x_hi,
            side_lo,
            side_hi,
            weight_mask,
            wide,
            bias,
            inner,
            residual,
            ridge,
        ),
        [(edge_shape, bf16), column, column],
        [grid_scratch, ((4, cols, depth), f32)],
        12,
        "conv_edge",
    )
    f_lo, f_hi = (shift(f_hi, "sy", 1), shift(f_lo, "sy", -1))
    (core,) = call(
        first_core_kernel,
        (inner, edge, residual, x_lo, x_hi, ridge),
        [plane],
        [((rows + 2, cols, channels, depth), f32), ((2, cols, depth), f32)],
        10,
        "first_core",
    )
    line = ((rows, depth), f32)
    row = ((cols + 2, depth), f32)
    first, w_lo, w_hi, r_hi, r_lo = call(
        first_rim_kernel,
        (inner, edge, f_lo, f_hi, y_lo, y_hi, x_lo, x_hi, side_lo, side_hi, residual, core),
        [plane, line, line, row, row],
        [],
        4,
        "first_rim",
    )
    r_lo, r_hi = (shift(r_hi, "sx", 1), shift(r_lo, "sx", -1))
    core, grams = call(
        second_core_kernel,
        (inner, edge, residual, first, ridge),
        [plane, ((2 * len(PRODUCTS), cols, depth), f32)],
        [((rows, cols, channels, depth), f32)],
        10,
        "second_core",
    )
    second, share = call(
        second_rim_kernel,
        (inner, edge, f_lo, f_hi, residual, first, w_lo, w_hi, r_lo, r_hi, core, grams),
        [plane, ((1, 128), f32)],
        [],
        4,
        "second_rim",
    )

    peers = lax.axis_size("sx") * lax.axis_size("sy")
    shares = lax.all_to_all(jnp.broadcast_to(share[None], (peers, 1, 128)), AXES, 0, 0)
    return tuple(
        call(
            final_kernel,
            (shares.reshape(peers, 128), residual, first, second),
            [plane, plane],
            [],
            8,
            "final",
        )
    )


def solution(mesh):
    placed = (
        P("sx", "sy", None, None),
        P(),
        P(),
        P("sx", "sy", None),
        P("sx", "sy", None, None),
        P("sx", "sy", None),
        P("sx", "sy", None),
    )
    return jax.shard_map(
        per_device,
        mesh=mesh,
        in_specs=placed,
        out_specs=(P("sx", "sy", None), P("sx", "sy", None)),
        check_vma=False,
    )
```

```python
import jax
import jax.numpy as jnp
from jax import lax
from jax.experimental import pallas as pl
from jax.experimental.pallas import tpu as pltpu
from jax.sharding import PartitionSpec as P

AXES = ("sx", "sy")
PREP_LIMIT = 58


def shift(value, axis, step):
    peers = lax.axis_size(axis)
    return lax.ppermute(value, axis, [(i, (i + step) % peers) for i in range(peers)])


def three(value):
    high = value.astype(jnp.bfloat16).astype(jnp.float32)
    rest = value - high
    mid = rest.astype(jnp.bfloat16).astype(jnp.float32)
    return high, mid, rest - mid


def paired(value):
    high, mid, low = three(value)
    return jnp.concatenate([high, mid], axis=0), jnp.concatenate([low, jnp.zeros_like(low)], axis=0)


def prep_kernel(
    own,
    ids_in,
    occupancy_in,
    target_in,
    mask_out,
    start_out,
    y_hi_out,
    y_lo_out,
    x_hi,
    x_lo,
    ids,
    occupancy,
    target,
    columns,
    present,
    message,
    mask,
    start,
    y_hi,
    y_lo,
    sems,
):
    rows, cols, channels, depth = own.shape
    half = present.shape[1]
    copies = [
        pltpu.make_async_copy(source, goal, sems.at[k])
        for k, (source, goal) in enumerate(
            (
                (ids_in, ids),
                (occupancy_in, occupancy),
                (target_in, target),
                (own.at[:, 0:1], columns.at[0]),
                (own.at[:, cols - 1 : cols], columns.at[1]),
                (own.at[rows - 2], message.at[0, 0:cols]),
                (own.at[rows - 1], message.at[0, cols : 2 * cols]),
                (own.at[0], message.at[1, 0:cols]),
                (own.at[1], message.at[1, cols : 2 * cols]),
                (message.at[0, 0 : 2 * cols], x_hi.at[0 : 2 * cols]),
                (message.at[1, 0 : 2 * cols], x_lo.at[0 : 2 * cols]),
                (message.at[0, 2 * cols :], x_hi.at[2 * cols :]),
                (message.at[1, 2 * cols :], x_lo.at[2 * cols :]),
                (mask, mask_out),
                (start, start_out),
                (y_lo, y_lo_out),
                (y_hi, y_hi_out),
            )
        )
    ]
    for copy in (*copies[5:9], *copies[:5]):
        copy.start()
    for k in range(2):
        copies[5 + 2 * k].wait()
        copies[6 + 2 * k].wait()
        copies[9 + k].start()
    copies[0].wait()
    copies[1].wait()
    present[...] = jnp.broadcast_to(
        jnp.where(ids[:, 13:14] >= 0, 1.0, 0.0).astype(jnp.float32), present.shape
    )
    for x in range(rows):
        blocks = [present[pl.ds(2 * cols * x + z, cols, stride=2), :] for z in range(depth // half)]
        mask[x] = occupancy[x].astype(jnp.float32) * jnp.concatenate(blocks, axis=1)
    copies[13].start()
    copies[2].wait()
    for x in range(rows):
        start[x] = mask[x] * target[x]
    copies[14].start()
    for k, (pair, row) in enumerate((((rows - 2, rows - 1), rows - 1), ((0, 1), 0))):
        pieces = (jnp.concatenate([mask[x] for x in pair], axis=0), *paired(start[row]))
        for at, piece in enumerate(pieces):
            message[k, 2 * cols + at] = piece.astype(jnp.bfloat16)
        copies[11 + k].start()
    copies[3].wait()
    copies[4].wait()
    blank = jnp.zeros((channels - 3 * rows, depth), jnp.float32)
    for k, (out, y) in enumerate(((y_lo, 0), (y_hi, cols - 1))):
        for x in range(rows):
            out[x] = columns[k, x, 0] * mask[x, y : y + 1, :].astype(jnp.bfloat16)
        terms = jnp.concatenate([*three(column_of(start, y)), blank], axis=0)
        out[rows] = terms.astype(jnp.bfloat16)
        copies[15 + k].start()
    for copy in copies[9:]:
        copy.wait()


def weights_kernel(taps, bias, mask, wide, bias_col, mask_out):
    mask_out[...] = mask[...]
    channels = taps.shape[1]
    width = 16 * channels
    row = lax.broadcasted_iota(jnp.int32, (channels, width), 0)
    lane = lax.broadcasted_iota(jnp.int32, (channels, width), 1)
    repeat = jnp.where(lane % channels == row, 1.0, 0.0).astype(jnp.bfloat16)
    group = lane // channels
    for z in range(3):
        every = [
            jnp.dot(taps[3 * k + z], repeat, preferred_element_type=jnp.float32) for k in range(9)
        ]
        for out_x in range(2):
            for out_y in range(2):
                total = jnp.zeros((channels, width), jnp.float32)
                for k in range(9):
                    at = (out_x + k // 3) * 4 + out_y + k % 3
                    total = jnp.where(group == at, every[k], total)
                start = ((z * 2 + out_x) * 2 + out_y) * channels
                wide[start : start + channels] = total.astype(jnp.bfloat16)
    square = (channels, channels)
    same = lax.broadcasted_iota(jnp.int32, square, 0) == lax.broadcasted_iota(jnp.int32, square, 1)
    column = jnp.sum(jnp.where(same, bias[...], 0.0), axis=1, keepdims=True)
    bias_col[...] = jnp.broadcast_to(column, bias_col.shape)


def mesh_flags():
    keep = []
    for axis in ("sy", "sx"):
        where = lax.axis_index(axis)
        keep += [where > 0, where < lax.axis_size(axis) - 1]
    return [jnp.where(k, 1.0, 0.0) for k in keep]


def conv_block(grid, masks, wide, bias_all, lane, grid_x, y, out, out_x):
    channels, depth = bias_all.shape
    window = jnp.concatenate(
        [grid[grid_x + k, y : y + 4].reshape(4 * channels, depth) for k in range(4)], axis=0
    )
    parts = jnp.dot(wide[...], window, preferred_element_type=jnp.float32)
    low = pltpu.roll(parts[0 : 4 * channels], 1, 1)
    high = pltpu.roll(parts[8 * channels :], depth - 1, 1)
    total = parts[4 * channels : 8 * channels]
    total = total + jnp.where(lane == 0, 0.0, low) + jnp.where(lane == depth - 1, 0.0, high)
    for step_x in range(2):
        for step_y in range(2):
            at = (step_x * 2 + step_y) * channels
            keep = masks[step_x](y + step_y)
            value = keep * (total[at : at + channels] + bias_all)
            out[out_x + step_x, y + step_y] = value.astype(jnp.bfloat16)


def splat(flag, shape):
    return jnp.full(shape, flag, jnp.float32).astype(jnp.bfloat16)


def fill_row(grid, grid_x, mask, middle, low, high):
    cols = grid.shape[1] - 2
    grid[grid_x, 0] = low
    for y in range(cols):
        grid[grid_x, y + 1] = middle(y) * mask(y).astype(jnp.bfloat16)
    grid[grid_x, cols + 1] = high


def fill_own(grid, grid_x, own, mask, y_lo, y_hi, flags, x):
    low = y_lo[x] * splat(flags[0], y_lo.shape[1:])
    high = y_hi[x] * splat(flags[1], y_hi.shape[1:])
    fill_row(grid, grid_x, mask_of(mask, x), lambda y: own[x, y], low, high)


def mask_of(mask, x):
    return lambda y: mask[x, y : y + 1, :]


def conv_inner_kernel(own, y_lo, y_hi, mask, wide, bias, out, grid):
    rows, cols, channels, depth = own.shape
    flags = mesh_flags()

    def fill(x, carry):
        fill_own(grid, x, own, mask, y_lo, y_hi, flags, x)
        return carry

    lax.fori_loop(0, rows, fill, 0)
    lane = lax.broadcasted_iota(jnp.int32, (4 * channels, depth), 1)
    bias_all = bias[...]

    def pair(i, carry):
        masks = (mask_of(mask, 2 * i + 1), mask_of(mask, 2 * i + 2))
        for y in range(0, cols, 2):
            conv_block(grid, masks, wide, bias_all, lane, 2 * i, y, out, 2 * i)
        return carry

    lax.fori_loop(0, rows // 2 - 1, pair, 0)


def sides_kernel(y_lo, y_hi, _, out_hi, out_lo):
    rows = y_lo.shape[0] - 1
    channels, depth = y_lo.shape[1:]
    clear = [splat(flag, y_lo.shape[1:]) for flag in mesh_flags()[:2]]
    sources = [ref[rows].astype(jnp.float32) for ref in (y_lo, y_hi)]
    for out, pair, row in ((out_hi, (rows - 2, rows - 1), rows - 1), (out_lo, (0, 1), 0)):
        for k, x in enumerate(pair):
            out[2 * k] = y_lo[x] * clear[0]
            out[2 * k + 1] = y_hi[x] * clear[1]
        rims = [
            terms[at : at + 1] for at in (row, rows + row, 2 * rows + row) for terms in sources
        ]
        blank = jnp.zeros((channels - 6, depth), jnp.float32)
        out[4] = jnp.concatenate([*rims, blank], axis=0).astype(jnp.bfloat16)


def conv_edge_kernel(
    own,
    y_lo,
    y_hi,
    x_lo,
    x_hi,
    side_lo,
    side_hi,
    mask,
    wide,
    bias,
    inner,
    start,
    ridge,
    out,
    out_hi,
    out_lo,
    grid,
    side_mask,
):
    rows, cols, channels, depth = own.shape
    flags = mesh_flags()
    for k, side in enumerate((x_lo, x_hi)):
        both = side[2 * cols].astype(jnp.float32) * flags[2 + k]
        side_mask[2 * k] = both[:cols]
        side_mask[2 * k + 1] = both[cols:]
    for x in range(2):
        for k, ref, side in ((0, x_lo, side_lo), (1, x_hi, side_hi)):
            clear = splat(flags[2 + k], (channels, depth))
            fill_row(
                grid,
                6 * k + x,
                mask_of(side_mask, 2 * k + x),
                lambda y: ref[x * cols + y],
                side[2 * x] * clear,
                side[2 * x + 1] * clear,
            )
        fill_own(grid, 2 + x, own, mask, y_lo, y_hi, flags, x)
        fill_own(grid, 4 + x, own, mask, y_lo, y_hi, flags, rows - 2 + x)
    lane = lax.broadcasted_iota(jnp.int32, (4 * channels, depth), 1)
    bias_all = bias[...]
    for side, masks in (
        (0, (mask_of(side_mask, 1), mask_of(mask, 0))),
        (1, (mask_of(mask, rows - 1), mask_of(side_mask, 2))),
    ):
        for y in range(0, cols, 2):
            conv_block(grid, masks, wide, bias_all, lane, 4 * side, y, out, 2 * side)
    lane = lanes((channels, depth))
    places = [field_at(inner, out, x) for x in range(rows + 2)]
    blank = jnp.zeros((channels - 3 * rows, depth), jnp.float32)
    for ref, y, beside in ((out_hi, cols - 1, cols - 2), (out_lo, 0, 1)):
        smooth = []
        for x, (field, at) in enumerate(places):
            ref[x] = field[at, y]
            near, next_in = (
                field[at, k].astype(jnp.float32) * start_at(start, x_lo, x_hi, x, k)
                for k in (y, beside)
            )
            smooth.append((near + near) + next_in)
        image = column_of(ridge, y) * column_of(start, y) + rim_rows(
            smooth, inner, out, y, lane, 1.0 / (8 * channels)
        )
        ref[rows + 2] = jnp.concatenate([*three(image), blank], axis=0).astype(jnp.bfloat16)


def two_sum(a, b):
    s = a + b
    t = s - a
    return s, (a - (s - t)) + (b - t)


def split(a):
    c = a * 4097.0
    high = c - (c - a)
    return high, a - high


def two_prod(a, b):
    p = a * b
    a_hi, a_lo = split(a)
    b_hi, b_lo = split(b)
    return p, ((a_hi * b_hi - p) + a_hi * b_lo + a_lo * b_hi) + a_lo * b_lo


def pair_add(a, b):
    s, t = two_sum(a[0], b[0])
    return two_sum(s, t + (a[1] + b[1]))


def pair_scale(a, c):
    p, t = two_prod(a[0], c)
    return two_sum(p, t + a[1] * c)


def field_at(inner, edge, x):
    n = inner.shape[0]
    if x < 2:
        return edge, x
    return (inner, x - 2) if x < n + 2 else (edge, x - n)


def along_y(smooth, dst, field, row, value_at):
    cols = smooth.shape[1]

    def product(y):
        return field[row, y].astype(jnp.float32) * value_at(y)

    here = product(0)
    pair = here
    for y in range(cols):
        if y + 1 < cols:
            following = product(y + 1)
            pair_next = here + following
        else:
            pair_next = here
            following = here
        smooth[dst, y] = pair + pair_next
        here = following
        pair = pair_next


def row_of(ref, x):
    return lambda y: ref[x, y : y + 1, :]


def close_column(both, lane, field):
    depth = both.shape[1]
    up = jnp.where(lane == depth - 1, 0.0, pltpu.roll(both, depth - 1, 1))
    down = jnp.where(lane == 0, 0.0, pltpu.roll(both, 1, 1))
    prod = ((both + both) + (up + down)) * field.astype(jnp.float32)
    return jnp.sum(prod, axis=0, keepdims=True)


def lanes(shape):
    return lax.broadcasted_iota(jnp.int32, shape, 1)


def along_x(smooth, x, ends, field, row, scale):
    cols, channels, depth = smooth.shape[1:]
    lane = lanes((channels, depth))
    sums = []
    for y in range(cols):
        mid = smooth[x, y]
        low = (smooth[x - 1, y] + mid) if ends[0] else mid
        high = (mid + smooth[x + 1, y]) if ends[1] else mid
        sums.append(close_column(low + high, lane, field[row, y]))
    return jnp.concatenate(sums, axis=0) * scale


def first_core_kernel(inner, edge, start, x_lo, x_hi, ridge, out, smooth, side_start):
    n, cols, channels, depth = inner.shape
    scale = 1.0 / (8 * channels)
    for k, side in enumerate((x_lo, x_hi)):
        upper = side[2 * cols + 1].astype(jnp.float32)
        lower = side[2 * cols + 2].astype(jnp.float32)
        side_start[k] = (upper[:cols] + upper[cols:]) + lower[:cols]
    along_y(smooth, 0, edge, 0, row_of(side_start, 0))
    along_y(smooth, 1, edge, 1, row_of(start, 0))
    along_y(smooth, n + 2, edge, 2, row_of(start, n + 1))
    along_y(smooth, n + 3, edge, 3, row_of(side_start, 1))

    def stage_y(k, carry):
        along_y(smooth, k + 2, inner, k, row_of(start, k + 1))
        return carry

    lax.fori_loop(0, n, stage_y, 0)

    def stage_x(k, carry):
        image = along_x(smooth, k + 2, (True, True), inner, k, scale)
        out[k + 1] = ridge[k + 1] * start[k + 1] + image
        return carry

    lax.fori_loop(0, n, stage_x, 0)
    for x, row in ((0, 1), (n + 1, 2)):
        image = along_x(smooth, x + 1, (True, True), edge, row, scale)
        out[x] = ridge[x] * start[x] + image


def rim_rows(g, inner, edge, y, lane, scale):
    sums = []
    for x in range(inner.shape[0] + 2):
        low, mid, high = g[x : x + 3]
        both = mid + mid
        both = both if low is None else both + low
        both = both if high is None else both + high
        at = field_at(inner, edge, x + 1)
        sums.append(close_column(both, lane, at[0][at[1], y]))
    return jnp.concatenate(sums, axis=0) * scale


def column_of(ref, y):
    return jnp.concatenate([ref[x, y : y + 1, :] for x in range(ref.shape[0])], axis=0)


def start_at(start, x_lo, x_hi, x, y):
    rows, cols = start.shape[:2]
    if 0 < x <= rows:
        return start[x - 1, y : y + 1, :]
    side = x_lo if x == 0 else x_hi
    upper = side[2 * cols + 1].astype(jnp.float32)
    lower = side[2 * cols + 2].astype(jnp.float32)
    return (upper[y : y + 1] + upper[cols + y : cols + y + 1]) + lower[y : y + 1]


def joined(terms, count, step):
    return (terms[:count] + terms[step : step + count]) + terms[2 * step : 2 * step + count]


def first_rim_kernel(
    inner,
    edge,
    f_lo,
    f_hi,
    y_lo,
    y_hi,
    x_lo,
    x_hi,
    side_lo,
    side_hi,
    start,
    core,
    out,
    w_lo,
    w_hi,
    out_hi,
    out_lo,
):
    n, cols, channels, depth = inner.shape
    rows = n + 2
    scale = 1.0 / (8 * channels)
    lane = lanes((channels, depth))
    out[...] = core[...]
    corners = [joined(side[4].astype(jnp.float32), 2, 2) for side in (side_lo, side_hi)]
    for k, (ref, rim, keep, flag, y) in enumerate(
        zip((f_lo, f_hi), (y_lo, y_hi), (w_lo, w_hi), mesh_flags(), (0, cols - 1))
    ):
        near = joined(rim[rows].astype(jnp.float32), rows, rows)
        values = [corners[0][k : k + 1], *(near[x : x + 1] for x in range(rows)), corners[1][k : k + 1]]
        beyond = [ref[x] for x in range(rows + 2)]
        g = [field.astype(jnp.float32) * (value * flag) for field, value in zip(beyond, values)]
        column = column_of(core, y) + rim_rows(g, inner, edge, y, lane, scale)
        g = [
            at[0][at[1], y].astype(jnp.float32) * start_at(start, x_lo, x_hi, x, y)
            for x, at in enumerate(field_at(inner, edge, x) for x in range(rows + 2))
        ]
        image = [
            close_column((g[x] + g[x + 1]) + (g[x + 1] + g[x + 2]), lane, beyond[x + 1])
            for x in range(rows)
        ]
        theirs = joined(ref[rows + 2].astype(jnp.float32), rows, rows)
        keep[...] = (theirs + jnp.concatenate(image, axis=0) * scale) * flag
        for x in range(rows):
            out[x, y : y + 1, :] = column[x : x + 1]
    for ref, x in ((out_hi, rows - 1), (out_lo, 0)):
        ref[0:1] = w_lo[x : x + 1]
        ref[1 : 1 + cols] = out[x]
        ref[1 + cols : 2 + cols] = w_hi[x : x + 1]


PRODUCTS = ((0, 0), (0, 1), (1, 1), (0, 2), (1, 2))


def add_products(sums, which, fields):
    for k in which:
        a, b = PRODUCTS[k]
        p, e = two_prod(fields[a], fields[b])
        s, t = two_sum(sums[k][0], p)
        sums[k] = (s, sums[k][1] + (t + e))


def second_core_kernel(inner, edge, start, first, ridge, out, grams, smooth):
    n, cols, channels, depth = inner.shape
    scale = 1.0 / (8 * channels)

    def stage_y(k, carry):
        along_y(smooth, k + 1, inner, k, row_of(first, k + 1))
        return carry

    lax.fori_loop(0, n, stage_y, 0)
    along_y(smooth, 0, edge, 1, row_of(first, 0))
    along_y(smooth, n + 1, edge, 2, row_of(first, n + 1))

    def stage_x(k, carry):
        image = along_x(smooth, k + 1, (True, True), inner, k, scale)
        out[k + 1] = ridge[k + 1] * first[k + 1] + image
        return carry

    lax.fori_loop(0, n, stage_x, 0)
    for x, row, ends in ((0, 1, (False, True)), (n + 1, 2, (True, False))):
        out[x] = ridge[x] * first[x] + along_x(smooth, x, ends, edge, row, scale)
    zero = jnp.zeros((cols, depth), jnp.float32)
    sums = [(zero, zero) for _ in PRODUCTS]
    for x in range(n + 2):
        add_products(sums, range(5), (start[x], first[x], out[x]))
    for k, (s, e) in enumerate(sums):
        grams[2 * k] = s
        grams[2 * k + 1] = e


def second_rim_kernel(
    inner, edge, f_lo, f_hi, start, first, w_lo, w_hi, x_lo, x_hi, core, grams, out, share
):
    n, cols, channels, depth = inner.shape
    rows = n + 2
    scale = 1.0 / (8 * channels)
    lane = lanes((channels, depth))
    flags = mesh_flags()
    out[...] = core[...]
    sums = [(grams[2 * k], grams[2 * k + 1]) for k in range(5)]
    added = []
    for ref, rim, flag, y in ((f_lo, w_lo, flags[0], 0), (f_hi, w_hi, flags[1], cols - 1)):
        g = [ref[x + 1].astype(jnp.float32) * (rim[x : x + 1] * flag) for x in range(rows)]
        added.append(rim_rows([None, *g, None], inner, edge, y, lane, scale))
    columns = [jnp.concatenate([column_of(ref, y) for y in (0, cols - 1)]) for ref in (start, first)]
    add_products(sums, (3, 4), (*columns, jnp.concatenate(added, axis=0)))
    for delta, y in zip(added, (0, cols - 1)):
        for x in range(rows):
            out[x, y : y + 1, :] = out[x, y : y + 1, :] + delta[x : x + 1]
    for rim, at, row, x, far in ((x_lo, 0, 1, 0, 0), (x_hi, 3, 2, rows - 1, rows + 1)):

        def product(y):
            value = rim[y : y + 1]
            if y == 0:
                return f_lo[far].astype(jnp.float32) * (value * flags[0])
            if y == cols + 1:
                return f_hi[far].astype(jnp.float32) * (value * flags[1])
            return edge[at, y - 1].astype(jnp.float32) * value

        parts = []
        here = product(1)
        pair = product(0) + here
        for y in range(cols):
            following = product(y + 2)
            pair_next = here + following
            parts.append(close_column(pair + pair_next, lane, edge[row, y]))
            here = following
            pair = pair_next
        delta = jnp.concatenate(parts, axis=0) * scale
        add_products(sums, (3, 4), (start[x], first[x], delta))
        out[x] = out[x] + delta
    lane = lanes((8, 128))
    line = lax.broadcasted_iota(jnp.int32, (8, 128), 0)

    def fold(s, e, axis, steps):
        for step in steps:
            t, d = two_sum(s, pltpu.roll(s, step, axis))
            s, e = (t, (e + pltpu.roll(e, step, axis)) + d)
        return s, e

    total = jnp.zeros((8, 128), jnp.float32)
    error = jnp.zeros((8, 128), jnp.float32)
    for k, (s, e) in enumerate(sums):
        while s.shape[0] > 8:
            half = s.shape[0] // 2
            t, d = two_sum(s[:half], s[half:])
            s, e = (t, e[:half] + e[half:] + d)
        while s.shape[1] > 128:
            half = s.shape[1] // 2
            t, d = two_sum(s[:, :half], s[:, half:])
            s, e = (t, e[:, :half] + e[:, half:] + d)
        s, e = fold(s, e, 0, (4, 2, 1))
        total = jnp.where(line == k, s, total)
        error = jnp.where(line == k, e, error)
    total, error = fold(total, error, 1, (64, 32, 16, 8, 4, 2, 1))
    placed = jnp.where(lane == line, total, 0.0) + jnp.where(lane == line + 8, error, 0.0)
    share[...] = jnp.sum(placed, axis=0, keepdims=True)


def final_kernel(shares, start, first, second, solution_out, residual_out):
    s = shares[...]
    e = jnp.zeros_like(s)
    while s.shape[0] > 8:
        half = s.shape[0] // 2
        t, d = two_sum(s[:half], s[half:])
        s, e = (t, e[:half] + e[half:] + d)
    for step in (4, 2, 1):
        t, d = two_sum(s, pltpu.roll(s, step, 0))
        s, e = (t, (e + pltpu.roll(e, step, 0)) + d)
    lane = lax.broadcasted_iota(jnp.int32, s.shape, 1)

    def pick(value, k):
        return jnp.broadcast_to(
            jnp.sum(jnp.where(lane == k, value, 0.0), axis=1, keepdims=True), s.shape
        )

    g00, g01, g11, g02, g12 = [
        two_sum(pick(s, k), pick(e, k) + pick(s, 8 + k)) for k in range(5)
    ]
    alpha = g00[0] / g01[0]
    fresh = pair_add(pair_add(g00, pair_scale(g01, -2.0 * alpha)), pair_scale(pair_scale(g11, alpha), alpha))
    grow = 1.0 + fresh[0] / g00[0]
    curve = pair_add(
        pair_add(
            pair_scale(pair_scale(g01, grow), grow),
            pair_scale(pair_scale(pair_add(g02, g11), -alpha), grow),
        ),
        pair_scale(pair_scale(g12, alpha), alpha),
    )
    beta = fresh[0] / curve[0]
    near = (alpha + beta * grow)[0:1, 0:1]
    far = (alpha * beta)[0:1, 0:1]
    for x in range(start.shape[0]):
        w0, w1, w2 = (start[x], first[x], second[x])
        solution_out[x] = near * w0 - far * w1
        residual_out[x] = (w0 - near * w1) + far * w2


def per_device(features, conv_weight, conv_bias, occupancy, block_ids, ridge, target):
    rows, cols, channels, depth = features.shape
    f32, bf16 = (jnp.float32, jnp.bfloat16)
    vmem = pl.BlockSpec(memory_space=pltpu.VMEM)

    def call(kernel, args, outs, scratch, limit, name):
        return pl.pallas_call(
            kernel,
            out_shape=[jax.ShapeDtypeStruct(shape, dtype) for shape, dtype in outs],
            in_specs=[vmem for _ in args],
            out_specs=[vmem for _ in outs],
            scratch_shapes=[pltpu.VMEM(shape, dtype) for shape, dtype in scratch],
            compiler_params=pltpu.CompilerParams(vmem_limit_bytes=limit << 20),
            name=name,
        )(*args)

    plane = ((rows, cols, depth), f32)
    blocks = block_ids.reshape(-1, block_ids.shape[3])
    edge_column = ((rows + 1, channels, depth), bf16)
    edge_rows = ((2 * cols + 3, channels, depth), bf16)
    outs = [plane, plane, edge_column, edge_column, edge_rows, edge_rows]
    weight_mask, residual, y_hi, y_lo, x_hi, x_lo = pl.pallas_call(
        prep_kernel,
        out_shape=[jax.ShapeDtypeStruct(shape, dtype) for shape, dtype in outs],
        in_specs=[pl.BlockSpec(memory_space=pl.ANY)] * 4,
        out_specs=[pl.BlockSpec(memory_space=pl.ANY)] * 6,
        scratch_shapes=[
            pltpu.VMEM(blocks.shape, jnp.int32),
            pltpu.VMEM(occupancy.shape, jnp.int32),
            pltpu.VMEM(target.shape, f32),
            pltpu.VMEM((2, rows, 1, channels, depth), bf16),
            pltpu.VMEM((blocks.shape[0], depth // block_ids.shape[2]), f32),
            pltpu.VMEM((2, *edge_rows[0]), bf16),
            *(pltpu.VMEM(shape, dtype) for shape, dtype in outs[:4]),
            pltpu.SemaphoreType.DMA((17,)),
        ],
        compiler_params=pltpu.CompilerParams(vmem_limit_bytes=PREP_LIMIT << 20),
        name="prep",
    )(features, blocks, occupancy, target)
    y_lo, y_hi = (shift(y_hi, "sy", 1), shift(y_lo, "sy", -1))
    x_lo, x_hi = (shift(x_hi, "sx", 1), shift(x_lo, "sx", -1))
    wide, bias, weight_mask = call(
        weights_kernel,
        (conv_weight, conv_bias[None], weight_mask),
        [((12 * channels, 16 * channels), bf16), ((channels, depth), f32), plane],
        [],
        8,
        "weights",
    )
    grid_scratch = ((rows, cols + 2, channels, depth), bf16)
    inner_shape = (rows - 2, cols, channels, depth)
    edge_shape = (4, cols, channels, depth)
    side_shape = (5, channels, depth)
    side_hi, side_lo = call(
        sides_kernel,
        (y_lo, y_hi, bias),
        [(side_shape, bf16), (side_shape, bf16)],
        [],
        4,
        "sides",
    )
    side_lo, side_hi = (shift(side_hi, "sx", 1), shift(side_lo, "sx", -1))
    (inner,) = call(
        conv_inner_kernel,
        (features, y_lo, y_hi, weight_mask, wide, bias),
        [(inner_shape, bf16)],
        [grid_scratch],
        12,
        "conv_inner",
    )
    column = ((rows + 3, channels, depth), bf16)
    edge, f_hi, f_lo = call(
        conv_edge_kernel,
        (
            features,
            y_lo,
            y_hi,
            x_lo,
            x_hi,
            side_lo,
            side_hi,
            weight_mask,
            wide,
            bias,
            inner,
            residual,
            ridge,
        ),
        [(edge_shape, bf16), column, column],
        [grid_scratch, ((4, cols, depth), f32)],
        12,
        "conv_edge",
    )
    f_lo, f_hi = (shift(f_hi, "sy", 1), shift(f_lo, "sy", -1))
    (core,) = call(
        first_core_kernel,
        (inner, edge, residual, x_lo, x_hi, ridge),
        [plane],
        [((rows + 2, cols, channels, depth), f32), ((2, cols, depth), f32)],
        10,
        "first_core",
    )
    line = ((rows, depth), f32)
    row = ((cols + 2, depth), f32)
    first, w_lo, w_hi, r_hi, r_lo = call(
        first_rim_kernel,
        (inner, edge, f_lo, f_hi, y_lo, y_hi, x_lo, x_hi, side_lo, side_hi, residual, core),
        [plane, line, line, row, row],
        [],
        4,
        "first_rim",
    )
    r_lo, r_hi = (shift(r_hi, "sx", 1), shift(r_lo, "sx", -1))
    core, grams = call(
        second_core_kernel,
        (inner, edge, residual, first, ridge),
        [plane, ((2 * len(PRODUCTS), cols, depth), f32)],
        [((rows, cols, channels, depth), f32)],
        10,
        "second_core",
    )
    second, share = call(
        second_rim_kernel,
        (inner, edge, f_lo, f_hi, residual, first, w_lo, w_hi, r_lo, r_hi, core, grams),
        [plane, ((1, 128), f32)],
        [],
        4,
        "second_rim",
    )

    peers = lax.axis_size("sx") * lax.axis_size("sy")
    shares = lax.all_to_all(jnp.broadcast_to(share[None], (peers, 1, 128)), AXES, 0, 0)
    return tuple(
        call(
            final_kernel,
            (shares.reshape(peers, 128), residual, first, second),
            [plane, plane],
            [],
            8,
            "final",
        )
    )


def solution(mesh):
    placed = (
        P("sx", "sy", None, None),
        P(),
        P(),
        P("sx", "sy", None),
        P("sx", "sy", None, None),
        P("sx", "sy", None),
        P("sx", "sy", None),
    )
    return jax.shard_map(
        per_device,
        mesh=mesh,
        in_specs=placed,
        out_specs=(P("sx", "sy", None), P("sx", "sy", None)),
        check_vma=False,
    )
```

```python
import jax
import jax.numpy as jnp
from jax import lax
from jax.experimental import pallas as pl
from jax.experimental.pallas import tpu as pltpu
from jax.sharding import PartitionSpec as P

AXES = ("sx", "sy")
PREP_LIMIT = 58


def shift(value, axis, step):
    peers = lax.axis_size(axis)
    return lax.ppermute(value, axis, [(i, (i + step) % peers) for i in range(peers)])


def three(value):
    high = value.astype(jnp.bfloat16).astype(jnp.float32)
    rest = value - high
    mid = rest.astype(jnp.bfloat16).astype(jnp.float32)
    return high, mid, rest - mid


def paired(value):
    high, mid, low = three(value)
    return jnp.concatenate([high, mid], axis=0), jnp.concatenate([low, jnp.zeros_like(low)], axis=0)


def prep_kernel(
    own,
    ids_in,
    occupancy_in,
    target_in,
    mask_out,
    start_out,
    y_hi_out,
    y_lo_out,
    x_hi,
    x_lo,
    ids,
    occupancy,
    target,
    columns,
    present,
    message,
    mask,
    start,
    y_hi,
    y_lo,
    sems,
):
    rows, cols, channels, depth = own.shape
    half = present.shape[1]
    copies = [
        pltpu.make_async_copy(source, goal, sems.at[k])
        for k, (source, goal) in enumerate(
            (
                (ids_in, ids),
                (occupancy_in, occupancy),
                (target_in, target),
                (own.at[:, 0:1], columns.at[0]),
                (own.at[:, cols - 1 : cols], columns.at[1]),
                (own.at[rows - 2], message.at[0, 0:cols]),
                (own.at[rows - 1], message.at[0, cols : 2 * cols]),
                (own.at[0], message.at[1, 0:cols]),
                (own.at[1], message.at[1, cols : 2 * cols]),
                (message.at[0, 0 : 2 * cols], x_hi.at[0 : 2 * cols]),
                (message.at[1, 0 : 2 * cols], x_lo.at[0 : 2 * cols]),
                (message.at[0, 2 * cols :], x_hi.at[2 * cols :]),
                (message.at[1, 2 * cols :], x_lo.at[2 * cols :]),
                (mask, mask_out),
                (start, start_out),
                (y_lo, y_lo_out),
                (y_hi, y_hi_out),
            )
        )
    ]
    for copy in (*copies[5:9], *copies[:5]):
        copy.start()
    for k in range(2):
        copies[5 + 2 * k].wait()
        copies[6 + 2 * k].wait()
        copies[9 + k].start()
    copies[0].wait()
    copies[1].wait()
    present[...] = jnp.broadcast_to(
        jnp.where(ids[:, 13:14] >= 0, 1.0, 0.0).astype(jnp.float32), present.shape
    )
    for x in range(rows):
        blocks = [present[pl.ds(2 * cols * x + z, cols, stride=2), :] for z in range(depth // half)]
        mask[x] = occupancy[x].astype(jnp.float32) * jnp.concatenate(blocks, axis=1)
    copies[13].start()
    copies[2].wait()
    for x in range(rows):
        start[x] = mask[x] * target[x]
    copies[14].start()
    for k, (pair, row) in enumerate((((rows - 2, rows - 1), rows - 1), ((0, 1), 0))):
        pieces = (jnp.concatenate([mask[x] for x in pair], axis=0), *paired(start[row]))
        for at, piece in enumerate(pieces):
            message[k, 2 * cols + at] = piece.astype(jnp.bfloat16)
        copies[11 + k].start()
    copies[3].wait()
    copies[4].wait()
    blank = jnp.zeros((channels - 3 * rows, depth), jnp.float32)
    for k, (out, y) in enumerate(((y_lo, 0), (y_hi, cols - 1))):
        for x in range(rows):
            out[x] = columns[k, x, 0] * mask[x, y : y + 1, :].astype(jnp.bfloat16)
        terms = jnp.concatenate([*three(column_of(start, y)), blank], axis=0)
        out[rows] = terms.astype(jnp.bfloat16)
        copies[15 + k].start()
    for copy in copies[9:]:
        copy.wait()


def weights_kernel(taps, bias, mask, wide, bias_col, mask_out):
    mask_out[...] = mask[...]
    channels = taps.shape[1]
    width = 16 * channels
    row = lax.broadcasted_iota(jnp.int32, (channels, width), 0)
    lane = lax.broadcasted_iota(jnp.int32, (channels, width), 1)
    repeat = jnp.where(lane % channels == row, 1.0, 0.0).astype(jnp.bfloat16)
    group = lane // channels
    for z in range(3):
        every = [
            jnp.dot(taps[3 * k + z], repeat, preferred_element_type=jnp.float32) for k in range(9)
        ]
        for out_x in range(2):
            for out_y in range(2):
                total = jnp.zeros((channels, width), jnp.float32)
                for k in range(9):
                    at = (out_x + k // 3) * 4 + out_y + k % 3
                    total = jnp.where(group == at, every[k], total)
                start = ((z * 2 + out_x) * 2 + out_y) * channels
                wide[start : start + channels] = total.astype(jnp.bfloat16)
    square = (channels, channels)
    same = lax.broadcasted_iota(jnp.int32, square, 0) == lax.broadcasted_iota(jnp.int32, square, 1)
    column = jnp.sum(jnp.where(same, bias[...], 0.0), axis=1, keepdims=True)
    bias_col[...] = jnp.broadcast_to(column, bias_col.shape)


def mesh_flags():
    keep = []
    for axis in ("sy", "sx"):
        where = lax.axis_index(axis)
        keep += [where > 0, where < lax.axis_size(axis) - 1]
    return [jnp.where(k, 1.0, 0.0) for k in keep]


def conv_block(grid, masks, wide, bias_all, lane, grid_x, y, out, out_x):
    channels, depth = bias_all.shape
    window = jnp.concatenate(
        [grid[grid_x + k, y : y + 4].reshape(4 * channels, depth) for k in range(4)], axis=0
    )
    parts = jnp.dot(wide[...], window, preferred_element_type=jnp.float32)
    low = pltpu.roll(parts[0 : 4 * channels], 1, 1)
    high = pltpu.roll(parts[8 * channels :], depth - 1, 1)
    total = parts[4 * channels : 8 * channels]
    total = total + jnp.where(lane == 0, 0.0, low) + jnp.where(lane == depth - 1, 0.0, high)
    for step_x in range(2):
        for step_y in range(2):
            at = (step_x * 2 + step_y) * channels
            keep = masks[step_x](y + step_y)
            value = keep * (total[at : at + channels] + bias_all)
            out[out_x + step_x, y + step_y] = value.astype(jnp.bfloat16)


def splat(flag, shape):
    return jnp.full(shape, flag, jnp.float32).astype(jnp.bfloat16)


def fill_row(grid, grid_x, mask, middle, low, high):
    cols = grid.shape[1] - 2
    grid[grid_x, 0] = low
    for y in range(cols):
        grid[grid_x, y + 1] = middle(y) * mask(y).astype(jnp.bfloat16)
    grid[grid_x, cols + 1] = high


def fill_own(grid, grid_x, own, mask, y_lo, y_hi, flags, x):
    low = y_lo[x] * splat(flags[0], y_lo.shape[1:])
    high = y_hi[x] * splat(flags[1], y_hi.shape[1:])
    fill_row(grid, grid_x, mask_of(mask, x), lambda y: own[x, y], low, high)


def mask_of(mask, x):
    return lambda y: mask[x, y : y + 1, :]


def conv_inner_kernel(own, y_lo, y_hi, mask, wide, bias, out, grid):
    rows, cols, channels, depth = own.shape
    flags = mesh_flags()

    def fill(x, carry):
        fill_own(grid, x, own, mask, y_lo, y_hi, flags, x)
        return carry

    lax.fori_loop(0, rows, fill, 0)
    lane = lax.broadcasted_iota(jnp.int32, (4 * channels, depth), 1)
    bias_all = bias[...]

    def pair(i, carry):
        masks = (mask_of(mask, 2 * i + 1), mask_of(mask, 2 * i + 2))
        for y in range(0, cols, 2):
            conv_block(grid, masks, wide, bias_all, lane, 2 * i, y, out, 2 * i)
        return carry

    lax.fori_loop(0, rows // 2 - 1, pair, 0)


def sides_kernel(y_lo, y_hi, _, out_hi, out_lo):
    rows = y_lo.shape[0] - 1
    channels, depth = y_lo.shape[1:]
    clear = [splat(flag, y_lo.shape[1:]) for flag in mesh_flags()[:2]]
    sources = [ref[rows].astype(jnp.float32) for ref in (y_lo, y_hi)]
    for out, pair, row in ((out_hi, (rows - 2, rows - 1), rows - 1), (out_lo, (0, 1), 0)):
        for k, x in enumerate(pair):
            out[2 * k] = y_lo[x] * clear[0]
            out[2 * k + 1] = y_hi[x] * clear[1]
        rims = [
            terms[at : at + 1] for at in (row, rows + row, 2 * rows + row) for terms in sources
        ]
        blank = jnp.zeros((channels - 6, depth), jnp.float32)
        out[4] = jnp.concatenate([*rims, blank], axis=0).astype(jnp.bfloat16)


def conv_edge_kernel(
    own,
    y_lo,
    y_hi,
    x_lo,
    x_hi,
    side_lo,
    side_hi,
    mask,
    wide,
    bias,
    inner,
    start,
    ridge,
    out,
    out_hi,
    out_lo,
    grid,
    side_mask,
):
    rows, cols, channels, depth = own.shape
    flags = mesh_flags()
    for k, side in enumerate((x_lo, x_hi)):
        both = side[2 * cols].astype(jnp.float32) * flags[2 + k]
        side_mask[2 * k] = both[:cols]
        side_mask[2 * k + 1] = both[cols:]
    for x in range(2):
        for k, ref, side in ((0, x_lo, side_lo), (1, x_hi, side_hi)):
            clear = splat(flags[2 + k], (channels, depth))
            fill_row(
                grid,
                6 * k + x,
                mask_of(side_mask, 2 * k + x),
                lambda y: ref[x * cols + y],
                side[2 * x] * clear,
                side[2 * x + 1] * clear,
            )
        fill_own(grid, 2 + x, own, mask, y_lo, y_hi, flags, x)
        fill_own(grid, 4 + x, own, mask, y_lo, y_hi, flags, rows - 2 + x)
    lane = lax.broadcasted_iota(jnp.int32, (4 * channels, depth), 1)
    bias_all = bias[...]
    for side, masks in (
        (0, (mask_of(side_mask, 1), mask_of(mask, 0))),
        (1, (mask_of(mask, rows - 1), mask_of(side_mask, 2))),
    ):
        for y in range(0, cols, 2):
            conv_block(grid, masks, wide, bias_all, lane, 4 * side, y, out, 2 * side)
    lane = lanes((channels, depth))
    places = [field_at(inner, out, x) for x in range(rows + 2)]
    blank = jnp.zeros((channels - 3 * rows, depth), jnp.float32)
    for ref, y, beside in ((out_hi, cols - 1, cols - 2), (out_lo, 0, 1)):
        smooth = []
        for x, (field, at) in enumerate(places):
            ref[x] = field[at, y]
            near, next_in = (
                field[at, k].astype(jnp.float32) * start_at(start, x_lo, x_hi, x, k)
                for k in (y, beside)
            )
            smooth.append((near + near) + next_in)
        image = column_of(ridge, y) * column_of(start, y) + rim_rows(
            smooth, inner, out, y, lane, 1.0 / (8 * channels)
        )
        ref[rows + 2] = jnp.concatenate([*three(image), blank], axis=0).astype(jnp.bfloat16)


def two_sum(a, b):
    s = a + b
    t = s - a
    return s, (a - (s - t)) + (b - t)


def split(a):
    c = a * 4097.0
    high = c - (c - a)
    return high, a - high


def two_prod(a, b):
    p = a * b
    a_hi, a_lo = split(a)
    b_hi, b_lo = split(b)
    return p, ((a_hi * b_hi - p) + a_hi * b_lo + a_lo * b_hi) + a_lo * b_lo


def pair_add(a, b):
    s, t = two_sum(a[0], b[0])
    return two_sum(s, t + (a[1] + b[1]))


def pair_scale(a, c):
    p, t = two_prod(a[0], c)
    return two_sum(p, t + a[1] * c)


def field_at(inner, edge, x):
    n = inner.shape[0]
    if x < 2:
        return edge, x
    return (inner, x - 2) if x < n + 2 else (edge, x - n)


def along_y(smooth, dst, field, row, value_at):
    cols = smooth.shape[1]

    def product(y):
        return field[row, y].astype(jnp.float32) * value_at(y)

    here = product(0)
    pair = here
    for y in range(cols):
        if y + 1 < cols:
            following = product(y + 1)
            pair_next = here + following
        else:
            pair_next = here
            following = here
        smooth[dst, y] = pair + pair_next
        here = following
        pair = pair_next


def row_of(ref, x):
    return lambda y: ref[x, y : y + 1, :]


def close_column(both, lane, field):
    depth = both.shape[1]
    up = jnp.where(lane == depth - 1, 0.0, pltpu.roll(both, depth - 1, 1))
    down = jnp.where(lane == 0, 0.0, pltpu.roll(both, 1, 1))
    prod = ((both + both) + (up + down)) * field.astype(jnp.float32)
    return jnp.sum(prod, axis=0, keepdims=True)


def lanes(shape):
    return lax.broadcasted_iota(jnp.int32, shape, 1)


def along_x(smooth, x, ends, field, row, scale):
    cols, channels, depth = smooth.shape[1:]
    lane = lanes((channels, depth))
    sums = []
    for y in range(cols):
        mid = smooth[x, y]
        low = (smooth[x - 1, y] + mid) if ends[0] else mid
        high = (mid + smooth[x + 1, y]) if ends[1] else mid
        sums.append(close_column(low + high, lane, field[row, y]))
    return jnp.concatenate(sums, axis=0) * scale


def first_core_kernel(inner, edge, start, x_lo, x_hi, ridge, out, smooth, side_start):
    n, cols, channels, depth = inner.shape
    scale = 1.0 / (8 * channels)
    for k, side in enumerate((x_lo, x_hi)):
        upper = side[2 * cols + 1].astype(jnp.float32)
        lower = side[2 * cols + 2].astype(jnp.float32)
        side_start[k] = (upper[:cols] + upper[cols:]) + lower[:cols]
    along_y(smooth, 0, edge, 0, row_of(side_start, 0))
    along_y(smooth, 1, edge, 1, row_of(start, 0))
    along_y(smooth, n + 2, edge, 2, row_of(start, n + 1))
    along_y(smooth, n + 3, edge, 3, row_of(side_start, 1))

    def stage_y(k, carry):
        along_y(smooth, k + 2, inner, k, row_of(start, k + 1))
        return carry

    lax.fori_loop(0, n, stage_y, 0)

    def stage_x(k, carry):
        image = along_x(smooth, k + 2, (True, True), inner, k, scale)
        out[k + 1] = ridge[k + 1] * start[k + 1] + image
        return carry

    lax.fori_loop(0, n, stage_x, 0)
    for x, row in ((0, 1), (n + 1, 2)):
        image = along_x(smooth, x + 1, (True, True), edge, row, scale)
        out[x] = ridge[x] * start[x] + image


def rim_rows(g, inner, edge, y, lane, scale):
    sums = []
    for x in range(inner.shape[0] + 2):
        low, mid, high = g[x : x + 3]
        both = mid + mid
        both = both if low is None else both + low
        both = both if high is None else both + high
        at = field_at(inner, edge, x + 1)
        sums.append(close_column(both, lane, at[0][at[1], y]))
    return jnp.concatenate(sums, axis=0) * scale


def column_of(ref, y):
    return jnp.concatenate([ref[x, y : y + 1, :] for x in range(ref.shape[0])], axis=0)


def start_at(start, x_lo, x_hi, x, y):
    rows, cols = start.shape[:2]
    if 0 < x <= rows:
        return start[x - 1, y : y + 1, :]
    side = x_lo if x == 0 else x_hi
    upper = side[2 * cols + 1].astype(jnp.float32)
    lower = side[2 * cols + 2].astype(jnp.float32)
    return (upper[y : y + 1] + upper[cols + y : cols + y + 1]) + lower[y : y + 1]


def joined(terms, count, step):
    return (terms[:count] + terms[step : step + count]) + terms[2 * step : 2 * step + count]


def first_rim_kernel(
    inner,
    edge,
    f_lo,
    f_hi,
    y_lo,
    y_hi,
    x_lo,
    x_hi,
    side_lo,
    side_hi,
    start,
    core,
    out,
    w_lo,
    w_hi,
    out_hi,
    out_lo,
):
    n, cols, channels, depth = inner.shape
    rows = n + 2
    scale = 1.0 / (8 * channels)
    lane = lanes((channels, depth))
    out[...] = core[...]
    corners = [joined(side[4].astype(jnp.float32), 2, 2) for side in (side_lo, side_hi)]
    for k, (ref, rim, keep, flag, y) in enumerate(
        zip((f_lo, f_hi), (y_lo, y_hi), (w_lo, w_hi), mesh_flags(), (0, cols - 1))
    ):
        near = joined(rim[rows].astype(jnp.float32), rows, rows)
        values = [corners[0][k : k + 1], *(near[x : x + 1] for x in range(rows)), corners[1][k : k + 1]]
        beyond = [ref[x] for x in range(rows + 2)]
        g = [field.astype(jnp.float32) * (value * flag) for field, value in zip(beyond, values)]
        column = column_of(core, y) + rim_rows(g, inner, edge, y, lane, scale)
        g = [
            at[0][at[1], y].astype(jnp.float32) * start_at(start, x_lo, x_hi, x, y)
            for x, at in enumerate(field_at(inner, edge, x) for x in range(rows + 2))
        ]
        image = [
            close_column((g[x] + g[x + 1]) + (g[x + 1] + g[x + 2]), lane, beyond[x + 1])
            for x in range(rows)
        ]
        theirs = joined(ref[rows + 2].astype(jnp.float32), rows, rows)
        keep[...] = (theirs + jnp.concatenate(image, axis=0) * scale) * flag
        for x in range(rows):
            out[x, y : y + 1, :] = column[x : x + 1]
    for ref, x in ((out_hi, rows - 1), (out_lo, 0)):
        ref[0:1] = w_lo[x : x + 1]
        ref[1 : 1 + cols] = out[x]
        ref[1 + cols : 2 + cols] = w_hi[x : x + 1]


PRODUCTS = ((0, 0), (0, 1), (1, 1), (0, 2), (1, 2))


def add_products(sums, which, fields):
    for k in which:
        a, b = PRODUCTS[k]
        p, e = two_prod(fields[a], fields[b])
        s, t = two_sum(sums[k][0], p)
        sums[k] = (s, sums[k][1] + (t + e))


def second_core_kernel(
    inner, edge, f_lo, f_hi, start, first, w_lo, w_hi, ridge, out, grams, smooth
):
    n, cols, channels, depth = inner.shape
    scale = 1.0 / (8 * channels)

    def stage_y(k, carry):
        along_y(smooth, k + 1, inner, k, row_of(first, k + 1))
        return carry

    lax.fori_loop(0, n, stage_y, 0)
    along_y(smooth, 0, edge, 1, row_of(first, 0))
    along_y(smooth, n + 1, edge, 2, row_of(first, n + 1))

    def stage_x(k, carry):
        image = along_x(smooth, k + 1, (True, True), inner, k, scale)
        out[k + 1] = ridge[k + 1] * first[k + 1] + image
        return carry

    lax.fori_loop(0, n, stage_x, 0)
    for x, row, ends in ((0, 1, (False, True)), (n + 1, 2, (True, False))):
        out[x] = ridge[x] * first[x] + along_x(smooth, x, ends, edge, row, scale)
    zero = jnp.zeros((cols, depth), jnp.float32)
    sums = [(zero, zero) for _ in PRODUCTS]
    for x in range(n + 2):
        add_products(sums, range(5), (start[x], first[x], out[x]))
    rows = n + 2
    lane = lanes((channels, depth))
    flags = mesh_flags()
    added = []
    for ref, rim, flag, y in ((f_lo, w_lo, flags[0], 0), (f_hi, w_hi, flags[1], cols - 1)):
        g = [ref[x + 1].astype(jnp.float32) * (rim[x : x + 1] * flag) for x in range(rows)]
        added.append(rim_rows([None, *g, None], inner, edge, y, lane, scale))
    columns = [jnp.concatenate([column_of(ref, y) for y in (0, cols - 1)]) for ref in (start, first)]
    add_products(sums, (3, 4), (*columns, jnp.concatenate(added, axis=0)))
    for delta, y in zip(added, (0, cols - 1)):
        for x in range(rows):
            out[x, y : y + 1, :] = out[x, y : y + 1, :] + delta[x : x + 1]
    for k, (s, e) in enumerate(sums):
        grams[2 * k] = s
        grams[2 * k + 1] = e


def second_rim_kernel(
    edge, f_lo, f_hi, start, first, x_lo, x_hi, core, grams, out, share
):
    rows, cols, depth = start.shape
    channels = edge.shape[2]
    scale = 1.0 / (8 * channels)
    lane = lanes((channels, depth))
    flags = mesh_flags()
    out[...] = core[...]
    sums = [(grams[2 * k], grams[2 * k + 1]) for k in range(5)]
    for rim, at, row, x, far in ((x_lo, 0, 1, 0, 0), (x_hi, 3, 2, rows - 1, rows + 1)):

        def product(y):
            value = rim[y : y + 1]
            if y == 0:
                return f_lo[far].astype(jnp.float32) * (value * flags[0])
            if y == cols + 1:
                return f_hi[far].astype(jnp.float32) * (value * flags[1])
            return edge[at, y - 1].astype(jnp.float32) * value

        parts = []
        here = product(1)
        pair = product(0) + here
        for y in range(cols):
            following = product(y + 2)
            pair_next = here + following
            parts.append(close_column(pair + pair_next, lane, edge[row, y]))
            here = following
            pair = pair_next
        delta = jnp.concatenate(parts, axis=0) * scale
        add_products(sums, (3, 4), (start[x], first[x], delta))
        out[x] = out[x] + delta
    lane = lanes((8, 128))
    line = lax.broadcasted_iota(jnp.int32, (8, 128), 0)

    def fold(s, e, axis, steps):
        for step in steps:
            t, d = two_sum(s, pltpu.roll(s, step, axis))
            s, e = (t, (e + pltpu.roll(e, step, axis)) + d)
        return s, e

    total = jnp.zeros((8, 128), jnp.float32)
    error = jnp.zeros((8, 128), jnp.float32)
    for k, (s, e) in enumerate(sums):
        while s.shape[0] > 8:
            half = s.shape[0] // 2
            t, d = two_sum(s[:half], s[half:])
            s, e = (t, e[:half] + e[half:] + d)
        while s.shape[1] > 128:
            half = s.shape[1] // 2
            t, d = two_sum(s[:, :half], s[:, half:])
            s, e = (t, e[:, :half] + e[:, half:] + d)
        s, e = fold(s, e, 0, (4, 2, 1))
        total = jnp.where(line == k, s, total)
        error = jnp.where(line == k, e, error)
    total, error = fold(total, error, 1, (64, 32, 16, 8, 4, 2, 1))
    placed = jnp.where(lane == line, total, 0.0) + jnp.where(lane == line + 8, error, 0.0)
    share[...] = jnp.sum(placed, axis=0, keepdims=True)


def final_kernel(shares, start, first, second, solution_out, residual_out):
    s = shares[...]
    e = jnp.zeros_like(s)
    while s.shape[0] > 8:
        half = s.shape[0] // 2
        t, d = two_sum(s[:half], s[half:])
        s, e = (t, e[:half] + e[half:] + d)
    for step in (4, 2, 1):
        t, d = two_sum(s, pltpu.roll(s, step, 0))
        s, e = (t, (e + pltpu.roll(e, step, 0)) + d)
    lane = lax.broadcasted_iota(jnp.int32, s.shape, 1)

    def pick(value, k):
        return jnp.broadcast_to(
            jnp.sum(jnp.where(lane == k, value, 0.0), axis=1, keepdims=True), s.shape
        )

    g00, g01, g11, g02, g12 = [
        two_sum(pick(s, k), pick(e, k) + pick(s, 8 + k)) for k in range(5)
    ]
    alpha = g00[0] / g01[0]
    fresh = pair_add(pair_add(g00, pair_scale(g01, -2.0 * alpha)), pair_scale(pair_scale(g11, alpha), alpha))
    grow = 1.0 + fresh[0] / g00[0]
    curve = pair_add(
        pair_add(
            pair_scale(pair_scale(g01, grow), grow),
            pair_scale(pair_scale(pair_add(g02, g11), -alpha), grow),
        ),
        pair_scale(pair_scale(g12, alpha), alpha),
    )
    beta = fresh[0] / curve[0]
    near = (alpha + beta * grow)[0:1, 0:1]
    far = (alpha * beta)[0:1, 0:1]
    for x in range(start.shape[0]):
        w0, w1, w2 = (start[x], first[x], second[x])
        solution_out[x] = near * w0 - far * w1
        residual_out[x] = (w0 - near * w1) + far * w2


def per_device(features, conv_weight, conv_bias, occupancy, block_ids, ridge, target):
    rows, cols, channels, depth = features.shape
    f32, bf16 = (jnp.float32, jnp.bfloat16)
    vmem = pl.BlockSpec(memory_space=pltpu.VMEM)

    def call(kernel, args, outs, scratch, limit, name):
        return pl.pallas_call(
            kernel,
            out_shape=[jax.ShapeDtypeStruct(shape, dtype) for shape, dtype in outs],
            in_specs=[vmem for _ in args],
            out_specs=[vmem for _ in outs],
            scratch_shapes=[pltpu.VMEM(shape, dtype) for shape, dtype in scratch],
            compiler_params=pltpu.CompilerParams(vmem_limit_bytes=limit << 20),
            name=name,
        )(*args)

    plane = ((rows, cols, depth), f32)
    blocks = block_ids.reshape(-1, block_ids.shape[3])
    edge_column = ((rows + 1, channels, depth), bf16)
    edge_rows = ((2 * cols + 3, channels, depth), bf16)
    outs = [plane, plane, edge_column, edge_column, edge_rows, edge_rows]
    weight_mask, residual, y_hi, y_lo, x_hi, x_lo = pl.pallas_call(
        prep_kernel,
        out_shape=[jax.ShapeDtypeStruct(shape, dtype) for shape, dtype in outs],
        in_specs=[pl.BlockSpec(memory_space=pl.ANY)] * 4,
        out_specs=[pl.BlockSpec(memory_space=pl.ANY)] * 6,
        scratch_shapes=[
            pltpu.VMEM(blocks.shape, jnp.int32),
            pltpu.VMEM(occupancy.shape, jnp.int32),
            pltpu.VMEM(target.shape, f32),
            pltpu.VMEM((2, rows, 1, channels, depth), bf16),
            pltpu.VMEM((blocks.shape[0], depth // block_ids.shape[2]), f32),
            pltpu.VMEM((2, *edge_rows[0]), bf16),
            *(pltpu.VMEM(shape, dtype) for shape, dtype in outs[:4]),
            pltpu.SemaphoreType.DMA((17,)),
        ],
        compiler_params=pltpu.CompilerParams(vmem_limit_bytes=PREP_LIMIT << 20),
        name="prep",
    )(features, blocks, occupancy, target)
    y_lo, y_hi = (shift(y_hi, "sy", 1), shift(y_lo, "sy", -1))
    x_lo, x_hi = (shift(x_hi, "sx", 1), shift(x_lo, "sx", -1))
    wide, bias, weight_mask = call(
        weights_kernel,
        (conv_weight, conv_bias[None], weight_mask),
        [((12 * channels, 16 * channels), bf16), ((channels, depth), f32), plane],
        [],
        8,
        "weights",
    )
    grid_scratch = ((rows, cols + 2, channels, depth), bf16)
    inner_shape = (rows - 2, cols, channels, depth)
    edge_shape = (4, cols, channels, depth)
    side_shape = (5, channels, depth)
    side_hi, side_lo = call(
        sides_kernel,
        (y_lo, y_hi, bias),
        [(side_shape, bf16), (side_shape, bf16)],
        [],
        4,
        "sides",
    )
    side_lo, side_hi = (shift(side_hi, "sx", 1), shift(side_lo, "sx", -1))
    (inner,) = call(
        conv_inner_kernel,
        (features, y_lo, y_hi, weight_mask, wide, bias),
        [(inner_shape, bf16)],
        [grid_scratch],
        12,
        "conv_inner",
    )
    column = ((rows + 3, channels, depth), bf16)
    edge, f_hi, f_lo = call(
        conv_edge_kernel,
        (
            features,
            y_lo,
            y_hi,
            x_lo,
            x_hi,
            side_lo,
            side_hi,
            weight_mask,
            wide,
            bias,
            inner,
            residual,
            ridge,
        ),
        [(edge_shape, bf16), column, column],
        [grid_scratch, ((4, cols, depth), f32)],
        12,
        "conv_edge",
    )
    f_lo, f_hi = (shift(f_hi, "sy", 1), shift(f_lo, "sy", -1))
    (core,) = call(
        first_core_kernel,
        (inner, edge, residual, x_lo, x_hi, ridge),
        [plane],
        [((rows + 2, cols, channels, depth), f32), ((2, cols, depth), f32)],
        10,
        "first_core",
    )
    line = ((rows, depth), f32)
    row = ((cols + 2, depth), f32)
    first, w_lo, w_hi, r_hi, r_lo = call(
        first_rim_kernel,
        (inner, edge, f_lo, f_hi, y_lo, y_hi, x_lo, x_hi, side_lo, side_hi, residual, core),
        [plane, line, line, row, row],
        [],
        4,
        "first_rim",
    )
    r_lo, r_hi = (shift(r_hi, "sx", 1), shift(r_lo, "sx", -1))
    core, grams = call(
        second_core_kernel,
        (inner, edge, f_lo, f_hi, residual, first, w_lo, w_hi, ridge),
        [plane, ((2 * len(PRODUCTS), cols, depth), f32)],
        [((rows, cols, channels, depth), f32)],
        10,
        "second_core",
    )
    second, share = call(
        second_rim_kernel,
        (edge, f_lo, f_hi, residual, first, r_lo, r_hi, core, grams),
        [plane, ((1, 128), f32)],
        [],
        4,
        "second_rim",
    )

    peers = lax.axis_size("sx") * lax.axis_size("sy")
    shares = lax.all_to_all(jnp.broadcast_to(share[None], (peers, 1, 128)), AXES, 0, 0)
    return tuple(
        call(
            final_kernel,
            (shares.reshape(peers, 128), residual, first, second),
            [plane, plane],
            [],
            8,
            "final",
        )
    )


def solution(mesh):
    placed = (
        P("sx", "sy", None, None),
        P(),
        P(),
        P("sx", "sy", None),
        P("sx", "sy", None, None),
        P("sx", "sy", None),
        P("sx", "sy", None),
    )
    return jax.shard_map(
        per_device,
        mesh=mesh,
        in_specs=placed,
        out_specs=(P("sx", "sy", None), P("sx", "sy", None)),
        check_vma=False,
    )
```

```python
import jax
import jax.numpy as jnp
from jax import lax
from jax.experimental import pallas as pl
from jax.experimental.pallas import tpu as pltpu
from jax.sharding import PartitionSpec as P

AXES = ("sx", "sy")
PREP_LIMIT = 58


def shift(value, axis, step):
    peers = lax.axis_size(axis)
    return lax.ppermute(value, axis, [(i, (i + step) % peers) for i in range(peers)])


def three(value):
    high = value.astype(jnp.bfloat16).astype(jnp.float32)
    rest = value - high
    mid = rest.astype(jnp.bfloat16).astype(jnp.float32)
    return high, mid, rest - mid


def paired(value):
    high, mid, low = three(value)
    return jnp.concatenate([high, mid], axis=0), jnp.concatenate([low, jnp.zeros_like(low)], axis=0)


def prep_kernel(
    own,
    ids_in,
    occupancy_in,
    target_in,
    mask_out,
    start_out,
    y_hi_out,
    y_lo_out,
    x_hi,
    x_lo,
    ids,
    occupancy,
    target,
    columns,
    present,
    message,
    mask,
    start,
    y_hi,
    y_lo,
    sems,
):
    rows, cols, channels, depth = own.shape
    half = present.shape[1]
    copies = [
        pltpu.make_async_copy(source, goal, sems.at[k])
        for k, (source, goal) in enumerate(
            (
                (ids_in, ids),
                (occupancy_in, occupancy),
                (target_in, target),
                (own.at[:, 0:1], columns.at[0]),
                (own.at[:, cols - 1 : cols], columns.at[1]),
                (own.at[rows - 2], message.at[0, 0:cols]),
                (own.at[rows - 1], message.at[0, cols : 2 * cols]),
                (own.at[0], message.at[1, 0:cols]),
                (own.at[1], message.at[1, cols : 2 * cols]),
                (message.at[0, 0 : 2 * cols], x_hi.at[0 : 2 * cols]),
                (message.at[1, 0 : 2 * cols], x_lo.at[0 : 2 * cols]),
                (message.at[0, 2 * cols :], x_hi.at[2 * cols :]),
                (message.at[1, 2 * cols :], x_lo.at[2 * cols :]),
                (mask, mask_out),
                (start, start_out),
                (y_lo, y_lo_out),
                (y_hi, y_hi_out),
            )
        )
    ]
    for copy in (*copies[5:9], *copies[:5]):
        copy.start()
    for k in range(2):
        copies[5 + 2 * k].wait()
        copies[6 + 2 * k].wait()
        copies[9 + k].start()
    copies[0].wait()
    copies[1].wait()
    present[...] = jnp.broadcast_to(
        jnp.where(ids[:, 13:14] >= 0, 1.0, 0.0).astype(jnp.float32), present.shape
    )
    for x in range(rows):
        blocks = [present[pl.ds(2 * cols * x + z, cols, stride=2), :] for z in range(depth // half)]
        mask[x] = occupancy[x].astype(jnp.float32) * jnp.concatenate(blocks, axis=1)
    copies[13].start()
    copies[2].wait()
    for x in range(rows):
        start[x] = mask[x] * target[x]
    copies[14].start()
    for k, (pair, row) in enumerate((((rows - 2, rows - 1), rows - 1), ((0, 1), 0))):
        pieces = (jnp.concatenate([mask[x] for x in pair], axis=0), *paired(start[row]))
        for at, piece in enumerate(pieces):
            message[k, 2 * cols + at] = piece.astype(jnp.bfloat16)
        copies[11 + k].start()
    copies[3].wait()
    copies[4].wait()
    blank = jnp.zeros((channels - 3 * rows, depth), jnp.float32)
    for k, (out, y) in enumerate(((y_lo, 0), (y_hi, cols - 1))):
        for x in range(rows):
            out[x] = columns[k, x, 0] * mask[x, y : y + 1, :].astype(jnp.bfloat16)
        terms = jnp.concatenate([*three(column_of(start, y)), blank], axis=0)
        out[rows] = terms.astype(jnp.bfloat16)
        copies[15 + k].start()
    for copy in copies[9:]:
        copy.wait()


def weights_kernel(taps, bias, mask, wide, bias_col, mask_out):
    mask_out[...] = mask[...]
    channels = taps.shape[1]
    width = 16 * channels
    row = lax.broadcasted_iota(jnp.int32, (channels, width), 0)
    lane = lax.broadcasted_iota(jnp.int32, (channels, width), 1)
    repeat = jnp.where(lane % channels == row, 1.0, 0.0).astype(jnp.bfloat16)
    group = lane // channels
    for z in range(3):
        every = [
            jnp.dot(taps[3 * k + z], repeat, preferred_element_type=jnp.float32) for k in range(9)
        ]
        for out_x in range(2):
            for out_y in range(2):
                total = jnp.zeros((channels, width), jnp.float32)
                for k in range(9):
                    at = (out_x + k // 3) * 4 + out_y + k % 3
                    total = jnp.where(group == at, every[k], total)
                start = ((z * 2 + out_x) * 2 + out_y) * channels
                wide[start : start + channels] = total.astype(jnp.bfloat16)
    square = (channels, channels)
    same = lax.broadcasted_iota(jnp.int32, square, 0) == lax.broadcasted_iota(jnp.int32, square, 1)
    column = jnp.sum(jnp.where(same, bias[...], 0.0), axis=1, keepdims=True)
    bias_col[...] = jnp.broadcast_to(column, bias_col.shape)


def mesh_flags():
    keep = []
    for axis in ("sy", "sx"):
        where = lax.axis_index(axis)
        keep += [where > 0, where < lax.axis_size(axis) - 1]
    return [jnp.where(k, 1.0, 0.0) for k in keep]


def conv_block(window_rows, masks, wide, bias_all, lane, y, out, out_x):
    channels, depth = bias_all.shape
    window = jnp.concatenate(
        [ref[x, y : y + 4].reshape(4 * channels, depth) for ref, x in window_rows], axis=0
    )
    parts = jnp.dot(wide[...], window, preferred_element_type=jnp.float32)
    low = pltpu.roll(parts[0 : 4 * channels], 1, 1)
    high = pltpu.roll(parts[8 * channels :], depth - 1, 1)
    total = parts[4 * channels : 8 * channels]
    total = total + jnp.where(lane == 0, 0.0, low) + jnp.where(lane == depth - 1, 0.0, high)
    for step_x in range(2):
        for step_y in range(2):
            at = (step_x * 2 + step_y) * channels
            keep = masks[step_x](y + step_y)
            value = keep * (total[at : at + channels] + bias_all)
            out[out_x + step_x, y + step_y] = value.astype(jnp.bfloat16)


def splat(flag, shape):
    return jnp.full(shape, flag, jnp.float32).astype(jnp.bfloat16)


def fill_row(grid, grid_x, mask, middle, low, high):
    cols = grid.shape[1] - 2
    grid[grid_x, 0] = low
    for y in range(cols):
        grid[grid_x, y + 1] = middle(y) * mask(y).astype(jnp.bfloat16)
    grid[grid_x, cols + 1] = high


def fill_own(grid, grid_x, own, mask, y_lo, y_hi, flags, x):
    low = y_lo[x] * splat(flags[0], y_lo.shape[1:])
    high = y_hi[x] * splat(flags[1], y_hi.shape[1:])
    fill_row(grid, grid_x, mask_of(mask, x), lambda y: own[x, y], low, high)


def mask_of(mask, x):
    return lambda y: mask[x, y : y + 1, :]


def conv_inner_kernel(own, y_lo, y_hi, mask, wide, bias, out, kept, grid):
    rows, cols, channels, depth = own.shape
    flags = mesh_flags()

    def fill(x, carry):
        fill_own(grid, x, own, mask, y_lo, y_hi, flags, x)
        return carry

    lax.fori_loop(0, rows, fill, 0)
    for k, x in enumerate((0, 1, rows - 2, rows - 1)):
        kept[k] = grid[x]
    lane = lax.broadcasted_iota(jnp.int32, (4 * channels, depth), 1)
    bias_all = bias[...]

    def pair(i, carry):
        masks = (mask_of(mask, 2 * i + 1), mask_of(mask, 2 * i + 2))
        for y in range(0, cols, 2):
            window_rows = [(grid, 2 * i + k) for k in range(4)]
            conv_block(window_rows, masks, wide, bias_all, lane, y, out, 2 * i)
        return carry

    lax.fori_loop(0, rows // 2 - 1, pair, 0)


def sides_kernel(y_lo, y_hi, _, out_hi, out_lo):
    rows = y_lo.shape[0] - 1
    channels, depth = y_lo.shape[1:]
    clear = [splat(flag, y_lo.shape[1:]) for flag in mesh_flags()[:2]]
    sources = [ref[rows].astype(jnp.float32) for ref in (y_lo, y_hi)]
    for out, pair, row in ((out_hi, (rows - 2, rows - 1), rows - 1), (out_lo, (0, 1), 0)):
        for k, x in enumerate(pair):
            out[2 * k] = y_lo[x] * clear[0]
            out[2 * k + 1] = y_hi[x] * clear[1]
        rims = [
            terms[at : at + 1] for at in (row, rows + row, 2 * rows + row) for terms in sources
        ]
        blank = jnp.zeros((channels - 6, depth), jnp.float32)
        out[4] = jnp.concatenate([*rims, blank], axis=0).astype(jnp.bfloat16)


def conv_edge_kernel(
    kept,
    x_lo,
    x_hi,
    side_lo,
    side_hi,
    mask,
    wide,
    bias,
    inner,
    start,
    ridge,
    out,
    out_hi,
    out_lo,
    grid,
    side_mask,
):
    rows, cols, depth = mask.shape
    channels = kept.shape[2]
    flags = mesh_flags()
    for k, side in enumerate((x_lo, x_hi)):
        both = side[2 * cols].astype(jnp.float32) * flags[2 + k]
        side_mask[2 * k] = both[:cols]
        side_mask[2 * k + 1] = both[cols:]
    for x in range(2):
        for k, ref, side in ((0, x_lo, side_lo), (1, x_hi, side_hi)):
            clear = splat(flags[2 + k], (channels, depth))
            fill_row(
                grid,
                2 * k + x,
                mask_of(side_mask, 2 * k + x),
                lambda y: ref[x * cols + y],
                side[2 * x] * clear,
                side[2 * x + 1] * clear,
            )
    lane = lax.broadcasted_iota(jnp.int32, (4 * channels, depth), 1)
    bias_all = bias[...]
    for side, masks in (
        (0, (mask_of(side_mask, 1), mask_of(mask, 0))),
        (1, (mask_of(mask, rows - 1), mask_of(side_mask, 2))),
    ):
        for y in range(0, cols, 2):
            pairs = (grid, kept) if side == 0 else (kept, grid)
            window_rows = [(ref, 2 * side + k) for ref in pairs for k in range(2)]
            conv_block(window_rows, masks, wide, bias_all, lane, y, out, 2 * side)
    lane = lanes((channels, depth))
    places = [field_at(inner, out, x) for x in range(rows + 2)]
    blank = jnp.zeros((channels - 3 * rows, depth), jnp.float32)
    for ref, y, beside in ((out_hi, cols - 1, cols - 2), (out_lo, 0, 1)):
        smooth = []
        for x, (field, at) in enumerate(places):
            ref[x] = field[at, y]
            near, next_in = (
                field[at, k].astype(jnp.float32) * start_at(start, x_lo, x_hi, x, k)
                for k in (y, beside)
            )
            smooth.append((near + near) + next_in)
        image = column_of(ridge, y) * column_of(start, y) + rim_rows(
            smooth, inner, out, y, lane, 1.0 / (8 * channels)
        )
        ref[rows + 2] = jnp.concatenate([*three(image), blank], axis=0).astype(jnp.bfloat16)


def two_sum(a, b):
    s = a + b
    t = s - a
    return s, (a - (s - t)) + (b - t)


def split(a):
    c = a * 4097.0
    high = c - (c - a)
    return high, a - high


def two_prod(a, b):
    p = a * b
    a_hi, a_lo = split(a)
    b_hi, b_lo = split(b)
    return p, ((a_hi * b_hi - p) + a_hi * b_lo + a_lo * b_hi) + a_lo * b_lo


def pair_add(a, b):
    s, t = two_sum(a[0], b[0])
    return two_sum(s, t + (a[1] + b[1]))


def pair_scale(a, c):
    p, t = two_prod(a[0], c)
    return two_sum(p, t + a[1] * c)


def field_at(inner, edge, x):
    n = inner.shape[0]
    if x < 2:
        return edge, x
    return (inner, x - 2) if x < n + 2 else (edge, x - n)


def along_y(smooth, dst, field, row, value_at):
    cols = smooth.shape[1]

    def product(y):
        return field[row, y].astype(jnp.float32) * value_at(y)

    here = product(0)
    pair = here
    for y in range(cols):
        if y + 1 < cols:
            following = product(y + 1)
            pair_next = here + following
        else:
            pair_next = here
            following = here
        smooth[dst, y] = pair + pair_next
        here = following
        pair = pair_next


def row_of(ref, x):
    return lambda y: ref[x, y : y + 1, :]


def close_column(both, lane, field):
    depth = both.shape[1]
    up = jnp.where(lane == depth - 1, 0.0, pltpu.roll(both, depth - 1, 1))
    down = jnp.where(lane == 0, 0.0, pltpu.roll(both, 1, 1))
    prod = ((both + both) + (up + down)) * field.astype(jnp.float32)
    return jnp.sum(prod, axis=0, keepdims=True)


def lanes(shape):
    return lax.broadcasted_iota(jnp.int32, shape, 1)


def along_x(smooth, x, ends, field, row, scale):
    cols, channels, depth = smooth.shape[1:]
    lane = lanes((channels, depth))
    sums = []
    for y in range(cols):
        mid = smooth[x, y]
        low = (smooth[x - 1, y] + mid) if ends[0] else mid
        high = (mid + smooth[x + 1, y]) if ends[1] else mid
        sums.append(close_column(low + high, lane, field[row, y]))
    return jnp.concatenate(sums, axis=0) * scale


def first_core_kernel(inner, edge, start, x_lo, x_hi, ridge, out, smooth, side_start):
    n, cols, channels, depth = inner.shape
    scale = 1.0 / (8 * channels)
    for k, side in enumerate((x_lo, x_hi)):
        upper = side[2 * cols + 1].astype(jnp.float32)
        lower = side[2 * cols + 2].astype(jnp.float32)
        side_start[k] = (upper[:cols] + upper[cols:]) + lower[:cols]
    along_y(smooth, 0, edge, 0, row_of(side_start, 0))
    along_y(smooth, 1, edge, 1, row_of(start, 0))
    along_y(smooth, n + 2, edge, 2, row_of(start, n + 1))
    along_y(smooth, n + 3, edge, 3, row_of(side_start, 1))

    def stage_y(k, carry):
        along_y(smooth, k + 2, inner, k, row_of(start, k + 1))
        return carry

    lax.fori_loop(0, n, stage_y, 0)

    def stage_x(k, carry):
        image = along_x(smooth, k + 2, (True, True), inner, k, scale)
        out[k + 1] = ridge[k + 1] * start[k + 1] + image
        return carry

    lax.fori_loop(0, n, stage_x, 0)
    for x, row in ((0, 1), (n + 1, 2)):
        image = along_x(smooth, x + 1, (True, True), edge, row, scale)
        out[x] = ridge[x] * start[x] + image


def rim_rows(g, inner, edge, y, lane, scale):
    sums = []
    for x in range(inner.shape[0] + 2):
        low, mid, high = g[x : x + 3]
        both = mid + mid
        both = both if low is None else both + low
        both = both if high is None else both + high
        at = field_at(inner, edge, x + 1)
        sums.append(close_column(both, lane, at[0][at[1], y]))
    return jnp.concatenate(sums, axis=0) * scale


def column_of(ref, y):
    return jnp.concatenate([ref[x, y : y + 1, :] for x in range(ref.shape[0])], axis=0)


def start_at(start, x_lo, x_hi, x, y):
    rows, cols = start.shape[:2]
    if 0 < x <= rows:
        return start[x - 1, y : y + 1, :]
    side = x_lo if x == 0 else x_hi
    upper = side[2 * cols + 1].astype(jnp.float32)
    lower = side[2 * cols + 2].astype(jnp.float32)
    return (upper[y : y + 1] + upper[cols + y : cols + y + 1]) + lower[y : y + 1]


def joined(terms, count, step):
    return (terms[:count] + terms[step : step + count]) + terms[2 * step : 2 * step + count]


def first_rim_kernel(
    inner,
    edge,
    f_lo,
    f_hi,
    y_lo,
    y_hi,
    x_lo,
    x_hi,
    side_lo,
    side_hi,
    start,
    core,
    out,
    w_lo,
    w_hi,
    out_hi,
    out_lo,
):
    n, cols, channels, depth = inner.shape
    rows = n + 2
    scale = 1.0 / (8 * channels)
    lane = lanes((channels, depth))
    out[...] = core[...]
    corners = [joined(side[4].astype(jnp.float32), 2, 2) for side in (side_lo, side_hi)]
    for k, (ref, rim, keep, flag, y) in enumerate(
        zip((f_lo, f_hi), (y_lo, y_hi), (w_lo, w_hi), mesh_flags(), (0, cols - 1))
    ):
        near = joined(rim[rows].astype(jnp.float32), rows, rows)
        values = [corners[0][k : k + 1], *(near[x : x + 1] for x in range(rows)), corners[1][k : k + 1]]
        beyond = [ref[x] for x in range(rows + 2)]
        g = [field.astype(jnp.float32) * (value * flag) for field, value in zip(beyond, values)]
        column = column_of(core, y) + rim_rows(g, inner, edge, y, lane, scale)
        g = [
            at[0][at[1], y].astype(jnp.float32) * start_at(start, x_lo, x_hi, x, y)
            for x, at in enumerate(field_at(inner, edge, x) for x in range(rows + 2))
        ]
        image = [
            close_column((g[x] + g[x + 1]) + (g[x + 1] + g[x + 2]), lane, beyond[x + 1])
            for x in range(rows)
        ]
        theirs = joined(ref[rows + 2].astype(jnp.float32), rows, rows)
        keep[...] = (theirs + jnp.concatenate(image, axis=0) * scale) * flag
        for x in range(rows):
            out[x, y : y + 1, :] = column[x : x + 1]
    for ref, x in ((out_hi, rows - 1), (out_lo, 0)):
        ref[0:1] = w_lo[x : x + 1]
        ref[1 : 1 + cols] = out[x]
        ref[1 + cols : 2 + cols] = w_hi[x : x + 1]


PRODUCTS = ((0, 0), (0, 1), (1, 1), (0, 2), (1, 2))


def add_products(sums, which, fields):
    for k in which:
        a, b = PRODUCTS[k]
        p, e = two_prod(fields[a], fields[b])
        s, t = two_sum(sums[k][0], p)
        sums[k] = (s, sums[k][1] + (t + e))


def second_core_kernel(
    inner, edge, f_lo, f_hi, start, first, w_lo, w_hi, ridge, out, grams, smooth
):
    n, cols, channels, depth = inner.shape
    scale = 1.0 / (8 * channels)

    def stage_y(k, carry):
        along_y(smooth, k + 1, inner, k, row_of(first, k + 1))
        return carry

    lax.fori_loop(0, n, stage_y, 0)
    along_y(smooth, 0, edge, 1, row_of(first, 0))
    along_y(smooth, n + 1, edge, 2, row_of(first, n + 1))

    def stage_x(k, carry):
        image = along_x(smooth, k + 1, (True, True), inner, k, scale)
        out[k + 1] = ridge[k + 1] * first[k + 1] + image
        return carry

    lax.fori_loop(0, n, stage_x, 0)
    for x, row, ends in ((0, 1, (False, True)), (n + 1, 2, (True, False))):
        out[x] = ridge[x] * first[x] + along_x(smooth, x, ends, edge, row, scale)
    zero = jnp.zeros((cols, depth), jnp.float32)
    sums = [(zero, zero) for _ in PRODUCTS]
    for x in range(n + 2):
        add_products(sums, range(5), (start[x], first[x], out[x]))
    rows = n + 2
    lane = lanes((channels, depth))
    flags = mesh_flags()
    added = []
    for ref, rim, flag, y in ((f_lo, w_lo, flags[0], 0), (f_hi, w_hi, flags[1], cols - 1)):
        g = [ref[x + 1].astype(jnp.float32) * (rim[x : x + 1] * flag) for x in range(rows)]
        added.append(rim_rows([None, *g, None], inner, edge, y, lane, scale))
    columns = [jnp.concatenate([column_of(ref, y) for y in (0, cols - 1)]) for ref in (start, first)]
    add_products(sums, (3, 4), (*columns, jnp.concatenate(added, axis=0)))
    for delta, y in zip(added, (0, cols - 1)):
        for x in range(rows):
            out[x, y : y + 1, :] = out[x, y : y + 1, :] + delta[x : x + 1]
    for k, (s, e) in enumerate(sums):
        grams[2 * k] = s
        grams[2 * k + 1] = e


def second_rim_kernel(
    edge, f_lo, f_hi, start, first, x_lo, x_hi, core, grams, out, share
):
    rows, cols, depth = start.shape
    channels = edge.shape[2]
    scale = 1.0 / (8 * channels)
    lane = lanes((channels, depth))
    flags = mesh_flags()
    out[...] = core[...]
    sums = [(grams[2 * k], grams[2 * k + 1]) for k in range(5)]
    for rim, at, row, x, far in ((x_lo, 0, 1, 0, 0), (x_hi, 3, 2, rows - 1, rows + 1)):

        def product(y):
            value = rim[y : y + 1]
            if y == 0:
                return f_lo[far].astype(jnp.float32) * (value * flags[0])
            if y == cols + 1:
                return f_hi[far].astype(jnp.float32) * (value * flags[1])
            return edge[at, y - 1].astype(jnp.float32) * value

        parts = []
        here = product(1)
        pair = product(0) + here
        for y in range(cols):
            following = product(y + 2)
            pair_next = here + following
            parts.append(close_column(pair + pair_next, lane, edge[row, y]))
            here = following
            pair = pair_next
        delta = jnp.concatenate(parts, axis=0) * scale
        add_products(sums, (3, 4), (start[x], first[x], delta))
        out[x] = out[x] + delta
    lane = lanes((8, 128))
    line = lax.broadcasted_iota(jnp.int32, (8, 128), 0)

    def fold(s, e, axis, steps):
        for step in steps:
            t, d = two_sum(s, pltpu.roll(s, step, axis))
            s, e = (t, (e + pltpu.roll(e, step, axis)) + d)
        return s, e

    total = jnp.zeros((8, 128), jnp.float32)
    error = jnp.zeros((8, 128), jnp.float32)
    for k, (s, e) in enumerate(sums):
        while s.shape[0] > 8:
            half = s.shape[0] // 2
            t, d = two_sum(s[:half], s[half:])
            s, e = (t, e[:half] + e[half:] + d)
        while s.shape[1] > 128:
            half = s.shape[1] // 2
            t, d = two_sum(s[:, :half], s[:, half:])
            s, e = (t, e[:, :half] + e[:, half:] + d)
        s, e = fold(s, e, 0, (4, 2, 1))
        total = jnp.where(line == k, s, total)
        error = jnp.where(line == k, e, error)
    total, error = fold(total, error, 1, (64, 32, 16, 8, 4, 2, 1))
    placed = jnp.where(lane == line, total, 0.0) + jnp.where(lane == line + 8, error, 0.0)
    share[...] = jnp.sum(placed, axis=0, keepdims=True)


def final_kernel(shares, start, first, second, solution_out, residual_out):
    s = shares[...]
    e = jnp.zeros_like(s)
    while s.shape[0] > 8:
        half = s.shape[0] // 2
        t, d = two_sum(s[:half], s[half:])
        s, e = (t, e[:half] + e[half:] + d)
    for step in (4, 2, 1):
        t, d = two_sum(s, pltpu.roll(s, step, 0))
        s, e = (t, (e + pltpu.roll(e, step, 0)) + d)
    lane = lax.broadcasted_iota(jnp.int32, s.shape, 1)

    def pick(value, k):
        return jnp.broadcast_to(
            jnp.sum(jnp.where(lane == k, value, 0.0), axis=1, keepdims=True), s.shape
        )

    g00, g01, g11, g02, g12 = [
        two_sum(pick(s, k), pick(e, k) + pick(s, 8 + k)) for k in range(5)
    ]
    alpha = g00[0] / g01[0]
    fresh = pair_add(pair_add(g00, pair_scale(g01, -2.0 * alpha)), pair_scale(pair_scale(g11, alpha), alpha))
    grow = 1.0 + fresh[0] / g00[0]
    curve = pair_add(
        pair_add(
            pair_scale(pair_scale(g01, grow), grow),
            pair_scale(pair_scale(pair_add(g02, g11), -alpha), grow),
        ),
        pair_scale(pair_scale(g12, alpha), alpha),
    )
    beta = fresh[0] / curve[0]
    near = (alpha + beta * grow)[0:1, 0:1]
    far = (alpha * beta)[0:1, 0:1]
    for x in range(start.shape[0]):
        w0, w1, w2 = (start[x], first[x], second[x])
        solution_out[x] = near * w0 - far * w1
        residual_out[x] = (w0 - near * w1) + far * w2


def per_device(features, conv_weight, conv_bias, occupancy, block_ids, ridge, target):
    rows, cols, channels, depth = features.shape
    f32, bf16 = (jnp.float32, jnp.bfloat16)
    vmem = pl.BlockSpec(memory_space=pltpu.VMEM)

    def call(kernel, args, outs, scratch, limit, name):
        return pl.pallas_call(
            kernel,
            out_shape=[jax.ShapeDtypeStruct(shape, dtype) for shape, dtype in outs],
            in_specs=[vmem for _ in args],
            out_specs=[vmem for _ in outs],
            scratch_shapes=[pltpu.VMEM(shape, dtype) for shape, dtype in scratch],
            compiler_params=pltpu.CompilerParams(vmem_limit_bytes=limit << 20),
            name=name,
        )(*args)

    plane = ((rows, cols, depth), f32)
    blocks = block_ids.reshape(-1, block_ids.shape[3])
    edge_column = ((rows + 1, channels, depth), bf16)
    edge_rows = ((2 * cols + 3, channels, depth), bf16)
    outs = [plane, plane, edge_column, edge_column, edge_rows, edge_rows]
    weight_mask, residual, y_hi, y_lo, x_hi, x_lo = pl.pallas_call(
        prep_kernel,
        out_shape=[jax.ShapeDtypeStruct(shape, dtype) for shape, dtype in outs],
        in_specs=[pl.BlockSpec(memory_space=pl.ANY)] * 4,
        out_specs=[pl.BlockSpec(memory_space=pl.ANY)] * 6,
        scratch_shapes=[
            pltpu.VMEM(blocks.shape, jnp.int32),
            pltpu.VMEM(occupancy.shape, jnp.int32),
            pltpu.VMEM(target.shape, f32),
            pltpu.VMEM((2, rows, 1, channels, depth), bf16),
            pltpu.VMEM((blocks.shape[0], depth // block_ids.shape[2]), f32),
            pltpu.VMEM((2, *edge_rows[0]), bf16),
            *(pltpu.VMEM(shape, dtype) for shape, dtype in outs[:4]),
            pltpu.SemaphoreType.DMA((17,)),
        ],
        compiler_params=pltpu.CompilerParams(vmem_limit_bytes=PREP_LIMIT << 20),
        name="prep",
    )(features, blocks, occupancy, target)
    y_lo, y_hi = (shift(y_hi, "sy", 1), shift(y_lo, "sy", -1))
    x_lo, x_hi = (shift(x_hi, "sx", 1), shift(x_lo, "sx", -1))
    wide, bias, weight_mask = call(
        weights_kernel,
        (conv_weight, conv_bias[None], weight_mask),
        [((12 * channels, 16 * channels), bf16), ((channels, depth), f32), plane],
        [],
        8,
        "weights",
    )
    grid_scratch = ((rows, cols + 2, channels, depth), bf16)
    kept_grid = ((4, cols + 2, channels, depth), bf16)
    inner_shape = (rows - 2, cols, channels, depth)
    edge_shape = (4, cols, channels, depth)
    side_shape = (5, channels, depth)
    side_hi, side_lo = call(
        sides_kernel,
        (y_lo, y_hi, bias),
        [(side_shape, bf16), (side_shape, bf16)],
        [],
        4,
        "sides",
    )
    side_lo, side_hi = (shift(side_hi, "sx", 1), shift(side_lo, "sx", -1))
    inner, kept = call(
        conv_inner_kernel,
        (features, y_lo, y_hi, weight_mask, wide, bias),
        [(inner_shape, bf16), kept_grid],
        [grid_scratch],
        12,
        "conv_inner",
    )
    column = ((rows + 3, channels, depth), bf16)
    edge, f_hi, f_lo = call(
        conv_edge_kernel,
        (
            kept,
            x_lo,
            x_hi,
            side_lo,
            side_hi,
            weight_mask,
            wide,
            bias,
            inner,
            residual,
            ridge,
        ),
        [(edge_shape, bf16), column, column],
        [kept_grid, ((4, cols, depth), f32)],
        12,
        "conv_edge",
    )
    f_lo, f_hi = (shift(f_hi, "sy", 1), shift(f_lo, "sy", -1))
    (core,) = call(
        first_core_kernel,
        (inner, edge, residual, x_lo, x_hi, ridge),
        [plane],
        [((rows + 2, cols, channels, depth), f32), ((2, cols, depth), f32)],
        10,
        "first_core",
    )
    line = ((rows, depth), f32)
    row = ((cols + 2, depth), f32)
    first, w_lo, w_hi, r_hi, r_lo = call(
        first_rim_kernel,
        (inner, edge, f_lo, f_hi, y_lo, y_hi, x_lo, x_hi, side_lo, side_hi, residual, core),
        [plane, line, line, row, row],
        [],
        4,
        "first_rim",
    )
    r_lo, r_hi = (shift(r_hi, "sx", 1), shift(r_lo, "sx", -1))
    core, grams = call(
        second_core_kernel,
        (inner, edge, f_lo, f_hi, residual, first, w_lo, w_hi, ridge),
        [plane, ((2 * len(PRODUCTS), cols, depth), f32)],
        [((rows, cols, channels, depth), f32)],
        10,
        "second_core",
    )
    second, share = call(
        second_rim_kernel,
        (edge, f_lo, f_hi, residual, first, r_lo, r_hi, core, grams),
        [plane, ((1, 128), f32)],
        [],
        4,
        "second_rim",
    )

    peers = lax.axis_size("sx") * lax.axis_size("sy")
    shares = lax.all_to_all(jnp.broadcast_to(share[None], (peers, 1, 128)), AXES, 0, 0)
    return tuple(
        call(
            final_kernel,
            (shares.reshape(peers, 128), residual, first, second),
            [plane, plane],
            [],
            8,
            "final",
        )
    )


def solution(mesh):
    placed = (
        P("sx", "sy", None, None),
        P(),
        P(),
        P("sx", "sy", None),
        P("sx", "sy", None, None),
        P("sx", "sy", None),
        P("sx", "sy", None),
    )
    return jax.shard_map(
        per_device,
        mesh=mesh,
        in_specs=placed,
        out_specs=(P("sx", "sy", None), P("sx", "sy", None)),
        check_vma=False,
    )
```
